32 devices in a mesh: rep: 8 (over z, y), voc: 4 (over x, core).
Axes of the slice: x: 2, y: 2, z: 4, core: 2. Of those that a mesh axis runs over, the one named last changes fastest.
Arguments:
- token_ids: int32 [8, 1024], P('rep'), may hold values from 0 to 31999
- target_ids: int32 [8, 1024], P('rep'), may hold values from 0 to 31999
- embedding: float32 [32000, 512], P('voc'), may hold values from -0.6 to 0.6
- w_qkv: float32 [512, 1536], P('voc'), may hold values from -0.25 to 0.25
- w_out: float32 [512, 512], P('voc'), may hold values from -0.5 to 0.5
- w_up: float32 [512, 2048], P('voc'), may hold values from -0.25 to 0.25
- w_down: float32 [2048, 512], P('voc'), may hold values from -0.125 to 0.125
- norm_gains: float32 [3, 512], replicated, may hold values from 0.5 to 1.5
- embed_mom: bfloat16 [32000, 512], P('voc'), may hold values from -0.0019989014 to 0.0019989014
- qkv_mom: bfloat16 [512, 1536], P('voc'), may hold values from -0.0019989014 to 0.0019989014
- out_mom: bfloat16 [512, 512], P('voc'), may hold values from -0.0019989014 to 0.0019989014
- up_mom: bfloat16 [512, 2048], P('voc'), may hold values from -0.0019989014 to 0.0019989014
- down_mom: bfloat16 [2048, 512], P('voc'), may hold values from -0.0019989014 to 0.0019989014
- gain_mom: bfloat16 [3, 512], replicated, may hold values from -0.0019989014 to 0.0019989014
- embed_err: bfloat16 [8, 32000, 512], P('rep', 'voc'), may hold values from -0.0019989014 to 0.0019989014
- qkv_err: bfloat16 [8, 512, 1536], P('rep', 'voc'), may hold values from -0.0019989014 to 0.0019989014
- out_err: bfloat16 [8, 512, 512], P('rep', 'voc'), may hold values from -0.0019989014 to 0.0019989014
- up_err: bfloat16 [8, 512, 2048], P('rep', 'voc'), may hold values from -0.0019989014 to 0.0019989014
- down_err: bfloat16 [8, 2048, 512], P('rep', 'voc'), may hold values from -0.0019989014 to 0.0019989014
- embed_factor: float32 [4, 512, 8], P('voc'), may hold values from -6 to 6
- qkv_factor: float32 [4, 1536, 8], P('voc'), may hold values from -6 to 6
- out_factor: float32 [4, 512, 8], P('voc'), may hold values from -6 to 6
- up_factor: float32 [4, 2048, 8], P('voc'), may hold values from -6 to 6
- down_factor: float32 [4, 512, 8], P('voc'), may hold values from -6 to 6
Outputs:
- losses: float32 [8], P('rep')
- norms: float32 [8], P('rep')
- embed_update: float32 [32000, 512], P('voc')
- new_qkv: float32 [512, 1536], P('voc')
- new_out: float32 [512, 512], P('voc')
- new_up: float32 [512, 2048], P('voc')
- new_down: float32 [2048, 512], P('voc')
- gain_update: float32 [3, 512], replicated
- next_embed_mom: float32 [32000, 512], P('voc')
- next_qkv_mom: float32 [512, 1536], P('voc')
- next_out_mom: float32 [512, 512], P('voc')
- next_up_mom: float32 [512, 2048], P('voc')
- next_down_mom: float32 [2048, 512], P('voc')
- next_gain_mom: float32 [3, 512], replicated
- next_embed_err: float32 [8, 32000, 512], P('rep', 'voc')
- next_qkv_err: float32 [8, 512, 1536], P('rep', 'voc')
- next_out_err: float32 [8, 512, 512], P('rep', 'voc')
- next_up_err: float32 [8, 512, 2048], P('rep', 'voc')
- next_down_err: float32 [8, 2048, 512], P('rep', 'voc')
- next_embed_factor: float32 [4, 512, 8], P('voc')
- next_qkv_factor: float32 [4, 1536, 8], P('voc')
- next_out_factor: float32 [4, 512, 8], P('voc')
- next_up_factor: float32 [4, 2048, 8], P('voc')
- next_down_factor: float32 [4, 512, 8], P('voc')
The draws below stay inside these ranges and needn't reach their ends.
All inputs are finite; a program needn't handle non-finite values.
Results may differ from the reference program's by a relative error of at most 0.009.
The reference program's roundings to bfloat16 on the way count: a program that leaves them out, or rounds other values in their place, can miss the bound.
Values may be sent and summed in bfloat16 or wider, within the bound.
A program may use at most 320 MiB of HBM per device.

```python
import math
import jax
import jax.numpy as jnp
import numpy as np
from jax import lax

D = 512
HEADS = 8
HD = 64
FF = 2048
V = 32000
RANK = 8
LEN = 1024
SEQ_DEV = 1
SEQS = 8
N_REP = 8
N_VOC = 4


def set_ends(drawn, own_key, smallest, high):
    spot = [jax.random.randint(jax.random.fold_in(own_key, axis), (), 0, length) for axis, length in enumerate(drawn.shape)]
    widest = drawn.shape.index(max(drawn.shape))
    beside = spot[:widest] + [(spot[widest] + 1) % drawn.shape[widest]] + spot[widest + 1:]
    return drawn.at[tuple(spot)].set(smallest).at[tuple(beside)].set(high)


def level_of(key, shape, shards, low, largest):
    loudness = 1.0
    for axis_at, parts in shards:
        heights = jax.random.uniform(jax.random.fold_in(jax.random.fold_in(key, 6), axis_at), (parts,), jnp.float32, low / len(shards), largest / len(shards))
        loudness = loudness * jnp.repeat(jnp.exp(heights), shape[axis_at] // parts).reshape((-1,) + (1,) * (len(shape) - 1 - axis_at))
    return loudness


def rank_bounds(count, slope):
    portions = [(1 << 20) // math.isqrt(rank ** slope) + 1 for rank in range(1, count + 1)]
    deviation = 1 + sum(portions) // (1 << 30)
    return np.cumsum(np.array([max(1, weight // deviation) for weight in portions]))


def skewed_ids(own_key, dims, amount, lean):
    grid = rank_bounds(amount, lean)
    pick = jax.random.randint(jax.random.fold_in(own_key, 1), dims, 0, int(grid[amount - 1]))
    standing = jnp.searchsorted(jnp.asarray(grid, jnp.int32), pick, side="right")
    return jax.random.permutation(jax.random.fold_in(own_key, 2), amount)[standing].astype(jnp.int32)


def normal_values(own_key, shape, scale, bound, cuts=(), held_as=jnp.bfloat16):
    result = jax.random.normal(own_key, shape, jnp.float32) * scale
    if len(cuts) > 0:
        result = level_of(own_key, shape, cuts, -0.22, 0.18) * result
    return jnp.clip(result, min=-bound, max=bound).astype(held_as)


def setup_inputs(seed: int = 0) -> dict:
    splits = jax.random.split(jax.random.key(seed), 25)
    return {
        "token_ids": set_ends(skewed_ids(splits[0], (SEQS, LEN), V, 2), jax.random.fold_in(splits[0], 3), 0, V - 1).astype(jnp.int32),
        "target_ids": set_ends(skewed_ids(splits[1], (SEQS, LEN), V, 2), jax.random.fold_in(splits[1], 3), 0, V - 1).astype(jnp.int32),
        "embedding": normal_values(splits[2], (V, D), 0.1, 0.6, ((0, 4),), jnp.float32),
        "w_qkv": normal_values(splits[3], (D, 3 * D), D ** -0.5, 0.25, ((0, 4),), jnp.float32),
        "w_out": normal_values(splits[4], (D, D), (D // 4) ** -0.5, 0.5, ((0, 4),), jnp.float32),
        "w_up": normal_values(splits[5], (D, FF), D ** -0.5, 0.25, ((0, 4),), jnp.float32),
        "w_down": normal_values(splits[6], (FF, D), FF ** -0.5, 0.125, ((0, 4),), jnp.float32),
        "norm_gains": jnp.clip(1.0 + 0.1 * jax.random.normal(splits[7], (3, D), jnp.float32), 0.5, 1.5),
        "embed_mom": normal_values(splits[8], (V, D), 0.0003, 0.0019989014, ((0, 4),)),
        "qkv_mom": normal_values(splits[9], (D, 3 * D), 0.0003, 0.0019989014, ((0, 4),)),
        "out_mom": normal_values(splits[10], (D, D), 0.0003, 0.0019989014, ((0, 4),)),
        "up_mom": normal_values(splits[11], (D, FF), 0.0003, 0.0019989014, ((0, 4),)),
        "down_mom": normal_values(splits[12], (FF, D), 0.0003, 0.0019989014, ((0, 4),)),
        "gain_mom": normal_values(splits[13], (3, D), 0.0003, 0.0019989014),
        "embed_err": normal_values(splits[14], (N_REP, V, D), 0.0003, 0.0019989014, ((0, 8), (1, 4))),
        "qkv_err": normal_values(splits[15], (N_REP, D, 3 * D), 0.0003, 0.0019989014, ((0, 8), (1, 4))),
        "out_err": normal_values(splits[16], (N_REP, D, D), 0.0003, 0.0019989014, ((0, 8), (1, 4))),
        "up_err": normal_values(splits[17], (N_REP, D, FF), 0.0003, 0.0019989014, ((0, 8), (1, 4))),
        "down_err": normal_values(splits[18], (N_REP, FF, D), 0.0003, 0.0019989014, ((0, 8), (1, 4))),
        "embed_factor": normal_values(splits[19], (N_VOC, D, RANK), 1.0, 6.0, ((0, 4),), jnp.float32),
        "qkv_factor": normal_values(splits[20], (N_VOC, 3 * D, RANK), 1.0, 6.0, ((0, 4),), jnp.float32),
        "out_factor": normal_values(splits[21], (N_VOC, D, RANK), 1.0, 6.0, ((0, 4),), jnp.float32),
        "up_factor": normal_values(splits[22], (N_VOC, FF, RANK), 1.0, 6.0, ((0, 4),), jnp.float32),
        "down_factor": normal_values(splits[23], (N_VOC, D, RANK), 1.0, 6.0, ((0, 4),), jnp.float32),
    }


@jax.custom_vjp
def low(v):
    return lax.optimization_barrier(v.astype(jnp.bfloat16)).astype(jnp.float32)

@jax.custom_vjp
def low_back(v):
    return v

def low_keep(v):
    return (low(v), None)

def low_pass(kept, grad):
    return (grad,)

def back_keep(v):
    return (v, None)

def back_low(kept, grad):
    return (low(grad),)
low.defvjp(low_keep, low_pass)
low_back.defvjp(back_keep, back_low)
HIGHEST_PREC = lax.Precision.HIGHEST
MOMENTUM = 0.9
LEARN_RATE = 10.0
CLIP_NORM = 1.0
ZLOSS_WEIGHT = 0.01

def rms_norm(values, weight):
    return values * lax.rsqrt(lax.optimization_barrier(jnp.mean(values * values, axis=-1, keepdims=True)) + 1e-06) * weight

def rotate(heads_in, length):
    halfway = heads_in.shape[-1] // 2
    positions = jnp.arange(length).astype(jnp.float32)
    inverse = 10000.0 ** (-jnp.arange(halfway).astype(jnp.float32) / halfway)
    angles = positions[:, None] * inverse[None, :]
    cosine_table = jnp.cos(angles)[:, None, :]
    sine_table = jnp.sin(angles)[:, None, :]
    first_half = heads_in[..., :halfway]
    second_half = heads_in[..., halfway:]
    return jnp.concatenate([first_half * cosine_table - second_half * sine_table, first_half * sine_table + second_half * cosine_table], axis=-1)

def orthonormal(matrix):
    columns = []
    for column_pos in range(matrix.shape[1]):
        vector = matrix[:, column_pos]
        for earlier in columns:
            vector = vector - jnp.sum(earlier * vector) * earlier
        vector = vector * lax.rsqrt(jnp.sum(vector * vector) + 1e-20)
        columns.append(vector)
    return jnp.stack(columns, axis=1)

def forward(params, token_rows, target_rows):
    embedding, w_qkv, w_out, w_up, w_down, norm_gains = params
    vocab_table = low(embedding)
    proj_qkv, proj_out, proj_up, proj_down = (low(w_qkv), low(w_out), low(w_up), low(w_down))
    seq_count, length = token_rows.shape
    tok_count = seq_count * length
    stream_in = vocab_table[token_rows.reshape(-1)]
    normed_in = low(rms_norm(stream_in, norm_gains[0]))
    packed = low_back(jnp.dot(normed_in, proj_qkv, precision=HIGHEST_PREC))
    packed = packed.reshape(seq_count, length, 3, HEADS, HD)
    queries = low(rotate(packed[:, :, 0], length))
    keys_all = low(rotate(packed[:, :, 1], length))
    values_all = low(packed[:, :, 2])
    scores = low_back(jnp.einsum('sqhd,skhd->shqk', queries, keys_all, precision=HIGHEST_PREC) * HD ** (-0.5))
    causal = jnp.arange(length)[:, None] >= jnp.arange(length)[None, :]
    attn_probs = low(jax.nn.softmax(jnp.where(causal, scores, -1e+30), axis=-1))
    mixed = low(low_back(jnp.einsum('shqk,skhd->sqhd', attn_probs, values_all, precision=HIGHEST_PREC)))
    stream_mid = stream_in + low_back(jnp.dot(mixed.reshape(tok_count, HEADS * HD), proj_out, precision=HIGHEST_PREC))
    normed_mid = low(rms_norm(stream_mid, norm_gains[1]))
    hidden = low_back(jnp.dot(normed_mid, proj_up, precision=HIGHEST_PREC))
    active = low(jax.nn.gelu(hidden, approximate=False))
    stream_out = stream_mid + low_back(jnp.dot(active, proj_down, precision=HIGHEST_PREC))
    normed_out = low(rms_norm(stream_out, norm_gains[2]))
    logits = low_back(jnp.dot(normed_out, vocab_table.T, precision=HIGHEST_PREC))
    partition = jax.nn.logsumexp(logits, axis=-1)
    picked = jnp.take_along_axis(logits, target_rows.reshape(-1, 1), axis=1)[:, 0]
    return jnp.mean(partition - picked) + ZLOSS_WEIGHT * jnp.mean(partition * partition)

def compress(clipped_grad, error_in, start_factor):
    block_rows = clipped_grad.shape[1] // N_VOC
    matrix = (clipped_grad + error_in.astype(jnp.float32)).reshape(N_REP, N_VOC, block_rows, -1)
    left_sum = jnp.einsum('wvrc,vck->vrk', matrix, start_factor, precision=HIGHEST_PREC)
    basis = jax.vmap(orthonormal)(left_sum)
    right_mean = jnp.einsum('wvrc,vrk->vck', matrix, basis, precision=HIGHEST_PREC) / N_REP
    mean_grad = jnp.einsum('vrk,vck->vrc', basis, right_mean, precision=HIGHEST_PREC).reshape(N_VOC * block_rows, -1)
    projected = jnp.einsum('vrk,wvrc->wvkc', basis, matrix, precision=HIGHEST_PREC)
    new_error = matrix - jnp.einsum('vrk,wvkc->wvrc', basis, projected, precision=HIGHEST_PREC)
    return (mean_grad, new_error.reshape(N_REP, N_VOC * block_rows, -1), right_mean)

def step_weight(weight, momentum_in, mean_grad):
    new_momentum = MOMENTUM * momentum_in.astype(jnp.float32) + mean_grad
    change = -LEARN_RATE * new_momentum
    return (weight + change, new_momentum, change)

def reference(token_ids, target_ids, embedding, w_qkv, w_out, w_up, w_down, norm_gains, embed_mom, qkv_mom, out_mom, up_mom, down_mom, gain_mom, embed_err, qkv_err, out_err, up_err, down_err, embed_factor, qkv_factor, out_factor, up_factor, down_factor):
    params = (embedding, w_qkv, w_out, w_up, w_down, norm_gains)
    token_groups = token_ids.reshape(N_REP, SEQ_DEV, LEN)
    target_groups = target_ids.reshape(N_REP, SEQ_DEV, LEN)

    def worker(pair):
        loss_value, pull_back = jax.vjp(lambda weights_in: forward(weights_in, pair[0], pair[1]), params)
        grads = pull_back(jnp.ones_like(loss_value))[0]
        squares = sum((jnp.sum(grad_part * grad_part) for grad_part in grads))
        norm_value = jnp.sqrt(squares)
        clip_factor = jnp.minimum(1.0, CLIP_NORM / norm_value)
        return (loss_value, norm_value, tuple((grad_part * clip_factor for grad_part in grads)))
    losses, norms, clipped = lax.map(worker, (token_groups, target_groups))
    errors = (embed_err, qkv_err, out_err, up_err, down_err)
    factors = (embed_factor, qkv_factor, out_factor, up_factor, down_factor)
    moments = (embed_mom, qkv_mom, out_mom, up_mom, down_mom)
    results = [compress(clipped[member], errors[member], factors[member]) for member in range(5)]
    updates = [step_weight(params[member], moments[member], results[member][0]) for member in range(5)]
    new_gains, next_gain_mom, gain_change = step_weight(norm_gains, gain_mom, lax.optimization_barrier(jnp.mean(clipped[5], axis=0)))
    return (losses, norms, updates[0][2], updates[1][0], updates[2][0], updates[3][0], updates[4][0], gain_change, updates[0][1], updates[1][1], updates[2][1], updates[3][1], updates[4][1], next_gain_mom, results[0][1], results[1][1], results[2][1], results[3][1], results[4][1], results[0][2], results[1][2], results[2][2], results[3][2], results[4][2])
```

```python
import functools

import jax
import jax.numpy as jnp
from jax import lax
from jax.experimental import pallas as pl
from jax.experimental.pallas import tpu as pltpu
from jax.sharding import PartitionSpec as P

HEADS = 8
HD = 64


HIGHEST_PREC = lax.Precision.HIGHEST
MOMENTUM = 0.9
LEARN_RATE = 10.0
CLIP_NORM = 1.0
ZLOSS_WEIGHT = 0.01


TB = 1024
RK = 8
F32 = jnp.float32
BF16 = jnp.bfloat16
MESH_ID = pl.DeviceIdType.MESH


def round_up(value, step):
    return (value + step - 1) // step * step


def halves(value):
    high = value.astype(BF16).astype(F32)
    return high, value - high


def dims_of(value, contract_left, contract_right):
    return (((contract_left,), (contract_right,)), ((), ()))


def left_of(matrix, start_t):
    s_high, s_low = halves(start_t)
    both = jnp.concatenate([s_high, s_low], axis=0).astype(BF16)
    high = matrix.astype(BF16)
    low = (matrix - high.astype(F32)).astype(BF16)
    nt = (((1,), (1,)), ((), ()))
    main = lax.dot_general(both, high, nt, preferred_element_type=F32)
    rest = lax.dot_general(s_high.astype(BF16), low, nt, preferred_element_type=F32)
    return main[:RK] + main[RK:] + rest


def left_of_bf16(matrix, start_t):
    s_high, s_low = halves(start_t)
    both = jnp.concatenate([s_high, s_low], axis=0).astype(BF16)
    main = lax.dot_general(both, matrix, (((1,), (1,)), ((), ())), preferred_element_type=F32)
    return main[:RK] + main[RK:]


def right_of(basis_t, matrix):
    b_high, b_low = halves(basis_t)
    both = jnp.concatenate([b_high, b_low], axis=0).astype(BF16)
    high = matrix.astype(BF16)
    low = (matrix - high.astype(F32)).astype(BF16)
    main = jnp.dot(both, high, preferred_element_type=F32)
    rest = jnp.dot(b_high.astype(BF16), low, preferred_element_type=F32)
    return main[:RK] + main[RK:] + rest


def product_of(basis_t, right_t):
    b_high, b_low = halves(basis_t)
    r_high, r_low = halves(right_t)
    zero_b, zero_r = jnp.zeros_like(b_high), jnp.zeros_like(r_high)
    left = jnp.concatenate([b_high, b_low, b_high, zero_b], axis=0).astype(BF16)
    right = jnp.concatenate([r_high, r_high, r_low, zero_r], axis=0).astype(BF16)
    return lax.dot_general(left, right, (((0,), (0,)), ((), ())), preferred_element_type=F32)


def keep_rows(value, first_row, rows):
    at = first_row + lax.broadcasted_iota(jnp.int32, value.shape, 0)
    return jnp.where(at < rows, value, jnp.zeros_like(value))


def fold_squares(value):
    squares = value * value
    rows, columns = value.shape
    by_sublane = jnp.sum(squares.reshape(rows // 8, 8, columns), axis=0)
    total = by_sublane[:, :512]
    for start in range(512, columns, 512):
        total = total + by_sublane[:, start : start + 512]
    return total


def small_places(rows_list):
    places, at = [], 0
    for rows in rows_list:
        places.append(at)
        at += round_up(rows, 128)
    return places, at


def sketch_kernel(rows, row_list, *refs):
    grads, errs, starts = refs[0:5], refs[5:10], refs[10:15]
    gq_ref, eq_ref, gs_ref, es_ref, sq_ref = refs[15:20]
    step = pl.program_id(0)
    places, _ = small_places(row_list)

    @pl.when(step == 0)
    def _():
        gs_ref[...] = jnp.zeros_like(gs_ref)
        es_ref[...] = jnp.zeros_like(es_ref)
        total = jnp.zeros(sq_ref.shape, F32)
        for k in range(4):
            grad = grads[k + 1][...]
            start_t = starts[k + 1][...]
            at = pl.ds(places[k], row_list[k])
            gs_ref[:, at] = left_of(grad, start_t)
            es_ref[:, at] = left_of_bf16(errs[k + 1][...], start_t)
            total = total + fold_squares(grad)
        sq_ref[...] = total

    start_t = starts[0][...]
    grad = keep_rows(grads[0][...], step * TB, rows)
    err = keep_rows(errs[0][...].astype(F32), step * TB, rows).astype(BF16)
    gq_ref[...] = left_of(grad, start_t)
    eq_ref[...] = left_of_bf16(err, start_t)
    sq_ref[...] += fold_squares(grad)


def whole(shape):
    return pl.BlockSpec(shape, lambda *_: (0,) * len(shape))


def sketch(grads, errs, starts_t):
    rows, width = grads[0].shape
    blocks = pl.cdiv(rows, TB)
    row_list = [g.shape[0] for g in grads[1:]]
    _, small = small_places(row_list)
    block = pl.BlockSpec((TB, width), lambda i: (i, 0))
    lanes = pl.BlockSpec((RK, TB), lambda i: (0, i))
    return pl.pallas_call(
        functools.partial(sketch_kernel, rows, row_list),
        grid=(blocks,),
        in_specs=[block]
        + [whole(g.shape) for g in grads[1:]]
        + [block]
        + [whole(e.shape) for e in errs[1:]]
        + [whole(s.shape) for s in starts_t],
        out_specs=[lanes, lanes, whole((RK, small)), whole((RK, small)), whole((8, 512))],
        out_shape=[
            jax.ShapeDtypeStruct((RK, blocks * TB), F32),
            jax.ShapeDtypeStruct((RK, blocks * TB), F32),
            jax.ShapeDtypeStruct((RK, small), F32),
            jax.ShapeDtypeStruct((RK, small), F32),
            jax.ShapeDtypeStruct((8, 512), F32),
        ],
        name="sketch",
    )(*grads, *errs, *starts_t)


def clip_of(norm_tile):
    return jnp.minimum(1.0, CLIP_NORM / norm_tile[0:1, 0:1])


def orthonormal_t(parts):
    row_at = lax.broadcasted_iota(jnp.int32, (RK, 1), 0)
    for row in range(RK):
        total = None
        for part in parts:
            term = part * part[row : row + 1, :]
            for start in range(0, term.shape[1], 128):
                piece = term[:, start : start + 128]
                total = piece if total is None else total + piece
        dots = jnp.sum(total, axis=1, keepdims=True)
        inverse = lax.rsqrt(dots[row : row + 1, :] + 1e-20)
        scale = jnp.where(row_at == row, inverse, 1.0)
        taken = jnp.where(row_at > row, -dots * inverse * inverse, 0.0)
        parts = [part * scale + taken * part[row : row + 1, :] for part in parts]
    return parts


def ring_sum(x, landing, y, send_sem, land_sem, spread_sem, gather_sem, axis, count):
    me = lax.axis_index(axis)
    first = []
    for step in range(1, count):
        peer = lax.rem(me + step, count)
        copy = pltpu.make_async_remote_copy(
            src_ref=x.at[peer],
            dst_ref=landing.at[step],
            send_sem=send_sem.at[step],
            recv_sem=land_sem.at[step],
            device_id={axis: peer},
            device_id_type=MESH_ID,
        )
        copy.start()
        first.append(copy)
    total = x[me]
    for step in range(1, count):
        first[step - 1].wait_recv()
        total = total + landing[step]
    y[me] = total
    second = []
    for step in range(1, count):
        peer = lax.rem(me + step, count)
        copy = pltpu.make_async_remote_copy(
            src_ref=y.at[me],
            dst_ref=y.at[me],
            send_sem=spread_sem.at[step],
            recv_sem=gather_sem.at[step],
            device_id={axis: peer},
            device_id_type=MESH_ID,
        )
        copy.start()
        second.append(copy)
    for copy in first:
        copy.wait_send()
    for step in range(1, count):
        source = lax.rem(me - step + count, count)
        pltpu.make_async_remote_copy(
            src_ref=y.at[source],
            dst_ref=y.at[source],
            send_sem=spread_sem.at[step],
            recv_sem=gather_sem.at[step],
            device_id={axis: source},
            device_id_type=MESH_ID,
        ).wait_recv()
    for copy in second:
        copy.wait_send()


def greet(axes):
    barrier = pltpu.get_barrier_semaphore()
    greeted = 0
    for axis, count in axes:
        me = lax.axis_index(axis)
        for step in range(1, count):
            pl.semaphore_signal(
                barrier,
                inc=1,
                device_id={axis: lax.rem(me + step, count)},
                device_id_type=MESH_ID,
            )
        greeted += count - 1
    pl.semaphore_wait(barrier, greeted)


def basis_kernel(
    workers, shards, row_list, gains_at,
    gq_ref, eq_ref, gs_ref, es_ref, gains_ref, sq_ref,
    ph_ref, phs_ref, gsum_ref, norm_ref,
    x, landing, y, small, sq_all, send_sem, land_sem, spread_sem, gather_sem, sq_send, sq_recv,
):
    greet((("rep", workers), ("voc", shards)))
    shard = lax.axis_index("voc")
    own = jnp.sum(sq_ref[...].reshape(8, 4, 128), axis=1)
    own = jnp.sum(jnp.sum(own, axis=0, keepdims=True), axis=1, keepdims=True)
    sq_all[shard] = jnp.broadcast_to(own, (8, 128))
    copies = []
    for step in range(1, shards):
        peer = lax.rem(shard + step, shards)
        copy = pltpu.make_async_remote_copy(
            src_ref=sq_all.at[shard],
            dst_ref=sq_all.at[shard],
            send_sem=sq_send.at[step],
            recv_sem=sq_recv.at[step],
            device_id={"voc": peer},
            device_id_type=MESH_ID,
        )
        copy.start()
        copies.append(copy)
    gains = gains_ref[...]
    total = jnp.sum(jnp.sum(gains * gains, axis=0, keepdims=True), axis=1, keepdims=True)
    small[...] = jnp.zeros_like(small)
    for step in range(1, shards):
        source = lax.rem(shard - step + shards, shards)
        pltpu.make_async_remote_copy(
            src_ref=sq_all.at[source],
            dst_ref=sq_all.at[source],
            send_sem=sq_send.at[step],
            recv_sem=sq_recv.at[step],
            device_id={"voc": source},
            device_id_type=MESH_ID,
        ).wait_recv()
    for copy in copies:
        copy.wait_send()
    for peer in range(shards):
        total = total + sq_all[peer][0:1, 0:1]
    norm = jnp.sqrt(total)
    norm_ref[...] = jnp.broadcast_to(norm, (8, 128))
    clip = jnp.minimum(1.0, CLIP_NORM / norm)

    chunk = gq_ref.shape[1] // workers
    part = small.shape[1] // workers
    span = gs_ref.shape[1]
    small[:, :span] = clip * gs_ref[...] + es_ref[...]
    small[:, gains_at : gains_at + gains.shape[1]] = clip * gains
    for j in range(workers):
        at = slice(j * chunk, (j + 1) * chunk)
        x[j, :, :chunk] = clip * gq_ref[:, at] + eq_ref[:, at]
        x[j, :, chunk:] = small[:, j * part : (j + 1) * part]
    ring_sum(x, landing, y, send_sem, land_sem, spread_sem, gather_sem, "rep", workers)
    parts = orthonormal_t([y[j, :, :chunk] for j in range(workers)])
    for j in range(workers):
        ph_ref[:, j * chunk : (j + 1) * chunk] = parts[j]
        small[:, j * part : (j + 1) * part] = y[j, :, chunk:]
    gsum_ref[...] = small[:, gains_at : gains_at + gains.shape[1]]
    places, _ = small_places(row_list)
    for place, rows in zip(places, row_list):
        lanes = round_up(rows, 128)
        phs_ref[:, place : place + lanes] = orthonormal_t([small[:, place : place + lanes]])[0]


def basis(sketches, gains, row_list, workers, shards):
    gq, eq, gs, es, sq = sketches
    gains_at = gs.shape[1]
    small = round_up(gains_at + gains.shape[1], workers * 128)
    lanes = (gq.shape[1] + small) // workers
    vmem = pl.BlockSpec(memory_space=pltpu.VMEM)
    return pl.pallas_call(
        functools.partial(basis_kernel, workers, shards, row_list, gains_at),
        in_specs=[vmem] * 6,
        out_specs=[vmem] * 4,
        out_shape=[
            jax.ShapeDtypeStruct(gq.shape, F32),
            jax.ShapeDtypeStruct(gs.shape, F32),
            jax.ShapeDtypeStruct(gains.shape, F32),
            jax.ShapeDtypeStruct((8, 128), F32),
        ],
        scratch_shapes=[
            pltpu.VMEM((workers, RK, lanes), F32),
            pltpu.VMEM((workers, RK, lanes), F32),
            pltpu.VMEM((workers, RK, lanes), F32),
            pltpu.VMEM((RK, small), F32),
            pltpu.VMEM((shards, 8, 128), F32),
        ]
        + [pltpu.SemaphoreType.DMA((workers,))] * 4
        + [pltpu.SemaphoreType.DMA((shards,))] * 2,
        compiler_params=pltpu.CompilerParams(collective_id=1, has_side_effects=True),
        name="basis",
    )(gq, eq, gs, es, gains, sq)


def residual_kernel(rows, row_list, *refs):
    grads, errs = refs[0:5], refs[5:10]
    ph_ref, phs_ref, norm_ref = refs[10:13]
    outs, rights = refs[13:18], refs[18:23]
    kept = refs[23]
    phase, step = pl.program_id(0), pl.program_id(1)
    places, _ = small_places(row_list)
    clip = clip_of(norm_ref[...])
    at = pl.multiple_of(step * TB, TB)

    @pl.when((phase == 0) & (step == 0))
    def _():
        rights[0][...] = jnp.zeros_like(rights[0])
        for k in range(4):
            matrix = clip * grads[k + 1][...] + errs[k + 1][...].astype(F32)
            basis_t = phs_ref[:, places[k] : places[k] + row_list[k]]
            right_t = right_of(basis_t, matrix)
            rights[k + 1][...] = right_t
            outs[k + 1][...] = matrix - product_of(basis_t, right_t)

    @pl.when(phase == 0)
    def _():
        matrix = clip * grads[0][...] + errs[0][...].astype(F32)
        matrix = keep_rows(matrix, step * TB, rows)
        kept[pl.ds(at, TB), :] = matrix
        rights[0][...] += right_of(ph_ref[:, pl.ds(at, TB)], matrix)

    @pl.when(phase == 1)
    def _():
        outs[0][...] = kept[pl.ds(at, TB), :] - product_of(ph_ref[:, pl.ds(at, TB)], rights[0][...])


def residual(grads, errs, ph, phs, norm):
    rows, width = grads[0].shape
    blocks = pl.cdiv(rows, TB)
    row_list = [g.shape[0] for g in grads[1:]]
    block_in = pl.BlockSpec((TB, width), lambda p, i: (jnp.where(p == 0, i, blocks - 1), 0))
    block_out = pl.BlockSpec((TB, width), lambda p, i: (jnp.where(p == 0, 0, i), 0))
    out = pl.pallas_call(
        functools.partial(residual_kernel, rows, row_list),
        grid=(2, blocks),
        in_specs=[block_in]
        + [whole(g.shape) for g in grads[1:]]
        + [block_in]
        + [whole(e.shape) for e in errs[1:]]
        + [whole(ph.shape), whole(phs.shape), whole(norm.shape)],
        out_specs=[block_out]
        + [whole(g.shape) for g in grads[1:]]
        + [whole((RK, g.shape[1])) for g in grads],
        out_shape=[jax.ShapeDtypeStruct(g.shape, F32) for g in grads]
        + [jax.ShapeDtypeStruct((RK, g.shape[1]), F32) for g in grads],
        scratch_shapes=[pltpu.VMEM((blocks * TB, width), F32)],
        compiler_params=pltpu.CompilerParams(vmem_limit_bytes=60 << 20),
        name="residual",
    )(*grads, *errs, ph, phs, norm)
    return out[:5], out[5:]


def mean_right_kernel(workers, r0, r1, r2, r3, r4, out_ref, flat, x, landing, y, s1, s2, s3, s4):
    greet((("rep", workers),))
    part = x.shape[2]
    flat[...] = jnp.zeros_like(flat)
    at = 0
    for ref in (r0, r1, r2, r3, r4):
        flat[:, at : at + ref.shape[1]] = ref[...]
        at += ref.shape[1]
    for j in range(workers):
        x[j] = flat[:, j * part : (j + 1) * part]
    ring_sum(x, landing, y, s1, s2, s3, s4, "rep", workers)
    for j in range(workers):
        out_ref[:, j * part : (j + 1) * part] = y[j] * (1.0 / workers)


def mean_right(rights, workers):
    lanes = round_up(sum(r.shape[1] for r in rights), workers * 128)
    vmem = pl.BlockSpec(memory_space=pltpu.VMEM)
    part = (workers, RK, lanes // workers)
    return pl.pallas_call(
        functools.partial(mean_right_kernel, workers),
        in_specs=[vmem] * 5,
        out_specs=vmem,
        out_shape=jax.ShapeDtypeStruct((RK, lanes), F32),
        scratch_shapes=[pltpu.VMEM((RK, lanes), F32)]
        + [pltpu.VMEM(part, F32)] * 3
        + [pltpu.SemaphoreType.DMA((workers,))] * 4,
        compiler_params=pltpu.CompilerParams(collective_id=2, has_side_effects=True),
        name="mean_right",
    )(*rights)


def update_kernel(row_list, widths, *refs):
    moms, weights = refs[0:5], refs[5:9]
    ph_ref, phs_ref, right_ref = refs[9:12]
    out_moms, outs = refs[12:17], refs[17:22]
    places, _ = small_places(row_list)

    @pl.when(pl.program_id(0) == 0)
    def _():
        at = widths[0]
        for k in range(4):
            basis_t = phs_ref[:, places[k] : places[k] + row_list[k]]
            mean = product_of(basis_t, right_ref[:, at : at + widths[k + 1]])
            at += widths[k + 1]
            moved = MOMENTUM * moms[k + 1][...].astype(F32) + mean
            out_moms[k + 1][...] = moved
            outs[k + 1][...] = weights[k][...] + -LEARN_RATE * moved

    mean = product_of(ph_ref[...], right_ref[:, : widths[0]])
    moved = MOMENTUM * moms[0][...].astype(F32) + mean
    out_moms[0][...] = moved
    outs[0][...] = -LEARN_RATE * moved


def update(moms, weights, ph, phs, right):
    rows, width = moms[0].shape
    blocks = pl.cdiv(rows, TB)
    row_list = [m.shape[0] for m in moms[1:]]
    widths = [m.shape[1] for m in moms]
    block = pl.BlockSpec((TB, width), lambda i: (i, 0))
    out = pl.pallas_call(
        functools.partial(update_kernel, row_list, widths),
        grid=(blocks,),
        in_specs=[block]
        + [whole(m.shape) for m in moms[1:]]
        + [whole(w.shape) for w in weights]
        + [pl.BlockSpec((RK, TB), lambda i: (0, i)), whole(phs.shape), whole(right.shape)],
        out_specs=([block] + [whole(m.shape) for m in moms[1:]]) * 2,
        out_shape=[jax.ShapeDtypeStruct(m.shape, F32) for m in moms] * 2,
        compiler_params=pltpu.CompilerParams(vmem_limit_bytes=60 << 20),
        name="update",
    )(*moms, *weights, ph, phs, right)
    return out[:5], out[5:]


def rms_norm(values, weight):
    return values * lax.rsqrt(jnp.mean(values * values, axis=-1, keepdims=True) + 1e-06) * weight


def rotate(heads_in, length):
    halfway = heads_in.shape[-1] // 2
    positions = jnp.arange(length).astype(jnp.float32)
    inverse = 10000.0 ** (-jnp.arange(halfway).astype(jnp.float32) / halfway)
    angles = positions[:, None] * inverse[None, :]
    cosine_table = jnp.cos(angles)[:, None, :]
    sine_table = jnp.sin(angles)[:, None, :]
    first_half = heads_in[..., :halfway]
    second_half = heads_in[..., halfway:]
    return jnp.concatenate(
        [
            first_half * cosine_table - second_half * sine_table,
            first_half * sine_table + second_half * cosine_table,
        ],
        axis=-1,
    )


def block_scores(rows_query, key_seq, first_row):
    row_count = rows_query.shape[0]
    scores = jnp.einsum(
        "qhd,khd->hqk", rows_query, key_seq, preferred_element_type=jnp.float32
    ) * HD ** (-0.5)
    causal = (first_row + jnp.arange(row_count))[:, None] >= jnp.arange(key_seq.shape[0])[None, :]
    return jnp.where(causal[None], scores, -1e30)


def attend(query_seq, key_seq, value_seq):
    length = query_seq.shape[0]
    block_len = min(512, length)
    mixed_parts, lse_parts = ([], [])
    for first_row in range(0, length, block_len):
        scores = block_scores(query_seq[first_row : first_row + block_len], key_seq, first_row)
        log_total = jax.nn.logsumexp(scores, axis=-1)
        attn_probs = jnp.exp(scores - log_total[..., None]).astype(jnp.bfloat16)
        mixed_parts.append(
            jnp.einsum("hqk,khd->qhd", attn_probs, value_seq, preferred_element_type=jnp.float32)
        )
        lse_parts.append(log_total)
    return (jnp.concatenate(mixed_parts, axis=0), jnp.concatenate(lse_parts, axis=1))


def attend_back(query_seq, key_seq, value_seq, lse_seq, grad_mixed):
    length = query_seq.shape[0]
    block_len = min(512, length)
    grad_query_parts = []
    grad_key = jnp.zeros(key_seq.shape, jnp.float32)
    grad_value = jnp.zeros(value_seq.shape, jnp.float32)
    for first_row in range(0, length, block_len):
        rows_query = query_seq[first_row : first_row + block_len]
        rows_grad = grad_mixed[first_row : first_row + block_len]
        scores = block_scores(rows_query, key_seq, first_row)
        attn_probs = jnp.exp(scores - lse_seq[:, first_row : first_row + block_len, None])
        grad_probs = jnp.einsum(
            "qhd,khd->hqk", rows_grad, value_seq, preferred_element_type=jnp.float32
        )
        row_delta = jnp.sum(attn_probs * grad_probs, axis=-1, keepdims=True)
        grad_scores = (attn_probs * (grad_probs - row_delta)).astype(jnp.bfloat16)
        grad_query_parts.append(
            jnp.einsum("hqk,khd->qhd", grad_scores, key_seq, preferred_element_type=jnp.float32)
            * HD ** (-0.5)
        )
        grad_key = grad_key + jnp.einsum(
            "hqk,qhd->khd", grad_scores, rows_query, preferred_element_type=jnp.float32
        ) * HD ** (-0.5)
        grad_value = grad_value + jnp.einsum(
            "hqk,qhd->khd",
            attn_probs.astype(jnp.bfloat16),
            rows_grad,
            preferred_element_type=jnp.float32,
        )
    return (jnp.concatenate(grad_query_parts, axis=0), grad_key, grad_value)


def layer_forward(stream_in, norm_gains, projections, seq_count, length):
    proj_qkv, proj_out, proj_up, proj_down = projections
    tok_count = seq_count * length
    normed_in = rms_norm(stream_in, norm_gains[0]).astype(jnp.bfloat16)
    packed = jnp.dot(normed_in, proj_qkv, preferred_element_type=jnp.float32).reshape(
        seq_count, length, 3, HEADS, HD
    )
    query_list, key_list, value_list, mixed_list, lse_list = ([], [], [], [], [])
    query_seq = rotate(packed[0, :, 0], length).astype(jnp.bfloat16)
    key_seq = rotate(packed[0, :, 1], length).astype(jnp.bfloat16)
    value_seq = packed[0, :, 2].astype(jnp.bfloat16)
    mixed_seq, lse_seq = attend(query_seq, key_seq, value_seq)
    query_list.append(query_seq)
    key_list.append(key_seq)
    value_list.append(value_seq)
    mixed_list.append(mixed_seq)
    lse_list.append(lse_seq)
    mixed = jnp.stack(mixed_list).reshape(tok_count, HEADS * HD).astype(jnp.bfloat16)
    stream_mid = stream_in + jnp.dot(mixed, proj_out, preferred_element_type=jnp.float32)
    normed_mid = rms_norm(stream_mid, norm_gains[1]).astype(jnp.bfloat16)
    hidden = jnp.dot(normed_mid, proj_up, preferred_element_type=jnp.float32)
    active = jax.nn.gelu(hidden, approximate=False).astype(jnp.bfloat16)
    stream_out = stream_mid + jnp.dot(active, proj_down, preferred_element_type=jnp.float32)
    kept = (
        stream_in,
        stream_mid,
        normed_in,
        query_list,
        key_list,
        value_list,
        lse_list,
        mixed,
        normed_mid,
        hidden,
        active,
    )
    return (stream_out, kept)


def layer_backward(grad_out, kept, norm_gains, projections, seq_count, length):
    proj_qkv, proj_out, proj_up, proj_down = projections
    (
        stream_in,
        stream_mid,
        normed_in,
        query_list,
        key_list,
        value_list,
        lse_list,
        mixed,
        normed_mid,
        hidden,
        active,
    ) = kept
    tok_count = seq_count * length
    grad_branch = grad_out.astype(jnp.bfloat16)
    grad_down = jnp.einsum("tf,td->fd", active, grad_branch, preferred_element_type=jnp.float32)
    grad_active = jnp.einsum(
        "td,fd->tf", grad_branch, proj_down, preferred_element_type=jnp.float32
    )
    gelu_pull = jax.vjp(lambda pre_act: jax.nn.gelu(pre_act, approximate=False), hidden)[1]
    grad_hidden = gelu_pull(grad_active)[0].astype(jnp.bfloat16)
    grad_up = jnp.einsum("td,tf->df", normed_mid, grad_hidden, preferred_element_type=jnp.float32)
    grad_normed_mid = jnp.einsum(
        "tf,df->td", grad_hidden, proj_up, preferred_element_type=jnp.float32
    )
    grad_mid_part, grad_gain_mid = jax.vjp(rms_norm, stream_mid, norm_gains[1])[1](grad_normed_mid)
    grad_mid = grad_out + grad_mid_part
    grad_attn = grad_mid.astype(jnp.bfloat16)
    grad_outproj = jnp.einsum("tc,td->cd", mixed, grad_attn, preferred_element_type=jnp.float32)
    grad_mixed = jnp.einsum("td,cd->tc", grad_attn, proj_out, preferred_element_type=jnp.float32)
    grad_mixed = grad_mixed.astype(jnp.bfloat16).reshape(seq_count, length, HEADS, HD)
    grad_query, grad_key, grad_value = attend_back(
        query_list[0], key_list[0], value_list[0], lse_list[0], grad_mixed[0]
    )
    unrotate = jax.vjp(lambda heads_in: rotate(heads_in, length), grad_query)[1]
    packed_grads = [jnp.stack([unrotate(grad_query)[0], unrotate(grad_key)[0], grad_value], axis=1)]
    grad_packed = jnp.stack(packed_grads).reshape(tok_count, 3 * HEADS * HD).astype(jnp.bfloat16)
    grad_qkv = jnp.einsum("td,tc->dc", normed_in, grad_packed, preferred_element_type=jnp.float32)
    grad_normed_in = jnp.einsum(
        "tc,dc->td", grad_packed, proj_qkv, preferred_element_type=jnp.float32
    )
    grad_in_part, grad_gain_in = jax.vjp(rms_norm, stream_in, norm_gains[0])[1](grad_normed_in)
    return (
        grad_mid + grad_in_part,
        (grad_qkv, grad_outproj, grad_up, grad_down),
        (grad_gain_in, grad_gain_mid),
    )


def body(
    token_ids,
    target_ids,
    embedding,
    w_qkv,
    w_out,
    w_up,
    w_down,
    norm_gains,
    embed_mom,
    qkv_mom,
    out_mom,
    up_mom,
    down_mom,
    gain_mom,
    embed_err,
    qkv_err,
    out_err,
    up_err,
    down_err,
    embed_factor,
    qkv_factor,
    out_factor,
    up_factor,
    down_factor,
):
    seq_count, length = token_ids.shape
    tok_count = seq_count * length
    vocab_rows = embedding.shape[0]
    shard_pos = lax.axis_index("voc")
    workers = lax.axis_size("rep")
    vocab_table = embedding.astype(jnp.bfloat16)
    slices = (w_qkv, w_out, w_up, w_down)
    projections = (
        lax.all_gather(w_qkv.astype(jnp.bfloat16), "voc", axis=0, tiled=True),
        lax.all_gather(w_out.astype(jnp.bfloat16), "voc", axis=0, tiled=True),
        lax.all_gather(w_up.astype(jnp.bfloat16), "voc", axis=0, tiled=True),
        lax.all_gather(w_down.astype(jnp.bfloat16), "voc", axis=0, tiled=True),
    )
    local_ids = token_ids.reshape(-1) - shard_pos * vocab_rows
    inside = (local_ids >= 0) & (local_ids < vocab_rows)
    safe_ids = jnp.clip(local_ids, 0, vocab_rows - 1)
    own_rows = jnp.where(inside[:, None], vocab_table[safe_ids].astype(jnp.float32), 0.0)
    stream_in = lax.psum(own_rows.astype(jnp.bfloat16), "voc").astype(jnp.float32)
    stream_out, kept = layer_forward(stream_in, norm_gains, projections, seq_count, length)
    normed_out = rms_norm(stream_out, norm_gains[2]).astype(jnp.bfloat16)
    logits = jnp.einsum("td,vd->tv", normed_out, vocab_table, preferred_element_type=jnp.float32)
    local_targets = target_ids.reshape(-1) - shard_pos * vocab_rows
    target_hit = jnp.arange(vocab_rows)[None, :] == local_targets[:, None]
    picked_local = jnp.sum(jnp.where(target_hit, logits, 0.0), axis=-1)
    local_top = jnp.max(logits, axis=-1)
    top_all = lax.pmax(local_top, "voc")
    total_all, picked = lax.psum(
        (jnp.sum(jnp.exp(logits - top_all[:, None]), axis=-1), picked_local), "voc"
    )
    partition = top_all + jnp.log(total_all)
    loss_value = jnp.mean(partition - picked) + ZLOSS_WEIGHT * jnp.mean(partition * partition)
    soft_probs = jnp.exp(logits - partition[:, None])
    grad_logits = (
        (
            soft_probs * (1.0 + 2.0 * ZLOSS_WEIGHT * partition)[:, None]
            - target_hit.astype(jnp.float32)
        )
        / tok_count
    ).astype(jnp.bfloat16)
    grad_table_head = jnp.einsum(
        "tv,td->vd", grad_logits, normed_out, preferred_element_type=jnp.float32
    )
    hidden_terms = jnp.dot(grad_logits, vocab_table, preferred_element_type=jnp.float32)
    grad_normed_out = lax.psum(hidden_terms, "voc")
    grad_stream, grad_gain_out = jax.vjp(rms_norm, stream_out, norm_gains[2])[1](grad_normed_out)
    grad_in, grad_mats, gain_pair = layer_backward(
        grad_stream, kept, norm_gains, projections, seq_count, length
    )
    lookup_grad = (
        jnp.zeros(embedding.shape, jnp.float32)
        .at[safe_ids]
        .add(jnp.where(inside[:, None], grad_in, 0.0))
    )
    grad_gains = jnp.stack([gain_pair[0], gain_pair[1], grad_gain_out])
    own_grads = [grad_table_head + lookup_grad] + [
        lax.dynamic_slice_in_dim(full_grad, shard_pos * own_slice.shape[0], own_slice.shape[0], 0)
        for full_grad, own_slice in zip(grad_mats, slices)
    ]
    errors = [e[0] for e in (embed_err, qkv_err, out_err, up_err, down_err)]
    starts_t = [
        f[0].T for f in (embed_factor, qkv_factor, out_factor, up_factor, down_factor)
    ]
    row_list = [g.shape[0] for g in own_grads[1:]]
    gains_flat = jnp.pad(grad_gains.reshape(RK, -1), ((0, 0), (0, 64)))
    sketches = sketch(own_grads, errors, starts_t)
    ph, phs, gain_sum, norm = basis(sketches, gains_flat, row_list, workers, lax.axis_size("voc"))
    new_errors, rights = residual(own_grads, errors, ph, phs, norm)
    right_mean = mean_right(rights, workers)
    new_moments, changed = update(
        (embed_mom, qkv_mom, out_mom, up_mom, down_mom),
        (w_qkv, w_out, w_up, w_down),
        ph,
        phs,
        right_mean,
    )
    total_norm = norm[0, 0]
    factors, at = [], 0
    for grad_part in own_grads:
        factors.append(right_mean[:, at : at + grad_part.shape[1]].T[None])
        at += grad_part.shape[1]
    gain_mean = gain_sum[:, :192].reshape(3, -1) / workers
    next_gain_mom = MOMENTUM * gain_mom.astype(jnp.float32) + gain_mean
    gain_change = -LEARN_RATE * next_gain_mom
    return (
        loss_value.reshape(1),
        total_norm.reshape(1),
        *changed,
        gain_change,
        *new_moments,
        next_gain_mom,
        *(e[None] for e in new_errors),
        *factors,
    )


def solution(mesh):
    in_specs = (
        P("rep", None),
        P("rep", None),
        P("voc", None),
        P("voc", None),
        P("voc", None),
        P("voc", None),
        P("voc", None),
        P(),
        P("voc", None),
        P("voc", None),
        P("voc", None),
        P("voc", None),
        P("voc", None),
        P(),
        P("rep", "voc", None),
        P("rep", "voc", None),
        P("rep", "voc", None),
        P("rep", "voc", None),
        P("rep", "voc", None),
        P("voc", None, None),
        P("voc", None, None),
        P("voc", None, None),
        P("voc", None, None),
        P("voc", None, None),
    )
    out_specs = (
        P("rep"),
        P("rep"),
        P("voc", None),
        P("voc", None),
        P("voc", None),
        P("voc", None),
        P("voc", None),
        P(),
        P("voc", None),
        P("voc", None),
        P("voc", None),
        P("voc", None),
        P("voc", None),
        P(),
        P("rep", "voc", None),
        P("rep", "voc", None),
        P("rep", "voc", None),
        P("rep", "voc", None),
        P("rep", "voc", None),
        P("voc", None, None),
        P("voc", None, None),
        P("voc", None, None),
        P("voc", None, None),
        P("voc", None, None),
    )
    return jax.shard_map(body, mesh=mesh, in_specs=in_specs, out_specs=out_specs, check_vma=False)
```

```python
import functools

import jax
import jax.numpy as jnp
from jax import lax
from jax.experimental import pallas as pl
from jax.experimental.pallas import tpu as pltpu
from jax.sharding import PartitionSpec as P

HD = 64


MOMENTUM = 0.9
LEARN_RATE = 10.0
CLIP_NORM = 1.0
ZLOSS_WEIGHT = 0.01


TB = 1024
RK = 8
F32 = jnp.float32
BF16 = jnp.bfloat16
MESH_ID = pl.DeviceIdType.MESH


def round_up(value, step):
    return (value + step - 1) // step * step


def halves(value):
    high = value.astype(BF16).astype(F32)
    return high, value - high


def dims_of(value, contract_left, contract_right):
    return (((contract_left,), (contract_right,)), ((), ()))


def left_of(matrix, start_t):
    s_high, s_low = halves(start_t)
    both = jnp.concatenate([s_high, s_low], axis=0).astype(BF16)
    high = matrix.astype(BF16)
    low = (matrix - high.astype(F32)).astype(BF16)
    nt = (((1,), (1,)), ((), ()))
    main = lax.dot_general(both, high, nt, preferred_element_type=F32)
    rest = lax.dot_general(s_high.astype(BF16), low, nt, preferred_element_type=F32)
    return main[:RK] + main[RK:] + rest


def left_of_bf16(matrix, start_t):
    s_high, s_low = halves(start_t)
    both = jnp.concatenate([s_high, s_low], axis=0).astype(BF16)
    main = lax.dot_general(both, matrix, (((1,), (1,)), ((), ())), preferred_element_type=F32)
    return main[:RK] + main[RK:]


def right_of(basis_t, matrix):
    b_high, b_low = halves(basis_t)
    both = jnp.concatenate([b_high, b_low], axis=0).astype(BF16)
    high = matrix.astype(BF16)
    low = (matrix - high.astype(F32)).astype(BF16)
    main = jnp.dot(both, high, preferred_element_type=F32)
    rest = jnp.dot(b_high.astype(BF16), low, preferred_element_type=F32)
    return main[:RK] + main[RK:] + rest


def product_of(basis_t, right_t):
    b_high, b_low = halves(basis_t)
    r_high, r_low = halves(right_t)
    zero_b, zero_r = jnp.zeros_like(b_high), jnp.zeros_like(r_high)
    left = jnp.concatenate([b_high, b_low, b_high, zero_b], axis=0).astype(BF16)
    right = jnp.concatenate([r_high, r_high, r_low, zero_r], axis=0).astype(BF16)
    return lax.dot_general(left, right, (((0,), (0,)), ((), ())), preferred_element_type=F32)


def keep_rows(value, first_row, rows):
    at = first_row + lax.broadcasted_iota(jnp.int32, value.shape, 0)
    return jnp.where(at < rows, value, jnp.zeros_like(value))


def fold_squares(value):
    squares = value * value
    rows, columns = value.shape
    by_sublane = jnp.sum(squares.reshape(rows // 8, 8, columns), axis=0)
    total = by_sublane[:, :512]
    for start in range(512, columns, 512):
        total = total + by_sublane[:, start : start + 512]
    return total


def small_places(rows_list):
    places, at = [], 0
    for rows in rows_list:
        places.append(at)
        at += round_up(rows, 128)
    return places, at


def sketch_kernel(rows, row_list, *refs):
    grads, errs, starts = refs[0:5], refs[5:10], refs[10:15]
    gq_ref, eq_ref, gs_ref, es_ref, sq_ref = refs[15:20]
    step = pl.program_id(0)
    places, _ = small_places(row_list)

    @pl.when(step == 0)
    def _():
        gs_ref[...] = jnp.zeros_like(gs_ref)
        es_ref[...] = jnp.zeros_like(es_ref)
        total = jnp.zeros(sq_ref.shape, F32)
        for k in range(4):
            grad = grads[k + 1][...]
            start_t = starts[k + 1][...]
            at = pl.ds(places[k], row_list[k])
            gs_ref[:, at] = left_of(grad, start_t)
            es_ref[:, at] = left_of_bf16(errs[k + 1][...], start_t)
            total = total + fold_squares(grad)
        sq_ref[...] = total

    start_t = starts[0][...]
    grad = keep_rows(grads[0][...], step * TB, rows)
    err = keep_rows(errs[0][...].astype(F32), step * TB, rows).astype(BF16)
    gq_ref[...] = left_of(grad, start_t)
    eq_ref[...] = left_of_bf16(err, start_t)
    sq_ref[...] += fold_squares(grad)


def whole(shape):
    return pl.BlockSpec(shape, lambda *_: (0,) * len(shape))


def sketch(grads, errs, starts_t):
    rows, width = grads[0].shape
    blocks = pl.cdiv(rows, TB)
    row_list = [g.shape[0] for g in grads[1:]]
    _, small = small_places(row_list)
    block = pl.BlockSpec((TB, width), lambda i: (i, 0))
    lanes = pl.BlockSpec((RK, TB), lambda i: (0, i))
    return pl.pallas_call(
        functools.partial(sketch_kernel, rows, row_list),
        grid=(blocks,),
        in_specs=[block]
        + [whole(g.shape) for g in grads[1:]]
        + [block]
        + [whole(e.shape) for e in errs[1:]]
        + [whole(s.shape) for s in starts_t],
        out_specs=[lanes, lanes, whole((RK, small)), whole((RK, small)), whole((8, 512))],
        out_shape=[
            jax.ShapeDtypeStruct((RK, blocks * TB), F32),
            jax.ShapeDtypeStruct((RK, blocks * TB), F32),
            jax.ShapeDtypeStruct((RK, small), F32),
            jax.ShapeDtypeStruct((RK, small), F32),
            jax.ShapeDtypeStruct((8, 512), F32),
        ],
        name="sketch",
    )(*grads, *errs, *starts_t)


def clip_of(norm_tile):
    return jnp.minimum(1.0, CLIP_NORM / norm_tile[0:1, 0:1])


def orthonormal_t(parts):
    row_at = lax.broadcasted_iota(jnp.int32, (RK, 1), 0)
    for row in range(RK):
        total = None
        for part in parts:
            term = part * part[row : row + 1, :]
            for start in range(0, term.shape[1], 128):
                piece = term[:, start : start + 128]
                total = piece if total is None else total + piece
        dots = jnp.sum(total, axis=1, keepdims=True)
        inverse = lax.rsqrt(dots[row : row + 1, :] + 1e-20)
        scale = jnp.where(row_at == row, inverse, 1.0)
        taken = jnp.where(row_at > row, -dots * inverse * inverse, 0.0)
        parts = [part * scale + taken * part[row : row + 1, :] for part in parts]
    return parts


def ring_sum(x, landing, y, send_sem, land_sem, spread_sem, gather_sem, axis, count):
    me = lax.axis_index(axis)
    first = []
    for step in range(1, count):
        peer = lax.rem(me + step, count)
        copy = pltpu.make_async_remote_copy(
            src_ref=x.at[peer],
            dst_ref=landing.at[step],
            send_sem=send_sem.at[step],
            recv_sem=land_sem.at[step],
            device_id={axis: peer},
            device_id_type=MESH_ID,
        )
        copy.start()
        first.append(copy)
    total = x[me]
    for step in range(1, count):
        first[step - 1].wait_recv()
        total = total + landing[step]
    y[me] = total
    second = []
    for step in range(1, count):
        peer = lax.rem(me + step, count)
        copy = pltpu.make_async_remote_copy(
            src_ref=y.at[me],
            dst_ref=y.at[me],
            send_sem=spread_sem.at[step],
            recv_sem=gather_sem.at[step],
            device_id={axis: peer},
            device_id_type=MESH_ID,
        )
        copy.start()
        second.append(copy)
    for copy in first:
        copy.wait_send()
    for step in range(1, count):
        source = lax.rem(me - step + count, count)
        pltpu.make_async_remote_copy(
            src_ref=y.at[source],
            dst_ref=y.at[source],
            send_sem=spread_sem.at[step],
            recv_sem=gather_sem.at[step],
            device_id={axis: source},
            device_id_type=MESH_ID,
        ).wait_recv()
    for copy in second:
        copy.wait_send()


def greet(axes):
    barrier = pltpu.get_barrier_semaphore()
    greeted = 0
    for axis, count in axes:
        me = lax.axis_index(axis)
        for step in range(1, count):
            pl.semaphore_signal(
                barrier,
                inc=1,
                device_id={axis: lax.rem(me + step, count)},
                device_id_type=MESH_ID,
            )
        greeted += count - 1
    pl.semaphore_wait(barrier, greeted)


def basis_kernel(
    workers, shards, row_list, gains_at,
    gq_ref, eq_ref, gs_ref, es_ref, gains_ref, sq_ref,
    ph_ref, phs_ref, gsum_ref, norm_ref,
    x, landing, y, small, sq_all, send_sem, land_sem, spread_sem, gather_sem, sq_send, sq_recv,
):
    greet((("rep", workers), ("voc", shards)))
    shard = lax.axis_index("voc")
    own = jnp.sum(sq_ref[...].reshape(8, 4, 128), axis=1)
    own = jnp.sum(jnp.sum(own, axis=0, keepdims=True), axis=1, keepdims=True)
    sq_all[shard] = jnp.broadcast_to(own, (8, 128))
    copies = []
    for step in range(1, shards):
        peer = lax.rem(shard + step, shards)
        copy = pltpu.make_async_remote_copy(
            src_ref=sq_all.at[shard],
            dst_ref=sq_all.at[shard],
            send_sem=sq_send.at[step],
            recv_sem=sq_recv.at[step],
            device_id={"voc": peer},
            device_id_type=MESH_ID,
        )
        copy.start()
        copies.append(copy)
    gains = gains_ref[...]
    total = jnp.sum(jnp.sum(gains * gains, axis=0, keepdims=True), axis=1, keepdims=True)
    small[...] = jnp.zeros_like(small)
    for step in range(1, shards):
        source = lax.rem(shard - step + shards, shards)
        pltpu.make_async_remote_copy(
            src_ref=sq_all.at[source],
            dst_ref=sq_all.at[source],
            send_sem=sq_send.at[step],
            recv_sem=sq_recv.at[step],
            device_id={"voc": source},
            device_id_type=MESH_ID,
        ).wait_recv()
    for copy in copies:
        copy.wait_send()
    for peer in range(shards):
        total = total + sq_all[peer][0:1, 0:1]
    norm = jnp.sqrt(total)
    norm_ref[...] = jnp.broadcast_to(norm, (8, 128))
    clip = jnp.minimum(1.0, CLIP_NORM / norm)

    chunk = gq_ref.shape[1] // workers
    part = small.shape[1] // workers
    span = gs_ref.shape[1]
    small[:, :span] = clip * gs_ref[...] + es_ref[...]
    small[:, gains_at : gains_at + gains.shape[1]] = clip * gains
    for j in range(workers):
        at = slice(j * chunk, (j + 1) * chunk)
        x[j, :, :chunk] = clip * gq_ref[:, at] + eq_ref[:, at]
        x[j, :, chunk:] = small[:, j * part : (j + 1) * part]
    ring_sum(x, landing, y, send_sem, land_sem, spread_sem, gather_sem, "rep", workers)
    parts = orthonormal_t([y[j, :, :chunk] for j in range(workers)])
    for j in range(workers):
        ph_ref[:, j * chunk : (j + 1) * chunk] = parts[j]
        small[:, j * part : (j + 1) * part] = y[j, :, chunk:]
    gsum_ref[...] = small[:, gains_at : gains_at + gains.shape[1]]
    places, _ = small_places(row_list)
    for place, rows in zip(places, row_list):
        lanes = round_up(rows, 128)
        phs_ref[:, place : place + lanes] = orthonormal_t([small[:, place : place + lanes]])[0]


def basis(sketches, gains, row_list, workers, shards):
    gq, eq, gs, es, sq = sketches
    gains_at = gs.shape[1]
    small = round_up(gains_at + gains.shape[1], workers * 128)
    lanes = (gq.shape[1] + small) // workers
    vmem = pl.BlockSpec(memory_space=pltpu.VMEM)
    return pl.pallas_call(
        functools.partial(basis_kernel, workers, shards, row_list, gains_at),
        in_specs=[vmem] * 6,
        out_specs=[vmem] * 4,
        out_shape=[
            jax.ShapeDtypeStruct(gq.shape, F32),
            jax.ShapeDtypeStruct(gs.shape, F32),
            jax.ShapeDtypeStruct(gains.shape, F32),
            jax.ShapeDtypeStruct((8, 128), F32),
        ],
        scratch_shapes=[
            pltpu.VMEM((workers, RK, lanes), F32),
            pltpu.VMEM((workers, RK, lanes), F32),
            pltpu.VMEM((workers, RK, lanes), F32),
            pltpu.VMEM((RK, small), F32),
            pltpu.VMEM((shards, 8, 128), F32),
        ]
        + [pltpu.SemaphoreType.DMA((workers,))] * 4
        + [pltpu.SemaphoreType.DMA((shards,))] * 2,
        compiler_params=pltpu.CompilerParams(collective_id=1, has_side_effects=True),
        name="basis",
    )(gq, eq, gs, es, gains, sq)


def residual_kernel(rows, row_list, *refs):
    grads, errs = refs[0:5], refs[5:10]
    ph_ref, phs_ref, norm_ref = refs[10:13]
    outs, rights = refs[13:18], refs[18:23]
    kept = refs[23]
    phase, step = pl.program_id(0), pl.program_id(1)
    places, _ = small_places(row_list)
    clip = clip_of(norm_ref[...])
    at = pl.multiple_of(step * TB, TB)

    @pl.when((phase == 0) & (step == 0))
    def _():
        rights[0][...] = jnp.zeros_like(rights[0])
        for k in range(4):
            matrix = clip * grads[k + 1][...] + errs[k + 1][...].astype(F32)
            basis_t = phs_ref[:, places[k] : places[k] + row_list[k]]
            right_t = right_of(basis_t, matrix)
            rights[k + 1][...] = right_t
            outs[k + 1][...] = matrix - product_of(basis_t, right_t)

    @pl.when(phase == 0)
    def _():
        matrix = clip * grads[0][...] + errs[0][...].astype(F32)
        matrix = keep_rows(matrix, step * TB, rows)
        kept[pl.ds(at, TB), :] = matrix
        rights[0][...] += right_of(ph_ref[:, pl.ds(at, TB)], matrix)

    @pl.when(phase == 1)
    def _():
        outs[0][...] = kept[pl.ds(at, TB), :] - product_of(ph_ref[:, pl.ds(at, TB)], rights[0][...])


def residual(grads, errs, ph, phs, norm):
    rows, width = grads[0].shape
    blocks = pl.cdiv(rows, TB)
    row_list = [g.shape[0] for g in grads[1:]]
    block_in = pl.BlockSpec((TB, width), lambda p, i: (jnp.where(p == 0, i, blocks - 1), 0))
    block_out = pl.BlockSpec((TB, width), lambda p, i: (jnp.where(p == 0, 0, i), 0))
    out = pl.pallas_call(
        functools.partial(residual_kernel, rows, row_list),
        grid=(2, blocks),
        in_specs=[block_in]
        + [whole(g.shape) for g in grads[1:]]
        + [block_in]
        + [whole(e.shape) for e in errs[1:]]
        + [whole(ph.shape), whole(phs.shape), whole(norm.shape)],
        out_specs=[block_out]
        + [whole(g.shape) for g in grads[1:]]
        + [whole((RK, g.shape[1])) for g in grads],
        out_shape=[jax.ShapeDtypeStruct(g.shape, F32) for g in grads]
        + [jax.ShapeDtypeStruct((RK, g.shape[1]), F32) for g in grads],
        scratch_shapes=[pltpu.VMEM((blocks * TB, width), F32)],
        compiler_params=pltpu.CompilerParams(vmem_limit_bytes=60 << 20),
        name="residual",
    )(*grads, *errs, ph, phs, norm)
    return out[:5], out[5:]


def mean_right_kernel(workers, r0, r1, r2, r3, r4, out_ref, flat, x, landing, y, s1, s2, s3, s4):
    greet((("rep", workers),))
    part = x.shape[2]
    flat[...] = jnp.zeros_like(flat)
    at = 0
    for ref in (r0, r1, r2, r3, r4):
        flat[:, at : at + ref.shape[1]] = ref[...]
        at += ref.shape[1]
    for j in range(workers):
        x[j] = flat[:, j * part : (j + 1) * part]
    ring_sum(x, landing, y, s1, s2, s3, s4, "rep", workers)
    for j in range(workers):
        out_ref[:, j * part : (j + 1) * part] = y[j] * (1.0 / workers)


def mean_right(rights, workers):
    lanes = round_up(sum(r.shape[1] for r in rights), workers * 128)
    vmem = pl.BlockSpec(memory_space=pltpu.VMEM)
    part = (workers, RK, lanes // workers)
    return pl.pallas_call(
        functools.partial(mean_right_kernel, workers),
        in_specs=[vmem] * 5,
        out_specs=vmem,
        out_shape=jax.ShapeDtypeStruct((RK, lanes), F32),
        scratch_shapes=[pltpu.VMEM((RK, lanes), F32)]
        + [pltpu.VMEM(part, F32)] * 3
        + [pltpu.SemaphoreType.DMA((workers,))] * 4,
        compiler_params=pltpu.CompilerParams(collective_id=2, has_side_effects=True),
        name="mean_right",
    )(*rights)


def update_kernel(row_list, widths, *refs):
    moms, weights = refs[0:5], refs[5:9]
    ph_ref, phs_ref, right_ref = refs[9:12]
    out_moms, outs = refs[12:17], refs[17:22]
    places, _ = small_places(row_list)

    @pl.when(pl.program_id(0) == 0)
    def _():
        at = widths[0]
        for k in range(4):
            basis_t = phs_ref[:, places[k] : places[k] + row_list[k]]
            mean = product_of(basis_t, right_ref[:, at : at + widths[k + 1]])
            at += widths[k + 1]
            moved = MOMENTUM * moms[k + 1][...].astype(F32) + mean
            out_moms[k + 1][...] = moved
            outs[k + 1][...] = weights[k][...] + -LEARN_RATE * moved

    mean = product_of(ph_ref[...], right_ref[:, : widths[0]])
    moved = MOMENTUM * moms[0][...].astype(F32) + mean
    out_moms[0][...] = moved
    outs[0][...] = -LEARN_RATE * moved


def update(moms, weights, ph, phs, right):
    rows, width = moms[0].shape
    blocks = pl.cdiv(rows, TB)
    row_list = [m.shape[0] for m in moms[1:]]
    widths = [m.shape[1] for m in moms]
    block = pl.BlockSpec((TB, width), lambda i: (i, 0))
    out = pl.pallas_call(
        functools.partial(update_kernel, row_list, widths),
        grid=(blocks,),
        in_specs=[block]
        + [whole(m.shape) for m in moms[1:]]
        + [whole(w.shape) for w in weights]
        + [pl.BlockSpec((RK, TB), lambda i: (0, i)), whole(phs.shape), whole(right.shape)],
        out_specs=([block] + [whole(m.shape) for m in moms[1:]]) * 2,
        out_shape=[jax.ShapeDtypeStruct(m.shape, F32) for m in moms] * 2,
        compiler_params=pltpu.CompilerParams(vmem_limit_bytes=60 << 20),
        name="update",
    )(*moms, *weights, ph, phs, right)
    return out[:5], out[5:]


EPS = 1e-06
QB = 256
INV_SQRT2 = 0.7071067811865476
INV_SQRT_2PI = 0.3989422804014327


def nt_dot(a, b):
    return lax.dot_general(a, b, (((1,), (1,)), ((), ())), preferred_element_type=F32)


def nn_dot(a, b):
    return jnp.dot(a, b, preferred_element_type=F32)


def scaled_rms(value, gain):
    return value * lax.rsqrt(jnp.mean(value * value, axis=1, keepdims=True) + EPS) * gain


def rms_back(grad, value, gain):
    inverse = lax.rsqrt(jnp.mean(value * value, axis=1, keepdims=True) + EPS)
    scaled = grad * gain
    along = jnp.mean(scaled * value, axis=1, keepdims=True)
    back = inverse * (scaled - value * (inverse * inverse * along))
    return back, jnp.sum(grad * value * inverse, axis=0, keepdims=True)


def turned(value_t, cos_t, sin_t, half):
    first, second = value_t[:half], value_t[half:]
    return jnp.concatenate([first * cos_t - second * sin_t, first * sin_t + second * cos_t], axis=0)


def turned_back(value_t, cos_t, sin_t, half):
    first, second = value_t[:half], value_t[half:]
    return jnp.concatenate([first * cos_t + second * sin_t, second * cos_t - first * sin_t], axis=0)


def causal_tile(scores_t, fill):
    size = scores_t.shape[1]
    key_at = lax.broadcasted_iota(jnp.int32, (size, size), 0)
    query_at = lax.broadcasted_iota(jnp.int32, (size, size), 1)
    tail = jnp.where(key_at <= query_at, scores_t[-size:], fill)
    if scores_t.shape[0] == size:
        return tail
    return jnp.concatenate([scores_t[:-size], tail], axis=0)


def forward_kernel(
    shards, axis,
    x0_ref, gains_ref, cos_ref, sin_ref, wqkv_ref, wo_own, wu_own, wd_own,
    n1_ref, qkv_ref, lse_ref, mixed_ref, x1_ref, n2_ref, x2_ref, n3_ref, wo_all, wu_all, wd_all, hid_any,
    hid_ref, hid_sem, wo_sems, wu_sems, wd_sems,
):
    tokens, width = x0_ref.shape
    half = HD // 2
    row_blocks = tokens // QB
    greet_all(axis, shards)
    shard = lax.axis_index(axis)
    spreads = []
    for own, full, sems in ((wo_own, wo_all, wo_sems), (wu_own, wu_all, wu_sems), (wd_own, wd_all, wd_sems)):
        full[shard] = own[...].astype(BF16)
        spreads.append(Spread(full, axis, shards, sems))
    pl.semaphore_wait(pltpu.get_barrier_semaphore(), shards - 1)
    for spread in spreads:
        spread.start()

    @pl.loop(0, row_blocks)
    def _(block):
        rows = pl.ds(pl.multiple_of(block * QB, QB), QB)
        n1_ref[rows, :] = scaled_rms(x0_ref[rows, :].astype(F32), gains_ref[0:1, :]).astype(BF16)

    group = 4 * HD

    @pl.loop(0, width // group)
    def _(at):
        n1 = n1_ref[...]
        for part in range(3):
            start = pl.multiple_of(part * width + at * group, group)
            packed_t = nn_dot(n1, wqkv_ref[:, pl.ds(start, group)]).T
            if part < 2:
                cos_t, sin_t = cos_ref[...], sin_ref[...]
                packed_t = jnp.concatenate(
                    [
                        turned(packed_t[head * HD : (head + 1) * HD], cos_t, sin_t, half)
                        for head in range(4)
                    ],
                    axis=0,
                )
            if part == 0:
                packed_t = packed_t * HD ** (-0.5)
            qkv_ref[part, pl.ds(pl.multiple_of(at * group, group), group), :] = packed_t.astype(BF16)

    spreads[0].relay()

    def attend(head):
        rows = pl.ds(pl.multiple_of(head * HD, HD), HD)
        query_t, key_t, value_t = qkv_ref[0, rows, :], qkv_ref[1, rows, :], qkv_ref[2, rows, :]
        keys = key_t.T
        mixed_parts, lse_parts = [], []
        for block in range(row_blocks):
            count = (block + 1) * QB
            scores = causal_tile(
                nn_dot(keys[:count], query_t[:, block * QB : count]), -1e30
            )
            top = jnp.max(scores, axis=0, keepdims=True)
            weight = jnp.exp(scores - top)
            total = jnp.sum(weight, axis=0, keepdims=True)
            probs = (weight * (1.0 / total)).astype(BF16)
            mixed_parts.append(nn_dot(value_t[:, :count], probs))
            lse_parts.append(top + jnp.log(total))
        mixed_ref[rows, :] = jnp.concatenate(mixed_parts, axis=1).astype(BF16)
        lse_ref[head] = jnp.concatenate(lse_parts, axis=1)

    heads = width // HD
    pl.loop(0, heads // 2)(attend)
    spreads[1].relay()
    pl.loop(heads // 2, heads)(attend)
    spreads[0].finish()
    spreads[2].relay()
    @pl.loop(0, row_blocks)
    def _(block):
        rows = pl.ds(pl.multiple_of(block * QB, QB), QB)
        mixed = mixed_ref[:, rows].T
        stream = x0_ref[rows, :].astype(F32) + nn_dot(mixed, wo_all[...].reshape(width, width))
        x1_ref[rows, :] = stream
        x2_ref[rows, :] = stream
        n2_ref[rows, :] = scaled_rms(stream, gains_ref[1:2, :]).astype(BF16)

    spreads[1].finish()
    spreads[2].finish()
    chunk = hid_ref.shape[2]
    chunks = wu_all.shape[2] // chunk
    parts = chunk // wd_all.shape[1]

    def put(slot, at):
        return pltpu.make_async_copy(
            hid_ref.at[slot],
            hid_any.at[:, pl.ds(pl.multiple_of(at * chunk, chunk), chunk)],
            hid_sem.at[slot],
        )

    @pl.loop(0, chunks)
    def _(at):
        slot = lax.rem(at, 2)
        lanes = pl.ds(pl.multiple_of(at * chunk, chunk), chunk)

        @pl.when(at >= 2)
        def _():
            put(slot, at - 2).wait()

        for block in range(row_blocks):
            rows = slice(block * QB, (block + 1) * QB)
            hidden = nn_dot(n2_ref[rows, :], wu_all[:, :, lanes].reshape(width, chunk))
            hid_ref[slot, rows, :] = hidden
            active = (0.5 * hidden * (1.0 + lax.erf(hidden * INV_SQRT2))).astype(BF16)
            down = wd_all[pl.ds(at * parts, parts)].reshape(chunk, width)
            x2_ref[rows, :] += nn_dot(active, down)
        put(slot, at).start()

    @pl.loop(0, row_blocks)
    def _(block):
        rows = pl.ds(pl.multiple_of(block * QB, QB), QB)
        n3_ref[rows, :] = scaled_rms(x2_ref[rows, :], gains_ref[2:3, :]).astype(BF16)

    for at in range(max(0, chunks - 2), chunks):
        put(at % 2, at).wait()


VM = pl.BlockSpec(memory_space=pltpu.VMEM)
ANYWHERE = pl.BlockSpec(memory_space=pl.ANY)


def layer_forward(x0, gains, cos_t, sin_t, wqkv, slices, shards, axis):
    tokens, width = x0.shape
    hidden = slices[1].shape[1]
    shape = jax.ShapeDtypeStruct
    chunk = min(512, hidden)
    sems = pltpu.SemaphoreType.DMA((4, max(2, shards // 2)))
    return pl.pallas_call(
        functools.partial(forward_kernel, shards, axis),
        in_specs=[VM] * 8,
        out_specs=[VM] * 11 + [ANYWHERE],
        out_shape=[
            shape((tokens, width), BF16),
            shape((3, width, tokens), BF16),
            shape((width // HD, 1, tokens), F32),
            shape((width, tokens), BF16),
            shape((tokens, width), F32),
            shape((tokens, width), BF16),
            shape((tokens, width), F32),
            shape((tokens, width), BF16),
        ]
        + [shape((shards, *w.shape), BF16) for w in slices]
        + [shape((tokens, hidden), F32)],
        scratch_shapes=[
            pltpu.VMEM((2, tokens, chunk), F32),
            pltpu.SemaphoreType.DMA((2,)),
            sems,
            sems,
            sems,
        ],
        compiler_params=pltpu.CompilerParams(
            collective_id=5, has_side_effects=True, vmem_limit_bytes=60 << 20
        ),
        name="layer_forward",
    )(x0, gains, cos_t, sin_t, wqkv, *slices)


def backward_kernel(shard_axis, *refs):
    anys, refs = refs[:13], refs[13:]
    gains_ref, cos_ref, sin_ref, lse_ref = refs[0:4]
    dx0_ref, gqkv_ref, gout_ref, gup_ref, gdown_ref, ggains_ref = refs[4:10]
    kept, refs = refs[10:23], refs[23:]
    dn3_ref, x2_ref, hid_ref, wd_ref, wu_ref, x1_ref, n2_ref, wo_ref, mixed_ref, qkv_ref, x0_ref, n1_ref, wqkv_ref = kept
    grad_ref, part_ref, low_ref, act_ref, dhid_ref, dmixed_ref, dpacked_ref, turn_ref, load_sem = refs
    shard = lax.axis_index(shard_axis) if shard_axis else 0
    tokens, width = x2_ref.shape
    half = HD // 2
    row_blocks = tokens // QB
    loads = [
        pltpu.make_async_copy(src, dst, load_sem.at[at])
        for at, (src, dst) in enumerate(zip(anys, kept))
    ]
    for load in loads:
        load.start()

    def block_rows(block):
        return pl.ds(pl.multiple_of(block * QB, QB), QB)

    loads[0].wait()
    loads[1].wait()
    ggains_ref[...] = jnp.zeros_like(ggains_ref)

    @pl.loop(0, row_blocks)
    def _(block):
        rows = block_rows(block)
        back, gain = rms_back(dn3_ref[:, rows].T, x2_ref[rows, :], gains_ref[2:3, :])
        grad_ref[rows, :] = back
        low_ref[rows, :] = back.astype(BF16)
        part_ref[rows, :] = jnp.zeros_like(back)
        ggains_ref[2:3, :] += gain

    for at in (2, 3, 4):
        loads[at].wait()
    chunk = min(512, wu_ref.shape[1])

    @pl.loop(0, wu_ref.shape[1] // chunk)
    def _(at):
        lanes = pl.ds(pl.multiple_of(at * chunk, chunk), chunk)
        for block in range(row_blocks):
            rows = slice(block * QB, (block + 1) * QB)
            grad_act = nt_dot(low_ref[rows, :], wd_ref[lanes, :])
            hidden = hid_ref[rows, lanes]
            share = 0.5 + 0.5 * lax.erf(hidden * INV_SQRT2)
            slope = share + hidden * (INV_SQRT_2PI * jnp.exp(-0.5 * hidden * hidden))
            act_ref[rows, lanes] = (hidden * share).astype(BF16)
            grad_hid = (slope * grad_act).astype(BF16)
            dhid_ref[rows, lanes] = grad_hid
            part_ref[rows, :] += nt_dot(grad_hid, wu_ref[:, lanes])

    own = gdown_ref.shape[0]
    gdown_ref[...] = nn_dot(act_ref[:, pl.ds(pl.multiple_of(shard * own, own), own)].T, low_ref[...])
    loads[5].wait()
    loads[6].wait()
    own = gup_ref.shape[0]
    turn_ref[...] = n2_ref[...].T
    own_rows = pl.ds(pl.multiple_of(shard * own, own), own)

    @pl.loop(0, wu_ref.shape[1] // chunk)
    def _(at):
        lanes = pl.ds(pl.multiple_of(at * chunk, chunk), chunk)
        gup_ref[:, lanes] = nn_dot(turn_ref[own_rows, :], dhid_ref[:, lanes])

    loads[7].wait()

    @pl.loop(0, row_blocks)
    def _(block):
        rows = block_rows(block)
        back, gain = rms_back(part_ref[rows, :], x1_ref[rows, :], gains_ref[1:2, :])
        back = grad_ref[rows, :] + back
        grad_ref[rows, :] = back
        low = back.astype(BF16)
        low_ref[rows, :] = low
        ggains_ref[1:2, :] += gain
        dmixed_ref[:, rows] = nt_dot(low, wo_ref[...]).astype(BF16).T

    loads[8].wait()
    loads[9].wait()
    own = gout_ref.shape[0]
    own_rows = pl.ds(pl.multiple_of(shard * own, own), own)
    gout_ref[...] = nn_dot(mixed_ref[own_rows, :], low_ref[...])

    @pl.loop(0, width // (2 * HD))
    def _(pair):
        made = ([], [], [])
        for side in range(2):
            head = pair * 2 + side
            rows = pl.ds(pl.multiple_of(head * HD, HD), HD)
            query_t, key_t, value_t = qkv_ref[0, rows, :], qkv_ref[1, rows, :], qkv_ref[2, rows, :]
            dmix_t = dmixed_ref[rows, :]
            query, key, value, dmix = query_t.T, key_t.T, value_t.T, dmix_t.T
            lse = lse_ref[head]
            dquery_parts = []
            dkey = [None] * row_blocks
            dvalue = [None] * row_blocks
            for block in range(row_blocks):
                count = (block + 1) * QB
                at = slice(block * QB, count)
                scores = nn_dot(key[:count], query_t[:, at])
                probs = causal_tile(jnp.exp(scores - lse[:, at]), 0.0)
                dprobs = nn_dot(value[:count], dmix_t[:, at])
                delta = jnp.sum(probs * dprobs, axis=0, keepdims=True)
                dscores = (probs * (dprobs - delta)).astype(BF16)
                dquery_parts.append(nn_dot(key_t[:, :count], dscores))
                more_key = nn_dot(dscores, query[at])
                more_value = nn_dot(probs.astype(BF16), dmix[at])
                for piece in range(block + 1):
                    cut = slice(piece * QB, (piece + 1) * QB)
                    if dkey[piece] is None:
                        dkey[piece], dvalue[piece] = more_key[cut], more_value[cut]
                    else:
                        dkey[piece] = dkey[piece] + more_key[cut]
                        dvalue[piece] = dvalue[piece] + more_value[cut]
            cos_t, sin_t = cos_ref[...], sin_ref[...]
            dquery_t = jnp.concatenate(dquery_parts, axis=1) * HD ** (-0.5)
            dkey_t = jnp.concatenate(dkey, axis=0).T
            made[0].append(turned_back(dquery_t, cos_t, sin_t, half).T)
            made[1].append(turned_back(dkey_t, cos_t, sin_t, half).T)
            made[2].append(jnp.concatenate(dvalue, axis=0))
        for part in range(3):
            lanes = pl.ds(pl.multiple_of(part * width + pair * 2 * HD, 2 * HD), 2 * HD)
            dpacked_ref[:, lanes] = jnp.concatenate(made[part], axis=1).astype(BF16)

    for at in (10, 11, 12):
        loads[at].wait()
    own = gqkv_ref.shape[0]
    turn_ref[...] = n1_ref[...].T
    own_rows = pl.ds(pl.multiple_of(shard * own, own), own)

    @pl.loop(0, 3)
    def _(at):
        lanes = pl.ds(pl.multiple_of(at * width, width), width)
        gqkv_ref[:, lanes] = nn_dot(turn_ref[own_rows, :], dpacked_ref[:, lanes])

    @pl.loop(0, row_blocks)
    def _(block):
        rows = block_rows(block)
        back, gain = rms_back(
            nt_dot(dpacked_ref[rows, :], wqkv_ref[...]), x0_ref[rows, :].astype(F32), gains_ref[0:1, :]
        )
        dx0_ref[rows, :] = grad_ref[rows, :] + back
        ggains_ref[0:1, :] += gain


def layer_backward(shard_axis, slice_shapes, dn3_t, gains, cos_t, sin_t, projections, x0, kept):
    n1, qkv, lse, mixed_t, x1, n2, x2, _, hid = kept
    wqkv, wo, wu, wd = projections
    tokens, width = x2.shape
    shape = jax.ShapeDtypeStruct
    moved = (dn3_t, x2, hid, wd, wu, x1, n2, wo, mixed_t, qkv, x0, n1, wqkv)
    return pl.pallas_call(
        functools.partial(backward_kernel, shard_axis),
        in_specs=[ANYWHERE] * 13 + [VM] * 3 + [VM],
        out_specs=[VM] * 6,
        out_shape=[shape((tokens, width), F32)]
        + [shape(s, F32) for s in slice_shapes]
        + [shape((8, width), F32)],
        scratch_shapes=[pltpu.VMEM(m.shape, m.dtype) for m in moved]
        + [
            pltpu.VMEM((tokens, width), F32),
            pltpu.VMEM((tokens, width), F32),
            pltpu.VMEM((tokens, width), BF16),
            pltpu.VMEM(hid.shape, BF16),
            pltpu.VMEM(hid.shape, BF16),
            pltpu.VMEM((width, tokens), BF16),
            pltpu.VMEM((tokens, 3 * width), BF16),
            pltpu.VMEM((width, tokens), BF16),
            pltpu.SemaphoreType.DMA((13,)),
        ],
        compiler_params=pltpu.CompilerParams(vmem_limit_bytes=62 << 20),
        name="layer_backward",
    )(*moved, gains, cos_t, sin_t, lse)


def gather_kernel(ids_ref, table_any, out_ref, rows_ref, sem):
    count = table_any.shape[0]
    tokens = out_ref.shape[0]
    rows_ref[...] = jnp.zeros_like(rows_ref)

    def fetch(token, row):
        return pltpu.make_async_copy(
            table_any.at[pl.ds(row, 1), :], rows_ref.at[pl.ds(token, 1), :], sem
        )

    @pl.loop(0, tokens)
    def _(token):
        row = ids_ref[token]

        @pl.when((row >= 0) & (row < count))
        def _():
            fetch(token, row).start()

    @pl.loop(0, tokens)
    def _(token):
        row = ids_ref[token]

        @pl.when((row >= 0) & (row < count))
        def _():
            fetch(token, row).wait()

    out_ref[...] = rows_ref[...].astype(BF16)


def gather_own(ids, table):
    tokens, width = ids.shape[0], table.shape[1]
    return pl.pallas_call(
        gather_kernel,
        grid_spec=pltpu.PrefetchScalarGridSpec(
            num_scalar_prefetch=1,
            grid=(1,),
            in_specs=[ANYWHERE],
            out_specs=whole((tokens, width)),
            scratch_shapes=[pltpu.VMEM((tokens, width), F32), pltpu.SemaphoreType.DMA],
        ),
        out_shape=jax.ShapeDtypeStruct((tokens, width), BF16),
        name="gather_own",
    )(ids, table)


class Spread:
    def __init__(self, full, axis, shards, sems):
        self.full, self.axis, self.sems = full, axis, sems
        self.shard = lax.axis_index(axis)
        self.core = lax.rem(self.shard, 2)
        self.chip = self.shard // 2
        self.partner = self.shard + 1 - 2 * self.core
        self.chips = shards // 2

    def chip_copy(self, peer_chip, slot, at):
        return pltpu.make_async_remote_copy(
            src_ref=self.full.at[slot], dst_ref=self.full.at[slot],
            send_sem=self.sems.at[0, at], recv_sem=self.sems.at[1, at],
            device_id={self.axis: peer_chip * 2 + self.core}, device_id_type=MESH_ID,
        )

    def core_copy(self, slot, at):
        return pltpu.make_async_remote_copy(
            src_ref=self.full.at[slot], dst_ref=self.full.at[slot],
            send_sem=self.sems.at[2, at], recv_sem=self.sems.at[3, at],
            device_id={self.axis: self.partner}, device_id_type=MESH_ID,
        )

    def source(self, at):
        return lax.rem(self.chip - at + self.chips, self.chips)

    def start(self):
        for at in range(1, self.chips):
            self.chip_copy(lax.rem(self.chip + at, self.chips), self.shard, at).start()
        self.core_copy(self.shard, 0).start()

    def relay(self):
        for at in range(1, self.chips):
            slot = self.source(at) * 2 + self.core
            self.chip_copy(self.source(at), slot, at).wait_recv()
            self.core_copy(slot, at).start()

    def finish(self):
        for at in range(self.chips):
            slot = self.source(at) * 2 + 1 - self.core
            self.core_copy(slot, at).wait_recv()
        for at in range(1, self.chips):
            self.chip_copy(lax.rem(self.chip + at, self.chips), self.shard, at).wait_send()
        for at in range(self.chips):
            self.core_copy(self.source(at) * 2 + self.core, at).wait_send()


def greet_all(axis, count):
    barrier = pltpu.get_barrier_semaphore()
    me = lax.axis_index(axis)
    for step in range(1, count):
        pl.semaphore_signal(
            barrier, inc=1, device_id={axis: lax.rem(me + step, count)}, device_id_type=MESH_ID
        )


def open_kernel(
    shards, axis, own_ref, weight_ref, x0_ref, full_ref,
    half_in, sums, core_send, core_recv, chip_send, chip_recv, back_send, back_recv, sems,
):
    greet_all(axis, shards)
    shard = lax.axis_index(axis)
    core = lax.rem(shard, 2)
    chip = shard // 2
    partner = shard + 1 - 2 * core
    chips = shards // 2
    half = own_ref.shape[0] // 2
    own_half = pl.ds(pl.multiple_of(core * half, half), half)
    other_half = pl.ds(pl.multiple_of((1 - core) * half, half), half)
    spread = Spread(full_ref, axis, shards, sems)
    full_ref[shard] = weight_ref[...].astype(BF16)

    def chip_copy(peer_chip, slot, at):
        return pltpu.make_async_remote_copy(
            src_ref=sums.at[slot], dst_ref=sums.at[slot],
            send_sem=chip_send.at[at], recv_sem=chip_recv.at[at],
            device_id={axis: peer_chip * 2 + core}, device_id_type=MESH_ID,
        )

    def back_copy(rows):
        return pltpu.make_async_remote_copy(
            src_ref=x0_ref.at[rows, :], dst_ref=x0_ref.at[rows, :],
            send_sem=back_send, recv_sem=back_recv,
            device_id={axis: partner}, device_id_type=MESH_ID,
        )

    pl.semaphore_wait(pltpu.get_barrier_semaphore(), shards - 1)
    first = pltpu.make_async_remote_copy(
        src_ref=own_ref.at[other_half, :], dst_ref=half_in,
        send_sem=core_send, recv_sem=core_recv,
        device_id={axis: partner}, device_id_type=MESH_ID,
    )
    first.start()
    first.wait_recv()
    sums[chip] = (own_ref[own_half, :].astype(F32) + half_in[...].astype(F32)).astype(BF16)
    for at in range(1, chips):
        chip_copy(lax.rem(chip + at, chips), chip, at).start()
    spread.start()
    first.wait_send()
    total = sums[chip].astype(F32)
    for at in range(1, chips):
        source = lax.rem(chip - at + chips, chips)
        chip_copy(source, source, at).wait_recv()
        total = total + sums[source].astype(F32)
    x0_ref[own_half, :] = total.astype(BF16)
    back_copy(own_half).start()
    spread.relay()
    back_copy(other_half).wait_recv()
    for at in range(1, chips):
        chip_copy(lax.rem(chip + at, chips), chip, at).wait_send()
    back_copy(own_half).wait_send()
    spread.finish()


def opening(own, weight, shards, axis):
    tokens, width = own.shape
    chips = shards // 2
    shape = jax.ShapeDtypeStruct
    return pl.pallas_call(
        functools.partial(open_kernel, shards, axis),
        in_specs=[VM] * 2,
        out_specs=[VM] * 2,
        out_shape=[shape((tokens, width), BF16), shape((shards, *weight.shape), BF16)],
        scratch_shapes=[
            pltpu.VMEM((tokens // 2, width), BF16),
            pltpu.VMEM((chips, tokens // 2, width), BF16),
        ]
        + [pltpu.SemaphoreType.DMA] * 2
        + [pltpu.SemaphoreType.DMA((max(2, chips),))] * 2
        + [pltpu.SemaphoreType.DMA] * 2
        + [pltpu.SemaphoreType.DMA((4, max(2, chips)))],
        compiler_params=pltpu.CompilerParams(collective_id=4, has_side_effects=True),
        name="opening",
    )(own, weight)


TOKEN_LANES = 256


def vocab_block(rows):
    best = 16
    for size in range(16, 1025, 16):
        if rows % size == 0:
            best = size
    return best


def head_kernel(
    shards, axis,
    n3_ref, target_ref, table_ref,
    gtable_ref, dn3_any, loss_ref,
    dn3_ref, back_in, out_sem, kept, n3_t, tops, running, stats, z_ref, half_in, half_out,
    stat_send, stat_recv, core_send, core_recv, chip_send, chip_recv, back_send, back_recv,
):
    phase, step = pl.program_id(0), pl.program_id(1)
    last = pl.num_programs(1) - 1
    shard = lax.axis_index(axis)
    core = lax.rem(shard, 2)
    chip = shard // 2
    partner = shard + 1 - 2 * core
    chips = shards // 2
    tokens, width = n3_ref.shape
    block_rows = table_ref.shape[0]
    half = width // 2
    own_half = pl.ds(pl.multiple_of(core * half, half), half)
    other_half = pl.ds(pl.multiple_of((1 - core) * half, half), half)

    def stat_copy(peer, slot, at):
        return pltpu.make_async_remote_copy(
            src_ref=stats.at[slot], dst_ref=stats.at[slot],
            send_sem=stat_send.at[at], recv_sem=stat_recv.at[at],
            device_id={axis: peer}, device_id_type=MESH_ID,
        )

    def core_copy():
        return pltpu.make_async_remote_copy(
            src_ref=dn3_ref.at[other_half, :], dst_ref=half_in,
            send_sem=core_send, recv_sem=core_recv,
            device_id={axis: partner}, device_id_type=MESH_ID,
        )

    def chip_copy(peer_chip, slot, at):
        return pltpu.make_async_remote_copy(
            src_ref=half_out.at[slot], dst_ref=half_out.at[slot],
            send_sem=chip_send.at[at], recv_sem=chip_recv.at[at],
            device_id={axis: peer_chip * 2 + core}, device_id_type=MESH_ID,
        )

    def back_copy():
        return pltpu.make_async_remote_copy(
            src_ref=dn3_ref.at[own_half, :], dst_ref=back_in,
            send_sem=back_send, recv_sem=back_recv,
            device_id={axis: partner}, device_id_type=MESH_ID,
        )

    @pl.when((phase == 0) & (step == 0))
    def _():
        barrier = pltpu.get_barrier_semaphore()
        for at in range(1, shards):
            pl.semaphore_signal(
                barrier, inc=1,
                device_id={axis: lax.rem(shard + at, shards)}, device_id_type=MESH_ID,
            )
        n3_t[...] = n3_ref[...].T
        row_at = lax.broadcasted_iota(jnp.int32, running.shape, 0)
        running[...] = jnp.where(row_at == 0, -1e30, 0.0)
        dn3_ref[...] = jnp.zeros_like(dn3_ref)

    def hits(lanes):
        row_at = lax.broadcasted_iota(jnp.int32, (block_rows, TOKEN_LANES), 0)
        return row_at == target_ref[:, lanes] - step * block_rows

    @pl.when(phase == 0)
    def _():
        table = table_ref[...].astype(BF16)
        for start in range(0, tokens, TOKEN_LANES):
            lanes = slice(start, start + TOKEN_LANES)
            logits = nn_dot(table, n3_t[:, lanes])
            top = jnp.max(logits, axis=0, keepdims=True)
            weight = jnp.exp(logits - top)
            kept[step, :, lanes] = weight
            tops[step, :, lanes] = top
            total = jnp.sum(weight, axis=0, keepdims=True)
            picked = jnp.sum(jnp.where(hits(lanes), logits, 0.0), axis=0, keepdims=True)
            old = running[0:1, lanes]
            new = jnp.maximum(old, top)
            running[0:1, lanes] = new
            running[1:2, lanes] = running[1:2, lanes] * jnp.exp(old - new) + total * jnp.exp(top - new)
            running[2:3, lanes] += picked

    @pl.when((phase == 1) & (step == 0))
    def _():
        stats[shard] = running[...]
        pl.semaphore_wait(pltpu.get_barrier_semaphore(), shards - 1)
        sends = [stat_copy(lax.rem(shard + at, shards), shard, at) for at in range(1, shards)]
        for send in sends:
            send.start()
        for at in range(1, shards):
            source = lax.rem(shard - at + shards, shards)
            stat_copy(source, source, at).wait_recv()
        for send in sends:
            send.wait_send()
        top = stats[0, 0:1, :]
        for at in range(1, shards):
            top = jnp.maximum(top, stats[at, 0:1, :])
        total, picked = jnp.zeros_like(top), jnp.zeros_like(top)
        for at in range(shards):
            total = total + stats[at, 1:2, :] * jnp.exp(stats[at, 0:1, :] - top)
            picked = picked + stats[at, 2:3, :]
        z = top + jnp.log(total)
        z_ref[...] = z
        terms = (z - picked) + ZLOSS_WEIGHT * (z * z)
        loss = jnp.sum(terms, axis=1, keepdims=True) * (1.0 / tokens)
        loss_ref[...] = jnp.broadcast_to(loss, loss_ref.shape)

    def grad_logits(lanes):
        z = z_ref[:, lanes]
        factor = jnp.exp(tops[step, :, lanes] - z) * (1.0 + 2.0 * ZLOSS_WEIGHT * z) * (1.0 / tokens)
        return (kept[step, :, lanes] * factor - jnp.where(hits(lanes), 1.0 / tokens, 0.0)).astype(BF16)

    @pl.when(phase == 1)
    def _():
        table_t = table_ref[...].astype(BF16).T
        for start in range(0, tokens, TOKEN_LANES):
            lanes = slice(start, start + TOKEN_LANES)
            dn3_ref[:, lanes] += nn_dot(table_t, grad_logits(lanes))

    @pl.when((phase == 2) & (step == 0))
    def _():
        core_copy().start()

    @pl.when((phase == 2) & (step == jnp.minimum(2, last)))
    def _():
        core_copy().wait()
        half_out[chip] = (dn3_ref[own_half, :] + half_in[...]).astype(BF16)
        for at in range(1, chips):
            chip_copy(lax.rem(chip + at, chips), chip, at).start()

    @pl.when(phase == 2)
    def _():
        total = None
        for start in range(0, tokens, TOKEN_LANES):
            lanes = slice(start, start + TOKEN_LANES)
            part = nn_dot(grad_logits(lanes), n3_ref[lanes, :])
            total = part if total is None else total + part
        gtable_ref[...] = total

    @pl.when((phase == 2) & (step == last))
    def _():
        for at in range(1, chips):
            source = lax.rem(chip - at + chips, chips)
            chip_copy(source, source, at).wait_recv()
        for at in range(1, chips):
            chip_copy(lax.rem(chip + at, chips), chip, at).wait_send()
        whole_sum = half_out[0].astype(F32)
        for at in range(1, chips):
            whole_sum = whole_sum + half_out[at].astype(F32)
        dn3_ref[own_half, :] = whole_sum
        back_copy().start()
        puts = [
            pltpu.make_async_copy(dn3_ref.at[own_half, :], dn3_any.at[own_half, :], out_sem.at[0]),
            pltpu.make_async_copy(back_in, dn3_any.at[other_half, :], out_sem.at[1]),
        ]
        puts[0].start()
        back_copy().wait()
        puts[1].start()
        for put in puts:
            put.wait()


def vocabulary_head(n3, local_targets, table, shards, axis):
    rows, width = table.shape
    tokens = n3.shape[0]
    size = vocab_block(rows)
    blocks = rows // size
    shape = jax.ShapeDtypeStruct
    return pl.pallas_call(
        functools.partial(head_kernel, shards, axis),
        grid=(3, blocks),
        in_specs=[
            whole((tokens, width)),
            whole((1, tokens)),
            pl.BlockSpec((size, width), lambda p, i: (jnp.where(p == 2, blocks - 1, i), 0)),
        ],
        out_specs=[
            pl.BlockSpec((size, width), lambda p, i: (jnp.where(p == 2, i, 0), 0)),
            pl.BlockSpec(memory_space=pl.ANY),
            whole((8, 128)),
        ],
        out_shape=[shape((rows, width), F32), shape((width, tokens), F32), shape((8, 128), F32)],
        scratch_shapes=[
            pltpu.VMEM((width, tokens), F32),
            pltpu.VMEM((width // 2, tokens), F32),
            pltpu.SemaphoreType.DMA((2,)),
            pltpu.VMEM((blocks, size, tokens), F32),
            pltpu.VMEM((width, tokens), BF16),
            pltpu.VMEM((blocks, 1, tokens), F32),
            pltpu.VMEM((8, tokens), F32),
            pltpu.VMEM((shards, 8, tokens), F32),
            pltpu.VMEM((1, tokens), F32),
            pltpu.VMEM((width // 2, tokens), F32),
            pltpu.VMEM((shards // 2, width // 2, tokens), BF16),
        ]
        + [pltpu.SemaphoreType.DMA((shards,))] * 2
        + [pltpu.SemaphoreType.DMA] * 2
        + [pltpu.SemaphoreType.DMA((max(2, shards // 2),))] * 2
        + [pltpu.SemaphoreType.DMA] * 2,
        compiler_params=pltpu.CompilerParams(
            collective_id=3, has_side_effects=True, vmem_limit_bytes=62 << 20
        ),
        name="vocabulary_head",
    )(n3, local_targets, table)


def body(
    token_ids,
    target_ids,
    embedding,
    w_qkv,
    w_out,
    w_up,
    w_down,
    norm_gains,
    embed_mom,
    qkv_mom,
    out_mom,
    up_mom,
    down_mom,
    gain_mom,
    embed_err,
    qkv_err,
    out_err,
    up_err,
    down_err,
    embed_factor,
    qkv_factor,
    out_factor,
    up_factor,
    down_factor,
):
    seq_count, length = token_ids.shape
    tok_count = seq_count * length
    vocab_rows = embedding.shape[0]
    shard_pos = lax.axis_index("voc")
    workers = lax.axis_size("rep")
    slices = (w_qkv, w_out, w_up, w_down)
    shards = lax.axis_size("voc")
    local_ids = token_ids.reshape(-1) - shard_pos * vocab_rows
    inside = (local_ids >= 0) & (local_ids < vocab_rows)
    safe_ids = jnp.clip(local_ids, 0, vocab_rows - 1)
    x0, qkv_all = opening(gather_own(local_ids, embedding), w_qkv, shards, "voc")
    wqkv = qkv_all.reshape(-1, w_qkv.shape[1])
    half = HD // 2
    angles = (10000.0 ** (-jnp.arange(half).astype(F32) / half))[:, None] * jnp.arange(length).astype(F32)[None, :]
    cos_t, sin_t = jnp.cos(angles), jnp.sin(angles)
    *kept, n3, wo, wu, wd, hid = layer_forward(
        x0, norm_gains, cos_t, sin_t, wqkv, slices[1:], shards, "voc"
    )
    kept = (*kept, n3, hid)
    projections = (wqkv, *(w.reshape(-1, w.shape[2]) for w in (wo, wu, wd)))
    local_targets = target_ids.reshape(1, -1) - shard_pos * vocab_rows
    grad_table_head, dn3_t, loss_tile = vocabulary_head(
        n3, local_targets, embedding, lax.axis_size("voc"), "voc"
    )
    loss_value = loss_tile[0, 0]
    grad_in, *grad_mats, grad_gains = layer_backward(
        "voc", [w.shape for w in slices], dn3_t, norm_gains, cos_t, sin_t, projections, x0, kept
    )
    grad_gains = grad_gains[:3]
    lookup_grad = (
        jnp.zeros(embedding.shape, jnp.float32)
        .at[safe_ids]
        .add(jnp.where(inside[:, None], grad_in, 0.0))
    )
    own_grads = [grad_table_head + lookup_grad] + grad_mats
    errors = [e[0] for e in (embed_err, qkv_err, out_err, up_err, down_err)]
    starts_t = [
        f[0].T for f in (embed_factor, qkv_factor, out_factor, up_factor, down_factor)
    ]
    row_list = [g.shape[0] for g in own_grads[1:]]
    gains_flat = jnp.pad(grad_gains.reshape(RK, -1), ((0, 0), (0, 64)))
    sketches = sketch(own_grads, errors, starts_t)
    ph, phs, gain_sum, norm = basis(sketches, gains_flat, row_list, workers, lax.axis_size("voc"))
    new_errors, rights = residual(own_grads, errors, ph, phs, norm)
    right_mean = mean_right(rights, workers)
    new_moments, changed = update(
        (embed_mom, qkv_mom, out_mom, up_mom, down_mom),
        (w_qkv, w_out, w_up, w_down),
        ph,
        phs,
        right_mean,
    )
    total_norm = norm[0, 0]
    factors, at = [], 0
    for grad_part in own_grads:
        factors.append(right_mean[:, at : at + grad_part.shape[1]].T[None])
        at += grad_part.shape[1]
    gain_mean = gain_sum[:, :192].reshape(3, -1) / workers
    next_gain_mom = MOMENTUM * gain_mom.astype(jnp.float32) + gain_mean
    gain_change = -LEARN_RATE * next_gain_mom
    return (
        loss_value.reshape(1),
        total_norm.reshape(1),
        *changed,
        gain_change,
        *new_moments,
        next_gain_mom,
        *(e[None] for e in new_errors),
        *factors,
    )


def solution(mesh):
    in_specs = (
        P("rep", None),
        P("rep", None),
        P("voc", None),
        P("voc", None),
        P("voc", None),
        P("voc", None),
        P("voc", None),
        P(),
        P("voc", None),
        P("voc", None),
        P("voc", None),
        P("voc", None),
        P("voc", None),
        P(),
        P("rep", "voc", None),
        P("rep", "voc", None),
        P("rep", "voc", None),
        P("rep", "voc", None),
        P("rep", "voc", None),
        P("voc", None, None),
        P("voc", None, None),
        P("voc", None, None),
        P("voc", None, None),
        P("voc", None, None),
    )
    out_specs = (
        P("rep"),
        P("rep"),
        P("voc", None),
        P("voc", None),
        P("voc", None),
        P("voc", None),
        P("voc", None),
        P(),
        P("voc", None),
        P("voc", None),
        P("voc", None),
        P("voc", None),
        P("voc", None),
        P(),
        P("rep", "voc", None),
        P("rep", "voc", None),
        P("rep", "voc", None),
        P("rep", "voc", None),
        P("rep", "voc", None),
        P("voc", None, None),
        P("voc", None, None),
        P("voc", None, None),
        P("voc", None, None),
        P("voc", None, None),
    )
    return jax.shard_map(body, mesh=mesh, in_specs=in_specs, out_specs=out_specs, check_vma=False)
```

```python
import functools

import jax
import jax.numpy as jnp
from jax import lax
from jax.experimental import pallas as pl
from jax.experimental.pallas import tpu as pltpu
from jax.sharding import PartitionSpec as P

HD = 64


MOMENTUM = 0.9
LEARN_RATE = 10.0
CLIP_NORM = 1.0
ZLOSS_WEIGHT = 0.01


TB = 1024
RK = 8
F32 = jnp.float32
BF16 = jnp.bfloat16
MESH_ID = pl.DeviceIdType.MESH


def round_up(value, step):
    return (value + step - 1) // step * step


def halves(value):
    high = value.astype(BF16).astype(F32)
    return high, value - high


def dims_of(value, contract_left, contract_right):
    return (((contract_left,), (contract_right,)), ((), ()))


def left_of(matrix, start_t):
    s_high, s_low = halves(start_t)
    both = jnp.concatenate([s_high, s_low], axis=0).astype(BF16)
    high = matrix.astype(BF16)
    low = (matrix - high.astype(F32)).astype(BF16)
    nt = (((1,), (1,)), ((), ()))
    main = lax.dot_general(both, high, nt, preferred_element_type=F32)
    rest = lax.dot_general(s_high.astype(BF16), low, nt, preferred_element_type=F32)
    return main[:RK] + main[RK:] + rest


def left_of_bf16(matrix, start_t):
    s_high, s_low = halves(start_t)
    both = jnp.concatenate([s_high, s_low], axis=0).astype(BF16)
    main = lax.dot_general(both, matrix, (((1,), (1,)), ((), ())), preferred_element_type=F32)
    return main[:RK] + main[RK:]


def right_of(basis_t, matrix):
    b_high, b_low = halves(basis_t)
    both = jnp.concatenate([b_high, b_low], axis=0).astype(BF16)
    high = matrix.astype(BF16)
    low = (matrix - high.astype(F32)).astype(BF16)
    main = jnp.dot(both, high, preferred_element_type=F32)
    rest = jnp.dot(b_high.astype(BF16), low, preferred_element_type=F32)
    return main[:RK] + main[RK:] + rest


def product_of(basis_t, right_t):
    b_high, b_low = halves(basis_t)
    r_high, r_low = halves(right_t)
    zero_b, zero_r = jnp.zeros_like(b_high), jnp.zeros_like(r_high)
    left = jnp.concatenate([b_high, b_low, b_high, zero_b], axis=0).astype(BF16)
    right = jnp.concatenate([r_high, r_high, r_low, zero_r], axis=0).astype(BF16)
    return lax.dot_general(left, right, (((0,), (0,)), ((), ())), preferred_element_type=F32)


def keep_rows(value, first_row, rows):
    at = first_row + lax.broadcasted_iota(jnp.int32, value.shape, 0)
    return jnp.where(at < rows, value, jnp.zeros_like(value))


def fold_squares(value):
    squares = value * value
    rows, columns = value.shape
    by_sublane = jnp.sum(squares.reshape(rows // 8, 8, columns), axis=0)
    total = by_sublane[:, :512]
    for start in range(512, columns, 512):
        total = total + by_sublane[:, start : start + 512]
    return total


def small_places(rows_list):
    places, at = [], 0
    for rows in rows_list:
        places.append(at)
        at += round_up(rows, 128)
    return places, at


def whole(shape):
    return pl.BlockSpec(shape, lambda *_: (0,) * len(shape))


def clip_of(norm_tile):
    return jnp.minimum(1.0, CLIP_NORM / norm_tile[0:1, 0:1])


def orthonormal_t(parts):
    row_at = lax.broadcasted_iota(jnp.int32, (RK, 1), 0)
    for row in range(RK):
        total = None
        for part in parts:
            term = part * part[row : row + 1, :]
            for start in range(0, term.shape[1], 128):
                piece = term[:, start : start + 128]
                total = piece if total is None else total + piece
        dots = jnp.sum(total, axis=1, keepdims=True)
        inverse = lax.rsqrt(dots[row : row + 1, :] + 1e-20)
        scale = jnp.where(row_at == row, inverse, 1.0)
        taken = jnp.where(row_at > row, -dots * inverse * inverse, 0.0)
        parts = [part * scale + taken * part[row : row + 1, :] for part in parts]
    return parts


def greet(axes):
    barrier = pltpu.get_barrier_semaphore()
    greeted = 0
    for axis, count in axes:
        me = lax.axis_index(axis)
        for step in range(1, count):
            pl.semaphore_signal(
                barrier,
                inc=1,
                device_id={axis: lax.rem(me + step, count)},
                device_id_type=MESH_ID,
            )
        greeted += count - 1
    pl.semaphore_wait(barrier, greeted)


def ring_copies(axis, count, src, dst, send_sem, recv_sem, place):
    me = lax.axis_index(axis)
    copies = []
    for step in range(1, count):
        peer = lax.rem(me + step, count)
        from_at, to_at = place(me, peer, step)
        copies.append(
            pltpu.make_async_remote_copy(
                src_ref=src.at[from_at], dst_ref=dst.at[to_at],
                send_sem=send_sem.at[step], recv_sem=recv_sem.at[step],
                device_id={axis: peer}, device_id_type=MESH_ID,
            )
        )
    return copies


def ring_start(axis, count, x, landing, sems):
    for copy in ring_copies(axis, count, x, landing, sems[0], sems[1], lambda me, peer, step: (peer, step)):
        copy.start()


def ring_middle(axis, count, x, landing, y, sems):
    me = lax.axis_index(axis)
    firsts = ring_copies(axis, count, x, landing, sems[0], sems[1], lambda me, peer, step: (peer, step))
    total = x[me].astype(F32)
    for step in range(1, count):
        firsts[step - 1].wait_recv()
        total = total + landing[step].astype(F32)
    y[me] = total.astype(y.dtype)
    for copy in ring_copies(axis, count, y, y, sems[2], sems[3], lambda me, peer, step: (me, me)):
        copy.start()
    for copy in firsts:
        copy.wait_send()


def ring_end(axis, count, y, sems):
    me = lax.axis_index(axis)
    for step in range(1, count):
        source = lax.rem(me - step + count, count)
        pltpu.make_async_remote_copy(
            src_ref=y.at[source], dst_ref=y.at[source],
            send_sem=sems[2].at[step], recv_sem=sems[3].at[step],
            device_id={axis: source}, device_id_type=MESH_ID,
        ).wait_recv()
    for copy in ring_copies(axis, count, y, y, sems[2], sems[3], lambda me, peer, step: (me, me)):
        copy.wait_send()


def settle_kernel(workers, shards, rows, row_list, widths, *refs):
    gq_ref, eq_ref, gs_ref, es_ref, gains_ref, sq_ref = refs[0:6]
    grads, errs = refs[6:11], refs[11:16]
    ph, phs, own_ref, mean_ref, norm_ref, gain_ref = refs[16:22]
    (
        x, landing, y, small, sq_all, flat, x16, landing16, y16,
        sem_a, sem_b, sem_c, sem_d, sem_e, sem_f, sem_g, sem_h, sq_send, sq_recv,
    ) = refs[22:]
    first_sems, second_sems = (sem_a, sem_b, sem_c, sem_d), (sem_e, sem_f, sem_g, sem_h)
    step = pl.program_id(0)
    last = pl.num_programs(0) - 1
    places, _ = small_places(row_list)
    starts = [sum(widths[:k]) for k in range(5)]
    gains_at = gs_ref.shape[1]
    at = pl.multiple_of(step * TB, TB)

    @pl.when(step == 0)
    def _():
        greet((("rep", workers), ("voc", shards)))
        shard = lax.axis_index("voc")
        own = jnp.sum(sq_ref[...].reshape(8, 4, 128), axis=1)
        own = jnp.sum(jnp.sum(own, axis=0, keepdims=True), axis=1, keepdims=True)
        sq_all[shard] = jnp.broadcast_to(own, (8, 128))
        copies = ring_copies("voc", shards, sq_all, sq_all, sq_send, sq_recv, lambda me, peer, step: (me, me))
        for copy in copies:
            copy.start()
        gains = gains_ref[...]
        total = jnp.sum(jnp.sum(gains * gains, axis=0, keepdims=True), axis=1, keepdims=True)
        small[...] = jnp.zeros_like(small)
        for gap in range(1, shards):
            source = lax.rem(shard - gap + shards, shards)
            pltpu.make_async_remote_copy(
                src_ref=sq_all.at[source], dst_ref=sq_all.at[source],
                send_sem=sq_send.at[gap], recv_sem=sq_recv.at[gap],
                device_id={"voc": source}, device_id_type=MESH_ID,
            ).wait_recv()
        for copy in copies:
            copy.wait_send()
        for peer in range(shards):
            total = total + sq_all[peer][0:1, 0:1]
        norm = jnp.sqrt(total)
        norm_ref[...] = jnp.broadcast_to(norm, (8, 128))
        clip = jnp.minimum(1.0, CLIP_NORM / norm)

        chunk = gq_ref.shape[1] // workers
        part = small.shape[1] // workers
        small[:, :gains_at] = clip * gs_ref[...] + es_ref[...]
        small[:, gains_at : gains_at + gains.shape[1]] = clip * gains
        for j in range(workers):
            lanes = slice(j * chunk, (j + 1) * chunk)
            x[j, :, :chunk] = clip * gq_ref[:, lanes] + eq_ref[:, lanes]
            x[j, :, chunk:] = small[:, j * part : (j + 1) * part]
        ring_start("rep", workers, x, landing, first_sems)
        ring_middle("rep", workers, x, landing, y, first_sems)
        ring_end("rep", workers, y, first_sems)
        parts = orthonormal_t([y[j, :, :chunk] for j in range(workers)])
        for j in range(workers):
            ph[:, j * chunk : (j + 1) * chunk] = parts[j]
            small[:, j * part : (j + 1) * part] = y[j, :, chunk:]
        gain_ref[...] = small[:, gains_at : gains_at + gains.shape[1]] * (1.0 / workers)
        flat[...] = jnp.zeros_like(flat)
        for k in range(4):
            place, size = places[k], row_list[k]
            basis_t = orthonormal_t([small[:, place : place + round_up(size, 128)]])[0]
            phs[:, place : place + round_up(size, 128)] = basis_t
            basis_t = basis_t[:, :size]
            matrix = clip * grads[k + 1][...] + errs[k + 1][...].astype(F32)
            right_t = right_of(basis_t, matrix)
            flat[:, starts[k + 1] : starts[k + 1] + widths[k + 1]] = right_t

    clip = clip_of(norm_ref[...])
    matrix = clip * grads[0][...] + errs[0][...].astype(F32)
    matrix = keep_rows(matrix, step * TB, rows)
    flat[:, : widths[0]] += right_of(ph[:, pl.ds(at, TB)], matrix)

    @pl.when(step == last)
    def _():
        half = x16.shape[2]
        for j in range(workers):
            low, high = j * 2 * half, (j * 2 + 1) * half
            pair = jnp.concatenate([flat[:, low : low + half], flat[:, high : high + half]], axis=0)
            x16[j] = pair.astype(BF16)
        ring_start("rep", workers, x16, landing16, second_sems)
        own_ref[...] = flat[...]
        ring_middle("rep", workers, x16, landing16, y16, second_sems)
        ring_end("rep", workers, y16, second_sems)
        for j in range(workers):
            pair = y16[j].astype(F32) * (1.0 / workers)
            low, high = j * 2 * half, (j * 2 + 1) * half
            mean_ref[:, low : low + half] = pair[:8]
            mean_ref[:, high : high + half] = pair[8:]


def finish_kernel(rows, row_list, widths, *refs):
    grads, errs, moms, weights = refs[0:5], refs[5:10], refs[10:15], refs[15:19]
    ph_ref, phs_ref, own_ref, mean_ref, norm_ref, gain_ref, gain_mom_ref = refs[19:26]
    new_errs, new_moms, changed, rights = refs[26:31], refs[31:36], refs[36:41], refs[41:46]
    gain_change_ref, next_gain_ref = refs[46:48]
    step = pl.program_id(0)
    places, _ = small_places(row_list)
    starts = [sum(widths[:k]) for k in range(5)]
    clip = clip_of(norm_ref[...])

    def settle_one(k, basis_t):
        lanes = slice(starts[k], starts[k] + widths[k])
        matrix = clip * grads[k][...] + errs[k][...].astype(F32)
        new_errs[k][...] = matrix - product_of(basis_t, own_ref[:, lanes])
        moved = MOMENTUM * moms[k][...].astype(F32) + product_of(basis_t, mean_ref[:, lanes])
        new_moms[k][...] = moved
        change = -LEARN_RATE * moved
        changed[k][...] = weights[k - 1][...] + change if k else change

    @pl.when(step == 0)
    def _():
        moved = MOMENTUM * gain_mom_ref[...].astype(F32) + gain_ref[: gain_mom_ref.shape[0], :]
        next_gain_ref[...] = moved
        gain_change_ref[...] = -LEARN_RATE * moved
        for k in range(5):
            rights[k][...] = mean_ref[:, starts[k] : starts[k] + widths[k]]
        for k in range(1, 5):
            settle_one(k, phs_ref[:, places[k - 1] : places[k - 1] + row_list[k - 1]])

    settle_one(0, ph_ref[...])


def held(shape):
    return pl.BlockSpec(shape, lambda *_: (0,) * len(shape), pipeline_mode=pl.Buffered(1))


def settle(sketches, gains, gain_mom, grads, errs, moms, weights, workers, shards):
    gq, eq, gs, es, sq = sketches
    rows, width = grads[0].shape
    blocks = pl.cdiv(rows, TB)
    row_list = [g.shape[0] for g in grads[1:]]
    widths = [g.shape[1] for g in grads]
    small = round_up(gs.shape[1] + gains.shape[1], workers * 128)
    lanes = (gq.shape[1] + small) // workers
    right_lanes = round_up(sum(widths), workers * 256)
    half = right_lanes // workers // 2
    shape = jax.ShapeDtypeStruct
    block = pl.BlockSpec((TB, width), lambda i: (i, 0))
    small_specs = [held(g.shape) for g in grads[1:]]
    made = [
        shape((RK, blocks * TB), F32),
        shape(gs.shape, F32),
        shape((RK, right_lanes), F32),
        shape((RK, right_lanes), F32),
        shape((8, 128), F32),
        shape(gains.shape, F32),
    ]
    operands = (gq, eq, gs, es, gains, sq)
    sums = pl.pallas_call(
        functools.partial(settle_kernel, workers, shards, rows, row_list, widths),
        grid=(blocks,),
        in_specs=[held(o.shape) for o in operands] + ([block] + small_specs) * 2,
        out_specs=[held(m.shape) for m in made],
        out_shape=made,
        scratch_shapes=[pltpu.VMEM((workers, RK, lanes), F32)] * 3
        + [
            pltpu.VMEM((RK, small), F32),
            pltpu.VMEM((shards, 8, 128), F32),
            pltpu.VMEM((RK, right_lanes), F32),
        ]
        + [pltpu.VMEM((workers, 16, half), BF16)] * 3
        + [pltpu.SemaphoreType.DMA((workers,))] * 8
        + [pltpu.SemaphoreType.DMA((shards,))] * 2,
        compiler_params=pltpu.CompilerParams(
            collective_id=1, has_side_effects=True, vmem_limit_bytes=60 << 20
        ),
        name="settle_sums",
    )(*operands, *grads, *errs)
    ph, phs, own, mean, norm, gain = sums
    out = pl.pallas_call(
        functools.partial(finish_kernel, rows, row_list, widths),
        grid=(blocks,),
        in_specs=([block] + small_specs) * 3
        + small_specs
        + [pl.BlockSpec((RK, TB), lambda i: (0, i))]
        + [held(m.shape) for m in made[1:]]
        + [held(gain_mom.shape)],
        out_specs=([block] + small_specs) * 3
        + [held((RK, w)) for w in widths]
        + [held(gain_mom.shape)] * 2,
        out_shape=[shape(g.shape, F32) for g in grads] * 3
        + [shape((RK, w), F32) for w in widths]
        + [shape(gain_mom.shape, F32)] * 2,
        compiler_params=pltpu.CompilerParams(vmem_limit_bytes=60 << 20),
        name="settle_finish",
    )(*grads, *errs, *moms, *weights, ph, phs, own, mean, norm, gain, gain_mom)
    return out[0:5], out[5:10], out[10:15], out[15:20], norm, out[20], out[21]


EPS = 1e-06
QB = 256
INV_SQRT2 = 0.7071067811865476
INV_SQRT_2PI = 0.3989422804014327


def nt_dot(a, b):
    return lax.dot_general(a, b, (((1,), (1,)), ((), ())), preferred_element_type=F32)


def nn_dot(a, b):
    return jnp.dot(a, b, preferred_element_type=F32)


def scaled_rms(value, gain):
    return value * lax.rsqrt(jnp.mean(value * value, axis=1, keepdims=True) + EPS) * gain


def rms_back(grad, value, gain):
    inverse = lax.rsqrt(jnp.mean(value * value, axis=1, keepdims=True) + EPS)
    scaled = grad * gain
    along = jnp.mean(scaled * value, axis=1, keepdims=True)
    back = inverse * (scaled - value * (inverse * inverse * along))
    return back, jnp.sum(grad * value * inverse, axis=0, keepdims=True)


def turned(value_t, cos_t, sin_t, half):
    first, second = value_t[:half], value_t[half:]
    return jnp.concatenate([first * cos_t - second * sin_t, first * sin_t + second * cos_t], axis=0)


def turned_back(value_t, cos_t, sin_t, half):
    first, second = value_t[:half], value_t[half:]
    return jnp.concatenate([first * cos_t + second * sin_t, second * cos_t - first * sin_t], axis=0)


def causal_tile(scores_t, fill):
    size = scores_t.shape[1]
    key_at = lax.broadcasted_iota(jnp.int32, (size, size), 0)
    query_at = lax.broadcasted_iota(jnp.int32, (size, size), 1)
    tail = jnp.where(key_at <= query_at, scores_t[-size:], fill)
    if scores_t.shape[0] == size:
        return tail
    return jnp.concatenate([scores_t[:-size], tail], axis=0)


def forward_kernel(
    shards, axis,
    x0_ref, gains_ref, cos_ref, sin_ref, wqkv_ref, wo_own, wu_own, wd_own,
    n1_ref, qkv_ref, lse_ref, mixed_ref, x1_ref, n2_ref, x2_ref, n3_ref, wo_all, wu_all, wd_all, hid_any,
    hid_ref, hid_sem, wo_sems, wu_sems, wd_sems,
):
    tokens, width = x0_ref.shape
    half = HD // 2
    row_blocks = tokens // QB
    greet_all(shards)
    shard = lax.axis_index(axis)
    spreads = []
    for own, full, sems in ((wo_own, wo_all, wo_sems), (wu_own, wu_all, wu_sems), (wd_own, wd_all, wd_sems)):
        full[shard] = own[...].astype(BF16)
        spreads.append(Spread(full, shards, sems))
    await_all(shards)
    for spread in spreads:
        spread.start()

    @pl.loop(0, row_blocks)
    def _(block):
        rows = pl.ds(pl.multiple_of(block * QB, QB), QB)
        n1_ref[rows, :] = scaled_rms(x0_ref[rows, :].astype(F32), gains_ref[0:1, :]).astype(BF16)

    group = 4 * HD

    @pl.loop(0, width // group)
    def _(at):
        n1 = n1_ref[...]
        for part in range(3):
            start = pl.multiple_of(part * width + at * group, group)
            packed_t = nn_dot(n1, wqkv_ref[:, pl.ds(start, group)]).T
            if part < 2:
                cos_t, sin_t = cos_ref[...], sin_ref[...]
                packed_t = jnp.concatenate(
                    [
                        turned(packed_t[head * HD : (head + 1) * HD], cos_t, sin_t, half)
                        for head in range(4)
                    ],
                    axis=0,
                )
            if part == 0:
                packed_t = packed_t * HD ** (-0.5)
            qkv_ref[part, pl.ds(pl.multiple_of(at * group, group), group), :] = packed_t.astype(BF16)

    spreads[0].relay()

    def attend(head):
        rows = pl.ds(pl.multiple_of(head * HD, HD), HD)
        query_t, key_t, value_t = qkv_ref[0, rows, :], qkv_ref[1, rows, :], qkv_ref[2, rows, :]
        keys = key_t.T
        mixed_parts, lse_parts = [], []
        for block in range(row_blocks):
            count = (block + 1) * QB
            scores = causal_tile(
                nn_dot(keys[:count], query_t[:, block * QB : count]), -1e30
            )
            top = jnp.max(scores, axis=0, keepdims=True)
            weight = jnp.exp(scores - top)
            total = jnp.sum(weight, axis=0, keepdims=True)
            probs = (weight * (1.0 / total)).astype(BF16)
            mixed_parts.append(nn_dot(value_t[:, :count], probs))
            lse_parts.append(top + jnp.log(total))
        mixed_ref[rows, :] = jnp.concatenate(mixed_parts, axis=1).astype(BF16)
        lse_ref[head] = jnp.concatenate(lse_parts, axis=1)

    heads = width // HD
    pl.loop(0, heads // 4)(attend)
    spreads[1].relay()
    spreads[0].relay_across()
    pl.loop(heads // 4, heads // 2)(attend)
    spreads[2].relay()
    pl.loop(heads // 2, 3 * heads // 4)(attend)
    spreads[1].relay_across()
    pl.loop(3 * heads // 4, heads)(attend)
    spreads[0].finish()

    @pl.loop(0, row_blocks)
    def _(block):
        rows = pl.ds(pl.multiple_of(block * QB, QB), QB)
        mixed = mixed_ref[:, rows].T
        stream = x0_ref[rows, :].astype(F32) + nn_dot(mixed, wo_all[...].reshape(width, width))
        x1_ref[rows, :] = stream
        x2_ref[rows, :] = stream
        n2_ref[rows, :] = scaled_rms(stream, gains_ref[1:2, :]).astype(BF16)

    spreads[2].relay_across()
    spreads[1].finish()
    spreads[2].finish()
    chunk = hid_ref.shape[2]
    chunks = wu_all.shape[2] // chunk
    parts = chunk // wd_all.shape[1]

    def put(slot, at):
        return pltpu.make_async_copy(
            hid_ref.at[slot],
            hid_any.at[:, pl.ds(pl.multiple_of(at * chunk, chunk), chunk)],
            hid_sem.at[slot],
        )

    @pl.loop(0, chunks)
    def _(at):
        slot = lax.rem(at, 2)
        lanes = pl.ds(pl.multiple_of(at * chunk, chunk), chunk)

        @pl.when(at >= 2)
        def _():
            put(slot, at - 2).wait()

        for block in range(row_blocks):
            rows = slice(block * QB, (block + 1) * QB)
            hidden = nn_dot(n2_ref[rows, :], wu_all[:, :, lanes].reshape(width, chunk))
            hid_ref[slot, rows, :] = hidden
            active = (0.5 * hidden * (1.0 + lax.erf(hidden * INV_SQRT2))).astype(BF16)
            down = wd_all[pl.ds(at * parts, parts)].reshape(chunk, width)
            x2_ref[rows, :] += nn_dot(active, down)
        put(slot, at).start()

    @pl.loop(0, row_blocks)
    def _(block):
        rows = pl.ds(pl.multiple_of(block * QB, QB), QB)
        n3_ref[rows, :] = scaled_rms(x2_ref[rows, :], gains_ref[2:3, :]).astype(BF16)

    for at in range(max(0, chunks - 2), chunks):
        put(at % 2, at).wait()


VM = pl.BlockSpec(memory_space=pltpu.VMEM)
ANYWHERE = pl.BlockSpec(memory_space=pl.ANY)


def layer_forward(x0, gains, cos_t, sin_t, wqkv, slices, shards, axis):
    tokens, width = x0.shape
    hidden = slices[1].shape[1]
    shape = jax.ShapeDtypeStruct
    chunk = min(512, hidden)
    sems = pltpu.SemaphoreType.DMA((8, max(2, shards // 2)))
    return pl.pallas_call(
        functools.partial(forward_kernel, shards, axis),
        in_specs=[VM] * 8,
        out_specs=[VM] * 11 + [ANYWHERE],
        out_shape=[
            shape((tokens, width), BF16),
            shape((3, width, tokens), BF16),
            shape((width // HD, 1, tokens), F32),
            shape((width, tokens), BF16),
            shape((tokens, width), F32),
            shape((tokens, width), BF16),
            shape((tokens, width), F32),
            shape((tokens, width), BF16),
        ]
        + [shape((shards, *w.shape), BF16) for w in slices]
        + [shape((tokens, hidden), F32)],
        scratch_shapes=[
            pltpu.VMEM((2, tokens, chunk), F32),
            pltpu.SemaphoreType.DMA((2,)),
            sems,
            sems,
            sems,
        ],
        compiler_params=pltpu.CompilerParams(
            collective_id=5, has_side_effects=True, vmem_limit_bytes=60 << 20
        ),
        name="layer_forward",
    )(x0, gains, cos_t, sin_t, wqkv, *slices)


def backward_kernel(shard_axis, *refs):
    anys, refs = refs[:13], refs[13:]
    gains_ref, cos_ref, sin_ref, lse_ref = refs[0:4]
    dx0_ref, gqkv_ref, gout_ref, gup_ref, gdown_ref, ggains_ref = refs[4:10]
    kept, refs = refs[10:23], refs[23:]
    dn3_ref, x2_ref, hid_ref, wd_ref, wu_ref, x1_ref, n2_ref, wo_ref, mixed_ref, qkv_ref, x0_ref, n1_ref, wqkv_ref = kept
    grad_ref, part_ref, low_ref, act_ref, dhid_ref, dmixed_ref, dpacked_ref, turn_ref, load_sem = refs
    shard = lax.axis_index(shard_axis) if shard_axis else 0
    tokens, width = x2_ref.shape
    half = HD // 2
    row_blocks = tokens // QB
    loads = [
        pltpu.make_async_copy(src, dst, load_sem.at[at])
        for at, (src, dst) in enumerate(zip(anys, kept))
    ]
    for load in loads:
        load.start()

    def block_rows(block):
        return pl.ds(pl.multiple_of(block * QB, QB), QB)

    loads[0].wait()
    loads[1].wait()
    ggains_ref[...] = jnp.zeros_like(ggains_ref)

    @pl.loop(0, row_blocks)
    def _(block):
        rows = block_rows(block)
        back, gain = rms_back(dn3_ref[:, rows].T, x2_ref[rows, :], gains_ref[2:3, :])
        grad_ref[rows, :] = back
        low_ref[rows, :] = back.astype(BF16)
        part_ref[rows, :] = jnp.zeros_like(back)
        ggains_ref[2:3, :] += gain

    for at in (2, 3, 4):
        loads[at].wait()
    chunk = min(512, wu_ref.shape[1])

    @pl.loop(0, wu_ref.shape[1] // chunk)
    def _(at):
        lanes = pl.ds(pl.multiple_of(at * chunk, chunk), chunk)
        for block in range(row_blocks):
            rows = slice(block * QB, (block + 1) * QB)
            grad_act = nt_dot(low_ref[rows, :], wd_ref[lanes, :])
            hidden = hid_ref[rows, lanes]
            share = 0.5 + 0.5 * lax.erf(hidden * INV_SQRT2)
            slope = share + hidden * (INV_SQRT_2PI * jnp.exp(-0.5 * hidden * hidden))
            act_ref[rows, lanes] = (hidden * share).astype(BF16)
            grad_hid = (slope * grad_act).astype(BF16)
            dhid_ref[rows, lanes] = grad_hid
            part_ref[rows, :] += nt_dot(grad_hid, wu_ref[:, lanes])

    own = gdown_ref.shape[0]
    gdown_ref[...] = nn_dot(act_ref[:, pl.ds(pl.multiple_of(shard * own, own), own)].T, low_ref[...])
    loads[5].wait()
    loads[6].wait()
    own = gup_ref.shape[0]
    turn_ref[...] = n2_ref[...].T
    own_rows = pl.ds(pl.multiple_of(shard * own, own), own)

    @pl.loop(0, wu_ref.shape[1] // chunk)
    def _(at):
        lanes = pl.ds(pl.multiple_of(at * chunk, chunk), chunk)
        gup_ref[:, lanes] = nn_dot(turn_ref[own_rows, :], dhid_ref[:, lanes])

    loads[7].wait()

    @pl.loop(0, row_blocks)
    def _(block):
        rows = block_rows(block)
        back, gain = rms_back(part_ref[rows, :], x1_ref[rows, :], gains_ref[1:2, :])
        back = grad_ref[rows, :] + back
        grad_ref[rows, :] = back
        low = back.astype(BF16)
        low_ref[rows, :] = low
        ggains_ref[1:2, :] += gain
        dmixed_ref[:, rows] = nt_dot(low, wo_ref[...]).astype(BF16).T

    loads[8].wait()
    loads[9].wait()
    own = gout_ref.shape[0]
    own_rows = pl.ds(pl.multiple_of(shard * own, own), own)
    gout_ref[...] = nn_dot(mixed_ref[own_rows, :], low_ref[...])

    @pl.loop(0, width // (2 * HD))
    def _(pair):
        made = ([], [], [])
        for side in range(2):
            head = pair * 2 + side
            rows = pl.ds(pl.multiple_of(head * HD, HD), HD)
            query_t, key_t, value_t = qkv_ref[0, rows, :], qkv_ref[1, rows, :], qkv_ref[2, rows, :]
            dmix_t = dmixed_ref[rows, :]
            query, key, value, dmix = query_t.T, key_t.T, value_t.T, dmix_t.T
            lse = lse_ref[head]
            dquery_parts = []
            dkey = [None] * row_blocks
            dvalue = [None] * row_blocks
            for block in range(row_blocks):
                count = (block + 1) * QB
                at = slice(block * QB, count)
                scores = nn_dot(key[:count], query_t[:, at])
                probs = causal_tile(jnp.exp(scores - lse[:, at]), 0.0)
                dprobs = nn_dot(value[:count], dmix_t[:, at])
                delta = jnp.sum(probs * dprobs, axis=0, keepdims=True)
                dscores = (probs * (dprobs - delta)).astype(BF16)
                dquery_parts.append(nn_dot(key_t[:, :count], dscores))
                more_key = nn_dot(dscores, query[at])
                more_value = nn_dot(probs.astype(BF16), dmix[at])
                for piece in range(block + 1):
                    cut = slice(piece * QB, (piece + 1) * QB)
                    if dkey[piece] is None:
                        dkey[piece], dvalue[piece] = more_key[cut], more_value[cut]
                    else:
                        dkey[piece] = dkey[piece] + more_key[cut]
                        dvalue[piece] = dvalue[piece] + more_value[cut]
            cos_t, sin_t = cos_ref[...], sin_ref[...]
            dquery_t = jnp.concatenate(dquery_parts, axis=1) * HD ** (-0.5)
            dkey_t = jnp.concatenate(dkey, axis=0).T
            made[0].append(turned_back(dquery_t, cos_t, sin_t, half).T)
            made[1].append(turned_back(dkey_t, cos_t, sin_t, half).T)
            made[2].append(jnp.concatenate(dvalue, axis=0))
        for part in range(3):
            lanes = pl.ds(pl.multiple_of(part * width + pair * 2 * HD, 2 * HD), 2 * HD)
            dpacked_ref[:, lanes] = jnp.concatenate(made[part], axis=1).astype(BF16)

    for at in (10, 11, 12):
        loads[at].wait()
    own = gqkv_ref.shape[0]
    turn_ref[...] = n1_ref[...].T
    own_rows = pl.ds(pl.multiple_of(shard * own, own), own)

    @pl.loop(0, 3)
    def _(at):
        lanes = pl.ds(pl.multiple_of(at * width, width), width)
        gqkv_ref[:, lanes] = nn_dot(turn_ref[own_rows, :], dpacked_ref[:, lanes])

    @pl.loop(0, row_blocks)
    def _(block):
        rows = block_rows(block)
        back, gain = rms_back(
            nt_dot(dpacked_ref[rows, :], wqkv_ref[...]), x0_ref[rows, :].astype(F32), gains_ref[0:1, :]
        )
        dx0_ref[rows, :] = grad_ref[rows, :] + back
        ggains_ref[0:1, :] += gain


def layer_backward(shard_axis, slice_shapes, dn3_t, gains, cos_t, sin_t, projections, x0, kept):
    n1, qkv, lse, mixed_t, x1, n2, x2, _, hid = kept
    wqkv, wo, wu, wd = projections
    tokens, width = x2.shape
    shape = jax.ShapeDtypeStruct
    moved = (dn3_t, x2, hid, wd, wu, x1, n2, wo, mixed_t, qkv, x0, n1, wqkv)
    return pl.pallas_call(
        functools.partial(backward_kernel, shard_axis),
        in_specs=[ANYWHERE] * 13 + [VM] * 3 + [VM],
        out_specs=[VM] * 6,
        out_shape=[shape((tokens, width), F32)]
        + [shape(s, F32) for s in slice_shapes]
        + [shape((8, width), F32)],
        scratch_shapes=[pltpu.VMEM(m.shape, m.dtype) for m in moved]
        + [
            pltpu.VMEM((tokens, width), F32),
            pltpu.VMEM((tokens, width), F32),
            pltpu.VMEM((tokens, width), BF16),
            pltpu.VMEM(hid.shape, BF16),
            pltpu.VMEM(hid.shape, BF16),
            pltpu.VMEM((width, tokens), BF16),
            pltpu.VMEM((tokens, 3 * width), BF16),
            pltpu.VMEM((width, tokens), BF16),
            pltpu.SemaphoreType.DMA((13,)),
        ],
        compiler_params=pltpu.CompilerParams(vmem_limit_bytes=62 << 20),
        name="layer_backward",
    )(*moved, gains, cos_t, sin_t, lse)


def scatter_sketch_kernel(axis, rows, row_list, ids_ref, *refs):
    table_any, dx0_ref = refs[0:2]
    grads, errs, starts = (None, *refs[2:6]), refs[6:11], refs[11:16]
    full_any, gq_ref, eq_ref, gs_ref, es_ref, sq_ref = refs[16:22]
    whole_ref, load_sem, store_sem = refs[22:25]
    phase, step = pl.program_id(0), pl.program_id(1)
    steps = pl.num_programs(1)
    places, _ = small_places(row_list)
    size = rows - (pl.cdiv(rows, TB) - 1) * TB

    def tile_copy(at, count, inward):
        tile = pl.ds(pl.multiple_of(at * TB, TB), count)
        if inward:
            return pltpu.make_async_copy(table_any.at[tile, :], whole_ref.at[tile, :], load_sem.at[at])
        return pltpu.make_async_copy(whole_ref.at[tile, :], full_any.at[tile, :], store_sem.at[at])

    blocks = pl.cdiv(rows, TB)
    sizes = [TB] * (blocks - 1) + [size]

    @pl.when((phase == 0) & (step == 0))
    def _():
        for at in range(blocks):
            tile_copy(at, sizes[at], True).start()
        gs_ref[...] = jnp.zeros_like(gs_ref)
        es_ref[...] = jnp.zeros_like(es_ref)
        total = jnp.zeros(sq_ref.shape, F32)
        for k in range(4):
            grad = grads[k + 1][...]
            start_t = starts[k + 1][...]
            at = pl.ds(places[k], row_list[k])
            gs_ref[:, at] = left_of(grad, start_t)
            es_ref[:, at] = left_of_bf16(errs[k + 1][...], start_t)
            total = total + fold_squares(grad)
        sq_ref[...] = total

    @pl.when(phase == 0)
    def _():
        err = keep_rows(errs[0][...].astype(F32), step * TB, rows).astype(BF16)
        eq_ref[...] = left_of_bf16(err, starts[0][...])

    @pl.when((phase == 1) & (step == 0))
    def _():
        for at in range(blocks):
            tile_copy(at, sizes[at], True).wait()
        first = lax.axis_index(axis) * rows if axis else 0
        if blocks * TB > rows:
            whole_ref[pl.ds(rows, blocks * TB - rows), :] = jnp.zeros((blocks * TB - rows, whole_ref.shape[1]), F32)
        spare = blocks * TB

        @pl.loop(0, dx0_ref.shape[0] // 8)
        def _(group):
            base = pl.multiple_of(group * 8, 8)
            for side in range(8):
                row = ids_ref[base + side] - first
                row = jnp.where((row >= 0) & (row < rows), row, spare)
                whole_ref[pl.ds(row, 1), :] += dx0_ref[pl.ds(base + side, 1), :]

    tile = pl.ds(pl.multiple_of(step * TB, TB), TB)

    @pl.when(phase == 1)
    def _():
        grad = whole_ref[tile, :]
        gq_ref[...] = left_of(grad, starts[0][...])
        sq_ref[...] += fold_squares(grad)

    for at in range(blocks):

        @pl.when((phase == 1) & (step == at))
        def _():
            tile_copy(at, sizes[at], False).start()

    @pl.when((phase == 1) & (step == steps - 1))
    def _():
        for at in range(blocks):
            tile_copy(at, sizes[at], False).wait()


def scatter_sketch(token_ids, table_grad, dx0, grads, errs, starts_t, axis):
    rows, width = table_grad.shape
    blocks = pl.cdiv(rows, TB)
    row_list = [g.shape[0] for g in grads]
    _, small = small_places(row_list)

    def whole_at(shape):
        return pl.BlockSpec(shape, lambda *_: (0,) * len(shape), pipeline_mode=pl.Buffered(1))

    def at_phase(wanted, size, place):
        def index(p, i, ids):
            return place(jnp.where(p == wanted, i, jnp.where(p < wanted, 0, blocks - 1)))

        return pl.BlockSpec(size, index)

    shape = jax.ShapeDtypeStruct
    full, *sketches = pl.pallas_call(
        functools.partial(scatter_sketch_kernel, axis, rows, row_list),
        grid_spec=pltpu.PrefetchScalarGridSpec(
            num_scalar_prefetch=1,
            grid=(2, blocks),
            in_specs=[ANYWHERE, whole_at(dx0.shape)]
            + [whole_at(g.shape) for g in grads]
            + [at_phase(0, (TB, width), lambda i: (i, 0))]
            + [whole_at(e.shape) for e in errs[1:]]
            + [whole_at(s.shape) for s in starts_t],
            out_specs=[
                ANYWHERE,
                at_phase(1, (RK, TB), lambda i: (0, i)),
                at_phase(0, (RK, TB), lambda i: (0, i)),
            ]
            + [whole_at((RK, small)), whole_at((RK, small)), whole_at((8, 512))],
            scratch_shapes=[
                pltpu.VMEM((blocks * TB + 8, width), F32),
                pltpu.SemaphoreType.DMA((blocks,)),
                pltpu.SemaphoreType.DMA((blocks,)),
            ],
        ),
        out_shape=[
            shape((rows, width), F32),
            shape((RK, blocks * TB), F32),
            shape((RK, blocks * TB), F32),
            shape((RK, small), F32),
            shape((RK, small), F32),
            shape((8, 512), F32),
        ],
        compiler_params=pltpu.CompilerParams(vmem_limit_bytes=60 << 20),
        name="scatter_sketch",
    )(token_ids.reshape(-1), table_grad, dx0, *grads, *errs, *starts_t)
    return full, sketches


class Spread:
    def __init__(self, full, shards, sems):
        self.full, self.sems = full, sems
        self.shard, self.worker = lax.axis_index("voc"), lax.axis_index("rep")
        self.core = lax.rem(self.shard, 2)
        self.chip = self.shard // 2
        self.chips = shards // 2
        self.side = lax.rem(self.worker, 2)
        self.rows = full.shape[1] // 2

    def region(self, slot, side):
        return self.full.at[slot, pl.ds(pl.multiple_of(side * self.rows, self.rows), self.rows), :]

    def copy(self, ref, at, pair, peer):
        return pltpu.make_async_remote_copy(
            src_ref=ref, dst_ref=ref, send_sem=self.sems.at[2 * pair, at], recv_sem=self.sems.at[2 * pair + 1, at],
            device_id=peer, device_id_type=MESH_ID,
        )

    def source(self, at):
        return lax.rem(self.chip - at + self.chips, self.chips)

    def own_to_chip(self, at):
        peer = lax.rem(self.chip + at, self.chips) * 2 + self.core
        return self.copy(self.region(self.shard, self.side), at, 0, {"voc": peer})

    def from_chip(self, at):
        slot = self.source(at) * 2 + self.core
        return self.copy(self.region(slot, self.side), at, 0, {"voc": slot})

    def across(self, at, side):
        slot = self.source(at) * 2 + self.core
        return self.copy(self.region(slot, side), at, 1, {"rep": self.worker + 1 - 2 * self.side})

    def to_core(self, at, side, pair, core):
        slot = self.source(at) * 2 + core
        return self.copy(self.region(slot, side), at, pair, {"voc": self.shard + 1 - 2 * self.core})

    def own_to_core(self, slot):
        return self.copy(self.full.at[slot], 0, 2, {"voc": self.shard + 1 - 2 * self.core})

    def start(self):
        for at in range(1, self.chips):
            self.own_to_chip(at).start()
        self.own_to_core(self.shard).start()

    def relay(self):
        for at in range(1, self.chips):
            self.from_chip(at).wait_recv()
            self.across(at, self.side).start()
            self.to_core(at, self.side, 2, self.core).start()

    def relay_across(self):
        for at in range(1, self.chips):
            self.across(at, 1 - self.side).wait_recv()
            self.to_core(at, 1 - self.side, 3, self.core).start()

    def finish(self):
        self.own_to_core(self.shard + 1 - 2 * self.core).wait_recv()
        for at in range(1, self.chips):
            self.to_core(at, self.side, 2, 1 - self.core).wait_recv()
            self.to_core(at, 1 - self.side, 3, 1 - self.core).wait_recv()
        self.own_to_core(self.shard).wait_send()
        for at in range(1, self.chips):
            self.own_to_chip(at).wait_send()
            self.across(at, self.side).wait_send()
            self.to_core(at, self.side, 2, self.core).wait_send()
            self.to_core(at, 1 - self.side, 3, self.core).wait_send()


def greet_all(shards):
    barrier = pltpu.get_barrier_semaphore()
    me = lax.axis_index("voc")
    for step in range(1, shards):
        pl.semaphore_signal(
            barrier, inc=1, device_id={"voc": lax.rem(me + step, shards)}, device_id_type=MESH_ID
        )
    worker = lax.axis_index("rep")
    pl.semaphore_signal(
        barrier, inc=1, device_id={"rep": worker + 1 - 2 * lax.rem(worker, 2)}, device_id_type=MESH_ID
    )


def await_all(shards):
    pl.semaphore_wait(pltpu.get_barrier_semaphore(), shards)


def open_kernel(
    shards, axis, own_ref, weight_ref, x0_ref, full_ref,
    half_in, sums, core_send, core_recv, chip_send, chip_recv, back_send, back_recv, sems,
):
    greet_all(shards)
    shard = lax.axis_index(axis)
    core = lax.rem(shard, 2)
    chip = shard // 2
    partner = shard + 1 - 2 * core
    chips = shards // 2
    half = own_ref.shape[0] // 2
    own_half = pl.ds(pl.multiple_of(core * half, half), half)
    other_half = pl.ds(pl.multiple_of((1 - core) * half, half), half)
    spread = Spread(full_ref, shards, sems)
    full_ref[shard] = weight_ref[...].astype(BF16)

    def chip_copy(peer_chip, slot, at):
        return pltpu.make_async_remote_copy(
            src_ref=sums.at[slot], dst_ref=sums.at[slot],
            send_sem=chip_send.at[at], recv_sem=chip_recv.at[at],
            device_id={axis: peer_chip * 2 + core}, device_id_type=MESH_ID,
        )

    def back_copy(rows):
        return pltpu.make_async_remote_copy(
            src_ref=x0_ref.at[rows, :], dst_ref=x0_ref.at[rows, :],
            send_sem=back_send, recv_sem=back_recv,
            device_id={axis: partner}, device_id_type=MESH_ID,
        )

    await_all(shards)
    spread.start()
    first = pltpu.make_async_remote_copy(
        src_ref=own_ref.at[other_half, :], dst_ref=half_in,
        send_sem=core_send, recv_sem=core_recv,
        device_id={axis: partner}, device_id_type=MESH_ID,
    )
    first.start()
    first.wait_recv()
    sums[chip] = (own_ref[own_half, :].astype(F32) + half_in[...].astype(F32)).astype(BF16)
    for at in range(1, chips):
        chip_copy(lax.rem(chip + at, chips), chip, at).start()
    first.wait_send()
    spread.relay()
    total = sums[chip].astype(F32)
    for at in range(1, chips):
        source = lax.rem(chip - at + chips, chips)
        chip_copy(source, source, at).wait_recv()
        total = total + sums[source].astype(F32)
    x0_ref[own_half, :] = total.astype(BF16)
    back_copy(own_half).start()
    spread.relay_across()
    back_copy(other_half).wait_recv()
    for at in range(1, chips):
        chip_copy(lax.rem(chip + at, chips), chip, at).wait_send()
    back_copy(own_half).wait_send()
    spread.finish()


def opening(own, weight, shards, axis):
    tokens, width = own.shape
    chips = shards // 2
    shape = jax.ShapeDtypeStruct
    return pl.pallas_call(
        functools.partial(open_kernel, shards, axis),
        in_specs=[VM] * 2,
        out_specs=[VM] * 2,
        out_shape=[shape((tokens, width), BF16), shape((shards, *weight.shape), BF16)],
        scratch_shapes=[
            pltpu.VMEM((tokens // 2, width), BF16),
            pltpu.VMEM((chips, tokens // 2, width), BF16),
        ]
        + [pltpu.SemaphoreType.DMA] * 2
        + [pltpu.SemaphoreType.DMA((max(2, chips),))] * 2
        + [pltpu.SemaphoreType.DMA] * 2
        + [pltpu.SemaphoreType.DMA((8, max(2, chips)))],
        compiler_params=pltpu.CompilerParams(collective_id=4, has_side_effects=True),
        name="opening",
    )(own, weight)


TOKEN_LANES = 256


def vocab_block(rows):
    best = 16
    for size in range(16, 1025, 16):
        if rows % size == 0:
            best = size
    return best


def head_kernel(
    shards, axis,
    n3_ref, target_ref, table_ref,
    gtable_ref, dn3_any, loss_ref,
    dn3_ref, back_in, out_sem, kept, n3_t, tops, running, stats, z_ref, half_in, half_out,
    stat_send, stat_recv, core_send, core_recv, chip_send, chip_recv, back_send, back_recv,
):
    phase, step = pl.program_id(0), pl.program_id(1)
    last = pl.num_programs(1) - 1
    shard = lax.axis_index(axis)
    core = lax.rem(shard, 2)
    chip = shard // 2
    partner = shard + 1 - 2 * core
    chips = shards // 2
    tokens, width = n3_ref.shape
    block_rows = table_ref.shape[0]
    half = width // 2
    own_half = pl.ds(pl.multiple_of(core * half, half), half)
    other_half = pl.ds(pl.multiple_of((1 - core) * half, half), half)

    def stat_copy(peer, slot, at):
        return pltpu.make_async_remote_copy(
            src_ref=stats.at[slot], dst_ref=stats.at[slot],
            send_sem=stat_send.at[at], recv_sem=stat_recv.at[at],
            device_id={axis: peer}, device_id_type=MESH_ID,
        )

    def core_copy():
        return pltpu.make_async_remote_copy(
            src_ref=dn3_ref.at[other_half, :], dst_ref=half_in,
            send_sem=core_send, recv_sem=core_recv,
            device_id={axis: partner}, device_id_type=MESH_ID,
        )

    def chip_copy(peer_chip, slot, at):
        return pltpu.make_async_remote_copy(
            src_ref=half_out.at[slot], dst_ref=half_out.at[slot],
            send_sem=chip_send.at[at], recv_sem=chip_recv.at[at],
            device_id={axis: peer_chip * 2 + core}, device_id_type=MESH_ID,
        )

    def back_copy():
        return pltpu.make_async_remote_copy(
            src_ref=dn3_ref.at[own_half, :], dst_ref=back_in,
            send_sem=back_send, recv_sem=back_recv,
            device_id={axis: partner}, device_id_type=MESH_ID,
        )

    @pl.when((phase == 0) & (step == 0))
    def _():
        barrier = pltpu.get_barrier_semaphore()
        for at in range(1, shards):
            pl.semaphore_signal(
                barrier, inc=1,
                device_id={axis: lax.rem(shard + at, shards)}, device_id_type=MESH_ID,
            )
        n3_t[...] = n3_ref[...].T
        row_at = lax.broadcasted_iota(jnp.int32, running.shape, 0)
        running[...] = jnp.where(row_at == 0, -1e30, 0.0)
        dn3_ref[...] = jnp.zeros_like(dn3_ref)

    def hits(lanes):
        row_at = lax.broadcasted_iota(jnp.int32, (block_rows, TOKEN_LANES), 0)
        return row_at == target_ref[:, lanes] - step * block_rows

    @pl.when(phase == 0)
    def _():
        table = table_ref[...].astype(BF16)
        for start in range(0, tokens, TOKEN_LANES):
            lanes = slice(start, start + TOKEN_LANES)
            logits = nn_dot(table, n3_t[:, lanes])
            top = jnp.max(logits, axis=0, keepdims=True)
            weight = jnp.exp(logits - top)
            kept[step, :, lanes] = weight
            tops[step, :, lanes] = top
            total = jnp.sum(weight, axis=0, keepdims=True)
            picked = jnp.sum(jnp.where(hits(lanes), logits, 0.0), axis=0, keepdims=True)
            old = running[0:1, lanes]
            new = jnp.maximum(old, top)
            running[0:1, lanes] = new
            running[1:2, lanes] = running[1:2, lanes] * jnp.exp(old - new) + total * jnp.exp(top - new)
            running[2:3, lanes] += picked

    @pl.when((phase == 1) & (step == 0))
    def _():
        stats[shard] = running[...]
        pl.semaphore_wait(pltpu.get_barrier_semaphore(), shards - 1)
        sends = [stat_copy(lax.rem(shard + at, shards), shard, at) for at in range(1, shards)]
        for send in sends:
            send.start()
        for at in range(1, shards):
            source = lax.rem(shard - at + shards, shards)
            stat_copy(source, source, at).wait_recv()
        for send in sends:
            send.wait_send()
        top = stats[0, 0:1, :]
        for at in range(1, shards):
            top = jnp.maximum(top, stats[at, 0:1, :])
        total, picked = jnp.zeros_like(top), jnp.zeros_like(top)
        for at in range(shards):
            total = total + stats[at, 1:2, :] * jnp.exp(stats[at, 0:1, :] - top)
            picked = picked + stats[at, 2:3, :]
        z = top + jnp.log(total)
        z_ref[...] = z
        terms = (z - picked) + ZLOSS_WEIGHT * (z * z)
        loss = jnp.sum(terms, axis=1, keepdims=True) * (1.0 / tokens)
        loss_ref[...] = jnp.broadcast_to(loss, loss_ref.shape)

    def grad_logits(lanes):
        z = z_ref[:, lanes]
        factor = jnp.exp(tops[step, :, lanes] - z) * (1.0 + 2.0 * ZLOSS_WEIGHT * z) * (1.0 / tokens)
        return (kept[step, :, lanes] * factor - jnp.where(hits(lanes), 1.0 / tokens, 0.0)).astype(BF16)

    @pl.when(phase == 1)
    def _():
        table_t = table_ref[...].astype(BF16).T
        for start in range(0, tokens, TOKEN_LANES):
            lanes = slice(start, start + TOKEN_LANES)
            dn3_ref[:, lanes] += nn_dot(table_t, grad_logits(lanes))

    @pl.when((phase == 2) & (step == 0))
    def _():
        core_copy().start()

    @pl.when((phase == 2) & (step == jnp.minimum(2, last)))
    def _():
        core_copy().wait()
        half_out[chip] = (dn3_ref[own_half, :] + half_in[...]).astype(BF16)
        for at in range(1, chips):
            chip_copy(lax.rem(chip + at, chips), chip, at).start()

    @pl.when(phase == 2)
    def _():
        total = None
        for start in range(0, tokens, TOKEN_LANES):
            lanes = slice(start, start + TOKEN_LANES)
            part = nn_dot(grad_logits(lanes), n3_ref[lanes, :])
            total = part if total is None else total + part
        gtable_ref[...] = total

    @pl.when((phase == 2) & (step == last))
    def _():
        for at in range(1, chips):
            source = lax.rem(chip - at + chips, chips)
            chip_copy(source, source, at).wait_recv()
        for at in range(1, chips):
            chip_copy(lax.rem(chip + at, chips), chip, at).wait_send()
        whole_sum = half_out[0].astype(F32)
        for at in range(1, chips):
            whole_sum = whole_sum + half_out[at].astype(F32)
        dn3_ref[own_half, :] = whole_sum
        back_copy().start()
        puts = [
            pltpu.make_async_copy(dn3_ref.at[own_half, :], dn3_any.at[own_half, :], out_sem.at[0]),
            pltpu.make_async_copy(back_in, dn3_any.at[other_half, :], out_sem.at[1]),
        ]
        puts[0].start()
        back_copy().wait()
        puts[1].start()
        for put in puts:
            put.wait()


def vocabulary_head(n3, local_targets, table, shards, axis):
    rows, width = table.shape
    tokens = n3.shape[0]
    size = vocab_block(rows)
    blocks = rows // size
    shape = jax.ShapeDtypeStruct
    return pl.pallas_call(
        functools.partial(head_kernel, shards, axis),
        grid=(3, blocks),
        in_specs=[
            whole((tokens, width)),
            whole((1, tokens)),
            pl.BlockSpec((size, width), lambda p, i: (jnp.where(p == 2, blocks - 1, i), 0)),
        ],
        out_specs=[
            pl.BlockSpec((size, width), lambda p, i: (jnp.where(p == 2, i, 0), 0)),
            pl.BlockSpec(memory_space=pl.ANY),
            whole((8, 128)),
        ],
        out_shape=[shape((rows, width), F32), shape((width, tokens), F32), shape((8, 128), F32)],
        scratch_shapes=[
            pltpu.VMEM((width, tokens), F32),
            pltpu.VMEM((width // 2, tokens), F32),
            pltpu.SemaphoreType.DMA((2,)),
            pltpu.VMEM((blocks, size, tokens), F32),
            pltpu.VMEM((width, tokens), BF16),
            pltpu.VMEM((blocks, 1, tokens), F32),
            pltpu.VMEM((8, tokens), F32),
            pltpu.VMEM((shards, 8, tokens), F32),
            pltpu.VMEM((1, tokens), F32),
            pltpu.VMEM((width // 2, tokens), F32),
            pltpu.VMEM((shards // 2, width // 2, tokens), BF16),
        ]
        + [pltpu.SemaphoreType.DMA((shards,))] * 2
        + [pltpu.SemaphoreType.DMA] * 2
        + [pltpu.SemaphoreType.DMA((max(2, shards // 2),))] * 2
        + [pltpu.SemaphoreType.DMA] * 2,
        compiler_params=pltpu.CompilerParams(
            collective_id=3, has_side_effects=True, vmem_limit_bytes=62 << 20
        ),
        name="vocabulary_head",
    )(n3, local_targets, table)


def body(
    token_ids,
    target_ids,
    embedding,
    w_qkv,
    w_out,
    w_up,
    w_down,
    norm_gains,
    embed_mom,
    qkv_mom,
    out_mom,
    up_mom,
    down_mom,
    gain_mom,
    embed_err,
    qkv_err,
    out_err,
    up_err,
    down_err,
    embed_factor,
    qkv_factor,
    out_factor,
    up_factor,
    down_factor,
):
    seq_count, length = token_ids.shape
    tok_count = seq_count * length
    vocab_rows = embedding.shape[0]
    shard_pos = lax.axis_index("voc")
    workers = lax.axis_size("rep")
    slices = (w_qkv, w_out, w_up, w_down)
    shards = lax.axis_size("voc")
    local_ids = token_ids.reshape(-1) - shard_pos * vocab_rows
    inside = (local_ids >= 0) & (local_ids < vocab_rows)
    rows = embedding.at[jnp.clip(local_ids, 0, vocab_rows - 1)].get(mode="promise_in_bounds")
    own_rows = jnp.where(inside[:, None], rows, 0.0).astype(BF16)
    x0, qkv_all = opening(own_rows, w_qkv, shards, "voc")
    wqkv = qkv_all.reshape(-1, w_qkv.shape[1])
    half = HD // 2
    angles = (10000.0 ** (-jnp.arange(half).astype(F32) / half))[:, None] * jnp.arange(length).astype(F32)[None, :]
    cos_t, sin_t = jnp.cos(angles), jnp.sin(angles)
    *kept, n3, wo, wu, wd, hid = layer_forward(
        x0, norm_gains, cos_t, sin_t, wqkv, slices[1:], shards, "voc"
    )
    kept = (*kept, n3, hid)
    projections = (wqkv, *(w.reshape(-1, w.shape[2]) for w in (wo, wu, wd)))
    local_targets = target_ids.reshape(1, -1) - shard_pos * vocab_rows
    grad_table_head, dn3_t, loss_tile = vocabulary_head(
        n3, local_targets, embedding, lax.axis_size("voc"), "voc"
    )
    loss_value = loss_tile[0, 0]
    grad_in, *grad_mats, grad_gains = layer_backward(
        "voc", [w.shape for w in slices], dn3_t, norm_gains, cos_t, sin_t, projections, x0, kept
    )
    errors = [e[0] for e in (embed_err, qkv_err, out_err, up_err, down_err)]
    starts_t = [
        f[0].T for f in (embed_factor, qkv_factor, out_factor, up_factor, down_factor)
    ]
    full_grad, sketches = scatter_sketch(
        token_ids, grad_table_head, grad_in, grad_mats, errors, starts_t, "voc"
    )
    new_errors, new_moments, changed, rights, norm, gain_change, next_gain_mom = settle(
        sketches,
        grad_gains,
        gain_mom,
        [full_grad, *grad_mats],
        errors,
        (embed_mom, qkv_mom, out_mom, up_mom, down_mom),
        slices,
        workers,
        shards,
    )
    return (
        loss_value.reshape(1),
        norm[0, 0].reshape(1),
        *changed,
        gain_change,
        *new_moments,
        next_gain_mom,
        *(e[None] for e in new_errors),
        *(r.T[None] for r in rights),
    )


def solution(mesh):
    in_specs = (
        P("rep", None),
        P("rep", None),
        P("voc", None),
        P("voc", None),
        P("voc", None),
        P("voc", None),
        P("voc", None),
        P(),
        P("voc", None),
        P("voc", None),
        P("voc", None),
        P("voc", None),
        P("voc", None),
        P(),
        P("rep", "voc", None),
        P("rep", "voc", None),
        P("rep", "voc", None),
        P("rep", "voc", None),
        P("rep", "voc", None),
        P("voc", None, None),
        P("voc", None, None),
        P("voc", None, None),
        P("voc", None, None),
        P("voc", None, None),
    )
    out_specs = (
        P("rep"),
        P("rep"),
        P("voc", None),
        P("voc", None),
        P("voc", None),
        P("voc", None),
        P("voc", None),
        P(),
        P("voc", None),
        P("voc", None),
        P("voc", None),
        P("voc", None),
        P("voc", None),
        P(),
        P("rep", "voc", None),
        P("rep", "voc", None),
        P("rep", "voc", None),
        P("rep", "voc", None),
        P("rep", "voc", None),
        P("voc", None, None),
        P("voc", None, None),
        P("voc", None, None),
        P("voc", None, None),
        P("voc", None, None),
    )
    return jax.shard_map(body, mesh=mesh, in_specs=in_specs, out_specs=out_specs, check_vma=False)
```

```python
import functools

import jax
import jax.numpy as jnp
import numpy as np
from jax import lax
from jax.experimental import pallas as pl
from jax.experimental.pallas import tpu as pltpu
from jax.sharding import PartitionSpec as P

HD = 64


MOMENTUM = 0.9
LEARN_RATE = 10.0
CLIP_NORM = 1.0
ZLOSS_WEIGHT = 0.01


TB = 1024
RK = 8
F32 = jnp.float32
BF16 = jnp.bfloat16
MESH_ID = pl.DeviceIdType.MESH


def round_up(value, step):
    return (value + step - 1) // step * step


def halves(value):
    high = value.astype(BF16).astype(F32)
    return high, value - high


def dims_of(value, contract_left, contract_right):
    return (((contract_left,), (contract_right,)), ((), ()))


def left_of(matrix, start_t):
    s_high, s_low = halves(start_t)
    both = jnp.concatenate([s_high, s_low], axis=0).astype(BF16)
    high = matrix.astype(BF16)
    low = (matrix - high.astype(F32)).astype(BF16)
    nt = (((1,), (1,)), ((), ()))
    main = lax.dot_general(both, high, nt, preferred_element_type=F32)
    rest = lax.dot_general(s_high.astype(BF16), low, nt, preferred_element_type=F32)
    return main[:RK] + main[RK:] + rest


def left_of_bf16(matrix, start_t):
    s_high, s_low = halves(start_t)
    both = jnp.concatenate([s_high, s_low], axis=0).astype(BF16)
    main = lax.dot_general(both, matrix, (((1,), (1,)), ((), ())), preferred_element_type=F32)
    return main[:RK] + main[RK:]


def right_of(basis_t, matrix):
    b_high, b_low = halves(basis_t)
    both = jnp.concatenate([b_high, b_low], axis=0).astype(BF16)
    high = matrix.astype(BF16)
    low = (matrix - high.astype(F32)).astype(BF16)
    main = jnp.dot(both, high, preferred_element_type=F32)
    rest = jnp.dot(b_high.astype(BF16), low, preferred_element_type=F32)
    return main[:RK] + main[RK:] + rest


def product_of(basis_t, right_t):
    b_high, b_low = halves(basis_t)
    r_high, r_low = halves(right_t)
    zero_b, zero_r = jnp.zeros_like(b_high), jnp.zeros_like(r_high)
    left = jnp.concatenate([b_high, b_low, b_high, zero_b], axis=0).astype(BF16)
    right = jnp.concatenate([r_high, r_high, r_low, zero_r], axis=0).astype(BF16)
    return lax.dot_general(left, right, (((0,), (0,)), ((), ())), preferred_element_type=F32)


def keep_rows(value, first_row, rows):
    at = first_row + lax.broadcasted_iota(jnp.int32, value.shape, 0)
    return jnp.where(at < rows, value, jnp.zeros_like(value))


def fold_squares(value):
    squares = value * value
    rows, columns = value.shape
    by_sublane = jnp.sum(squares.reshape(rows // 8, 8, columns), axis=0)
    total = by_sublane[:, :512]
    for start in range(512, columns, 512):
        total = total + by_sublane[:, start : start + 512]
    return total


def small_places(rows_list):
    places, at = [], 0
    for rows in rows_list:
        places.append(at)
        at += round_up(rows, 128)
    return places, at


def whole(shape):
    return pl.BlockSpec(shape, lambda *_: (0,) * len(shape))


def clip_of(norm_tile):
    return jnp.minimum(1.0, CLIP_NORM / norm_tile[0:1, 0:1])


def orthonormal_t(parts):
    row_at = lax.broadcasted_iota(jnp.int32, (RK, 1), 0)
    for row in range(RK):
        total = None
        for part in parts:
            term = part * part[row : row + 1, :]
            for start in range(0, term.shape[1], 128):
                piece = term[:, start : start + 128]
                total = piece if total is None else total + piece
        dots = jnp.sum(total, axis=1, keepdims=True)
        inverse = lax.rsqrt(dots[row : row + 1, :] + 1e-20)
        scale = jnp.where(row_at == row, inverse, 1.0)
        taken = jnp.where(row_at > row, -dots * inverse * inverse, 0.0)
        parts = [part * scale + taken * part[row : row + 1, :] for part in parts]
    return parts


def greet(axes):
    barrier = pltpu.get_barrier_semaphore()
    greeted = 0
    for axis, count in axes:
        me = lax.axis_index(axis)
        for step in range(1, count):
            pl.semaphore_signal(
                barrier,
                inc=1,
                device_id={axis: lax.rem(me + step, count)},
                device_id_type=MESH_ID,
            )
        greeted += count - 1
    pl.semaphore_wait(barrier, greeted)


def ring_copies(axis, count, src, dst, send_sem, recv_sem, place):
    me = lax.axis_index(axis)
    copies = []
    for step in range(1, count):
        peer = lax.rem(me + step, count)
        from_at, to_at = place(me, peer, step)
        copies.append(
            pltpu.make_async_remote_copy(
                src_ref=src.at[from_at], dst_ref=dst.at[to_at],
                send_sem=send_sem.at[step], recv_sem=recv_sem.at[step],
                device_id={axis: peer}, device_id_type=MESH_ID,
            )
        )
    return copies


def ring_start(axis, count, x, landing, sems):
    for copy in ring_copies(axis, count, x, landing, sems[0], sems[1], lambda me, peer, step: (peer, step)):
        copy.start()


def ring_middle(axis, count, x, landing, y, sems):
    me = lax.axis_index(axis)
    firsts = ring_copies(axis, count, x, landing, sems[0], sems[1], lambda me, peer, step: (peer, step))
    total = x[me].astype(F32)
    for step in range(1, count):
        firsts[step - 1].wait_recv()
        total = total + landing[step].astype(F32)
    y[me] = total.astype(y.dtype)
    for copy in ring_copies(axis, count, y, y, sems[2], sems[3], lambda me, peer, step: (me, me)):
        copy.start()
    for copy in firsts:
        copy.wait_send()


def ring_end(axis, count, y, sems):
    me = lax.axis_index(axis)
    for step in range(1, count):
        source = lax.rem(me - step + count, count)
        pltpu.make_async_remote_copy(
            src_ref=y.at[source], dst_ref=y.at[source],
            send_sem=sems[2].at[step], recv_sem=sems[3].at[step],
            device_id={axis: source}, device_id_type=MESH_ID,
        ).wait_recv()
    for copy in ring_copies(axis, count, y, y, sems[2], sems[3], lambda me, peer, step: (me, me)):
        copy.wait_send()


def settle_kernel(workers, shards, rows, row_list, widths, *refs):
    gq_ref, eq_ref, gs_ref, es_ref, gains_ref, sq_ref = refs[0:6]
    grads, errs = refs[6:11], refs[11:16]
    ph, phs, own_ref, mean_ref, norm_ref, gain_ref = refs[16:22]
    (
        x, landing, y, small, sq_all, flat, x16, landing16, y16, table16, table_send, table_recv,
        sem_a, sem_b, sem_c, sem_d, sem_e, sem_f, sem_g, sem_h, sq_send, sq_recv,
    ) = refs[22:]
    first_sems, second_sems = (sem_a, sem_b, sem_c, sem_d), (sem_e, sem_f, sem_g, sem_h)
    step = pl.program_id(0)
    last = pl.num_programs(0) - 1
    places, _ = small_places(row_list)
    starts = [sum(widths[:k]) for k in range(5)]
    gains_at = gs_ref.shape[1]
    at = pl.multiple_of(step * TB, TB)

    @pl.when(step == 0)
    def _():
        greet((("rep", workers), ("voc", shards)))
        shard = lax.axis_index("voc")
        own = jnp.sum(sq_ref[...].reshape(8, 4, 128), axis=1)
        own = jnp.sum(jnp.sum(own, axis=0, keepdims=True), axis=1, keepdims=True)
        sq_all[shard] = jnp.broadcast_to(own, (8, 128))
        copies = ring_copies("voc", shards, sq_all, sq_all, sq_send, sq_recv, lambda me, peer, step: (me, me))
        for copy in copies:
            copy.start()
        gains = gains_ref[...]
        total = jnp.sum(jnp.sum(gains * gains, axis=0, keepdims=True), axis=1, keepdims=True)
        small[...] = jnp.zeros_like(small)
        for gap in range(1, shards):
            source = lax.rem(shard - gap + shards, shards)
            pltpu.make_async_remote_copy(
                src_ref=sq_all.at[source], dst_ref=sq_all.at[source],
                send_sem=sq_send.at[gap], recv_sem=sq_recv.at[gap],
                device_id={"voc": source}, device_id_type=MESH_ID,
            ).wait_recv()
        for copy in copies:
            copy.wait_send()
        for peer in range(shards):
            total = total + sq_all[peer][0:1, 0:1]
        norm = jnp.sqrt(total)
        norm_ref[...] = jnp.broadcast_to(norm, (8, 128))
        clip = jnp.minimum(1.0, CLIP_NORM / norm)

        chunk = gq_ref.shape[1] // workers
        part = small.shape[1] // workers
        small[:, :gains_at] = clip * gs_ref[...] + es_ref[...]
        small[:, gains_at : gains_at + gains.shape[1]] = clip * gains
        for j in range(workers):
            lanes = slice(j * chunk, (j + 1) * chunk)
            x[j, :, :chunk] = clip * gq_ref[:, lanes] + eq_ref[:, lanes]
            x[j, :, chunk:] = small[:, j * part : (j + 1) * part]
        ring_start("rep", workers, x, landing, first_sems)
        ring_middle("rep", workers, x, landing, y, first_sems)
        ring_end("rep", workers, y, first_sems)
        parts = orthonormal_t([y[j, :, :chunk] for j in range(workers)])
        for j in range(workers):
            ph[:, j * chunk : (j + 1) * chunk] = parts[j]
            small[:, j * part : (j + 1) * part] = y[j, :, chunk:]
        gain_ref[...] = small[:, gains_at : gains_at + gains.shape[1]] * (1.0 / workers)
        flat[...] = jnp.zeros_like(flat)
        for k in range(4):
            place, size = places[k], row_list[k]
            basis_t = orthonormal_t([small[:, place : place + round_up(size, 128)]])[0]
            phs[:, place : place + round_up(size, 128)] = basis_t
            basis_t = basis_t[:, :size]
            matrix = clip * grads[k + 1][...] + errs[k + 1][...].astype(F32)
            right_t = right_of(basis_t, matrix)
            flat[:, starts[k + 1] : starts[k + 1] + widths[k + 1]] = right_t
        half = x16.shape[2]
        for j in range(workers):
            low, high = starts[1] + j * 2 * half, starts[1] + (j * 2 + 1) * half
            pair = jnp.concatenate([flat[:, low : low + half], flat[:, high : high + half]], axis=0)
            x16[j] = pair.astype(BF16)
        ring_start("rep", workers, x16, landing16, second_sems)

    clip = clip_of(norm_ref[...])
    matrix = clip * grads[0][...] + errs[0][...].astype(F32)
    matrix = keep_rows(matrix, step * TB, rows)
    flat[:, : widths[0]] += right_of(ph[:, pl.ds(at, TB)], matrix)

    @pl.when(step == last // 2)
    def _():
        ring_middle("rep", workers, x16, landing16, y16, second_sems)

    @pl.when(step == last)
    def _():
        me = lax.axis_index("rep")
        split = widths[0] // 2
        table16[me] = jnp.concatenate([flat[:, :split], flat[:, split : 2 * split]], axis=0).astype(BF16)
        copies = ring_copies(
            "rep", workers, table16, table16, table_send, table_recv, lambda me, peer, step: (me, me)
        )
        for copy in copies:
            copy.start()
        own_ref[...] = flat[...]
        ring_end("rep", workers, y16, second_sems)
        half = x16.shape[2]
        for j in range(workers):
            pair = y16[j].astype(F32) * (1.0 / workers)
            low, high = starts[1] + j * 2 * half, starts[1] + (j * 2 + 1) * half
            mean_ref[:, low : low + half] = pair[:8]
            mean_ref[:, high : high + half] = pair[8:]
        for gap in range(1, workers):
            source = lax.rem(me - gap + workers, workers)
            pltpu.make_async_remote_copy(
                src_ref=table16.at[source], dst_ref=table16.at[source],
                send_sem=table_send.at[gap], recv_sem=table_recv.at[gap],
                device_id={"rep": source}, device_id_type=MESH_ID,
            ).wait_recv()
        total = table16[0].astype(F32)
        for j in range(1, workers):
            total = total + table16[j].astype(F32)
        total = total * (1.0 / workers)
        mean_ref[:, :split] = total[:8]
        mean_ref[:, split : 2 * split] = total[8:]
        for copy in copies:
            copy.wait_send()


def finish_kernel(rows, row_list, widths, *refs):
    grads, errs, moms, weights = refs[0:5], refs[5:10], refs[10:15], refs[15:19]
    ph_ref, phs_ref, own_ref, mean_ref, norm_ref, gain_ref, gain_mom_ref, loss_ref = refs[19:27]
    new_errs, new_moms, changed, rights = refs[27:32], refs[32:37], refs[37:42], refs[42:47]
    gain_change_ref, next_gain_ref, loss_out, norm_out = refs[47:51]
    step = pl.program_id(0)
    places, _ = small_places(row_list)
    starts = [sum(widths[:k]) for k in range(5)]
    clip = clip_of(norm_ref[...])

    def settle_one(k, basis_t):
        lanes = slice(starts[k], starts[k] + widths[k])
        matrix = clip * grads[k][...] + errs[k][...].astype(F32)
        new_errs[k][...] = matrix - product_of(basis_t, own_ref[:, lanes])
        moved = MOMENTUM * moms[k][...].astype(F32) + product_of(basis_t, mean_ref[:, lanes])
        new_moms[k][...] = moved
        change = -LEARN_RATE * moved
        changed[k][...] = weights[k - 1][...] + change if k else change

    @pl.when(step == 0)
    def _():
        moved = MOMENTUM * gain_mom_ref[...].astype(F32) + gain_ref[: gain_mom_ref.shape[0], :]
        next_gain_ref[...] = moved
        gain_change_ref[...] = -LEARN_RATE * moved
        loss_out[0] = jnp.max(loss_ref[...])
        norm_out[0] = jnp.max(norm_ref[...])
        for k in range(5):
            rights[k][...] = mean_ref[:, starts[k] : starts[k] + widths[k]]
        for k in range(1, 5):
            settle_one(k, phs_ref[:, places[k - 1] : places[k - 1] + row_list[k - 1]])

    settle_one(0, ph_ref[...])


def held(shape):
    return pl.BlockSpec(shape, lambda *_: (0,) * len(shape), pipeline_mode=pl.Buffered(1))


def settle(loss_tile, sketches, gains, gain_mom, grads, errs, moms, weights, workers, shards):
    gq, eq, gs, es, sq = sketches
    rows, width = grads[0].shape
    blocks = pl.cdiv(rows, TB)
    row_list = [g.shape[0] for g in grads[1:]]
    widths = [g.shape[1] for g in grads]
    small = round_up(gs.shape[1] + gains.shape[1], workers * 128)
    lanes = (gq.shape[1] + small) // workers
    small_lanes = round_up(sum(widths[1:]), workers * 256)
    right_lanes = widths[0] + small_lanes
    half = small_lanes // workers // 2
    shape = jax.ShapeDtypeStruct
    block = pl.BlockSpec((TB, width), lambda i: (i, 0))
    small_specs = [held(g.shape) for g in grads[1:]]
    made = [
        shape((RK, blocks * TB), F32),
        shape(gs.shape, F32),
        shape((RK, right_lanes), F32),
        shape((RK, right_lanes), F32),
        shape((8, 128), F32),
        shape(gains.shape, F32),
    ]
    operands = (gq, eq, gs, es, gains, sq)
    sums = pl.pallas_call(
        functools.partial(settle_kernel, workers, shards, rows, row_list, widths),
        grid=(blocks,),
        in_specs=[held(o.shape) for o in operands] + ([block] + small_specs) * 2,
        out_specs=[held(m.shape) for m in made],
        out_shape=made,
        scratch_shapes=[pltpu.VMEM((workers, RK, lanes), F32)] * 3
        + [
            pltpu.VMEM((RK, small), F32),
            pltpu.VMEM((shards, 8, 128), F32),
            pltpu.VMEM((RK, right_lanes), F32),
        ]
        + [pltpu.VMEM((workers, 16, half), BF16)] * 3
        + [pltpu.VMEM((workers, 16, width // 2), BF16)]
        + [pltpu.SemaphoreType.DMA((workers,))] * 2
        + [pltpu.SemaphoreType.DMA((workers,))] * 8
        + [pltpu.SemaphoreType.DMA((shards,))] * 2,
        compiler_params=pltpu.CompilerParams(
            collective_id=1, has_side_effects=True, vmem_limit_bytes=60 << 20
        ),
        name="settle_sums",
    )(*operands, *grads, *errs)
    ph, phs, own, mean, norm, gain = sums
    out = pl.pallas_call(
        functools.partial(finish_kernel, rows, row_list, widths),
        grid=(blocks,),
        in_specs=([block] + small_specs) * 3
        + small_specs
        + [pl.BlockSpec((RK, TB), lambda i: (0, i))]
        + [held(m.shape) for m in made[1:]]
        + [held(gain_mom.shape), held(loss_tile.shape)],
        out_specs=([block] + small_specs) * 3
        + [held((RK, w)) for w in widths]
        + [held(gain_mom.shape)] * 2
        + [pl.BlockSpec(memory_space=pltpu.SMEM)] * 2,
        out_shape=[shape(g.shape, F32) for g in grads] * 3
        + [shape((RK, w), F32) for w in widths]
        + [shape(gain_mom.shape, F32)] * 2
        + [shape((1,), F32)] * 2,
        compiler_params=pltpu.CompilerParams(vmem_limit_bytes=60 << 20),
        name="settle_finish",
    )(*grads, *errs, *moms, *weights, ph, phs, own, mean, norm, gain, gain_mom, loss_tile)
    return out[0:5], out[5:10], out[10:15], out[15:20], *out[20:24]


EPS = 1e-06
QB = 256
INV_SQRT2 = 0.7071067811865476
INV_SQRT_2PI = 0.3989422804014327


def nt_dot(a, b):
    return lax.dot_general(a, b, (((1,), (1,)), ((), ())), preferred_element_type=F32)


def nn_dot(a, b):
    return jnp.dot(a, b, preferred_element_type=F32)


def scaled_rms(value, gain):
    return value * lax.rsqrt(jnp.mean(value * value, axis=1, keepdims=True) + EPS) * gain


def rms_back(grad, value, gain):
    inverse = lax.rsqrt(jnp.mean(value * value, axis=1, keepdims=True) + EPS)
    scaled = grad * gain
    along = jnp.mean(scaled * value, axis=1, keepdims=True)
    back = inverse * (scaled - value * (inverse * inverse * along))
    return back, jnp.sum(grad * value * inverse, axis=0, keepdims=True)


def turned(value_t, cos_t, sin_t, half):
    first, second = value_t[:half], value_t[half:]
    return jnp.concatenate([first * cos_t - second * sin_t, first * sin_t + second * cos_t], axis=0)


def turned_back(value_t, cos_t, sin_t, half):
    first, second = value_t[:half], value_t[half:]
    return jnp.concatenate([first * cos_t + second * sin_t, second * cos_t - first * sin_t], axis=0)


def causal_tile(scores_t, fill):
    size = scores_t.shape[1]
    key_at = lax.broadcasted_iota(jnp.int32, (size, size), 0)
    query_at = lax.broadcasted_iota(jnp.int32, (size, size), 1)
    tail = jnp.where(key_at <= query_at, scores_t[-size:], fill)
    if scores_t.shape[0] == size:
        return tail
    return jnp.concatenate([scores_t[:-size], tail], axis=0)


def forward_kernel(
    shards, axis,
    x0_ref, gains_ref, cos_ref, sin_ref, wqkv_ref, wo_own, wu_own, wd_own,
    n1_ref, qkv_ref, lse_ref, mixed_ref, x1_ref, n2_ref, x2_ref, n3_ref, wo_all, wu_all, wd_all, hid_any,
    hid_ref, hid_sem, wo_sems, wu_sems, wd_sems,
):
    tokens, width = x0_ref.shape
    half = HD // 2
    row_blocks = tokens // QB
    greet_all(shards)
    shard = lax.axis_index(axis)
    spreads = []
    for own, full, sems in ((wo_own, wo_all, wo_sems), (wu_own, wu_all, wu_sems), (wd_own, wd_all, wd_sems)):
        full[shard] = own[...].astype(BF16)
        spreads.append(Spread(full, shards, sems))
    await_all(shards)
    for spread in spreads:
        spread.start()

    @pl.loop(0, row_blocks)
    def _(block):
        rows = pl.ds(pl.multiple_of(block * QB, QB), QB)
        n1_ref[rows, :] = scaled_rms(x0_ref[rows, :].astype(F32), gains_ref[0:1, :]).astype(BF16)

    group = 4 * HD

    @pl.loop(0, width // group)
    def _(at):
        n1 = n1_ref[...]
        for part in range(3):
            start = pl.multiple_of(part * width + at * group, group)
            packed_t = nn_dot(n1, wqkv_ref[:, pl.ds(start, group)]).T
            if part < 2:
                cos_t, sin_t = cos_ref[...], sin_ref[...]
                packed_t = jnp.concatenate(
                    [
                        turned(packed_t[head * HD : (head + 1) * HD], cos_t, sin_t, half)
                        for head in range(4)
                    ],
                    axis=0,
                )
            if part == 0:
                packed_t = packed_t * HD ** (-0.5)
            qkv_ref[part, pl.ds(pl.multiple_of(at * group, group), group), :] = packed_t.astype(BF16)

    spreads[0].relay()

    @pl.loop(0, width // (2 * HD))
    def _(pair):
        @pl.when(pair == 1)
        def _():
            spreads[1].relay()
            spreads[0].relay_across()

        @pl.when(pair == 2)
        def _():
            spreads[2].relay()

        @pl.when(pair == 3)
        def _():
            spreads[1].relay_across()

        places = [pl.ds(pl.multiple_of((pair * 2 + side) * HD, HD), HD) for side in range(2)]
        keys = [qkv_ref[1, places[side], :].T for side in range(2)]

        def scores_of(side, block):
            count = (block + 1) * QB
            query_t = qkv_ref[0, places[side], block * QB : count]
            return causal_tile(nn_dot(keys[side][:count], query_t), -1e30)

        work = [(side, block) for side in range(2) for block in range(row_blocks)]
        ahead = scores_of(*work[0])
        mixed_parts, lse_parts = ([], []), ([], [])
        for at, (side, block) in enumerate(work):
            scores = ahead
            if at + 1 < len(work):
                ahead = scores_of(*work[at + 1])
            top = jnp.max(scores, axis=0, keepdims=True)
            weight = jnp.exp(scores - top)
            total = jnp.sum(weight, axis=0, keepdims=True)
            probs = (weight * (1.0 / total)).astype(BF16)
            value_t = qkv_ref[2, places[side], : (block + 1) * QB]
            mixed_parts[side].append(nn_dot(value_t, probs))
            lse_parts[side].append(top + jnp.log(total))
        for side in range(2):
            mixed_ref[places[side], :] = jnp.concatenate(mixed_parts[side], axis=1).astype(BF16)
            lse_ref[pair * 2 + side] = jnp.concatenate(lse_parts[side], axis=1)

    spreads[0].finish()

    @pl.loop(0, row_blocks)
    def _(block):
        rows = pl.ds(pl.multiple_of(block * QB, QB), QB)
        mixed = mixed_ref[:, rows].T
        stream = x0_ref[rows, :].astype(F32) + nn_dot(mixed, wo_all[...].reshape(width, width))
        x1_ref[rows, :] = stream
        x2_ref[rows, :] = stream
        n2_ref[rows, :] = scaled_rms(stream, gains_ref[1:2, :]).astype(BF16)

    spreads[2].relay_across()
    spreads[1].finish()
    spreads[2].finish()
    chunk = hid_ref.shape[2]
    chunks = wu_all.shape[2] // chunk
    parts = chunk // wd_all.shape[1]

    def put(slot, at):
        return pltpu.make_async_copy(
            hid_ref.at[slot],
            hid_any.at[:, pl.ds(pl.multiple_of(at * chunk, chunk), chunk)],
            hid_sem.at[slot],
        )

    @pl.loop(0, chunks)
    def _(at):
        slot = lax.rem(at, 2)
        lanes = pl.ds(pl.multiple_of(at * chunk, chunk), chunk)

        @pl.when(at >= 2)
        def _():
            put(slot, at - 2).wait()

        for block in range(row_blocks):
            rows = slice(block * QB, (block + 1) * QB)
            hidden = nn_dot(n2_ref[rows, :], wu_all[:, :, lanes].reshape(width, chunk))
            hid_ref[slot, rows, :] = hidden
            active = (0.5 * hidden * (1.0 + lax.erf(hidden * INV_SQRT2))).astype(BF16)
            down = wd_all[pl.ds(at * parts, parts)].reshape(chunk, width)
            x2_ref[rows, :] += nn_dot(active, down)
        put(slot, at).start()

    @pl.loop(0, row_blocks)
    def _(block):
        rows = pl.ds(pl.multiple_of(block * QB, QB), QB)
        n3_ref[rows, :] = scaled_rms(x2_ref[rows, :], gains_ref[2:3, :]).astype(BF16)

    for at in range(max(0, chunks - 2), chunks):
        put(at % 2, at).wait()


VM = pl.BlockSpec(memory_space=pltpu.VMEM)
ANYWHERE = pl.BlockSpec(memory_space=pl.ANY)


def layer_forward(x0, gains, cos_t, sin_t, wqkv, slices, shards, axis):
    tokens, width = x0.shape
    hidden = slices[1].shape[1]
    shape = jax.ShapeDtypeStruct
    chunk = min(512, hidden)
    sems = pltpu.SemaphoreType.DMA((8, max(2, shards // 2)))
    return pl.pallas_call(
        functools.partial(forward_kernel, shards, axis),
        in_specs=[VM] * 8,
        out_specs=[VM] * 11 + [ANYWHERE],
        out_shape=[
            shape((tokens, width), BF16),
            shape((3, width, tokens), BF16),
            shape((width // HD, 1, tokens), F32),
            shape((width, tokens), BF16),
            shape((tokens, width), F32),
            shape((tokens, width), BF16),
            shape((tokens, width), F32),
            shape((tokens, width), BF16),
        ]
        + [shape((shards, *w.shape), BF16) for w in slices]
        + [shape((tokens, hidden), F32)],
        scratch_shapes=[
            pltpu.VMEM((2, tokens, chunk), F32),
            pltpu.SemaphoreType.DMA((2,)),
            sems,
            sems,
            sems,
        ],
        compiler_params=pltpu.CompilerParams(
            collective_id=5, has_side_effects=True, vmem_limit_bytes=60 << 20
        ),
        name="layer_forward",
    )(x0, gains, cos_t, sin_t, wqkv, *slices)


def backward_kernel(shard_axis, *refs):
    anys, refs = refs[:13], refs[13:]
    gains_ref, cos_ref, sin_ref, lse_ref = refs[0:4]
    dx0_ref, gqkv_ref, gout_ref, gup_ref, gdown_ref, ggains_ref = refs[4:10]
    kept, refs = refs[10:23], refs[23:]
    dn3_ref, x2_ref, hid_ref, wd_ref, wu_ref, x1_ref, n2_ref, wo_ref, mixed_ref, qkv_ref, x0_ref, n1_ref, wqkv_ref = kept
    grad_ref, part_ref, low_ref, act_ref, dhid_ref, dmixed_ref, dpacked_ref, turn_ref, load_sem = refs
    shard = lax.axis_index(shard_axis) if shard_axis else 0
    tokens, width = x2_ref.shape
    half = HD // 2
    row_blocks = tokens // QB
    loads = [
        pltpu.make_async_copy(src, dst, load_sem.at[at])
        for at, (src, dst) in enumerate(zip(anys, kept))
    ]
    for load in loads:
        load.start()

    def block_rows(block):
        return pl.ds(pl.multiple_of(block * QB, QB), QB)

    loads[0].wait()
    loads[1].wait()
    ggains_ref[...] = jnp.zeros_like(ggains_ref)

    @pl.loop(0, row_blocks)
    def _(block):
        rows = block_rows(block)
        back, gain = rms_back(dn3_ref[:, rows].T, x2_ref[rows, :], gains_ref[2:3, :])
        grad_ref[rows, :] = back
        low_ref[rows, :] = back.astype(BF16)
        part_ref[rows, :] = jnp.zeros_like(back)
        ggains_ref[2:3, :] += gain

    for at in (2, 3, 4):
        loads[at].wait()
    chunk = min(512, wu_ref.shape[1])

    @pl.loop(0, wu_ref.shape[1] // chunk)
    def _(at):
        lanes = pl.ds(pl.multiple_of(at * chunk, chunk), chunk)
        for block in range(row_blocks):
            rows = slice(block * QB, (block + 1) * QB)
            grad_act = nt_dot(low_ref[rows, :], wd_ref[lanes, :])
            hidden = hid_ref[rows, lanes]
            share = 0.5 + 0.5 * lax.erf(hidden * INV_SQRT2)
            slope = share + hidden * (INV_SQRT_2PI * jnp.exp(-0.5 * hidden * hidden))
            act_ref[rows, lanes] = (hidden * share).astype(BF16)
            grad_hid = (slope * grad_act).astype(BF16)
            dhid_ref[rows, lanes] = grad_hid
            part_ref[rows, :] += nt_dot(grad_hid, wu_ref[:, lanes])

    own = gdown_ref.shape[0]
    gdown_ref[...] = nn_dot(act_ref[:, pl.ds(pl.multiple_of(shard * own, own), own)].T, low_ref[...])
    loads[5].wait()
    loads[6].wait()
    own = gup_ref.shape[0]
    turn_ref[...] = n2_ref[...].T
    own_rows = pl.ds(pl.multiple_of(shard * own, own), own)

    @pl.loop(0, wu_ref.shape[1] // chunk)
    def _(at):
        lanes = pl.ds(pl.multiple_of(at * chunk, chunk), chunk)
        gup_ref[:, lanes] = nn_dot(turn_ref[own_rows, :], dhid_ref[:, lanes])

    loads[7].wait()

    @pl.loop(0, row_blocks)
    def _(block):
        rows = block_rows(block)
        back, gain = rms_back(part_ref[rows, :], x1_ref[rows, :], gains_ref[1:2, :])
        back = grad_ref[rows, :] + back
        grad_ref[rows, :] = back
        low = back.astype(BF16)
        low_ref[rows, :] = low
        ggains_ref[1:2, :] += gain
        dmixed_ref[:, rows] = nt_dot(low, wo_ref[...]).astype(BF16).T

    loads[8].wait()
    loads[9].wait()
    own = gout_ref.shape[0]
    own_rows = pl.ds(pl.multiple_of(shard * own, own), own)
    gout_ref[...] = nn_dot(mixed_ref[own_rows, :], low_ref[...])

    @pl.loop(0, width // (2 * HD))
    def _(pair):
        made = ([], [], [])
        places = [pl.ds(pl.multiple_of((pair * 2 + side) * HD, HD), HD) for side in range(2)]
        natural = [
            [ref[rows, :].T for ref in (qkv_ref.at[0], qkv_ref.at[1], qkv_ref.at[2], dmixed_ref)]
            for rows in places
        ]

        def products_of(side, block):
            count = (block + 1) * QB
            at = slice(block * QB, count)
            _, key, value, _ = natural[side]
            scores = nn_dot(key[:count], qkv_ref[0, places[side], at])
            return scores, nn_dot(value[:count], dmixed_ref[places[side], at])

        work = [(side, block) for side in range(2) for block in range(row_blocks)]
        ahead = products_of(*work[0])
        dquery_parts = []
        for place, (side, block) in enumerate(work):
            if block == 0:
                dquery_parts = []
                dkey = [None] * row_blocks
                dvalue = [None] * row_blocks
            scores, dprobs = ahead
            if place + 1 < len(work):
                ahead = products_of(*work[place + 1])
            count = (block + 1) * QB
            at = slice(block * QB, count)
            query, _, _, dmix = natural[side]
            probs = causal_tile(jnp.exp(scores - lse_ref[pair * 2 + side][:, at]), 0.0)
            delta = jnp.sum(probs * dprobs, axis=0, keepdims=True)
            dscores = (probs * (dprobs - delta)).astype(BF16)
            dquery_parts.append(nn_dot(qkv_ref[1, places[side], :count], dscores))
            more_key = nn_dot(dscores, query[at])
            more_value = nn_dot(probs.astype(BF16), dmix[at])
            for piece in range(block + 1):
                cut = slice(piece * QB, (piece + 1) * QB)
                if dkey[piece] is None:
                    dkey[piece], dvalue[piece] = more_key[cut], more_value[cut]
                else:
                    dkey[piece] = dkey[piece] + more_key[cut]
                    dvalue[piece] = dvalue[piece] + more_value[cut]
            if block == row_blocks - 1:
                cos_t, sin_t = cos_ref[...], sin_ref[...]
                dquery_t = jnp.concatenate(dquery_parts, axis=1) * HD ** (-0.5)
                dkey_t = jnp.concatenate(dkey, axis=0).T
                made[0].append(turned_back(dquery_t, cos_t, sin_t, half).T)
                made[1].append(turned_back(dkey_t, cos_t, sin_t, half).T)
                made[2].append(jnp.concatenate(dvalue, axis=0))
        for part in range(3):
            lanes = pl.ds(pl.multiple_of(part * width + pair * 2 * HD, 2 * HD), 2 * HD)
            dpacked_ref[:, lanes] = jnp.concatenate(made[part], axis=1).astype(BF16)

    for at in (10, 11, 12):
        loads[at].wait()
    own = gqkv_ref.shape[0]
    turn_ref[...] = n1_ref[...].T
    own_rows = pl.ds(pl.multiple_of(shard * own, own), own)

    @pl.loop(0, 3)
    def _(at):
        lanes = pl.ds(pl.multiple_of(at * width, width), width)
        gqkv_ref[:, lanes] = nn_dot(turn_ref[own_rows, :], dpacked_ref[:, lanes])

    @pl.loop(0, row_blocks)
    def _(block):
        rows = block_rows(block)
        back, gain = rms_back(
            nt_dot(dpacked_ref[rows, :], wqkv_ref[...]), x0_ref[rows, :].astype(F32), gains_ref[0:1, :]
        )
        dx0_ref[rows, :] = grad_ref[rows, :] + back
        ggains_ref[0:1, :] += gain


def layer_backward(shard_axis, slice_shapes, dn3_t, gains, cos_t, sin_t, projections, x0, kept):
    n1, qkv, lse, mixed_t, x1, n2, x2, _, hid = kept
    wqkv, wo, wu, wd = projections
    tokens, width = x2.shape
    shape = jax.ShapeDtypeStruct
    moved = (dn3_t, x2, hid, wd, wu, x1, n2, wo, mixed_t, qkv, x0, n1, wqkv)
    return pl.pallas_call(
        functools.partial(backward_kernel, shard_axis),
        in_specs=[ANYWHERE] * 13 + [VM] * 3 + [VM],
        out_specs=[VM] * 6,
        out_shape=[shape((tokens, width), F32)]
        + [shape(s, F32) for s in slice_shapes]
        + [shape((8, width), F32)],
        scratch_shapes=[pltpu.VMEM(m.shape, m.dtype) for m in moved]
        + [
            pltpu.VMEM((tokens, width), F32),
            pltpu.VMEM((tokens, width), F32),
            pltpu.VMEM((tokens, width), BF16),
            pltpu.VMEM(hid.shape, BF16),
            pltpu.VMEM(hid.shape, BF16),
            pltpu.VMEM((width, tokens), BF16),
            pltpu.VMEM((tokens, 3 * width), BF16),
            pltpu.VMEM((width, tokens), BF16),
            pltpu.SemaphoreType.DMA((13,)),
        ],
        compiler_params=pltpu.CompilerParams(vmem_limit_bytes=62 << 20),
        name="layer_backward",
    )(*moved, gains, cos_t, sin_t, lse)


def scatter_sketch_kernel(axis, rows, row_list, ids_ref, *refs):
    table_any, dx0_ref = refs[0:2]
    grads, errs, starts = (None, *refs[2:6]), refs[6:11], refs[11:16]
    full_any, gq_ref, eq_ref, gs_ref, es_ref, sq_ref = refs[16:22]
    whole_ref, load_sem, store_sem = refs[22:25]
    phase, step = pl.program_id(0), pl.program_id(1)
    steps = pl.num_programs(1)
    places, _ = small_places(row_list)
    size = rows - (pl.cdiv(rows, TB) - 1) * TB

    def tile_copy(at, count, inward):
        tile = pl.ds(pl.multiple_of(at * TB, TB), count)
        if inward:
            return pltpu.make_async_copy(table_any.at[tile, :], whole_ref.at[tile, :], load_sem.at[at])
        return pltpu.make_async_copy(whole_ref.at[tile, :], full_any.at[tile, :], store_sem.at[at])

    blocks = pl.cdiv(rows, TB)
    sizes = [TB] * (blocks - 1) + [size]

    @pl.when((phase == 0) & (step == 0))
    def _():
        for at in range(blocks):
            tile_copy(at, sizes[at], True).start()
        gs_ref[...] = jnp.zeros_like(gs_ref)
        es_ref[...] = jnp.zeros_like(es_ref)
        total = jnp.zeros(sq_ref.shape, F32)
        for k in range(4):
            grad = grads[k + 1][...]
            start_t = starts[k + 1][...]
            at = pl.ds(places[k], row_list[k])
            gs_ref[:, at] = left_of(grad, start_t)
            es_ref[:, at] = left_of_bf16(errs[k + 1][...], start_t)
            total = total + fold_squares(grad)
        sq_ref[...] = total

    @pl.when(phase == 0)
    def _():
        err = keep_rows(errs[0][...].astype(F32), step * TB, rows).astype(BF16)
        eq_ref[...] = left_of_bf16(err, starts[0][...])

    @pl.when((phase == 1) & (step == 0))
    def _():
        for at in range(blocks):
            tile_copy(at, sizes[at], True).wait()
        first = lax.axis_index(axis) * rows if axis else 0
        if blocks * TB > rows:
            whole_ref[pl.ds(rows, blocks * TB - rows), :] = jnp.zeros((blocks * TB - rows, whole_ref.shape[1]), F32)
        spare = blocks * TB

        @pl.loop(0, dx0_ref.shape[0] // 8)
        def _(group):
            base = pl.multiple_of(group * 8, 8)
            for side in range(8):
                row = ids_ref[base + side] - first
                row = jnp.where((row >= 0) & (row < rows), row, spare)
                whole_ref[pl.ds(row, 1), :] += dx0_ref[pl.ds(base + side, 1), :]

    tile = pl.ds(pl.multiple_of(step * TB, TB), TB)

    @pl.when(phase == 1)
    def _():
        grad = whole_ref[tile, :]
        gq_ref[...] = left_of(grad, starts[0][...])
        sq_ref[...] += fold_squares(grad)

    for at in range(blocks):

        @pl.when((phase == 1) & (step == at))
        def _():
            tile_copy(at, sizes[at], False).start()

    @pl.when((phase == 1) & (step == steps - 1))
    def _():
        for at in range(blocks):
            tile_copy(at, sizes[at], False).wait()


def scatter_sketch(token_ids, table_grad, dx0, grads, errs, starts_t, axis):
    rows, width = table_grad.shape
    blocks = pl.cdiv(rows, TB)
    row_list = [g.shape[0] for g in grads]
    _, small = small_places(row_list)

    def whole_at(shape):
        return pl.BlockSpec(shape, lambda *_: (0,) * len(shape), pipeline_mode=pl.Buffered(1))

    def at_phase(wanted, size, place):
        def index(p, i, ids):
            return place(jnp.where(p == wanted, i, jnp.where(p < wanted, 0, blocks - 1)))

        return pl.BlockSpec(size, index)

    shape = jax.ShapeDtypeStruct
    full, *sketches = pl.pallas_call(
        functools.partial(scatter_sketch_kernel, axis, rows, row_list),
        grid_spec=pltpu.PrefetchScalarGridSpec(
            num_scalar_prefetch=1,
            grid=(2, blocks),
            in_specs=[ANYWHERE, whole_at(dx0.shape)]
            + [whole_at(g.shape) for g in grads]
            + [at_phase(0, (TB, width), lambda i: (i, 0))]
            + [whole_at(e.shape) for e in errs[1:]]
            + [whole_at(s.shape) for s in starts_t],
            out_specs=[
                ANYWHERE,
                at_phase(1, (RK, TB), lambda i: (0, i)),
                at_phase(0, (RK, TB), lambda i: (0, i)),
            ]
            + [whole_at((RK, small)), whole_at((RK, small)), whole_at((8, 512))],
            scratch_shapes=[
                pltpu.VMEM((blocks * TB + 8, width), F32),
                pltpu.SemaphoreType.DMA((blocks,)),
                pltpu.SemaphoreType.DMA((blocks,)),
            ],
        ),
        out_shape=[
            shape((rows, width), F32),
            shape((RK, blocks * TB), F32),
            shape((RK, blocks * TB), F32),
            shape((RK, small), F32),
            shape((RK, small), F32),
            shape((8, 512), F32),
        ],
        compiler_params=pltpu.CompilerParams(vmem_limit_bytes=60 << 20),
        name="scatter_sketch",
    )(token_ids.reshape(-1), table_grad, dx0, *grads, *errs, *starts_t)
    return full, sketches


class Spread:
    def __init__(self, full, shards, sems):
        self.full, self.sems = full, sems
        self.shard, self.worker = lax.axis_index("voc"), lax.axis_index("rep")
        self.core = lax.rem(self.shard, 2)
        self.chip = self.shard // 2
        self.chips = shards // 2
        self.side = lax.rem(self.worker, 2)
        self.rows = full.shape[1] // 2

    def region(self, slot, side):
        return self.full.at[slot, pl.ds(pl.multiple_of(side * self.rows, self.rows), self.rows), :]

    def copy(self, ref, at, pair, peer):
        return pltpu.make_async_remote_copy(
            src_ref=ref, dst_ref=ref, send_sem=self.sems.at[2 * pair, at], recv_sem=self.sems.at[2 * pair + 1, at],
            device_id=peer, device_id_type=MESH_ID,
        )

    def source(self, at):
        return lax.rem(self.chip - at + self.chips, self.chips)

    def own_to_chip(self, at):
        peer = lax.rem(self.chip + at, self.chips) * 2 + self.core
        return self.copy(self.region(self.shard, self.side), at, 0, {"voc": peer})

    def from_chip(self, at):
        slot = self.source(at) * 2 + self.core
        return self.copy(self.region(slot, self.side), at, 0, {"voc": slot})

    def across(self, at, side):
        slot = self.source(at) * 2 + self.core
        return self.copy(self.region(slot, side), at, 1, {"rep": self.worker + 1 - 2 * self.side})

    def to_core(self, at, side, pair, core):
        slot = self.source(at) * 2 + core
        return self.copy(self.region(slot, side), at, pair, {"voc": self.shard + 1 - 2 * self.core})

    def own_to_core(self, slot):
        return self.copy(self.full.at[slot], 0, 2, {"voc": self.shard + 1 - 2 * self.core})

    def start(self):
        for at in range(1, self.chips):
            self.own_to_chip(at).start()
        self.own_to_core(self.shard).start()

    def relay(self):
        for at in range(1, self.chips):
            self.from_chip(at).wait_recv()
            self.across(at, self.side).start()
            self.to_core(at, self.side, 2, self.core).start()

    def relay_across(self):
        for at in range(1, self.chips):
            self.across(at, 1 - self.side).wait_recv()
            self.to_core(at, 1 - self.side, 3, self.core).start()

    def finish(self):
        self.own_to_core(self.shard + 1 - 2 * self.core).wait_recv()
        for at in range(1, self.chips):
            self.to_core(at, self.side, 2, 1 - self.core).wait_recv()
            self.to_core(at, 1 - self.side, 3, 1 - self.core).wait_recv()
        self.own_to_core(self.shard).wait_send()
        for at in range(1, self.chips):
            self.own_to_chip(at).wait_send()
            self.across(at, self.side).wait_send()
            self.to_core(at, self.side, 2, self.core).wait_send()
            self.to_core(at, 1 - self.side, 3, self.core).wait_send()


def greet_all(shards):
    barrier = pltpu.get_barrier_semaphore()
    me = lax.axis_index("voc")
    for step in range(1, shards):
        pl.semaphore_signal(
            barrier, inc=1, device_id={"voc": lax.rem(me + step, shards)}, device_id_type=MESH_ID
        )
    worker = lax.axis_index("rep")
    pl.semaphore_signal(
        barrier, inc=1, device_id={"rep": worker + 1 - 2 * lax.rem(worker, 2)}, device_id_type=MESH_ID
    )


def await_all(shards):
    pl.semaphore_wait(pltpu.get_barrier_semaphore(), shards)


def open_kernel(
    shards, axis, count, ids_ref, rows_ref, weight_ref, x0_ref, full_ref, own_ref,
    half_in, sums, core_send, core_recv, chip_send, chip_recv, back_send, back_recv, sems,
):
    greet_all(shards)
    shard = lax.axis_index(axis)
    core = lax.rem(shard, 2)
    chip = shard // 2
    partner = shard + 1 - 2 * core
    chips = shards // 2
    half = own_ref.shape[0] // 2
    own_half = pl.ds(pl.multiple_of(core * half, half), half)
    other_half = pl.ds(pl.multiple_of((1 - core) * half, half), half)
    spread = Spread(full_ref, shards, sems)
    full_ref[shard] = weight_ref[...].astype(BF16)
    local = ids_ref[...] - shard * count
    inside = jnp.where((local >= 0) & (local < count), 1.0, 0.0)
    inside = jnp.broadcast_to(inside, (8, local.shape[1])).T[:, 0:1]
    own_ref[...] = jnp.where(inside > 0.5, rows_ref[...], 0.0).astype(BF16)

    def chip_copy(peer_chip, slot, at):
        return pltpu.make_async_remote_copy(
            src_ref=sums.at[slot], dst_ref=sums.at[slot],
            send_sem=chip_send.at[at], recv_sem=chip_recv.at[at],
            device_id={axis: peer_chip * 2 + core}, device_id_type=MESH_ID,
        )

    def back_copy(rows):
        return pltpu.make_async_remote_copy(
            src_ref=x0_ref.at[rows, :], dst_ref=x0_ref.at[rows, :],
            send_sem=back_send, recv_sem=back_recv,
            device_id={axis: partner}, device_id_type=MESH_ID,
        )

    await_all(shards)
    spread.start()
    first = pltpu.make_async_remote_copy(
        src_ref=own_ref.at[other_half, :], dst_ref=half_in,
        send_sem=core_send, recv_sem=core_recv,
        device_id={axis: partner}, device_id_type=MESH_ID,
    )
    first.start()
    first.wait_recv()
    sums[chip] = (own_ref[own_half, :].astype(F32) + half_in[...].astype(F32)).astype(BF16)
    for at in range(1, chips):
        chip_copy(lax.rem(chip + at, chips), chip, at).start()
    first.wait_send()
    spread.relay()
    total = sums[chip].astype(F32)
    for at in range(1, chips):
        source = lax.rem(chip - at + chips, chips)
        chip_copy(source, source, at).wait_recv()
        total = total + sums[source].astype(F32)
    x0_ref[own_half, :] = total.astype(BF16)
    back_copy(own_half).start()
    spread.relay_across()
    back_copy(other_half).wait_recv()
    for at in range(1, chips):
        chip_copy(lax.rem(chip + at, chips), chip, at).wait_send()
    back_copy(own_half).wait_send()
    spread.finish()


def opening(token_ids, rows, count, weight, shards, axis):
    tokens, width = rows.shape
    chips = shards // 2
    shape = jax.ShapeDtypeStruct
    return pl.pallas_call(
        functools.partial(open_kernel, shards, axis, count),
        in_specs=[VM] * 3,
        out_specs=[VM] * 2,
        out_shape=[shape((tokens, width), BF16), shape((shards, *weight.shape), BF16)],
        scratch_shapes=[
            pltpu.VMEM((tokens, width), BF16),
            pltpu.VMEM((tokens // 2, width), BF16),
            pltpu.VMEM((chips, tokens // 2, width), BF16),
        ]
        + [pltpu.SemaphoreType.DMA] * 2
        + [pltpu.SemaphoreType.DMA((max(2, chips),))] * 2
        + [pltpu.SemaphoreType.DMA] * 2
        + [pltpu.SemaphoreType.DMA((8, max(2, chips)))],
        compiler_params=pltpu.CompilerParams(collective_id=4, has_side_effects=True),
        name="opening",
    )(token_ids, rows, weight)


TOKEN_LANES = 256


def vocab_block(rows):
    best = 8
    for size in range(8, 1025, 8):
        if rows % size == 0:
            best = size
    return best


def head_kernel(
    shards, axis,
    n3_ref, target_ref, table_ref,
    gtable_ref, dn3_any, loss_ref,
    dn3_ref, back_in, out_sem, kept, n3_t, tops, running, stats, z_ref, half_in, half_out,
    stat_send, stat_recv, core_send, core_recv, chip_send, chip_recv, back_send, back_recv,
):
    phase, step = pl.program_id(0), pl.program_id(1)
    last = pl.num_programs(1) - 1
    shard = lax.axis_index(axis)
    core = lax.rem(shard, 2)
    chip = shard // 2
    partner = shard + 1 - 2 * core
    chips = shards // 2
    tokens, width = n3_ref.shape
    block_rows = table_ref.shape[0]
    half = width // 2
    own_half = pl.ds(pl.multiple_of(core * half, half), half)
    other_half = pl.ds(pl.multiple_of((1 - core) * half, half), half)

    def stat_copy(peer, slot, at):
        return pltpu.make_async_remote_copy(
            src_ref=stats.at[slot], dst_ref=stats.at[slot],
            send_sem=stat_send.at[at], recv_sem=stat_recv.at[at],
            device_id={axis: peer}, device_id_type=MESH_ID,
        )

    def core_copy():
        return pltpu.make_async_remote_copy(
            src_ref=dn3_ref.at[other_half, :], dst_ref=half_in,
            send_sem=core_send, recv_sem=core_recv,
            device_id={axis: partner}, device_id_type=MESH_ID,
        )

    def chip_copy(peer_chip, slot, at):
        return pltpu.make_async_remote_copy(
            src_ref=half_out.at[slot], dst_ref=half_out.at[slot],
            send_sem=chip_send.at[at], recv_sem=chip_recv.at[at],
            device_id={axis: peer_chip * 2 + core}, device_id_type=MESH_ID,
        )

    def back_copy():
        return pltpu.make_async_remote_copy(
            src_ref=dn3_ref.at[own_half, :], dst_ref=back_in,
            send_sem=back_send, recv_sem=back_recv,
            device_id={axis: partner}, device_id_type=MESH_ID,
        )

    @pl.when((phase == 0) & (step == 0))
    def _():
        barrier = pltpu.get_barrier_semaphore()
        for at in range(1, shards):
            pl.semaphore_signal(
                barrier, inc=1,
                device_id={axis: lax.rem(shard + at, shards)}, device_id_type=MESH_ID,
            )
        n3_t[...] = n3_ref[...].T
        row_at = lax.broadcasted_iota(jnp.int32, running.shape, 0)
        running[...] = jnp.where(row_at == 0, -1e30, 0.0)
        dn3_ref[...] = jnp.zeros_like(dn3_ref)

    def hits(lanes):
        row_at = lax.broadcasted_iota(jnp.int32, (block_rows, TOKEN_LANES), 0)
        return row_at == target_ref[:, lanes] - (shard * (last + 1) + step) * block_rows

    @pl.when(phase == 0)
    def _():
        table = table_ref[...].astype(BF16)
        ahead = nn_dot(table, n3_t[:, :TOKEN_LANES])
        for start in range(0, tokens, TOKEN_LANES):
            lanes = slice(start, start + TOKEN_LANES)
            logits = ahead
            if start + TOKEN_LANES < tokens:
                ahead = nn_dot(table, n3_t[:, start + TOKEN_LANES : start + 2 * TOKEN_LANES])
            top = jnp.max(logits, axis=0, keepdims=True)
            weight = jnp.exp(logits - top)
            kept[step, :, lanes] = weight
            tops[step, :, lanes] = top
            total = jnp.sum(weight, axis=0, keepdims=True)
            picked = jnp.sum(jnp.where(hits(lanes), logits, 0.0), axis=0, keepdims=True)
            old = running[0:1, lanes]
            new = jnp.maximum(old, top)
            running[0:1, lanes] = new
            running[1:2, lanes] = running[1:2, lanes] * jnp.exp(old - new) + total * jnp.exp(top - new)
            running[2:3, lanes] += picked

    @pl.when((phase == 1) & (step == 0))
    def _():
        stats[shard] = running[...]
        pl.semaphore_wait(pltpu.get_barrier_semaphore(), shards - 1)
        sends = [stat_copy(lax.rem(shard + at, shards), shard, at) for at in range(1, shards)]
        for send in sends:
            send.start()
        for at in range(1, shards):
            source = lax.rem(shard - at + shards, shards)
            stat_copy(source, source, at).wait_recv()
        for send in sends:
            send.wait_send()
        top = stats[0, 0:1, :]
        for at in range(1, shards):
            top = jnp.maximum(top, stats[at, 0:1, :])
        total, picked = jnp.zeros_like(top), jnp.zeros_like(top)
        for at in range(shards):
            total = total + stats[at, 1:2, :] * jnp.exp(stats[at, 0:1, :] - top)
            picked = picked + stats[at, 2:3, :]
        z = top + jnp.log(total)
        z_ref[...] = z
        terms = (z - picked) + ZLOSS_WEIGHT * (z * z)
        loss = jnp.sum(terms, axis=1, keepdims=True) * (1.0 / tokens)
        loss_ref[...] = jnp.broadcast_to(loss, loss_ref.shape)

    def grad_logits(lanes):
        z = z_ref[:, lanes]
        factor = jnp.exp(tops[step, :, lanes] - z) * (1.0 + 2.0 * ZLOSS_WEIGHT * z) * (1.0 / tokens)
        return (kept[step, :, lanes] * factor - jnp.where(hits(lanes), 1.0 / tokens, 0.0)).astype(BF16)

    @pl.when(phase == 1)
    def _():
        table_t = table_ref[...].astype(BF16).T
        for start in range(0, tokens, TOKEN_LANES):
            lanes = slice(start, start + TOKEN_LANES)
            dn3_ref[:, lanes] += nn_dot(table_t, grad_logits(lanes))

    @pl.when((phase == 2) & (step == 0))
    def _():
        core_copy().start()

    @pl.when((phase == 2) & (step == jnp.minimum(2, last)))
    def _():
        core_copy().wait()
        half_out[chip] = (dn3_ref[own_half, :] + half_in[...]).astype(BF16)
        for at in range(1, chips):
            chip_copy(lax.rem(chip + at, chips), chip, at).start()

    @pl.when(phase == 2)
    def _():
        total = None
        for start in range(0, tokens, TOKEN_LANES):
            lanes = slice(start, start + TOKEN_LANES)
            part = nn_dot(grad_logits(lanes), n3_ref[lanes, :])
            total = part if total is None else total + part
        gtable_ref[...] = total

    @pl.when((phase == 2) & (step == last))
    def _():
        for at in range(1, chips):
            source = lax.rem(chip - at + chips, chips)
            chip_copy(source, source, at).wait_recv()
        for at in range(1, chips):
            chip_copy(lax.rem(chip + at, chips), chip, at).wait_send()
        whole_sum = half_out[0].astype(F32)
        for at in range(1, chips):
            whole_sum = whole_sum + half_out[at].astype(F32)
        dn3_ref[own_half, :] = whole_sum
        back_copy().start()
        puts = [
            pltpu.make_async_copy(dn3_ref.at[own_half, :], dn3_any.at[own_half, :], out_sem.at[0]),
            pltpu.make_async_copy(back_in, dn3_any.at[other_half, :], out_sem.at[1]),
        ]
        puts[0].start()
        back_copy().wait()
        puts[1].start()
        for put in puts:
            put.wait()


def vocabulary_head(n3, targets, table, shards, axis):
    rows, width = table.shape
    tokens = n3.shape[0]
    size = vocab_block(rows)
    blocks = rows // size
    shape = jax.ShapeDtypeStruct
    return pl.pallas_call(
        functools.partial(head_kernel, shards, axis),
        grid=(3, blocks),
        in_specs=[
            whole((tokens, width)),
            whole((1, tokens)),
            pl.BlockSpec((size, width), lambda p, i: (jnp.where(p == 2, blocks - 1, i), 0)),
        ],
        out_specs=[
            pl.BlockSpec((size, width), lambda p, i: (jnp.where(p == 2, i, 0), 0)),
            pl.BlockSpec(memory_space=pl.ANY),
            whole((8, 128)),
        ],
        out_shape=[shape((rows, width), F32), shape((width, tokens), F32), shape((8, 128), F32)],
        scratch_shapes=[
            pltpu.VMEM((width, tokens), F32),
            pltpu.VMEM((width // 2, tokens), F32),
            pltpu.SemaphoreType.DMA((2,)),
            pltpu.VMEM((blocks, size, tokens), F32),
            pltpu.VMEM((width, tokens), BF16),
            pltpu.VMEM((blocks, 1, tokens), F32),
            pltpu.VMEM((8, tokens), F32),
            pltpu.VMEM((shards, 8, tokens), F32),
            pltpu.VMEM((1, tokens), F32),
            pltpu.VMEM((width // 2, tokens), F32),
            pltpu.VMEM((shards // 2, width // 2, tokens), BF16),
        ]
        + [pltpu.SemaphoreType.DMA((shards,))] * 2
        + [pltpu.SemaphoreType.DMA] * 2
        + [pltpu.SemaphoreType.DMA((max(2, shards // 2),))] * 2
        + [pltpu.SemaphoreType.DMA] * 2,
        compiler_params=pltpu.CompilerParams(
            collective_id=3, has_side_effects=True, vmem_limit_bytes=62 << 20
        ),
        name="vocabulary_head",
    )(n3, targets, table)


def body(
    token_ids,
    target_ids,
    embedding,
    w_qkv,
    w_out,
    w_up,
    w_down,
    norm_gains,
    embed_mom,
    qkv_mom,
    out_mom,
    up_mom,
    down_mom,
    gain_mom,
    embed_err,
    qkv_err,
    out_err,
    up_err,
    down_err,
    embed_factor,
    qkv_factor,
    out_factor,
    up_factor,
    down_factor,
):
    seq_count, length = token_ids.shape
    tok_count = seq_count * length
    vocab_rows = embedding.shape[0]
    shard_pos = lax.axis_index("voc")
    workers = lax.axis_size("rep")
    slices = (w_qkv, w_out, w_up, w_down)
    shards = lax.axis_size("voc")
    local_ids = token_ids.reshape(-1) - shard_pos * vocab_rows
    rows = embedding.at[local_ids].get(mode="clip")
    x0, qkv_all = opening(token_ids, rows, vocab_rows, w_qkv, shards, "voc")
    wqkv = qkv_all.reshape(-1, w_qkv.shape[1])
    half = HD // 2
    inverse = np.float32(10000.0) ** (-np.arange(half, dtype=np.float32) / np.float32(half))
    angles = inverse[:, None] * np.arange(length, dtype=np.float32)[None, :]
    cos_t, sin_t = jnp.asarray(np.cos(angles)), jnp.asarray(np.sin(angles))
    *kept, n3, wo, wu, wd, hid = layer_forward(
        x0, norm_gains, cos_t, sin_t, wqkv, slices[1:], shards, "voc"
    )
    kept = (*kept, n3, hid)
    projections = (wqkv, *(w.reshape(-1, w.shape[2]) for w in (wo, wu, wd)))
    grad_table_head, dn3_t, loss_tile = vocabulary_head(
        n3, target_ids.reshape(1, -1), embedding, lax.axis_size("voc"), "voc"
    )
    grad_in, *grad_mats, grad_gains = layer_backward(
        "voc", [w.shape for w in slices], dn3_t, norm_gains, cos_t, sin_t, projections, x0, kept
    )
    errors = [e[0] for e in (embed_err, qkv_err, out_err, up_err, down_err)]
    starts_t = [
        f[0].T for f in (embed_factor, qkv_factor, out_factor, up_factor, down_factor)
    ]
    full_grad, sketches = scatter_sketch(
        token_ids, grad_table_head, grad_in, grad_mats, errors, starts_t, "voc"
    )
    new_errors, new_moments, changed, rights, gain_change, next_gain_mom, loss, norm = settle(
        loss_tile,
        sketches,
        grad_gains,
        gain_mom,
        [full_grad, *grad_mats],
        errors,
        (embed_mom, qkv_mom, out_mom, up_mom, down_mom),
        slices,
        workers,
        shards,
    )
    return (
        loss,
        norm,
        *changed,
        gain_change,
        *new_moments,
        next_gain_mom,
        *(e[None] for e in new_errors),
        *(r.T[None] for r in rights),
    )


def solution(mesh):
    in_specs = (
        P("rep", None),
        P("rep", None),
        P("voc", None),
        P("voc", None),
        P("voc", None),
        P("voc", None),
        P("voc", None),
        P(),
        P("voc", None),
        P("voc", None),
        P("voc", None),
        P("voc", None),
        P("voc", None),
        P(),
        P("rep", "voc", None),
        P("rep", "voc", None),
        P("rep", "voc", None),
        P("rep", "voc", None),
        P("rep", "voc", None),
        P("voc", None, None),
        P("voc", None, None),
        P("voc", None, None),
        P("voc", None, None),
        P("voc", None, None),
    )
    out_specs = (
        P("rep"),
        P("rep"),
        P("voc", None),
        P("voc", None),
        P("voc", None),
        P("voc", None),
        P("voc", None),
        P(),
        P("voc", None),
        P("voc", None),
        P("voc", None),
        P("voc", None),
        P("voc", None),
        P(),
        P("rep", "voc", None),
        P("rep", "voc", None),
        P("rep", "voc", None),
        P("rep", "voc", None),
        P("rep", "voc", None),
        P("voc", None, None),
        P("voc", None, None),
        P("voc", None, None),
        P("voc", None, None),
        P("voc", None, None),
    )
    return jax.shard_map(body, mesh=mesh, in_specs=in_specs, out_specs=out_specs, check_vma=False)
```

```python
import functools

import jax
import jax.numpy as jnp
import numpy as np
from jax import lax
from jax.experimental import pallas as pl
from jax.experimental.pallas import tpu as pltpu
from jax.sharding import PartitionSpec as P

HD = 64


MOMENTUM = 0.9
LEARN_RATE = 10.0
CLIP_NORM = 1.0
ZLOSS_WEIGHT = 0.01


TB = 1024
RK = 8
F32 = jnp.float32
BF16 = jnp.bfloat16
MESH_ID = pl.DeviceIdType.MESH
VM = pl.BlockSpec(memory_space=pltpu.VMEM)
ANYWHERE = pl.BlockSpec(memory_space=pl.ANY)


def round_up(value, step):
    return (value + step - 1) // step * step


def halves(value):
    high = value.astype(BF16).astype(F32)
    return high, value - high


def dims_of(value, contract_left, contract_right):
    return (((contract_left,), (contract_right,)), ((), ()))


def left_of(matrix, start_t):
    s_high, s_low = halves(start_t)
    both = jnp.concatenate([s_high, s_low], axis=0).astype(BF16)
    high = matrix.astype(BF16)
    low = (matrix - high.astype(F32)).astype(BF16)
    nt = (((1,), (1,)), ((), ()))
    main = lax.dot_general(both, high, nt, preferred_element_type=F32)
    rest = lax.dot_general(s_high.astype(BF16), low, nt, preferred_element_type=F32)
    return main[:RK] + main[RK:] + rest


def left_of_bf16(matrix, start_t):
    s_high, s_low = halves(start_t)
    both = jnp.concatenate([s_high, s_low], axis=0).astype(BF16)
    main = lax.dot_general(both, matrix, (((1,), (1,)), ((), ())), preferred_element_type=F32)
    return main[:RK] + main[RK:]


def right_of(basis_t, matrix):
    b_high, b_low = halves(basis_t)
    both = jnp.concatenate([b_high, b_low], axis=0).astype(BF16)
    high = matrix.astype(BF16)
    low = (matrix - high.astype(F32)).astype(BF16)
    main = jnp.dot(both, high, preferred_element_type=F32)
    rest = jnp.dot(b_high.astype(BF16), low, preferred_element_type=F32)
    return main[:RK] + main[RK:] + rest


def product_of(basis_t, right_t):
    b_high, b_low = halves(basis_t)
    r_high, r_low = halves(right_t)
    zero_b, zero_r = jnp.zeros_like(b_high), jnp.zeros_like(r_high)
    left = jnp.concatenate([b_high, b_low, b_high, zero_b], axis=0).astype(BF16)
    right = jnp.concatenate([r_high, r_high, r_low, zero_r], axis=0).astype(BF16)
    return lax.dot_general(left, right, (((0,), (0,)), ((), ())), preferred_element_type=F32)


def keep_rows(value, first_row, rows):
    at = first_row + lax.broadcasted_iota(jnp.int32, value.shape, 0)
    return jnp.where(at < rows, value, jnp.zeros_like(value))


def fold_squares(value):
    squares = value * value
    rows, columns = value.shape
    by_sublane = jnp.sum(squares.reshape(rows // 8, 8, columns), axis=0)
    total = by_sublane[:, :512]
    for start in range(512, columns, 512):
        total = total + by_sublane[:, start : start + 512]
    return total


def small_places(rows_list):
    places, at = [], 0
    for rows in rows_list:
        places.append(at)
        at += round_up(rows, 128)
    return places, at


def whole(shape):
    return pl.BlockSpec(shape, lambda *_: (0,) * len(shape))


def clip_of(norm_tile):
    return jnp.minimum(1.0, CLIP_NORM / norm_tile[0:1, 0:1])


def orthonormal_t(parts):
    row_at = lax.broadcasted_iota(jnp.int32, (RK, 1), 0)
    for row in range(RK):
        total = None
        for part in parts:
            term = part * part[row : row + 1, :]
            for start in range(0, term.shape[1], 128):
                piece = term[:, start : start + 128]
                total = piece if total is None else total + piece
        dots = jnp.sum(total, axis=1, keepdims=True)
        inverse = lax.rsqrt(dots[row : row + 1, :] + 1e-20)
        scale = jnp.where(row_at == row, inverse, 1.0)
        taken = jnp.where(row_at > row, -dots * inverse * inverse, 0.0)
        parts = [part * scale + taken * part[row : row + 1, :] for part in parts]
    return parts


def greet(axes):
    barrier = pltpu.get_barrier_semaphore()
    greeted = 0
    for axis, count in axes:
        me = lax.axis_index(axis)
        for step in range(1, count):
            pl.semaphore_signal(
                barrier,
                inc=1,
                device_id={axis: lax.rem(me + step, count)},
                device_id_type=MESH_ID,
            )
        greeted += count - 1
    pl.semaphore_wait(barrier, greeted)


def ring_copies(axis, count, src, dst, send_sem, recv_sem, place):
    me = lax.axis_index(axis)
    copies = []
    for step in range(1, count):
        peer = lax.rem(me + step, count)
        from_at, to_at = place(me, peer, step)
        copies.append(
            pltpu.make_async_remote_copy(
                src_ref=src.at[from_at], dst_ref=dst.at[to_at],
                send_sem=send_sem.at[step], recv_sem=recv_sem.at[step],
                device_id={axis: peer}, device_id_type=MESH_ID,
            )
        )
    return copies


def ring_start(axis, count, x, landing, sems):
    for copy in ring_copies(axis, count, x, landing, sems[0], sems[1], lambda me, peer, step: (peer, step)):
        copy.start()


def ring_middle(axis, count, x, landing, y, sems):
    me = lax.axis_index(axis)
    firsts = ring_copies(axis, count, x, landing, sems[0], sems[1], lambda me, peer, step: (peer, step))
    total = x[me].astype(F32)
    for step in range(1, count):
        firsts[step - 1].wait_recv()
        total = total + landing[step].astype(F32)
    y[me] = total.astype(y.dtype)
    for copy in ring_copies(axis, count, y, y, sems[2], sems[3], lambda me, peer, step: (me, me)):
        copy.start()
    for copy in firsts:
        copy.wait_send()


def ring_end(axis, count, y, sems):
    me = lax.axis_index(axis)
    for step in range(1, count):
        source = lax.rem(me - step + count, count)
        pltpu.make_async_remote_copy(
            src_ref=y.at[source], dst_ref=y.at[source],
            send_sem=sems[2].at[step], recv_sem=sems[3].at[step],
            device_id={axis: source}, device_id_type=MESH_ID,
        ).wait_recv()
    for copy in ring_copies(axis, count, y, y, sems[2], sems[3], lambda me, peer, step: (me, me)):
        copy.wait_send()


def settle_kernel(workers, shards, rows, row_list, widths, *refs):
    gq_ref, eq_ref, gs_ref, es_ref, gains_ref, sq_ref = refs[0:6]
    anys = refs[6:16]
    ph, phs, own_ref, mean_ref, norm_ref, gain_ref = refs[16:22]
    (
        x, landing, y, small, sq_all, flat, x16, landing16, y16, table16, table_send, table_recv,
        sem_a, sem_b, sem_c, sem_d, sem_e, sem_f, sem_g, sem_h, sq_send, sq_recv, load_sem,
    ) = refs[22:-10]
    grads, errs = refs[-10:-5], refs[-5:]
    first_sems, second_sems = (sem_a, sem_b, sem_c, sem_d), (sem_e, sem_f, sem_g, sem_h)
    places, _ = small_places(row_list)
    starts = [sum(widths[:k]) for k in range(5)]
    gains_at = gs_ref.shape[1]
    blocks = pl.cdiv(rows, TB)
    tiles = [pl.ds(at * TB, min(TB, rows - at * TB)) for at in range(blocks)]
    pairs = [(anys[k].at[tile, :], kept.at[tile, :]) for k, kept in ((0, grads[0]), (5, errs[0])) for tile in tiles]
    pairs += [(anys[k], grads[k]) for k in range(1, 5)] + [(anys[5 + k], errs[k]) for k in range(1, 5)]
    loads = [pltpu.make_async_copy(src, dst, load_sem.at[at]) for at, (src, dst) in enumerate(pairs)]
    for copy in loads:
        copy.start()
    greet((("rep", workers), ("voc", shards)))
    shard = lax.axis_index("voc")
    own = jnp.sum(sq_ref[...].reshape(8, 4, 128), axis=1)
    own = jnp.sum(jnp.sum(own, axis=0, keepdims=True), axis=1, keepdims=True)
    sq_all[shard] = jnp.broadcast_to(own, (8, 128))
    copies = ring_copies("voc", shards, sq_all, sq_all, sq_send, sq_recv, lambda me, peer, step: (me, me))
    for copy in copies:
        copy.start()
    gains = gains_ref[...]
    total = jnp.sum(jnp.sum(gains * gains, axis=0, keepdims=True), axis=1, keepdims=True)
    small[...] = jnp.zeros_like(small)
    for gap in range(1, shards):
        source = lax.rem(shard - gap + shards, shards)
        pltpu.make_async_remote_copy(
            src_ref=sq_all.at[source], dst_ref=sq_all.at[source],
            send_sem=sq_send.at[gap], recv_sem=sq_recv.at[gap],
            device_id={"voc": source}, device_id_type=MESH_ID,
        ).wait_recv()
    for copy in copies:
        copy.wait_send()
    for peer in range(shards):
        total = total + sq_all[peer][0:1, 0:1]
    norm = jnp.sqrt(total)
    norm_ref[...] = jnp.broadcast_to(norm, (8, 128))
    clip = jnp.minimum(1.0, CLIP_NORM / norm)

    chunk = gq_ref.shape[1] // workers
    part = small.shape[1] // workers
    small[:, :gains_at] = clip * gs_ref[...] + es_ref[...]
    small[:, gains_at : gains_at + gains.shape[1]] = clip * gains
    for j in range(workers):
        lanes = slice(j * chunk, (j + 1) * chunk)
        x[j, :, :chunk] = clip * gq_ref[:, lanes] + eq_ref[:, lanes]
        x[j, :, chunk:] = small[:, j * part : (j + 1) * part]
    ring_start("rep", workers, x, landing, first_sems)
    ring_middle("rep", workers, x, landing, y, first_sems)
    for copy in loads:
        copy.wait()
    for k in range(1, 5):
        grads[k][...] = clip * grads[k][...] + errs[k][...].astype(F32)

    @pl.loop(0, blocks)
    def _(step):
        tile = pl.ds(pl.multiple_of(step * TB, TB), TB)
        matrix = clip * grads[0][tile, :] + errs[0][tile, :].astype(F32)
        grads[0][tile, :] = keep_rows(matrix, step * TB, rows)

    ring_end("rep", workers, y, first_sems)
    parts = orthonormal_t([y[j, :, :chunk] for j in range(workers)])
    for j in range(workers):
        ph[:, j * chunk : (j + 1) * chunk] = parts[j]
        small[:, j * part : (j + 1) * part] = y[j, :, chunk:]
    gain_ref[...] = small[:, gains_at : gains_at + gains.shape[1]] * (1.0 / workers)
    flat[...] = jnp.zeros_like(flat)
    for k in range(4):
        place, size = places[k], row_list[k]
        basis_t = orthonormal_t([small[:, place : place + round_up(size, 128)]])[0]
        phs[:, place : place + round_up(size, 128)] = basis_t
        basis_t = basis_t[:, :size]
        right_t = right_of(basis_t, grads[k + 1][...])
        flat[:, starts[k + 1] : starts[k + 1] + widths[k + 1]] = right_t
    half = x16.shape[2]
    for j in range(workers):
        low, high = starts[1] + j * 2 * half, starts[1] + (j * 2 + 1) * half
        pair = jnp.concatenate([flat[:, low : low + half], flat[:, high : high + half]], axis=0)
        x16[j] = pair.astype(BF16)
    ring_start("rep", workers, x16, landing16, second_sems)

    @pl.loop(0, blocks)
    def _(step):
        tile = pl.ds(pl.multiple_of(step * TB, TB), TB)
        flat[:, : widths[0]] += right_of(ph[:, tile], grads[0][tile, :])

    me = lax.axis_index("rep")
    split = widths[0] // 2
    table16[me] = jnp.concatenate([flat[:, :split], flat[:, split : 2 * split]], axis=0).astype(BF16)
    copies = ring_copies(
        "rep", workers, table16, table16, table_send, table_recv, lambda me, peer, step: (me, me)
    )
    for copy in copies:
        copy.start()
    own_ref[...] = flat[...]
    ring_middle("rep", workers, x16, landing16, y16, second_sems)
    ring_end("rep", workers, y16, second_sems)
    half = x16.shape[2]
    for j in range(workers):
        pair = y16[j].astype(F32) * (1.0 / workers)
        low, high = starts[1] + j * 2 * half, starts[1] + (j * 2 + 1) * half
        mean_ref[:, low : low + half] = pair[:8]
        mean_ref[:, high : high + half] = pair[8:]
    for gap in range(1, workers):
        source = lax.rem(me - gap + workers, workers)
        pltpu.make_async_remote_copy(
            src_ref=table16.at[source], dst_ref=table16.at[source],
            send_sem=table_send.at[gap], recv_sem=table_recv.at[gap],
            device_id={"rep": source}, device_id_type=MESH_ID,
        ).wait_recv()
    total = table16[0].astype(F32)
    for j in range(1, workers):
        total = total + table16[j].astype(F32)
    total = total * (1.0 / workers)
    mean_ref[:, :split] = total[:8]
    mean_ref[:, split : 2 * split] = total[8:]
    for copy in copies:
        copy.wait_send()


def finish_kernel(rows, row_list, widths, *refs):
    grads, errs, moms, weights = refs[0:5], refs[5:10], refs[10:15], refs[15:19]
    ph_ref, phs_ref, own_ref, mean_ref, norm_ref, gain_ref, gain_mom_ref, loss_ref = refs[19:27]
    new_errs, new_moms, changed, rights = refs[27:32], refs[32:37], refs[37:42], refs[42:47]
    gain_change_ref, next_gain_ref, loss_out, norm_out = refs[47:51]
    step = pl.program_id(0)
    places, _ = small_places(row_list)
    starts = [sum(widths[:k]) for k in range(5)]
    clip = clip_of(norm_ref[...])

    def settle_one(k, basis_t):
        lanes = slice(starts[k], starts[k] + widths[k])
        matrix = clip * grads[k][...] + errs[k][...].astype(F32)
        new_errs[k][...] = matrix - product_of(basis_t, own_ref[:, lanes])
        moved = MOMENTUM * moms[k][...].astype(F32) + product_of(basis_t, mean_ref[:, lanes])
        new_moms[k][...] = moved
        change = -LEARN_RATE * moved
        changed[k][...] = weights[k - 1][...] + change if k else change

    @pl.when(step == 0)
    def _():
        moved = MOMENTUM * gain_mom_ref[...].astype(F32) + gain_ref[: gain_mom_ref.shape[0], :]
        next_gain_ref[...] = moved
        gain_change_ref[...] = -LEARN_RATE * moved
        loss_out[0] = jnp.max(loss_ref[...])
        norm_out[0] = jnp.max(norm_ref[...])
        for k in range(5):
            rights[k][...] = mean_ref[:, starts[k] : starts[k] + widths[k]]
        for k in range(1, 5):
            settle_one(k, phs_ref[:, places[k - 1] : places[k - 1] + row_list[k - 1]])

    settle_one(0, ph_ref[...])


def held(shape):
    return pl.BlockSpec(shape, lambda *_: (0,) * len(shape), pipeline_mode=pl.Buffered(1))


def settle(loss_tile, sketches, gains, gain_mom, grads, errs, moms, weights, workers, shards):
    gq, eq, gs, es, sq = sketches
    rows, width = grads[0].shape
    blocks = pl.cdiv(rows, TB)
    row_list = [g.shape[0] for g in grads[1:]]
    widths = [g.shape[1] for g in grads]
    small = round_up(gs.shape[1] + gains.shape[1], workers * 128)
    lanes = (gq.shape[1] + small) // workers
    small_lanes = round_up(sum(widths[1:]), workers * 256)
    right_lanes = widths[0] + small_lanes
    half = small_lanes // workers // 2
    shape = jax.ShapeDtypeStruct
    block = pl.BlockSpec((TB, width), lambda i: (i, 0))
    small_specs = [held(g.shape) for g in grads[1:]]
    made = [
        shape((RK, blocks * TB), F32),
        shape(gs.shape, F32),
        shape((RK, right_lanes), F32),
        shape((RK, right_lanes), F32),
        shape((8, 128), F32),
        shape(gains.shape, F32),
    ]
    operands = (gq, eq, gs, es, gains, sq)
    sums = pl.pallas_call(
        functools.partial(settle_kernel, workers, shards, rows, row_list, widths),
        in_specs=[VM] * 6 + [ANYWHERE] * 10,
        out_specs=[VM] * 6,
        out_shape=made,
        scratch_shapes=[pltpu.VMEM((workers, RK, lanes), F32)] * 3
        + [
            pltpu.VMEM((RK, small), F32),
            pltpu.VMEM((shards, 8, 128), F32),
            pltpu.VMEM((RK, right_lanes), F32),
        ]
        + [pltpu.VMEM((workers, 16, half), BF16)] * 3
        + [pltpu.VMEM((workers, 16, width // 2), BF16)]
        + [pltpu.SemaphoreType.DMA((workers,))] * 2
        + [pltpu.SemaphoreType.DMA((workers,))] * 8
        + [pltpu.SemaphoreType.DMA((shards,))] * 2
        + [pltpu.SemaphoreType.DMA((2 * blocks + 8,))]
        + [pltpu.VMEM((blocks * TB, width), F32)]
        + [pltpu.VMEM(g.shape, F32) for g in grads[1:]]
        + [pltpu.VMEM((blocks * TB, width), BF16)]
        + [pltpu.VMEM(e.shape, BF16) for e in errs[1:]],
        compiler_params=pltpu.CompilerParams(
            collective_id=1, has_side_effects=True, vmem_limit_bytes=60 << 20
        ),
        name="settle_sums",
    )(*operands, *grads, *errs)
    ph, phs, own, mean, norm, gain = sums
    out = pl.pallas_call(
        functools.partial(finish_kernel, rows, row_list, widths),
        grid=(blocks,),
        in_specs=([block] + small_specs) * 3
        + small_specs
        + [pl.BlockSpec((RK, TB), lambda i: (0, i))]
        + [held(m.shape) for m in made[1:]]
        + [held(gain_mom.shape), held(loss_tile.shape)],
        out_specs=([block] + small_specs) * 3
        + [held((RK, w)) for w in widths]
        + [held(gain_mom.shape)] * 2
        + [pl.BlockSpec(memory_space=pltpu.SMEM)] * 2,
        out_shape=[shape(g.shape, F32) for g in grads] * 3
        + [shape((RK, w), F32) for w in widths]
        + [shape(gain_mom.shape, F32)] * 2
        + [shape((1,), F32)] * 2,
        compiler_params=pltpu.CompilerParams(vmem_limit_bytes=60 << 20),
        name="settle_finish",
    )(*grads, *errs, *moms, *weights, ph, phs, own, mean, norm, gain, gain_mom, loss_tile)
    return out[0:5], out[5:10], out[10:15], out[15:20], *out[20:24]


EPS = 1e-06
QB = 256
INV_SQRT2 = 0.7071067811865476
INV_SQRT_2PI = 0.3989422804014327


def nt_dot(a, b):
    return lax.dot_general(a, b, (((1,), (1,)), ((), ())), preferred_element_type=F32)


def nn_dot(a, b):
    return jnp.dot(a, b, preferred_element_type=F32)


def scaled_rms(value, gain):
    return value * lax.rsqrt(jnp.mean(value * value, axis=1, keepdims=True) + EPS) * gain


def rms_back(grad, value, gain):
    inverse = lax.rsqrt(jnp.mean(value * value, axis=1, keepdims=True) + EPS)
    scaled = grad * gain
    along = jnp.mean(scaled * value, axis=1, keepdims=True)
    back = inverse * (scaled - value * (inverse * inverse * along))
    return back, jnp.sum(grad * value * inverse, axis=0, keepdims=True)


def turned(value_t, cos_t, sin_t, half):
    first, second = value_t[:half], value_t[half:]
    return jnp.concatenate([first * cos_t - second * sin_t, first * sin_t + second * cos_t], axis=0)


def turned_back(value_t, cos_t, sin_t, half):
    first, second = value_t[:half], value_t[half:]
    return jnp.concatenate([first * cos_t + second * sin_t, second * cos_t - first * sin_t], axis=0)


def causal_tile(scores_t, fill):
    size = scores_t.shape[1]
    key_at = lax.broadcasted_iota(jnp.int32, (size, size), 0)
    query_at = lax.broadcasted_iota(jnp.int32, (size, size), 1)
    tail = jnp.where(key_at <= query_at, scores_t[-size:], fill)
    if scores_t.shape[0] == size:
        return tail
    return jnp.concatenate([scores_t[:-size], tail], axis=0)


def forward_kernel(
    shards, axis,
    x0_ref, gains_ref, cos_ref, sin_ref, wqkv_ref, wo_own, wu_own, wd_own,
    n1_ref, qkv_ref, lse_ref, mixed_ref, x1_ref, n2_ref, x2_ref, n3_ref, wo_all, wu_all, wd_all, hid_any,
    hid_ref, hid_sem, wo_sems, wu_sems, wd_sems,
):
    tokens, width = x0_ref.shape
    half = HD // 2
    row_blocks = tokens // QB
    greet_all(shards)
    shard = lax.axis_index(axis)
    spreads = []
    for own, full, sems in ((wo_own, wo_all, wo_sems), (wu_own, wu_all, wu_sems), (wd_own, wd_all, wd_sems)):
        full[shard] = own[...].astype(BF16)
        spreads.append(Spread(full, shards, sems))
    await_all(shards)
    for spread in spreads:
        spread.start()

    @pl.loop(0, row_blocks)
    def _(block):
        rows = pl.ds(pl.multiple_of(block * QB, QB), QB)
        n1_ref[rows, :] = scaled_rms(x0_ref[rows, :].astype(F32), gains_ref[0:1, :]).astype(BF16)

    group = 4 * HD

    @pl.loop(0, width // group)
    def _(at):
        n1 = n1_ref[...]
        for part in range(3):
            start = pl.multiple_of(part * width + at * group, group)
            packed_t = nn_dot(n1, wqkv_ref[:, pl.ds(start, group)]).T
            if part < 2:
                cos_t, sin_t = cos_ref[...], sin_ref[...]
                packed_t = jnp.concatenate(
                    [
                        turned(packed_t[head * HD : (head + 1) * HD], cos_t, sin_t, half)
                        for head in range(4)
                    ],
                    axis=0,
                )
            if part == 0:
                packed_t = packed_t * HD ** (-0.5)
            qkv_ref[part, pl.ds(pl.multiple_of(at * group, group), group), :] = packed_t.astype(BF16)

    spreads[0].relay()

    @pl.loop(0, width // (2 * HD))
    def _(pair):
        @pl.when(pair == 1)
        def _():
            spreads[1].relay()
            spreads[0].relay_across()

        @pl.when(pair == 2)
        def _():
            spreads[2].relay()

        @pl.when(pair == 3)
        def _():
            spreads[1].relay_across()

        places = [pl.ds(pl.multiple_of((pair * 2 + side) * HD, HD), HD) for side in range(2)]
        keys = [qkv_ref[1, places[side], :].T for side in range(2)]

        def scores_of(side, block):
            count = (block + 1) * QB
            query_t = qkv_ref[0, places[side], block * QB : count]
            return causal_tile(nn_dot(keys[side][:count], query_t), -1e30)

        work = [(side, block) for side in range(2) for block in range(row_blocks)]
        ahead = scores_of(*work[0])
        mixed_parts, lse_parts = ([], []), ([], [])
        for at, (side, block) in enumerate(work):
            scores = ahead
            if at + 1 < len(work):
                ahead = scores_of(*work[at + 1])
            top = jnp.max(scores, axis=0, keepdims=True)
            weight = jnp.exp(scores - top)
            total = jnp.sum(weight, axis=0, keepdims=True)
            probs = (weight * (1.0 / total)).astype(BF16)
            value_t = qkv_ref[2, places[side], : (block + 1) * QB]
            mixed_parts[side].append(nn_dot(value_t, probs))
            lse_parts[side].append(top + jnp.log(total))
        for side in range(2):
            mixed_ref[places[side], :] = jnp.concatenate(mixed_parts[side], axis=1).astype(BF16)
            lse_ref[pair * 2 + side] = jnp.concatenate(lse_parts[side], axis=1)

    spreads[0].finish()

    @pl.loop(0, row_blocks)
    def _(block):
        rows = pl.ds(pl.multiple_of(block * QB, QB), QB)
        mixed = mixed_ref[:, rows].T
        stream = x0_ref[rows, :].astype(F32) + nn_dot(mixed, wo_all[...].reshape(width, width))
        x1_ref[rows, :] = stream
        x2_ref[rows, :] = stream
        n2_ref[rows, :] = scaled_rms(stream, gains_ref[1:2, :]).astype(BF16)

    spreads[2].relay_across()
    spreads[1].finish()
    spreads[2].finish()
    chunk = hid_ref.shape[2]
    chunks = wu_all.shape[2] // chunk
    parts = chunk // wd_all.shape[1]

    def put(slot, at):
        return pltpu.make_async_copy(
            hid_ref.at[slot],
            hid_any.at[:, pl.ds(pl.multiple_of(at * chunk, chunk), chunk)],
            hid_sem.at[slot],
        )

    @pl.loop(0, chunks)
    def _(at):
        slot = lax.rem(at, 2)
        lanes = pl.ds(pl.multiple_of(at * chunk, chunk), chunk)

        @pl.when(at >= 2)
        def _():
            put(slot, at - 2).wait()

        for block in range(row_blocks):
            rows = slice(block * QB, (block + 1) * QB)
            hidden = nn_dot(n2_ref[rows, :], wu_all[:, :, lanes].reshape(width, chunk))
            hid_ref[slot, rows, :] = hidden
            active = (0.5 * hidden * (1.0 + lax.erf(hidden * INV_SQRT2))).astype(BF16)
            down = wd_all[pl.ds(at * parts, parts)].reshape(chunk, width)
            x2_ref[rows, :] += nn_dot(active, down)
        put(slot, at).start()

    @pl.loop(0, row_blocks)
    def _(block):
        rows = pl.ds(pl.multiple_of(block * QB, QB), QB)
        n3_ref[rows, :] = scaled_rms(x2_ref[rows, :], gains_ref[2:3, :]).astype(BF16)

    for at in range(max(0, chunks - 2), chunks):
        put(at % 2, at).wait()


def layer_forward(x0, gains, cos_t, sin_t, wqkv, slices, shards, axis):
    tokens, width = x0.shape
    hidden = slices[1].shape[1]
    shape = jax.ShapeDtypeStruct
    chunk = min(512, hidden)
    sems = pltpu.SemaphoreType.DMA((8, max(2, shards // 2)))
    return pl.pallas_call(
        functools.partial(forward_kernel, shards, axis),
        in_specs=[VM] * 8,
        out_specs=[VM] * 11 + [ANYWHERE],
        out_shape=[
            shape((tokens, width), BF16),
            shape((3, width, tokens), BF16),
            shape((width // HD, 1, tokens), F32),
            shape((width, tokens), BF16),
            shape((tokens, width), F32),
            shape((tokens, width), BF16),
            shape((tokens, width), F32),
            shape((tokens, width), BF16),
        ]
        + [shape((shards, *w.shape), BF16) for w in slices]
        + [shape((tokens, hidden), F32)],
        scratch_shapes=[
            pltpu.VMEM((2, tokens, chunk), F32),
            pltpu.SemaphoreType.DMA((2,)),
            sems,
            sems,
            sems,
        ],
        compiler_params=pltpu.CompilerParams(
            collective_id=5, has_side_effects=True, vmem_limit_bytes=60 << 20
        ),
        name="layer_forward",
    )(x0, gains, cos_t, sin_t, wqkv, *slices)


def backward_kernel(shard_axis, *refs):
    anys, refs = refs[:13], refs[13:]
    gains_ref, cos_ref, sin_ref, lse_ref = refs[0:4]
    dx0_ref, gqkv_ref, gout_ref, gup_ref, gdown_ref, ggains_ref = refs[4:10]
    kept, refs = refs[10:23], refs[23:]
    dn3_ref, x2_ref, hid_ref, wd_ref, wu_ref, x1_ref, n2_ref, wo_ref, mixed_ref, qkv_ref, x0_ref, n1_ref, wqkv_ref = kept
    grad_ref, part_ref, low_ref, act_ref, dhid_ref, dmixed_ref, dpacked_ref, turn_ref, load_sem = refs
    shard = lax.axis_index(shard_axis) if shard_axis else 0
    tokens, width = x2_ref.shape
    half = HD // 2
    row_blocks = tokens // QB
    loads = [
        pltpu.make_async_copy(src, dst, load_sem.at[at])
        for at, (src, dst) in enumerate(zip(anys, kept))
    ]
    for load in loads:
        load.start()

    def block_rows(block):
        return pl.ds(pl.multiple_of(block * QB, QB), QB)

    loads[0].wait()
    loads[1].wait()
    ggains_ref[...] = jnp.zeros_like(ggains_ref)

    @pl.loop(0, row_blocks)
    def _(block):
        rows = block_rows(block)
        back, gain = rms_back(dn3_ref[:, rows].T, x2_ref[rows, :], gains_ref[2:3, :])
        grad_ref[rows, :] = back
        low_ref[rows, :] = back.astype(BF16)
        part_ref[rows, :] = jnp.zeros_like(back)
        ggains_ref[2:3, :] += gain

    for at in (2, 3, 4):
        loads[at].wait()
    chunk = min(512, wu_ref.shape[1])

    @pl.loop(0, wu_ref.shape[1] // chunk)
    def _(at):
        lanes = pl.ds(pl.multiple_of(at * chunk, chunk), chunk)
        for block in range(row_blocks):
            rows = slice(block * QB, (block + 1) * QB)
            grad_act = nt_dot(low_ref[rows, :], wd_ref[lanes, :])
            hidden = hid_ref[rows, lanes]
            share = 0.5 + 0.5 * lax.erf(hidden * INV_SQRT2)
            slope = share + hidden * (INV_SQRT_2PI * jnp.exp(-0.5 * hidden * hidden))
            act_ref[rows, lanes] = (hidden * share).astype(BF16)
            grad_hid = (slope * grad_act).astype(BF16)
            dhid_ref[rows, lanes] = grad_hid
            part_ref[rows, :] += nt_dot(grad_hid, wu_ref[:, lanes])

    own = gdown_ref.shape[0]
    gdown_ref[...] = nn_dot(act_ref[:, pl.ds(pl.multiple_of(shard * own, own), own)].T, low_ref[...])
    loads[5].wait()
    loads[6].wait()
    own = gup_ref.shape[0]
    turn_ref[...] = n2_ref[...].T
    own_rows = pl.ds(pl.multiple_of(shard * own, own), own)

    @pl.loop(0, wu_ref.shape[1] // chunk)
    def _(at):
        lanes = pl.ds(pl.multiple_of(at * chunk, chunk), chunk)
        gup_ref[:, lanes] = nn_dot(turn_ref[own_rows, :], dhid_ref[:, lanes])

    loads[7].wait()

    @pl.loop(0, row_blocks)
    def _(block):
        rows = block_rows(block)
        back, gain = rms_back(part_ref[rows, :], x1_ref[rows, :], gains_ref[1:2, :])
        back = grad_ref[rows, :] + back
        grad_ref[rows, :] = back
        low = back.astype(BF16)
        low_ref[rows, :] = low
        ggains_ref[1:2, :] += gain
        dmixed_ref[:, rows] = nt_dot(low, wo_ref[...]).astype(BF16).T

    loads[8].wait()
    loads[9].wait()
    own = gout_ref.shape[0]
    own_rows = pl.ds(pl.multiple_of(shard * own, own), own)
    gout_ref[...] = nn_dot(mixed_ref[own_rows, :], low_ref[...])

    @pl.loop(0, width // (2 * HD))
    def _(pair):
        made = ([], [], [])
        places = [pl.ds(pl.multiple_of((pair * 2 + side) * HD, HD), HD) for side in range(2)]
        natural = [
            [ref[rows, :].T for ref in (qkv_ref.at[0], qkv_ref.at[1], qkv_ref.at[2], dmixed_ref)]
            for rows in places
        ]

        def products_of(side, block):
            count = (block + 1) * QB
            at = slice(block * QB, count)
            _, key, value, _ = natural[side]
            scores = nn_dot(key[:count], qkv_ref[0, places[side], at])
            return scores, nn_dot(value[:count], dmixed_ref[places[side], at])

        work = [(side, block) for side in range(2) for block in range(row_blocks)]
        ahead = products_of(*work[0])
        dquery_parts = []
        for place, (side, block) in enumerate(work):
            if block == 0:
                dquery_parts = []
                dkey = [None] * row_blocks
                dvalue = [None] * row_blocks
            scores, dprobs = ahead
            if place + 1 < len(work):
                ahead = products_of(*work[place + 1])
            count = (block + 1) * QB
            at = slice(block * QB, count)
            query, _, _, dmix = natural[side]
            probs = causal_tile(jnp.exp(scores - lse_ref[pair * 2 + side][:, at]), 0.0)
            delta = jnp.sum(probs * dprobs, axis=0, keepdims=True)
            dscores = (probs * (dprobs - delta)).astype(BF16)
            dquery_parts.append(nn_dot(qkv_ref[1, places[side], :count], dscores))
            more_key = nn_dot(dscores, query[at])
            more_value = nn_dot(probs.astype(BF16), dmix[at])
            for piece in range(block + 1):
                cut = slice(piece * QB, (piece + 1) * QB)
                if dkey[piece] is None:
                    dkey[piece], dvalue[piece] = more_key[cut], more_value[cut]
                else:
                    dkey[piece] = dkey[piece] + more_key[cut]
                    dvalue[piece] = dvalue[piece] + more_value[cut]
            if block == row_blocks - 1:
                cos_t, sin_t = cos_ref[...], sin_ref[...]
                dquery_t = jnp.concatenate(dquery_parts, axis=1) * HD ** (-0.5)
                dkey_t = jnp.concatenate(dkey, axis=0).T
                made[0].append(turned_back(dquery_t, cos_t, sin_t, half).T)
                made[1].append(turned_back(dkey_t, cos_t, sin_t, half).T)
                made[2].append(jnp.concatenate(dvalue, axis=0))
        for part in range(3):
            lanes = pl.ds(pl.multiple_of(part * width + pair * 2 * HD, 2 * HD), 2 * HD)
            dpacked_ref[:, lanes] = jnp.concatenate(made[part], axis=1).astype(BF16)

    for at in (10, 11, 12):
        loads[at].wait()
    own = gqkv_ref.shape[0]
    turn_ref[...] = n1_ref[...].T
    own_rows = pl.ds(pl.multiple_of(shard * own, own), own)

    @pl.loop(0, 3)
    def _(at):
        lanes = pl.ds(pl.multiple_of(at * width, width), width)
        gqkv_ref[:, lanes] = nn_dot(turn_ref[own_rows, :], dpacked_ref[:, lanes])

    @pl.loop(0, row_blocks)
    def _(block):
        rows = block_rows(block)
        back, gain = rms_back(
            nt_dot(dpacked_ref[rows, :], wqkv_ref[...]), x0_ref[rows, :].astype(F32), gains_ref[0:1, :]
        )
        dx0_ref[rows, :] = grad_ref[rows, :] + back
        ggains_ref[0:1, :] += gain


def layer_backward(shard_axis, slice_shapes, dn3_t, gains, cos_t, sin_t, projections, x0, kept):
    n1, qkv, lse, mixed_t, x1, n2, x2, _, hid = kept
    wqkv, wo, wu, wd = projections
    tokens, width = x2.shape
    shape = jax.ShapeDtypeStruct
    moved = (dn3_t, x2, hid, wd, wu, x1, n2, wo, mixed_t, qkv, x0, n1, wqkv)
    return pl.pallas_call(
        functools.partial(backward_kernel, shard_axis),
        in_specs=[ANYWHERE] * 13 + [VM] * 3 + [VM],
        out_specs=[VM] * 6,
        out_shape=[shape((tokens, width), F32)]
        + [shape(s, F32) for s in slice_shapes]
        + [shape((8, width), F32)],
        scratch_shapes=[pltpu.VMEM(m.shape, m.dtype) for m in moved]
        + [
            pltpu.VMEM((tokens, width), F32),
            pltpu.VMEM((tokens, width), F32),
            pltpu.VMEM((tokens, width), BF16),
            pltpu.VMEM(hid.shape, BF16),
            pltpu.VMEM(hid.shape, BF16),
            pltpu.VMEM((width, tokens), BF16),
            pltpu.VMEM((tokens, 3 * width), BF16),
            pltpu.VMEM((width, tokens), BF16),
            pltpu.SemaphoreType.DMA((13,)),
        ],
        compiler_params=pltpu.CompilerParams(vmem_limit_bytes=62 << 20),
        name="layer_backward",
    )(*moved, gains, cos_t, sin_t, lse)


def scatter_sketch_kernel(axis, rows, row_list, ids_ref, *refs):
    anys, starts = refs[0:11], refs[11:16]
    full_any, gq_ref, eq_ref, gs_ref, es_ref, sq_ref = refs[16:22]
    dx0_ref, whole_ref, table_err_ref = refs[22:25]
    grads, errs = refs[25:29], refs[29:33]
    load_sem, small_sem, store_sem = refs[33:36]
    places, _ = small_places(row_list)
    blocks = pl.cdiv(rows, TB)
    padded = blocks * TB
    tiles = [pl.ds(at * TB, min(TB, rows - at * TB)) for at in range(blocks)]
    smalls = [
        pltpu.make_async_copy(src, dst, small_sem.at[at])
        for at, (src, dst) in enumerate(zip((*anys[2:6], *anys[7:11], anys[1]), (*grads, *errs, dx0_ref)))
    ]
    for copy in smalls[:8]:
        copy.start()
    loads = [
        pltpu.make_async_copy(anys[0].at[tile, :], whole_ref.at[tile, :], load_sem.at[0, at])
        for at, tile in enumerate(tiles)
    ]
    err_loads = [
        pltpu.make_async_copy(anys[6].at[tile, :], table_err_ref.at[tile, :], load_sem.at[1, at])
        for at, tile in enumerate(tiles)
    ]
    for copy in loads:
        copy.start()
    smalls[8].start()
    for copy in err_loads:
        copy.start()
    if padded > rows:
        rest = pl.ds(rows, padded - rows)
        whole_ref[rest, :] = jnp.zeros((padded - rows, whole_ref.shape[1]), F32)
        table_err_ref[rest, :] = jnp.zeros((padded - rows, whole_ref.shape[1]), BF16)
    gs_ref[...] = jnp.zeros_like(gs_ref)
    es_ref[...] = jnp.zeros_like(es_ref)
    for copy in smalls[:8]:
        copy.wait()
    total = jnp.zeros(sq_ref.shape, F32)
    for k in range(4):
        grad = grads[k][...]
        start_t = starts[k + 1][...]
        at = pl.ds(places[k], row_list[k])
        gs_ref[:, at] = left_of(grad, start_t)
        es_ref[:, at] = left_of_bf16(errs[k][...], start_t)
        total = total + fold_squares(grad)
    sq_ref[...] = total
    smalls[8].wait()
    for copy in loads:
        copy.wait()
    first = lax.axis_index(axis) * rows if axis else 0

    @pl.loop(0, dx0_ref.shape[0] // 8)
    def _(group):
        base = pl.multiple_of(group * 8, 8)
        for side in range(8):
            row = ids_ref[base + side] - first
            row = jnp.where((row >= 0) & (row < rows), row, padded)
            whole_ref[pl.ds(row, 1), :] += dx0_ref[pl.ds(base + side, 1), :]

    stores = [
        pltpu.make_async_copy(whole_ref.at[tile, :], full_any.at[tile, :], store_sem.at[at])
        for at, tile in enumerate(tiles)
    ]
    for copy in stores:
        copy.start()
    for copy in err_loads:
        copy.wait()

    @pl.loop(0, blocks)
    def _(step):
        at = pl.multiple_of(step * TB, TB)
        start_t = starts[0][...]
        grad = whole_ref[pl.ds(at, TB), :]
        gq_ref[:, pl.ds(at, TB)] = left_of(grad, start_t)
        eq_ref[:, pl.ds(at, TB)] = left_of_bf16(table_err_ref[pl.ds(at, TB), :], start_t)
        sq_ref[...] += fold_squares(grad)

    for copy in stores:
        copy.wait()


def scatter_sketch(token_ids, table_grad, dx0, grads, errs, starts_t, axis):
    rows, width = table_grad.shape
    blocks = pl.cdiv(rows, TB)
    row_list = [g.shape[0] for g in grads]
    _, small = small_places(row_list)

    def whole_at(shape):
        return pl.BlockSpec(shape, lambda *_: (0,) * len(shape), pipeline_mode=pl.Buffered(1))

    shape = jax.ShapeDtypeStruct
    made = [(RK, blocks * TB)] * 2 + [(RK, small)] * 2 + [(8, 512)]
    full, *sketches = pl.pallas_call(
        functools.partial(scatter_sketch_kernel, axis, rows, row_list),
        grid_spec=pltpu.PrefetchScalarGridSpec(
            num_scalar_prefetch=1,
            grid=(1,),
            in_specs=[ANYWHERE] * 11 + [whole_at(s.shape) for s in starts_t],
            out_specs=[ANYWHERE] + [whole_at(m) for m in made],
            scratch_shapes=[
                pltpu.VMEM(dx0.shape, F32),
                pltpu.VMEM((blocks * TB + 8, width), F32),
                pltpu.VMEM((blocks * TB, width), BF16),
            ]
            + [pltpu.VMEM(g.shape, F32) for g in grads]
            + [pltpu.VMEM(e.shape, BF16) for e in errs[1:]]
            + [
                pltpu.SemaphoreType.DMA((2, blocks)),
                pltpu.SemaphoreType.DMA((9,)),
                pltpu.SemaphoreType.DMA((blocks,)),
            ],
        ),
        out_shape=[shape((rows, width), F32)] + [shape(m, F32) for m in made],
        compiler_params=pltpu.CompilerParams(vmem_limit_bytes=60 << 20),
        name="scatter_sketch",
    )(token_ids.reshape(-1), table_grad, dx0, *grads, *errs, *starts_t)
    return full, sketches


class Spread:
    def __init__(self, full, shards, sems):
        self.full, self.sems = full, sems
        self.shard, self.worker = lax.axis_index("voc"), lax.axis_index("rep")
        self.core = lax.rem(self.shard, 2)
        self.chip = self.shard // 2
        self.chips = shards // 2
        self.side = lax.rem(self.worker, 2)
        self.rows = full.shape[1] // 2

    def region(self, slot, side):
        return self.full.at[slot, pl.ds(pl.multiple_of(side * self.rows, self.rows), self.rows), :]

    def copy(self, ref, at, pair, peer):
        return pltpu.make_async_remote_copy(
            src_ref=ref, dst_ref=ref, send_sem=self.sems.at[2 * pair, at], recv_sem=self.sems.at[2 * pair + 1, at],
            device_id=peer, device_id_type=MESH_ID,
        )

    def source(self, at):
        return lax.rem(self.chip - at + self.chips, self.chips)

    def own_to_chip(self, at):
        peer = lax.rem(self.chip + at, self.chips) * 2 + self.core
        return self.copy(self.region(self.shard, self.side), at, 0, {"voc": peer})

    def from_chip(self, at):
        slot = self.source(at) * 2 + self.core
        return self.copy(self.region(slot, self.side), at, 0, {"voc": slot})

    def across(self, at, side):
        slot = self.source(at) * 2 + self.core
        return self.copy(self.region(slot, side), at, 1, {"rep": self.worker + 1 - 2 * self.side})

    def to_core(self, at, side, pair, core):
        slot = self.source(at) * 2 + core
        return self.copy(self.region(slot, side), at, pair, {"voc": self.shard + 1 - 2 * self.core})

    def own_to_core(self, slot):
        return self.copy(self.full.at[slot], 0, 2, {"voc": self.shard + 1 - 2 * self.core})

    def start(self):
        for at in range(1, self.chips):
            self.own_to_chip(at).start()
        self.own_to_core(self.shard).start()

    def relay(self):
        for at in range(1, self.chips):
            self.from_chip(at).wait_recv()
            self.across(at, self.side).start()
            self.to_core(at, self.side, 2, self.core).start()

    def relay_across(self):
        for at in range(1, self.chips):
            self.across(at, 1 - self.side).wait_recv()
            self.to_core(at, 1 - self.side, 3, self.core).start()

    def finish(self):
        self.own_to_core(self.shard + 1 - 2 * self.core).wait_recv()
        for at in range(1, self.chips):
            self.to_core(at, self.side, 2, 1 - self.core).wait_recv()
            self.to_core(at, 1 - self.side, 3, 1 - self.core).wait_recv()
        self.own_to_core(self.shard).wait_send()
        for at in range(1, self.chips):
            self.own_to_chip(at).wait_send()
            self.across(at, self.side).wait_send()
            self.to_core(at, self.side, 2, self.core).wait_send()
            self.to_core(at, 1 - self.side, 3, self.core).wait_send()


def greet_all(shards):
    barrier = pltpu.get_barrier_semaphore()
    me = lax.axis_index("voc")
    for step in range(1, shards):
        pl.semaphore_signal(
            barrier, inc=1, device_id={"voc": lax.rem(me + step, shards)}, device_id_type=MESH_ID
        )
    worker = lax.axis_index("rep")
    pl.semaphore_signal(
        barrier, inc=1, device_id={"rep": worker + 1 - 2 * lax.rem(worker, 2)}, device_id_type=MESH_ID
    )


def await_all(shards):
    pl.semaphore_wait(pltpu.get_barrier_semaphore(), shards)


def open_kernel(
    shards, axis, count, ids_ref, rows_ref, weight_ref, x0_ref, full_ref, own_ref,
    half_in, sums, core_send, core_recv, chip_send, chip_recv, back_send, back_recv, sems,
):
    greet_all(shards)
    shard = lax.axis_index(axis)
    core = lax.rem(shard, 2)
    chip = shard // 2
    partner = shard + 1 - 2 * core
    chips = shards // 2
    half = own_ref.shape[0] // 2
    own_half = pl.ds(pl.multiple_of(core * half, half), half)
    other_half = pl.ds(pl.multiple_of((1 - core) * half, half), half)
    spread = Spread(full_ref, shards, sems)
    full_ref[shard] = weight_ref[...].astype(BF16)
    local = ids_ref[...] - shard * count
    inside = jnp.where((local >= 0) & (local < count), 1.0, 0.0)
    inside = jnp.broadcast_to(inside, (8, local.shape[1])).T[:, 0:1]
    own_ref[...] = jnp.where(inside > 0.5, rows_ref[...], 0.0).astype(BF16)

    def chip_copy(peer_chip, slot, at):
        return pltpu.make_async_remote_copy(
            src_ref=sums.at[slot], dst_ref=sums.at[slot],
            send_sem=chip_send.at[at], recv_sem=chip_recv.at[at],
            device_id={axis: peer_chip * 2 + core}, device_id_type=MESH_ID,
        )

    def back_copy(rows):
        return pltpu.make_async_remote_copy(
            src_ref=x0_ref.at[rows, :], dst_ref=x0_ref.at[rows, :],
            send_sem=back_send, recv_sem=back_recv,
            device_id={axis: partner}, device_id_type=MESH_ID,
        )

    await_all(shards)
    spread.start()
    first = pltpu.make_async_remote_copy(
        src_ref=own_ref.at[other_half, :], dst_ref=half_in,
        send_sem=core_send, recv_sem=core_recv,
        device_id={axis: partner}, device_id_type=MESH_ID,
    )
    first.start()
    first.wait_recv()
    sums[chip] = (own_ref[own_half, :].astype(F32) + half_in[...].astype(F32)).astype(BF16)
    for at in range(1, chips):
        chip_copy(lax.rem(chip + at, chips), chip, at).start()
    first.wait_send()
    spread.relay()
    total = sums[chip].astype(F32)
    for at in range(1, chips):
        source = lax.rem(chip - at + chips, chips)
        chip_copy(source, source, at).wait_recv()
        total = total + sums[source].astype(F32)
    x0_ref[own_half, :] = total.astype(BF16)
    back_copy(own_half).start()
    spread.relay_across()
    back_copy(other_half).wait_recv()
    for at in range(1, chips):
        chip_copy(lax.rem(chip + at, chips), chip, at).wait_send()
    back_copy(own_half).wait_send()
    spread.finish()


def opening(token_ids, rows, count, weight, shards, axis):
    tokens, width = rows.shape
    chips = shards // 2
    shape = jax.ShapeDtypeStruct
    return pl.pallas_call(
        functools.partial(open_kernel, shards, axis, count),
        in_specs=[VM] * 3,
        out_specs=[VM] * 2,
        out_shape=[shape((tokens, width), BF16), shape((shards, *weight.shape), BF16)],
        scratch_shapes=[
            pltpu.VMEM((tokens, width), BF16),
            pltpu.VMEM((tokens // 2, width), BF16),
            pltpu.VMEM((chips, tokens // 2, width), BF16),
        ]
        + [pltpu.SemaphoreType.DMA] * 2
        + [pltpu.SemaphoreType.DMA((max(2, chips),))] * 2
        + [pltpu.SemaphoreType.DMA] * 2
        + [pltpu.SemaphoreType.DMA((8, max(2, chips)))],
        compiler_params=pltpu.CompilerParams(collective_id=4, has_side_effects=True),
        name="opening",
    )(token_ids, rows, weight)


TOKEN_LANES = 256


def vocab_block(rows):
    best = 8
    for size in range(8, 1025, 8):
        if rows % size == 0:
            best = size
    return best


def head_kernel(
    shards, axis,
    n3_ref, target_ref, table_ref,
    gtable_ref, dn3_any, loss_ref,
    dn3_ref, back_in, out_sem, kept, n3_t, tops, running, stats, z_ref, half_in, half_out,
    stat_send, stat_recv, core_send, core_recv, chip_send, chip_recv, back_send, back_recv,
):
    phase, step = pl.program_id(0), pl.program_id(1)
    last = pl.num_programs(1) - 1
    shard = lax.axis_index(axis)
    core = lax.rem(shard, 2)
    chip = shard // 2
    partner = shard + 1 - 2 * core
    chips = shards // 2
    tokens, width = n3_ref.shape
    block_rows = table_ref.shape[0]
    half = width // 2
    own_half = pl.ds(pl.multiple_of(core * half, half), half)
    other_half = pl.ds(pl.multiple_of((1 - core) * half, half), half)

    def stat_copy(peer, slot, at):
        return pltpu.make_async_remote_copy(
            src_ref=stats.at[slot], dst_ref=stats.at[slot],
            send_sem=stat_send.at[at], recv_sem=stat_recv.at[at],
            device_id={axis: peer}, device_id_type=MESH_ID,
        )

    def core_copy():
        return pltpu.make_async_remote_copy(
            src_ref=dn3_ref.at[other_half, :], dst_ref=half_in,
            send_sem=core_send, recv_sem=core_recv,
            device_id={axis: partner}, device_id_type=MESH_ID,
        )

    def chip_copy(peer_chip, slot, at):
        return pltpu.make_async_remote_copy(
            src_ref=half_out.at[slot], dst_ref=half_out.at[slot],
            send_sem=chip_send.at[at], recv_sem=chip_recv.at[at],
            device_id={axis: peer_chip * 2 + core}, device_id_type=MESH_ID,
        )

    def back_copy():
        return pltpu.make_async_remote_copy(
            src_ref=dn3_ref.at[own_half, :], dst_ref=back_in,
            send_sem=back_send, recv_sem=back_recv,
            device_id={axis: partner}, device_id_type=MESH_ID,
        )

    @pl.when((phase == 0) & (step == 0))
    def _():
        barrier = pltpu.get_barrier_semaphore()
        for at in range(1, shards):
            pl.semaphore_signal(
                barrier, inc=1,
                device_id={axis: lax.rem(shard + at, shards)}, device_id_type=MESH_ID,
            )
        n3_t[...] = n3_ref[...].T
        row_at = lax.broadcasted_iota(jnp.int32, running.shape, 0)
        running[...] = jnp.where(row_at == 0, -1e30, 0.0)
        dn3_ref[...] = jnp.zeros_like(dn3_ref)

    def hits(lanes):
        row_at = lax.broadcasted_iota(jnp.int32, (block_rows, TOKEN_LANES), 0)
        return row_at == target_ref[:, lanes] - (shard * (last + 1) + step) * block_rows

    @pl.when(phase == 0)
    def _():
        table = table_ref[...].astype(BF16)
        ahead = nn_dot(table, n3_t[:, :TOKEN_LANES])
        for start in range(0, tokens, TOKEN_LANES):
            lanes = slice(start, start + TOKEN_LANES)
            logits = ahead
            if start + TOKEN_LANES < tokens:
                ahead = nn_dot(table, n3_t[:, start + TOKEN_LANES : start + 2 * TOKEN_LANES])
            top = jnp.max(logits, axis=0, keepdims=True)
            weight = jnp.exp(logits - top)
            kept[step, :, lanes] = weight
            tops[step, :, lanes] = top
            total = jnp.sum(weight, axis=0, keepdims=True)
            picked = jnp.sum(jnp.where(hits(lanes), logits, 0.0), axis=0, keepdims=True)
            old = running[0:1, lanes]
            new = jnp.maximum(old, top)
            running[0:1, lanes] = new
            running[1:2, lanes] = running[1:2, lanes] * jnp.exp(old - new) + total * jnp.exp(top - new)
            running[2:3, lanes] += picked

    @pl.when((phase == 1) & (step == 0))
    def _():
        stats[shard] = running[...]
        pl.semaphore_wait(pltpu.get_barrier_semaphore(), shards - 1)
        sends = [stat_copy(lax.rem(shard + at, shards), shard, at) for at in range(1, shards)]
        for send in sends:
            send.start()
        for at in range(1, shards):
            source = lax.rem(shard - at + shards, shards)
            stat_copy(source, source, at).wait_recv()
        for send in sends:
            send.wait_send()
        top = stats[0, 0:1, :]
        for at in range(1, shards):
            top = jnp.maximum(top, stats[at, 0:1, :])
        total, picked = jnp.zeros_like(top), jnp.zeros_like(top)
        for at in range(shards):
            total = total + stats[at, 1:2, :] * jnp.exp(stats[at, 0:1, :] - top)
            picked = picked + stats[at, 2:3, :]
        z = top + jnp.log(total)
        z_ref[...] = z
        terms = (z - picked) + ZLOSS_WEIGHT * (z * z)
        loss = jnp.sum(terms, axis=1, keepdims=True) * (1.0 / tokens)
        loss_ref[...] = jnp.broadcast_to(loss, loss_ref.shape)

    def grad_logits(lanes):
        z = z_ref[:, lanes]
        factor = jnp.exp(tops[step, :, lanes] - z) * (1.0 + 2.0 * ZLOSS_WEIGHT * z) * (1.0 / tokens)
        return (kept[step, :, lanes] * factor - jnp.where(hits(lanes), 1.0 / tokens, 0.0)).astype(BF16)

    @pl.when(phase == 1)
    def _():
        table_t = table_ref[...].astype(BF16).T
        for start in range(0, tokens, TOKEN_LANES):
            lanes = slice(start, start + TOKEN_LANES)
            dn3_ref[:, lanes] += nn_dot(table_t, grad_logits(lanes))

    @pl.when((phase == 2) & (step == 0))
    def _():
        core_copy().start()

    @pl.when((phase == 2) & (step == jnp.minimum(2, last)))
    def _():
        core_copy().wait()
        half_out[chip] = (dn3_ref[own_half, :] + half_in[...]).astype(BF16)
        for at in range(1, chips):
            chip_copy(lax.rem(chip + at, chips), chip, at).start()

    @pl.when(phase == 2)
    def _():
        total = None
        for start in range(0, tokens, TOKEN_LANES):
            lanes = slice(start, start + TOKEN_LANES)
            part = nn_dot(grad_logits(lanes), n3_ref[lanes, :])
            total = part if total is None else total + part
        gtable_ref[...] = total

    @pl.when((phase == 2) & (step == last))
    def _():
        for at in range(1, chips):
            source = lax.rem(chip - at + chips, chips)
            chip_copy(source, source, at).wait_recv()
        for at in range(1, chips):
            chip_copy(lax.rem(chip + at, chips), chip, at).wait_send()
        whole_sum = half_out[0].astype(F32)
        for at in range(1, chips):
            whole_sum = whole_sum + half_out[at].astype(F32)
        dn3_ref[own_half, :] = whole_sum
        back_copy().start()
        puts = [
            pltpu.make_async_copy(dn3_ref.at[own_half, :], dn3_any.at[own_half, :], out_sem.at[0]),
            pltpu.make_async_copy(back_in, dn3_any.at[other_half, :], out_sem.at[1]),
        ]
        puts[0].start()
        back_copy().wait()
        puts[1].start()
        for put in puts:
            put.wait()


def vocabulary_head(n3, targets, table, shards, axis):
    rows, width = table.shape
    tokens = n3.shape[0]
    size = vocab_block(rows)
    blocks = rows // size
    shape = jax.ShapeDtypeStruct
    return pl.pallas_call(
        functools.partial(head_kernel, shards, axis),
        grid=(3, blocks),
        in_specs=[
            whole((tokens, width)),
            whole((1, tokens)),
            pl.BlockSpec((size, width), lambda p, i: (jnp.where(p == 2, blocks - 1, i), 0)),
        ],
        out_specs=[
            pl.BlockSpec((size, width), lambda p, i: (jnp.where(p == 2, i, 0), 0)),
            pl.BlockSpec(memory_space=pl.ANY),
            whole((8, 128)),
        ],
        out_shape=[shape((rows, width), F32), shape((width, tokens), F32), shape((8, 128), F32)],
        scratch_shapes=[
            pltpu.VMEM((width, tokens), F32),
            pltpu.VMEM((width // 2, tokens), F32),
            pltpu.SemaphoreType.DMA((2,)),
            pltpu.VMEM((blocks, size, tokens), F32),
            pltpu.VMEM((width, tokens), BF16),
            pltpu.VMEM((blocks, 1, tokens), F32),
            pltpu.VMEM((8, tokens), F32),
            pltpu.VMEM((shards, 8, tokens), F32),
            pltpu.VMEM((1, tokens), F32),
            pltpu.VMEM((width // 2, tokens), F32),
            pltpu.VMEM((shards // 2, width // 2, tokens), BF16),
        ]
        + [pltpu.SemaphoreType.DMA((shards,))] * 2
        + [pltpu.SemaphoreType.DMA] * 2
        + [pltpu.SemaphoreType.DMA((max(2, shards // 2),))] * 2
        + [pltpu.SemaphoreType.DMA] * 2,
        compiler_params=pltpu.CompilerParams(
            collective_id=3, has_side_effects=True, vmem_limit_bytes=62 << 20
        ),
        name="vocabulary_head",
    )(n3, targets, table)


def body(
    token_ids,
    target_ids,
    embedding,
    w_qkv,
    w_out,
    w_up,
    w_down,
    norm_gains,
    embed_mom,
    qkv_mom,
    out_mom,
    up_mom,
    down_mom,
    gain_mom,
    embed_err,
    qkv_err,
    out_err,
    up_err,
    down_err,
    embed_factor,
    qkv_factor,
    out_factor,
    up_factor,
    down_factor,
):
    seq_count, length = token_ids.shape
    tok_count = seq_count * length
    vocab_rows = embedding.shape[0]
    shard_pos = lax.axis_index("voc")
    workers = lax.axis_size("rep")
    slices = (w_qkv, w_out, w_up, w_down)
    shards = lax.axis_size("voc")
    local_ids = token_ids.reshape(-1) - shard_pos * vocab_rows
    rows = embedding.at[local_ids].get(mode="clip")
    x0, qkv_all = opening(token_ids, rows, vocab_rows, w_qkv, shards, "voc")
    wqkv = qkv_all.reshape(-1, w_qkv.shape[1])
    half = HD // 2
    inverse = np.float32(10000.0) ** (-np.arange(half, dtype=np.float32) / np.float32(half))
    angles = inverse[:, None] * np.arange(length, dtype=np.float32)[None, :]
    cos_t, sin_t = jnp.asarray(np.cos(angles)), jnp.asarray(np.sin(angles))
    *kept, n3, wo, wu, wd, hid = layer_forward(
        x0, norm_gains, cos_t, sin_t, wqkv, slices[1:], shards, "voc"
    )
    kept = (*kept, n3, hid)
    projections = (wqkv, *(w.reshape(-1, w.shape[2]) for w in (wo, wu, wd)))
    grad_table_head, dn3_t, loss_tile = vocabulary_head(
        n3, target_ids.reshape(1, -1), embedding, lax.axis_size("voc"), "voc"
    )
    grad_in, *grad_mats, grad_gains = layer_backward(
        "voc", [w.shape for w in slices], dn3_t, norm_gains, cos_t, sin_t, projections, x0, kept
    )
    errors = [e[0] for e in (embed_err, qkv_err, out_err, up_err, down_err)]
    starts_t = [
        f[0].T for f in (embed_factor, qkv_factor, out_factor, up_factor, down_factor)
    ]
    full_grad, sketches = scatter_sketch(
        token_ids, grad_table_head, grad_in, grad_mats, errors, starts_t, "voc"
    )
    new_errors, new_moments, changed, rights, gain_change, next_gain_mom, loss, norm = settle(
        loss_tile,
        sketches,
        grad_gains,
        gain_mom,
        [full_grad, *grad_mats],
        errors,
        (embed_mom, qkv_mom, out_mom, up_mom, down_mom),
        slices,
        workers,
        shards,
    )
    return (
        loss,
        norm,
        *changed,
        gain_change,
        *new_moments,
        next_gain_mom,
        *(e[None] for e in new_errors),
        *(r.T[None] for r in rights),
    )


def solution(mesh):
    in_specs = (
        P("rep", None),
        P("rep", None),
        P("voc", None),
        P("voc", None),
        P("voc", None),
        P("voc", None),
        P("voc", None),
        P(),
        P("voc", None),
        P("voc", None),
        P("voc", None),
        P("voc", None),
        P("voc", None),
        P(),
        P("rep", "voc", None),
        P("rep", "voc", None),
        P("rep", "voc", None),
        P("rep", "voc", None),
        P("rep", "voc", None),
        P("voc", None, None),
        P("voc", None, None),
        P("voc", None, None),
        P("voc", None, None),
        P("voc", None, None),
    )
    out_specs = (
        P("rep"),
        P("rep"),
        P("voc", None),
        P("voc", None),
        P("voc", None),
        P("voc", None),
        P("voc", None),
        P(),
        P("voc", None),
        P("voc", None),
        P("voc", None),
        P("voc", None),
        P("voc", None),
        P(),
        P("rep", "voc", None),
        P("rep", "voc", None),
        P("rep", "voc", None),
        P("rep", "voc", None),
        P("rep", "voc", None),
        P("voc", None, None),
        P("voc", None, None),
        P("voc", None, None),
        P("voc", None, None),
        P("voc", None, None),
    )
    return jax.shard_map(body, mesh=mesh, in_specs=in_specs, out_specs=out_specs, check_vma=False)
```

```python
import functools

import jax
import jax.numpy as jnp
import numpy as np
from jax import lax
from jax.experimental import pallas as pl
from jax.experimental.pallas import tpu as pltpu
from jax.sharding import PartitionSpec as P

HD = 64


MOMENTUM = 0.9
LEARN_RATE = 10.0
CLIP_NORM = 1.0
ZLOSS_WEIGHT = 0.01


TB = 1024
RK = 8
F32 = jnp.float32
BF16 = jnp.bfloat16
MESH_ID = pl.DeviceIdType.MESH
VM = pl.BlockSpec(memory_space=pltpu.VMEM)
ANYWHERE = pl.BlockSpec(memory_space=pl.ANY)


def round_up(value, step):
    return (value + step - 1) // step * step


def halves(value):
    high = value.astype(BF16).astype(F32)
    return high, value - high


def dims_of(value, contract_left, contract_right):
    return (((contract_left,), (contract_right,)), ((), ()))


def left_of(matrix, start_t):
    s_high, s_low = halves(start_t)
    both = jnp.concatenate([s_high, s_low], axis=0).astype(BF16)
    high = matrix.astype(BF16)
    low = (matrix - high.astype(F32)).astype(BF16)
    nt = (((1,), (1,)), ((), ()))
    main = lax.dot_general(both, high, nt, preferred_element_type=F32)
    rest = lax.dot_general(s_high.astype(BF16), low, nt, preferred_element_type=F32)
    return main[:RK] + main[RK:] + rest


def left_of_bf16(matrix, start_t):
    s_high, s_low = halves(start_t)
    both = jnp.concatenate([s_high, s_low], axis=0).astype(BF16)
    main = lax.dot_general(both, matrix, (((1,), (1,)), ((), ())), preferred_element_type=F32)
    return main[:RK] + main[RK:]


def right_of(basis_t, matrix):
    b_high, b_low = halves(basis_t)
    both = jnp.concatenate([b_high, b_low], axis=0).astype(BF16)
    high = matrix.astype(BF16)
    low = (matrix - high.astype(F32)).astype(BF16)
    main = jnp.dot(both, high, preferred_element_type=F32)
    rest = jnp.dot(b_high.astype(BF16), low, preferred_element_type=F32)
    return main[:RK] + main[RK:] + rest


def product_of(basis_t, right_t):
    b_high, b_low = halves(basis_t)
    r_high, r_low = halves(right_t)
    zero_b, zero_r = jnp.zeros_like(b_high), jnp.zeros_like(r_high)
    left = jnp.concatenate([b_high, b_low, b_high, zero_b], axis=0).astype(BF16)
    right = jnp.concatenate([r_high, r_high, r_low, zero_r], axis=0).astype(BF16)
    return lax.dot_general(left, right, (((0,), (0,)), ((), ())), preferred_element_type=F32)


def keep_rows(value, first_row, rows):
    at = first_row + lax.broadcasted_iota(jnp.int32, value.shape, 0)
    return jnp.where(at < rows, value, jnp.zeros_like(value))


def fold_squares(value):
    squares = value * value
    rows, columns = value.shape
    by_sublane = jnp.sum(squares.reshape(rows // 8, 8, columns), axis=0)
    total = by_sublane[:, :512]
    for start in range(512, columns, 512):
        total = total + by_sublane[:, start : start + 512]
    return total


def small_places(rows_list):
    places, at = [], 0
    for rows in rows_list:
        places.append(at)
        at += round_up(rows, 128)
    return places, at


def whole(shape):
    return pl.BlockSpec(shape, lambda *_: (0,) * len(shape))


def clip_of(norm_tile):
    return jnp.minimum(1.0, CLIP_NORM / norm_tile[0:1, 0:1])


def orthonormal_t(parts):
    row_at = lax.broadcasted_iota(jnp.int32, (RK, 1), 0)
    for row in range(RK):
        total = None
        for part in parts:
            term = part * part[row : row + 1, :]
            for start in range(0, term.shape[1], 128):
                piece = term[:, start : start + 128]
                total = piece if total is None else total + piece
        dots = jnp.sum(total, axis=1, keepdims=True)
        inverse = lax.rsqrt(dots[row : row + 1, :] + 1e-20)
        scale = jnp.where(row_at == row, inverse, 1.0)
        taken = jnp.where(row_at > row, -dots * inverse * inverse, 0.0)
        parts = [part * scale + taken * part[row : row + 1, :] for part in parts]
    return parts


def greet(axes):
    barrier = pltpu.get_barrier_semaphore()
    greeted = 0
    for axis, count in axes:
        me = lax.axis_index(axis)
        for step in range(1, count):
            pl.semaphore_signal(
                barrier,
                inc=1,
                device_id={axis: lax.rem(me + step, count)},
                device_id_type=MESH_ID,
            )
        greeted += count - 1
    pl.semaphore_wait(barrier, greeted)


def ring_copies(axis, count, src, dst, send_sem, recv_sem, place):
    me = lax.axis_index(axis)
    copies = []
    for step in range(1, count):
        peer = lax.rem(me + step, count)
        from_at, to_at = place(me, peer, step)
        copies.append(
            pltpu.make_async_remote_copy(
                src_ref=src.at[from_at], dst_ref=dst.at[to_at],
                send_sem=send_sem.at[step], recv_sem=recv_sem.at[step],
                device_id={axis: peer}, device_id_type=MESH_ID,
            )
        )
    return copies


def ring_start(axis, count, x, landing, sems):
    for copy in ring_copies(axis, count, x, landing, sems[0], sems[1], lambda me, peer, step: (peer, step)):
        copy.start()


def ring_middle(axis, count, x, landing, y, sems):
    me = lax.axis_index(axis)
    firsts = ring_copies(axis, count, x, landing, sems[0], sems[1], lambda me, peer, step: (peer, step))
    total = x[me].astype(F32)
    for step in range(1, count):
        firsts[step - 1].wait_recv()
        total = total + landing[step].astype(F32)
    y[me] = total.astype(y.dtype)
    for copy in ring_copies(axis, count, y, y, sems[2], sems[3], lambda me, peer, step: (me, me)):
        copy.start()
    for copy in firsts:
        copy.wait_send()


def ring_end(axis, count, y, sems):
    me = lax.axis_index(axis)
    for step in range(1, count):
        source = lax.rem(me - step + count, count)
        pltpu.make_async_remote_copy(
            src_ref=y.at[source], dst_ref=y.at[source],
            send_sem=sems[2].at[step], recv_sem=sems[3].at[step],
            device_id={axis: source}, device_id_type=MESH_ID,
        ).wait_recv()
    for copy in ring_copies(axis, count, y, y, sems[2], sems[3], lambda me, peer, step: (me, me)):
        copy.wait_send()


def settle_kernel(workers, shards, rows, row_list, widths, *refs):
    gq_ref, eq_ref, gs_ref, es_ref, gains_ref, sq_ref = refs[0:6]
    anys = refs[6:16]
    ph, phs, own_ref, mean_ref, norm_ref, gain_ref = refs[16:22]
    (
        x, landing, y, small, sq_all, flat, x16, landing16, y16, table16, table_send, table_recv,
        sem_a, sem_b, sem_c, sem_d, sem_e, sem_f, sem_g, sem_h, sq_send, sq_recv, load_sem,
    ) = refs[22:-10]
    grads, errs = refs[-10:-5], refs[-5:]
    first_sems, second_sems = (sem_a, sem_b, sem_c, sem_d), (sem_e, sem_f, sem_g, sem_h)
    places, _ = small_places(row_list)
    starts = [sum(widths[:k]) for k in range(5)]
    gains_at = gs_ref.shape[1]
    blocks = pl.cdiv(rows, TB)
    tiles = [pl.ds(at * TB, min(TB, rows - at * TB)) for at in range(blocks)]
    pairs = [(anys[k].at[tile, :], kept.at[tile, :]) for k, kept in ((0, grads[0]), (5, errs[0])) for tile in tiles]
    pairs += [(anys[k], grads[k]) for k in range(1, 5)] + [(anys[5 + k], errs[k]) for k in range(1, 5)]
    loads = [pltpu.make_async_copy(src, dst, load_sem.at[at]) for at, (src, dst) in enumerate(pairs)]
    for copy in loads:
        copy.start()
    greet((("rep", workers), ("voc", shards)))
    shard = lax.axis_index("voc")
    own = jnp.sum(sq_ref[...].reshape(8, 4, 128), axis=1)
    own = jnp.sum(jnp.sum(own, axis=0, keepdims=True), axis=1, keepdims=True)
    sq_all[shard] = jnp.broadcast_to(own, (8, 128))
    copies = ring_copies("voc", shards, sq_all, sq_all, sq_send, sq_recv, lambda me, peer, step: (me, me))
    for copy in copies:
        copy.start()
    gains = gains_ref[...]
    total = jnp.sum(jnp.sum(gains * gains, axis=0, keepdims=True), axis=1, keepdims=True)
    small[...] = jnp.zeros_like(small)
    for gap in range(1, shards):
        source = lax.rem(shard - gap + shards, shards)
        pltpu.make_async_remote_copy(
            src_ref=sq_all.at[source], dst_ref=sq_all.at[source],
            send_sem=sq_send.at[gap], recv_sem=sq_recv.at[gap],
            device_id={"voc": source}, device_id_type=MESH_ID,
        ).wait_recv()
    for copy in copies:
        copy.wait_send()
    for peer in range(shards):
        total = total + sq_all[peer][0:1, 0:1]
    norm = jnp.sqrt(total)
    norm_ref[...] = jnp.broadcast_to(norm, (8, 128))
    clip = jnp.minimum(1.0, CLIP_NORM / norm)

    chunk = gq_ref.shape[1] // workers
    part = small.shape[1] // workers
    small[:, :gains_at] = clip * gs_ref[...] + es_ref[...]
    small[:, gains_at : gains_at + gains.shape[1]] = clip * gains
    for j in range(workers):
        lanes = slice(j * chunk, (j + 1) * chunk)
        x[j, :, :chunk] = clip * gq_ref[:, lanes] + eq_ref[:, lanes]
        x[j, :, chunk:] = small[:, j * part : (j + 1) * part]
    ring_start("rep", workers, x, landing, first_sems)
    ring_middle("rep", workers, x, landing, y, first_sems)
    for copy in loads:
        copy.wait()
    for k in range(1, 5):
        grads[k][...] = clip * grads[k][...] + errs[k][...].astype(F32)

    @pl.loop(0, blocks)
    def _(step):
        tile = pl.ds(pl.multiple_of(step * TB, TB), TB)
        matrix = clip * grads[0][tile, :] + errs[0][tile, :].astype(F32)
        grads[0][tile, :] = keep_rows(matrix, step * TB, rows)

    ring_end("rep", workers, y, first_sems)
    parts = orthonormal_t([y[j, :, :chunk] for j in range(workers)])
    for j in range(workers):
        ph[:, j * chunk : (j + 1) * chunk] = parts[j]
        small[:, j * part : (j + 1) * part] = y[j, :, chunk:]
    gain_ref[...] = small[:, gains_at : gains_at + gains.shape[1]] * (1.0 / workers)
    flat[...] = jnp.zeros_like(flat)
    for k in range(4):
        place, size = places[k], row_list[k]
        basis_t = orthonormal_t([small[:, place : place + round_up(size, 128)]])[0]
        phs[:, place : place + round_up(size, 128)] = basis_t
        basis_t = basis_t[:, :size]
        right_t = right_of(basis_t, grads[k + 1][...])
        flat[:, starts[k + 1] : starts[k + 1] + widths[k + 1]] = right_t
    half = x16.shape[2]
    for j in range(workers):
        low, high = starts[1] + j * 2 * half, starts[1] + (j * 2 + 1) * half
        pair = jnp.concatenate([flat[:, low : low + half], flat[:, high : high + half]], axis=0)
        x16[j] = pair.astype(BF16)
    ring_start("rep", workers, x16, landing16, second_sems)

    @pl.loop(0, blocks)
    def _(step):
        tile = pl.ds(pl.multiple_of(step * TB, TB), TB)
        flat[:, : widths[0]] += right_of(ph[:, tile], grads[0][tile, :])

    me = lax.axis_index("rep")
    split = widths[0] // 2
    table16[me] = jnp.concatenate([flat[:, :split], flat[:, split : 2 * split]], axis=0).astype(BF16)
    copies = ring_copies(
        "rep", workers, table16, table16, table_send, table_recv, lambda me, peer, step: (me, me)
    )
    for copy in copies:
        copy.start()
    own_ref[...] = flat[...]
    ring_middle("rep", workers, x16, landing16, y16, second_sems)
    ring_end("rep", workers, y16, second_sems)
    half = x16.shape[2]
    for j in range(workers):
        pair = y16[j].astype(F32) * (1.0 / workers)
        low, high = starts[1] + j * 2 * half, starts[1] + (j * 2 + 1) * half
        mean_ref[:, low : low + half] = pair[:8]
        mean_ref[:, high : high + half] = pair[8:]
    for gap in range(1, workers):
        source = lax.rem(me - gap + workers, workers)
        pltpu.make_async_remote_copy(
            src_ref=table16.at[source], dst_ref=table16.at[source],
            send_sem=table_send.at[gap], recv_sem=table_recv.at[gap],
            device_id={"rep": source}, device_id_type=MESH_ID,
        ).wait_recv()
    total = table16[0].astype(F32)
    for j in range(1, workers):
        total = total + table16[j].astype(F32)
    total = total * (1.0 / workers)
    mean_ref[:, :split] = total[:8]
    mean_ref[:, split : 2 * split] = total[8:]
    for copy in copies:
        copy.wait_send()


def finish_kernel(rows, row_list, widths, *refs):
    grads, errs, moms, weights = refs[0:5], refs[5:10], refs[10:15], refs[15:19]
    ph_ref, phs_ref, own_ref, mean_ref, norm_ref, gain_ref, gain_mom_ref, loss_ref = refs[19:27]
    new_errs, new_moms, changed, rights = refs[27:32], refs[32:37], refs[37:42], refs[42:47]
    gain_change_ref, next_gain_ref, loss_out, norm_out = refs[47:51]
    step = pl.program_id(0)
    places, _ = small_places(row_list)
    starts = [sum(widths[:k]) for k in range(5)]
    clip = clip_of(norm_ref[...])

    def settle_one(k, basis_t):
        lanes = slice(starts[k], starts[k] + widths[k])
        matrix = clip * grads[k][...] + errs[k][...].astype(F32)
        new_errs[k][...] = matrix - product_of(basis_t, own_ref[:, lanes])
        moved = MOMENTUM * moms[k][...].astype(F32) + product_of(basis_t, mean_ref[:, lanes])
        new_moms[k][...] = moved
        change = -LEARN_RATE * moved
        changed[k][...] = weights[k - 1][...] + change if k else change

    @pl.when(step == 0)
    def _():
        moved = MOMENTUM * gain_mom_ref[...].astype(F32) + gain_ref[: gain_mom_ref.shape[0], :]
        next_gain_ref[...] = moved
        gain_change_ref[...] = -LEARN_RATE * moved
        loss_out[0] = jnp.max(loss_ref[...])
        norm_out[0] = jnp.max(norm_ref[...])
        for k in range(5):
            rights[k][...] = mean_ref[:, starts[k] : starts[k] + widths[k]]
        for k in range(1, 5):
            settle_one(k, phs_ref[:, places[k - 1] : places[k - 1] + row_list[k - 1]])

    settle_one(0, ph_ref[...])


def held(shape):
    return pl.BlockSpec(shape, lambda *_: (0,) * len(shape), pipeline_mode=pl.Buffered(1))


def settle(loss_tile, sketches, gains, gain_mom, grads, errs, moms, weights, workers, shards):
    gq, eq, gs, es, sq = sketches
    rows, width = grads[0].shape
    blocks = pl.cdiv(rows, TB)
    row_list = [g.shape[0] for g in grads[1:]]
    widths = [g.shape[1] for g in grads]
    small = round_up(gs.shape[1] + gains.shape[1], workers * 128)
    lanes = (gq.shape[1] + small) // workers
    small_lanes = round_up(sum(widths[1:]), workers * 256)
    right_lanes = widths[0] + small_lanes
    half = small_lanes // workers // 2
    shape = jax.ShapeDtypeStruct
    block = pl.BlockSpec((TB, width), lambda i: (i, 0))
    small_specs = [held(g.shape) for g in grads[1:]]
    made = [
        shape((RK, blocks * TB), F32),
        shape(gs.shape, F32),
        shape((RK, right_lanes), F32),
        shape((RK, right_lanes), F32),
        shape((8, 128), F32),
        shape(gains.shape, F32),
    ]
    operands = (gq, eq, gs, es, gains, sq)
    sums = pl.pallas_call(
        functools.partial(settle_kernel, workers, shards, rows, row_list, widths),
        in_specs=[VM] * 6 + [ANYWHERE] * 10,
        out_specs=[VM] * 6,
        out_shape=made,
        scratch_shapes=[pltpu.VMEM((workers, RK, lanes), F32)] * 3
        + [
            pltpu.VMEM((RK, small), F32),
            pltpu.VMEM((shards, 8, 128), F32),
            pltpu.VMEM((RK, right_lanes), F32),
        ]
        + [pltpu.VMEM((workers, 16, half), BF16)] * 3
        + [pltpu.VMEM((workers, 16, width // 2), BF16)]
        + [pltpu.SemaphoreType.DMA((workers,))] * 2
        + [pltpu.SemaphoreType.DMA((workers,))] * 8
        + [pltpu.SemaphoreType.DMA((shards,))] * 2
        + [pltpu.SemaphoreType.DMA((2 * blocks + 8,))]
        + [pltpu.VMEM((blocks * TB, width), F32)]
        + [pltpu.VMEM(g.shape, F32) for g in grads[1:]]
        + [pltpu.VMEM((blocks * TB, width), BF16)]
        + [pltpu.VMEM(e.shape, BF16) for e in errs[1:]],
        compiler_params=pltpu.CompilerParams(
            collective_id=1, has_side_effects=True, vmem_limit_bytes=60 << 20
        ),
        name="settle_sums",
    )(*operands, *grads, *errs)
    ph, phs, own, mean, norm, gain = sums
    out = pl.pallas_call(
        functools.partial(finish_kernel, rows, row_list, widths),
        grid=(blocks,),
        in_specs=([block] + small_specs) * 3
        + small_specs
        + [pl.BlockSpec((RK, TB), lambda i: (0, i))]
        + [held(m.shape) for m in made[1:]]
        + [held(gain_mom.shape), held(loss_tile.shape)],
        out_specs=([block] + small_specs) * 3
        + [held((RK, w)) for w in widths]
        + [held(gain_mom.shape)] * 2
        + [pl.BlockSpec(memory_space=pltpu.SMEM)] * 2,
        out_shape=[shape(g.shape, F32) for g in grads] * 3
        + [shape((RK, w), F32) for w in widths]
        + [shape(gain_mom.shape, F32)] * 2
        + [shape((1,), F32)] * 2,
        compiler_params=pltpu.CompilerParams(vmem_limit_bytes=60 << 20),
        name="settle_finish",
    )(*grads, *errs, *moms, *weights, ph, phs, own, mean, norm, gain, gain_mom, loss_tile)
    return out[0:5], out[5:10], out[10:15], out[15:20], *out[20:24]


EPS = 1e-06
QB = 256
INV_SQRT2 = 0.7071067811865476
INV_SQRT_2PI = 0.3989422804014327


def nt_dot(a, b):
    return lax.dot_general(a, b, (((1,), (1,)), ((), ())), preferred_element_type=F32)


def nn_dot(a, b):
    return jnp.dot(a, b, preferred_element_type=F32)


def scaled_rms(value, gain):
    return value * lax.rsqrt(jnp.mean(value * value, axis=1, keepdims=True) + EPS) * gain


def rms_back(grad, value, gain):
    inverse = lax.rsqrt(jnp.mean(value * value, axis=1, keepdims=True) + EPS)
    scaled = grad * gain
    along = jnp.mean(scaled * value, axis=1, keepdims=True)
    back = inverse * (scaled - value * (inverse * inverse * along))
    return back, jnp.sum(grad * value * inverse, axis=0, keepdims=True)


def turned(value_t, cos_t, sin_t, half):
    first, second = value_t[:half], value_t[half:]
    return jnp.concatenate([first * cos_t - second * sin_t, first * sin_t + second * cos_t], axis=0)


def turned_back(value_t, cos_t, sin_t, half):
    first, second = value_t[:half], value_t[half:]
    return jnp.concatenate([first * cos_t + second * sin_t, second * cos_t - first * sin_t], axis=0)


def causal_tile(scores_t, fill):
    size = scores_t.shape[1]
    key_at = lax.broadcasted_iota(jnp.int32, (size, size), 0)
    query_at = lax.broadcasted_iota(jnp.int32, (size, size), 1)
    tail = jnp.where(key_at <= query_at, scores_t[-size:], fill)
    if scores_t.shape[0] == size:
        return tail
    return jnp.concatenate([scores_t[:-size], tail], axis=0)


def forward_kernel(
    shards, axis,
    x0_ref, gains_ref, cos_ref, sin_ref, wqkv_ref, wo_own, wu_own, wd_own,
    n1_ref, qkv_ref, lse_ref, mixed_ref, x1_ref, n2_ref, x2_ref, n3_ref, wo_all, wu_all, wd_all, hid_any,
    hid_ref, hid_sem, wo_sems, wu_sems, wd_sems,
):
    tokens, width = x0_ref.shape
    half = HD // 2
    row_blocks = tokens // QB
    greet_all(shards)
    shard = lax.axis_index(axis)
    spreads = []
    for own, full, sems in ((wo_own, wo_all, wo_sems), (wu_own, wu_all, wu_sems), (wd_own, wd_all, wd_sems)):
        full[shard] = own[...].astype(BF16)
        spreads.append(Spread(full, shards, sems))
    await_all(shards)
    for spread in spreads:
        spread.start()

    @pl.loop(0, row_blocks)
    def _(block):
        rows = pl.ds(pl.multiple_of(block * QB, QB), QB)
        n1_ref[rows, :] = scaled_rms(x0_ref[rows, :].astype(F32), gains_ref[0:1, :]).astype(BF16)

    group = 4 * HD

    @pl.loop(0, width // group)
    def _(at):
        n1 = n1_ref[...]
        for part in range(3):
            start = pl.multiple_of(part * width + at * group, group)
            packed_t = nn_dot(n1, wqkv_ref[:, pl.ds(start, group)]).T
            if part < 2:
                cos_t, sin_t = cos_ref[...], sin_ref[...]
                packed_t = jnp.concatenate(
                    [
                        turned(packed_t[head * HD : (head + 1) * HD], cos_t, sin_t, half)
                        for head in range(4)
                    ],
                    axis=0,
                )
            if part == 0:
                packed_t = packed_t * HD ** (-0.5)
            qkv_ref[part, pl.ds(pl.multiple_of(at * group, group), group), :] = packed_t.astype(BF16)

    spreads[0].relay()

    @pl.loop(0, width // (2 * HD))
    def _(pair):
        @pl.when(pair == 1)
        def _():
            spreads[1].relay()
            spreads[0].relay_across()

        @pl.when(pair == 2)
        def _():
            spreads[2].relay()

        @pl.when(pair == 3)
        def _():
            spreads[1].relay_across()

        places = [pl.ds(pl.multiple_of((pair * 2 + side) * HD, HD), HD) for side in range(2)]
        keys = [qkv_ref[1, places[side], :].T for side in range(2)]

        def scores_of(side, block):
            count = (block + 1) * QB
            query_t = qkv_ref[0, places[side], block * QB : count]
            return causal_tile(nn_dot(keys[side][:count], query_t), -1e30)

        work = [(side, block) for side in range(2) for block in range(row_blocks)]
        ahead = scores_of(*work[0])
        mixed_parts, lse_parts = ([], []), ([], [])
        for at, (side, block) in enumerate(work):
            scores = ahead
            if at + 1 < len(work):
                ahead = scores_of(*work[at + 1])
            top = jnp.max(scores, axis=0, keepdims=True)
            weight = jnp.exp(scores - top)
            total = jnp.sum(weight, axis=0, keepdims=True)
            probs = (weight * (1.0 / total)).astype(BF16)
            value_t = qkv_ref[2, places[side], : (block + 1) * QB]
            mixed_parts[side].append(nn_dot(value_t, probs))
            lse_parts[side].append(top + jnp.log(total))
        for side in range(2):
            mixed_ref[places[side], :] = jnp.concatenate(mixed_parts[side], axis=1).astype(BF16)
            lse_ref[pair * 2 + side] = jnp.concatenate(lse_parts[side], axis=1)

    spreads[0].finish()

    @pl.loop(0, row_blocks)
    def _(block):
        rows = pl.ds(pl.multiple_of(block * QB, QB), QB)
        mixed = mixed_ref[:, rows].T
        stream = x0_ref[rows, :].astype(F32) + nn_dot(mixed, wo_all[...].reshape(width, width))
        x1_ref[rows, :] = stream
        x2_ref[rows, :] = stream
        n2_ref[rows, :] = scaled_rms(stream, gains_ref[1:2, :]).astype(BF16)

    spreads[2].relay_across()
    spreads[1].finish()
    spreads[2].finish()
    chunk = hid_ref.shape[2]
    chunks = wu_all.shape[2] // chunk
    parts = chunk // wd_all.shape[1]

    def put(slot, at):
        return pltpu.make_async_copy(
            hid_ref.at[slot],
            hid_any.at[:, pl.ds(pl.multiple_of(at * chunk, chunk), chunk)],
            hid_sem.at[slot],
        )

    @pl.loop(0, chunks)
    def _(at):
        slot = lax.rem(at, 2)
        lanes = pl.ds(pl.multiple_of(at * chunk, chunk), chunk)

        @pl.when(at >= 2)
        def _():
            put(slot, at - 2).wait()

        for block in range(row_blocks):
            rows = slice(block * QB, (block + 1) * QB)
            hidden = nn_dot(n2_ref[rows, :], wu_all[:, :, lanes].reshape(width, chunk))
            hid_ref[slot, rows, :] = hidden
            active = (0.5 * hidden * (1.0 + lax.erf(hidden * INV_SQRT2))).astype(BF16)
            down = wd_all[pl.ds(at * parts, parts)].reshape(chunk, width)
            x2_ref[rows, :] += nn_dot(active, down)
        put(slot, at).start()

    @pl.loop(0, row_blocks)
    def _(block):
        rows = pl.ds(pl.multiple_of(block * QB, QB), QB)
        n3_ref[rows, :] = scaled_rms(x2_ref[rows, :], gains_ref[2:3, :]).astype(BF16)

    for at in range(max(0, chunks - 2), chunks):
        put(at % 2, at).wait()


def layer_forward(x0, gains, cos_t, sin_t, wqkv, slices, shards, axis):
    tokens, width = x0.shape
    hidden = slices[1].shape[1]
    shape = jax.ShapeDtypeStruct
    chunk = min(512, hidden)
    sems = pltpu.SemaphoreType.DMA((8, max(2, shards // 2)))
    return pl.pallas_call(
        functools.partial(forward_kernel, shards, axis),
        in_specs=[VM] * 8,
        out_specs=[VM] * 11 + [ANYWHERE],
        out_shape=[
            shape((tokens, width), BF16),
            shape((3, width, tokens), BF16),
            shape((width // HD, 1, tokens), F32),
            shape((width, tokens), BF16),
            shape((tokens, width), F32),
            shape((tokens, width), BF16),
            shape((tokens, width), F32),
            shape((tokens, width), BF16),
        ]
        + [shape((shards, *w.shape), BF16) for w in slices]
        + [shape((tokens, hidden), F32)],
        scratch_shapes=[
            pltpu.VMEM((2, tokens, chunk), F32),
            pltpu.SemaphoreType.DMA((2,)),
            sems,
            sems,
            sems,
        ],
        compiler_params=pltpu.CompilerParams(
            collective_id=5, has_side_effects=True, vmem_limit_bytes=60 << 20
        ),
        name="layer_forward",
    )(x0, gains, cos_t, sin_t, wqkv, *slices)


def backward_kernel(shard_axis, *refs):
    anys, refs = refs[:13], refs[13:]
    gains_ref, cos_ref, sin_ref, lse_ref = refs[0:4]
    dx0_ref, gqkv_ref, gout_ref, gup_ref, gdown_ref, ggains_ref = refs[4:10]
    kept, refs = refs[10:23], refs[23:]
    dn3_ref, x2_ref, hid_ref, wd_ref, wu_ref, x1_ref, n2_ref, wo_ref, mixed_ref, qkv_ref, x0_ref, n1_ref, wqkv_ref = kept
    grad_ref, part_ref, low_ref, act_ref, dhid_ref, dmixed_ref, dpacked_ref, turn_ref, load_sem = refs
    shard = lax.axis_index(shard_axis) if shard_axis else 0
    tokens, width = x2_ref.shape
    half = HD // 2
    row_blocks = tokens // QB
    loads = [
        pltpu.make_async_copy(src, dst, load_sem.at[at])
        for at, (src, dst) in enumerate(zip(anys, kept))
    ]
    for load in loads:
        load.start()

    def block_rows(block):
        return pl.ds(pl.multiple_of(block * QB, QB), QB)

    loads[0].wait()
    loads[1].wait()
    ggains_ref[...] = jnp.zeros_like(ggains_ref)

    @pl.loop(0, row_blocks)
    def _(block):
        rows = block_rows(block)
        back, gain = rms_back(dn3_ref[:, rows].T, x2_ref[rows, :], gains_ref[2:3, :])
        grad_ref[rows, :] = back
        low_ref[rows, :] = back.astype(BF16)
        part_ref[rows, :] = jnp.zeros_like(back)
        ggains_ref[2:3, :] += gain

    for at in (2, 3, 4):
        loads[at].wait()
    chunk = min(512, wu_ref.shape[1])

    @pl.loop(0, wu_ref.shape[1] // chunk)
    def _(at):
        lanes = pl.ds(pl.multiple_of(at * chunk, chunk), chunk)
        for block in range(row_blocks):
            rows = slice(block * QB, (block + 1) * QB)
            grad_act = nt_dot(low_ref[rows, :], wd_ref[lanes, :])
            hidden = hid_ref[rows, lanes]
            share = 0.5 + 0.5 * lax.erf(hidden * INV_SQRT2)
            slope = share + hidden * (INV_SQRT_2PI * jnp.exp(-0.5 * hidden * hidden))
            act_ref[rows, lanes] = (hidden * share).astype(BF16)
            grad_hid = (slope * grad_act).astype(BF16)
            dhid_ref[rows, lanes] = grad_hid
            part_ref[rows, :] += nt_dot(grad_hid, wu_ref[:, lanes])

    own = gdown_ref.shape[0]
    gdown_ref[...] = nn_dot(act_ref[:, pl.ds(pl.multiple_of(shard * own, own), own)].T, low_ref[...])
    loads[5].wait()
    loads[6].wait()
    own = gup_ref.shape[0]
    turn_ref[...] = n2_ref[...].T
    own_rows = pl.ds(pl.multiple_of(shard * own, own), own)

    @pl.loop(0, wu_ref.shape[1] // chunk)
    def _(at):
        lanes = pl.ds(pl.multiple_of(at * chunk, chunk), chunk)
        gup_ref[:, lanes] = nn_dot(turn_ref[own_rows, :], dhid_ref[:, lanes])

    loads[7].wait()

    @pl.loop(0, row_blocks)
    def _(block):
        rows = block_rows(block)
        back, gain = rms_back(part_ref[rows, :], x1_ref[rows, :], gains_ref[1:2, :])
        back = grad_ref[rows, :] + back
        grad_ref[rows, :] = back
        low = back.astype(BF16)
        low_ref[rows, :] = low
        ggains_ref[1:2, :] += gain
        dmixed_ref[:, rows] = nt_dot(low, wo_ref[...]).astype(BF16).T

    loads[8].wait()
    loads[9].wait()
    own = gout_ref.shape[0]
    own_rows = pl.ds(pl.multiple_of(shard * own, own), own)
    gout_ref[...] = nn_dot(mixed_ref[own_rows, :], low_ref[...])

    @pl.loop(0, width // (2 * HD))
    def _(pair):
        made = ([], [], [])
        places = [pl.ds(pl.multiple_of((pair * 2 + side) * HD, HD), HD) for side in range(2)]
        natural = [
            [ref[rows, :].T for ref in (qkv_ref.at[0], qkv_ref.at[1], qkv_ref.at[2], dmixed_ref)]
            for rows in places
        ]

        def products_of(side, block):
            count = (block + 1) * QB
            at = slice(block * QB, count)
            _, key, value, _ = natural[side]
            scores = nn_dot(key[:count], qkv_ref[0, places[side], at])
            return scores, nn_dot(value[:count], dmixed_ref[places[side], at])

        work = [(side, block) for side in range(2) for block in range(row_blocks)]
        ahead = products_of(*work[0])
        dquery_parts = []
        for place, (side, block) in enumerate(work):
            if block == 0:
                dquery_parts = []
                dkey = [None] * row_blocks
                dvalue = [None] * row_blocks
            scores, dprobs = ahead
            if place + 1 < len(work):
                ahead = products_of(*work[place + 1])
            count = (block + 1) * QB
            at = slice(block * QB, count)
            query, _, _, dmix = natural[side]
            probs = causal_tile(jnp.exp(scores - lse_ref[pair * 2 + side][:, at]), 0.0)
            delta = jnp.sum(probs * dprobs, axis=0, keepdims=True)
            dscores = (probs * (dprobs - delta)).astype(BF16)
            dquery_parts.append(nn_dot(qkv_ref[1, places[side], :count], dscores))
            more_key = nn_dot(dscores, query[at])
            more_value = nn_dot(probs.astype(BF16), dmix[at])
            for piece in range(block + 1):
                cut = slice(piece * QB, (piece + 1) * QB)
                if dkey[piece] is None:
                    dkey[piece], dvalue[piece] = more_key[cut], more_value[cut]
                else:
                    dkey[piece] = dkey[piece] + more_key[cut]
                    dvalue[piece] = dvalue[piece] + more_value[cut]
            if block == row_blocks - 1:
                cos_t, sin_t = cos_ref[...], sin_ref[...]
                dquery_t = jnp.concatenate(dquery_parts, axis=1) * HD ** (-0.5)
                dkey_t = jnp.concatenate(dkey, axis=0).T
                made[0].append(turned_back(dquery_t, cos_t, sin_t, half).T)
                made[1].append(turned_back(dkey_t, cos_t, sin_t, half).T)
                made[2].append(jnp.concatenate(dvalue, axis=0))
        for part in range(3):
            lanes = pl.ds(pl.multiple_of(part * width + pair * 2 * HD, 2 * HD), 2 * HD)
            dpacked_ref[:, lanes] = jnp.concatenate(made[part], axis=1).astype(BF16)

    for at in (10, 11, 12):
        loads[at].wait()
    own = gqkv_ref.shape[0]
    turn_ref[...] = n1_ref[...].T
    own_rows = pl.ds(pl.multiple_of(shard * own, own), own)

    @pl.loop(0, 3)
    def _(at):
        lanes = pl.ds(pl.multiple_of(at * width, width), width)
        gqkv_ref[:, lanes] = nn_dot(turn_ref[own_rows, :], dpacked_ref[:, lanes])

    @pl.loop(0, row_blocks)
    def _(block):
        rows = block_rows(block)
        back, gain = rms_back(
            nt_dot(dpacked_ref[rows, :], wqkv_ref[...]), x0_ref[rows, :].astype(F32), gains_ref[0:1, :]
        )
        dx0_ref[rows, :] = grad_ref[rows, :] + back
        ggains_ref[0:1, :] += gain


def layer_backward(shard_axis, slice_shapes, dn3_t, gains, cos_t, sin_t, projections, x0, kept):
    n1, qkv, lse, mixed_t, x1, n2, x2, _, hid = kept
    wqkv, wo, wu, wd = projections
    tokens, width = x2.shape
    shape = jax.ShapeDtypeStruct
    moved = (dn3_t, x2, hid, wd, wu, x1, n2, wo, mixed_t, qkv, x0, n1, wqkv)
    return pl.pallas_call(
        functools.partial(backward_kernel, shard_axis),
        in_specs=[ANYWHERE] * 13 + [VM] * 3 + [VM],
        out_specs=[VM] * 6,
        out_shape=[shape((tokens, width), F32)]
        + [shape(s, F32) for s in slice_shapes]
        + [shape((8, width), F32)],
        scratch_shapes=[pltpu.VMEM(m.shape, m.dtype) for m in moved]
        + [
            pltpu.VMEM((tokens, width), F32),
            pltpu.VMEM((tokens, width), F32),
            pltpu.VMEM((tokens, width), BF16),
            pltpu.VMEM(hid.shape, BF16),
            pltpu.VMEM(hid.shape, BF16),
            pltpu.VMEM((width, tokens), BF16),
            pltpu.VMEM((tokens, 3 * width), BF16),
            pltpu.VMEM((width, tokens), BF16),
            pltpu.SemaphoreType.DMA((13,)),
        ],
        compiler_params=pltpu.CompilerParams(vmem_limit_bytes=62 << 20),
        name="layer_backward",
    )(*moved, gains, cos_t, sin_t, lse)


def scatter_sketch_kernel(axis, rows, row_list, ids_ref, *refs):
    anys, starts = refs[0:11], refs[11:16]
    full_any, gq_ref, eq_ref, gs_ref, es_ref, sq_ref = refs[16:22]
    dx0_ref, whole_ref, table_err_ref = refs[22:25]
    grads, errs = refs[25:29], refs[29:33]
    load_sem, small_sem, store_sem = refs[33:36]
    places, _ = small_places(row_list)
    blocks = pl.cdiv(rows, TB)
    padded = blocks * TB
    tiles = [pl.ds(at * TB, min(TB, rows - at * TB)) for at in range(blocks)]
    smalls = [
        pltpu.make_async_copy(src, dst, small_sem.at[at])
        for at, (src, dst) in enumerate(zip((*anys[2:6], *anys[7:11], anys[1]), (*grads, *errs, dx0_ref)))
    ]
    for copy in smalls[:8]:
        copy.start()
    loads = [
        pltpu.make_async_copy(anys[0].at[tile, :], whole_ref.at[tile, :], load_sem.at[0, at])
        for at, tile in enumerate(tiles)
    ]
    err_loads = [
        pltpu.make_async_copy(anys[6].at[tile, :], table_err_ref.at[tile, :], load_sem.at[1, at])
        for at, tile in enumerate(tiles)
    ]
    for copy in loads:
        copy.start()
    smalls[8].start()
    for copy in err_loads:
        copy.start()
    if padded > rows:
        rest = pl.ds(rows, padded - rows)
        whole_ref[rest, :] = jnp.zeros((padded - rows, whole_ref.shape[1]), F32)
        table_err_ref[rest, :] = jnp.zeros((padded - rows, whole_ref.shape[1]), BF16)
    gs_ref[...] = jnp.zeros_like(gs_ref)
    es_ref[...] = jnp.zeros_like(es_ref)
    for copy in smalls[:8]:
        copy.wait()
    total = jnp.zeros(sq_ref.shape, F32)
    for k in range(4):
        grad = grads[k][...]
        start_t = starts[k + 1][...]
        at = pl.ds(places[k], row_list[k])
        gs_ref[:, at] = left_of(grad, start_t)
        es_ref[:, at] = left_of_bf16(errs[k][...], start_t)
        total = total + fold_squares(grad)
    sq_ref[...] = total
    smalls[8].wait()
    for copy in loads:
        copy.wait()
    first = lax.axis_index(axis) * rows if axis else 0

    @pl.loop(0, dx0_ref.shape[0] // 8)
    def _(group):
        base = pl.multiple_of(group * 8, 8)
        for side in range(8):
            row = ids_ref[base + side] - first
            row = jnp.where((row >= 0) & (row < rows), row, padded)
            whole_ref[pl.ds(row, 1), :] += dx0_ref[pl.ds(base + side, 1), :]

    stores = [
        pltpu.make_async_copy(whole_ref.at[tile, :], full_any.at[tile, :], store_sem.at[at])
        for at, tile in enumerate(tiles)
    ]
    for copy in stores:
        copy.start()
    for copy in err_loads:
        copy.wait()

    @pl.loop(0, blocks)
    def _(step):
        at = pl.multiple_of(step * TB, TB)
        start_t = starts[0][...]
        grad = whole_ref[pl.ds(at, TB), :]
        gq_ref[:, pl.ds(at, TB)] = left_of(grad, start_t)
        eq_ref[:, pl.ds(at, TB)] = left_of_bf16(table_err_ref[pl.ds(at, TB), :], start_t)
        sq_ref[...] += fold_squares(grad)

    for copy in stores:
        copy.wait()


def scatter_sketch(token_ids, table_grad, dx0, grads, errs, starts_t, axis):
    rows, width = table_grad.shape
    blocks = pl.cdiv(rows, TB)
    row_list = [g.shape[0] for g in grads]
    _, small = small_places(row_list)

    def whole_at(shape):
        return pl.BlockSpec(shape, lambda *_: (0,) * len(shape), pipeline_mode=pl.Buffered(1))

    shape = jax.ShapeDtypeStruct
    made = [(RK, blocks * TB)] * 2 + [(RK, small)] * 2 + [(8, 512)]
    full, *sketches = pl.pallas_call(
        functools.partial(scatter_sketch_kernel, axis, rows, row_list),
        grid_spec=pltpu.PrefetchScalarGridSpec(
            num_scalar_prefetch=1,
            grid=(1,),
            in_specs=[ANYWHERE] * 11 + [whole_at(s.shape) for s in starts_t],
            out_specs=[ANYWHERE] + [whole_at(m) for m in made],
            scratch_shapes=[
                pltpu.VMEM(dx0.shape, F32),
                pltpu.VMEM((blocks * TB + 8, width), F32),
                pltpu.VMEM((blocks * TB, width), BF16),
            ]
            + [pltpu.VMEM(g.shape, F32) for g in grads]
            + [pltpu.VMEM(e.shape, BF16) for e in errs[1:]]
            + [
                pltpu.SemaphoreType.DMA((2, blocks)),
                pltpu.SemaphoreType.DMA((9,)),
                pltpu.SemaphoreType.DMA((blocks,)),
            ],
        ),
        out_shape=[shape((rows, width), F32)] + [shape(m, F32) for m in made],
        compiler_params=pltpu.CompilerParams(vmem_limit_bytes=60 << 20),
        name="scatter_sketch",
    )(token_ids.reshape(-1), table_grad, dx0, *grads, *errs, *starts_t)
    return full, sketches


class Spread:
    def __init__(self, full, shards, sems):
        self.full, self.sems = full, sems
        self.shard, self.worker = lax.axis_index("voc"), lax.axis_index("rep")
        self.core = lax.rem(self.shard, 2)
        self.chip = self.shard // 2
        self.chips = shards // 2
        self.side = lax.rem(self.worker, 2)
        self.rows = full.shape[1] // 2

    def region(self, slot, side):
        return self.full.at[slot, pl.ds(pl.multiple_of(side * self.rows, self.rows), self.rows), :]

    def copy(self, ref, at, pair, peer):
        return pltpu.make_async_remote_copy(
            src_ref=ref, dst_ref=ref, send_sem=self.sems.at[2 * pair, at], recv_sem=self.sems.at[2 * pair + 1, at],
            device_id=peer, device_id_type=MESH_ID,
        )

    def source(self, at):
        return lax.rem(self.chip - at + self.chips, self.chips)

    def own_to_chip(self, at):
        peer = lax.rem(self.chip + at, self.chips) * 2 + self.core
        return self.copy(self.region(self.shard, self.side), at, 0, {"voc": peer})

    def from_chip(self, at):
        slot = self.source(at) * 2 + self.core
        return self.copy(self.region(slot, self.side), at, 0, {"voc": slot})

    def across(self, at, side):
        slot = self.source(at) * 2 + self.core
        return self.copy(self.region(slot, side), at, 1, {"rep": self.worker + 1 - 2 * self.side})

    def to_core(self, at, side, pair, core):
        slot = self.source(at) * 2 + core
        return self.copy(self.region(slot, side), at, pair, {"voc": self.shard + 1 - 2 * self.core})

    def own_to_core(self, slot):
        return self.copy(self.full.at[slot], 0, 2, {"voc": self.shard + 1 - 2 * self.core})

    def start(self):
        for at in range(1, self.chips):
            self.own_to_chip(at).start()
        self.own_to_core(self.shard).start()

    def relay(self):
        for at in range(1, self.chips):
            self.from_chip(at).wait_recv()
            self.across(at, self.side).start()
            self.to_core(at, self.side, 2, self.core).start()

    def relay_across(self):
        for at in range(1, self.chips):
            self.across(at, 1 - self.side).wait_recv()
            self.to_core(at, 1 - self.side, 3, self.core).start()

    def finish(self):
        self.own_to_core(self.shard + 1 - 2 * self.core).wait_recv()
        for at in range(1, self.chips):
            self.to_core(at, self.side, 2, 1 - self.core).wait_recv()
            self.to_core(at, 1 - self.side, 3, 1 - self.core).wait_recv()
        self.own_to_core(self.shard).wait_send()
        for at in range(1, self.chips):
            self.own_to_chip(at).wait_send()
            self.across(at, self.side).wait_send()
            self.to_core(at, self.side, 2, self.core).wait_send()
            self.to_core(at, 1 - self.side, 3, self.core).wait_send()


def greet_all(shards):
    barrier = pltpu.get_barrier_semaphore()
    me = lax.axis_index("voc")
    for step in range(1, shards):
        pl.semaphore_signal(
            barrier, inc=1, device_id={"voc": lax.rem(me + step, shards)}, device_id_type=MESH_ID
        )
    worker = lax.axis_index("rep")
    pl.semaphore_signal(
        barrier, inc=1, device_id={"rep": worker + 1 - 2 * lax.rem(worker, 2)}, device_id_type=MESH_ID
    )


def await_all(shards):
    pl.semaphore_wait(pltpu.get_barrier_semaphore(), shards)


def open_kernel(
    shards, axis, count, ids_ref, lanes_ref, table_any, weight_ref, x0_ref, full_ref,
    own_ref, rows_ref, mask_ref, table_ref, table_sem,
    half_in, sums, core_send, core_recv, chip_send, chip_recv, back_send, back_recv, sems,
):
    tile_rows = count // table_sem.shape[0]
    loads = [
        pltpu.make_async_copy(
            table_any.at[pl.ds(at * tile_rows, tile_rows), :],
            table_ref.at[pl.ds(at * tile_rows, tile_rows), :],
            table_sem.at[at],
        )
        for at in range(table_sem.shape[0])
    ]
    for load in loads:
        load.start()
    greet_all(shards)
    shard = lax.axis_index(axis)
    core = lax.rem(shard, 2)
    chip = shard // 2
    partner = shard + 1 - 2 * core
    chips = shards // 2
    half = x0_ref.shape[0] // 2
    own_half = pl.ds(pl.multiple_of(core * half, half), half)
    other_half = pl.ds(pl.multiple_of((1 - core) * half, half), half)
    spread = Spread(full_ref, shards, sems)
    full_ref[shard] = weight_ref[...].astype(BF16)
    local = lanes_ref[...] - shard * count
    inside = jnp.where((local >= 0) & (local < count), 1.0, 0.0)
    mask_ref[...] = jnp.broadcast_to(inside, (128, local.shape[1])).T

    def take(side):
        @pl.loop(0, half // 8)
        def _(group):
            base = pl.multiple_of(side * half + group * 8, 8)
            for within in range(8):
                row = jnp.clip(ids_ref[base + within] - shard * count, 0, count - 1)
                rows_ref[pl.ds(base + within, 1), :] = table_ref[pl.ds(row, 1), :]

        rows = pl.ds(pl.multiple_of(side * half, half), half)
        own_ref[rows, :] = jnp.where(mask_ref[rows, 0:1] > 0.5, rows_ref[rows, :], 0.0).astype(BF16)

    def chip_copy(peer_chip, slot, at):
        return pltpu.make_async_remote_copy(
            src_ref=sums.at[slot], dst_ref=sums.at[slot],
            send_sem=chip_send.at[at], recv_sem=chip_recv.at[at],
            device_id={axis: peer_chip * 2 + core}, device_id_type=MESH_ID,
        )

    def back_copy(rows):
        return pltpu.make_async_remote_copy(
            src_ref=x0_ref.at[rows, :], dst_ref=x0_ref.at[rows, :],
            send_sem=back_send, recv_sem=back_recv,
            device_id={axis: partner}, device_id_type=MESH_ID,
        )

    await_all(shards)
    spread.start()
    for load in loads:
        load.wait()
    take(1 - core)
    first = pltpu.make_async_remote_copy(
        src_ref=own_ref.at[other_half, :], dst_ref=half_in,
        send_sem=core_send, recv_sem=core_recv,
        device_id={axis: partner}, device_id_type=MESH_ID,
    )
    first.start()
    take(core)
    first.wait_recv()
    sums[chip] = (own_ref[own_half, :].astype(F32) + half_in[...].astype(F32)).astype(BF16)
    for at in range(1, chips):
        chip_copy(lax.rem(chip + at, chips), chip, at).start()
    first.wait_send()
    spread.relay()
    total = sums[chip].astype(F32)
    for at in range(1, chips):
        source = lax.rem(chip - at + chips, chips)
        chip_copy(source, source, at).wait_recv()
        total = total + sums[source].astype(F32)
    x0_ref[own_half, :] = total.astype(BF16)
    back_copy(own_half).start()
    spread.relay_across()
    back_copy(other_half).wait_recv()
    for at in range(1, chips):
        chip_copy(lax.rem(chip + at, chips), chip, at).wait_send()
    back_copy(own_half).wait_send()
    spread.finish()


def opening(token_ids, table, weight, shards, axis):
    tokens, (count, width) = token_ids.shape[1], table.shape
    chips = shards // 2
    shape = jax.ShapeDtypeStruct
    return pl.pallas_call(
        functools.partial(open_kernel, shards, axis, count),
        in_specs=[pl.BlockSpec(memory_space=pltpu.SMEM), VM, ANYWHERE, VM],
        out_specs=[VM] * 2,
        out_shape=[shape((tokens, width), BF16), shape((shards, *weight.shape), BF16)],
        scratch_shapes=[
            pltpu.VMEM((tokens, width), BF16),
            pltpu.VMEM((tokens, width), F32),
            pltpu.VMEM((tokens, 128), F32),
            pltpu.VMEM((count, width), F32),
            pltpu.SemaphoreType.DMA((4,)),
            pltpu.VMEM((tokens // 2, width), BF16),
            pltpu.VMEM((chips, tokens // 2, width), BF16),
        ]
        + [pltpu.SemaphoreType.DMA] * 2
        + [pltpu.SemaphoreType.DMA((max(2, chips),))] * 2
        + [pltpu.SemaphoreType.DMA] * 2
        + [pltpu.SemaphoreType.DMA((8, max(2, chips)))],
        compiler_params=pltpu.CompilerParams(
            collective_id=4, has_side_effects=True, vmem_limit_bytes=60 << 20
        ),
        name="opening",
    )(token_ids.reshape(-1), token_ids, table, weight)


TOKEN_LANES = 256


def vocab_block(rows):
    best = 8
    for size in range(8, 1025, 8):
        if rows % size == 0:
            best = size
    return best


def head_kernel(
    shards, axis,
    n3_ref, target_ref, table_ref,
    gtable_ref, dn3_any, loss_ref,
    dn3_ref, back_in, out_sem, kept, n3_t, tops, running, stats, z_ref, half_in, half_out,
    stat_send, stat_recv, core_send, core_recv, chip_send, chip_recv, back_send, back_recv,
):
    phase, step = pl.program_id(0), pl.program_id(1)
    last = pl.num_programs(1) - 1
    shard = lax.axis_index(axis)
    core = lax.rem(shard, 2)
    chip = shard // 2
    partner = shard + 1 - 2 * core
    chips = shards // 2
    tokens, width = n3_ref.shape
    block_rows = table_ref.shape[0]
    half = width // 2
    own_half = pl.ds(pl.multiple_of(core * half, half), half)
    other_half = pl.ds(pl.multiple_of((1 - core) * half, half), half)

    def stat_copy(peer, slot, at):
        return pltpu.make_async_remote_copy(
            src_ref=stats.at[slot], dst_ref=stats.at[slot],
            send_sem=stat_send.at[at], recv_sem=stat_recv.at[at],
            device_id={axis: peer}, device_id_type=MESH_ID,
        )

    def core_copy():
        return pltpu.make_async_remote_copy(
            src_ref=dn3_ref.at[other_half, :], dst_ref=half_in,
            send_sem=core_send, recv_sem=core_recv,
            device_id={axis: partner}, device_id_type=MESH_ID,
        )

    def chip_copy(peer_chip, slot, at):
        return pltpu.make_async_remote_copy(
            src_ref=half_out.at[slot], dst_ref=half_out.at[slot],
            send_sem=chip_send.at[at], recv_sem=chip_recv.at[at],
            device_id={axis: peer_chip * 2 + core}, device_id_type=MESH_ID,
        )

    def back_copy():
        return pltpu.make_async_remote_copy(
            src_ref=dn3_ref.at[own_half, :], dst_ref=back_in,
            send_sem=back_send, recv_sem=back_recv,
            device_id={axis: partner}, device_id_type=MESH_ID,
        )

    @pl.when((phase == 0) & (step == 0))
    def _():
        barrier = pltpu.get_barrier_semaphore()
        for at in range(1, shards):
            pl.semaphore_signal(
                barrier, inc=1,
                device_id={axis: lax.rem(shard + at, shards)}, device_id_type=MESH_ID,
            )
        n3_t[...] = n3_ref[...].T
        row_at = lax.broadcasted_iota(jnp.int32, running.shape, 0)
        running[...] = jnp.where(row_at == 0, -1e30, 0.0)
        dn3_ref[...] = jnp.zeros_like(dn3_ref)

    def hits(lanes):
        row_at = lax.broadcasted_iota(jnp.int32, (block_rows, TOKEN_LANES), 0)
        return row_at == target_ref[:, lanes] - (shard * (last + 1) + step) * block_rows

    @pl.when(phase == 0)
    def _():
        table = table_ref[...].astype(BF16)
        ahead = nn_dot(table, n3_t[:, :TOKEN_LANES])
        for start in range(0, tokens, TOKEN_LANES):
            lanes = slice(start, start + TOKEN_LANES)
            logits = ahead
            if start + TOKEN_LANES < tokens:
                ahead = nn_dot(table, n3_t[:, start + TOKEN_LANES : start + 2 * TOKEN_LANES])
            top = jnp.max(logits, axis=0, keepdims=True)
            weight = jnp.exp(logits - top)
            kept[step, :, lanes] = weight
            tops[step, :, lanes] = top
            total = jnp.sum(weight, axis=0, keepdims=True)
            picked = jnp.sum(jnp.where(hits(lanes), logits, 0.0), axis=0, keepdims=True)
            old = running[0:1, lanes]
            new = jnp.maximum(old, top)
            running[0:1, lanes] = new
            running[1:2, lanes] = running[1:2, lanes] * jnp.exp(old - new) + total * jnp.exp(top - new)
            running[2:3, lanes] += picked

    @pl.when((phase == 1) & (step == 0))
    def _():
        stats[shard] = running[...]
        pl.semaphore_wait(pltpu.get_barrier_semaphore(), shards - 1)
        sends = [stat_copy(lax.rem(shard + at, shards), shard, at) for at in range(1, shards)]
        for send in sends:
            send.start()
        for at in range(1, shards):
            source = lax.rem(shard - at + shards, shards)
            stat_copy(source, source, at).wait_recv()
        for send in sends:
            send.wait_send()
        top = stats[0, 0:1, :]
        for at in range(1, shards):
            top = jnp.maximum(top, stats[at, 0:1, :])
        total, picked = jnp.zeros_like(top), jnp.zeros_like(top)
        for at in range(shards):
            total = total + stats[at, 1:2, :] * jnp.exp(stats[at, 0:1, :] - top)
            picked = picked + stats[at, 2:3, :]
        z = top + jnp.log(total)
        z_ref[...] = z
        terms = (z - picked) + ZLOSS_WEIGHT * (z * z)
        loss = jnp.sum(terms, axis=1, keepdims=True) * (1.0 / tokens)
        loss_ref[...] = jnp.broadcast_to(loss, loss_ref.shape)

    def grad_logits(lanes):
        z = z_ref[:, lanes]
        factor = jnp.exp(tops[step, :, lanes] - z) * (1.0 + 2.0 * ZLOSS_WEIGHT * z) * (1.0 / tokens)
        return (kept[step, :, lanes] * factor - jnp.where(hits(lanes), 1.0 / tokens, 0.0)).astype(BF16)

    @pl.when(phase == 1)
    def _():
        table_t = table_ref[...].astype(BF16).T
        for start in range(0, tokens, TOKEN_LANES):
            lanes = slice(start, start + TOKEN_LANES)
            dn3_ref[:, lanes] += nn_dot(table_t, grad_logits(lanes))

    @pl.when((phase == 2) & (step == 0))
    def _():
        core_copy().start()

    @pl.when((phase == 2) & (step == jnp.minimum(2, last)))
    def _():
        core_copy().wait()
        half_out[chip] = (dn3_ref[own_half, :] + half_in[...]).astype(BF16)
        for at in range(1, chips):
            chip_copy(lax.rem(chip + at, chips), chip, at).start()

    @pl.when(phase == 2)
    def _():
        total = None
        for start in range(0, tokens, TOKEN_LANES):
            lanes = slice(start, start + TOKEN_LANES)
            part = nn_dot(grad_logits(lanes), n3_ref[lanes, :])
            total = part if total is None else total + part
        gtable_ref[...] = total

    @pl.when((phase == 2) & (step == last))
    def _():
        for at in range(1, chips):
            source = lax.rem(chip - at + chips, chips)
            chip_copy(source, source, at).wait_recv()
        for at in range(1, chips):
            chip_copy(lax.rem(chip + at, chips), chip, at).wait_send()
        whole_sum = half_out[0].astype(F32)
        for at in range(1, chips):
            whole_sum = whole_sum + half_out[at].astype(F32)
        dn3_ref[own_half, :] = whole_sum
        back_copy().start()
        puts = [
            pltpu.make_async_copy(dn3_ref.at[own_half, :], dn3_any.at[own_half, :], out_sem.at[0]),
            pltpu.make_async_copy(back_in, dn3_any.at[other_half, :], out_sem.at[1]),
        ]
        puts[0].start()
        back_copy().wait()
        puts[1].start()
        for put in puts:
            put.wait()


def vocabulary_head(n3, targets, table, shards, axis):
    rows, width = table.shape
    tokens = n3.shape[0]
    size = vocab_block(rows)
    blocks = rows // size
    shape = jax.ShapeDtypeStruct
    return pl.pallas_call(
        functools.partial(head_kernel, shards, axis),
        grid=(3, blocks),
        in_specs=[
            whole((tokens, width)),
            whole((1, tokens)),
            pl.BlockSpec((size, width), lambda p, i: (jnp.where(p == 2, blocks - 1, i), 0)),
        ],
        out_specs=[
            pl.BlockSpec((size, width), lambda p, i: (jnp.where(p == 2, i, 0), 0)),
            pl.BlockSpec(memory_space=pl.ANY),
            whole((8, 128)),
        ],
        out_shape=[shape((rows, width), F32), shape((width, tokens), F32), shape((8, 128), F32)],
        scratch_shapes=[
            pltpu.VMEM((width, tokens), F32),
            pltpu.VMEM((width // 2, tokens), F32),
            pltpu.SemaphoreType.DMA((2,)),
            pltpu.VMEM((blocks, size, tokens), F32),
            pltpu.VMEM((width, tokens), BF16),
            pltpu.VMEM((blocks, 1, tokens), F32),
            pltpu.VMEM((8, tokens), F32),
            pltpu.VMEM((shards, 8, tokens), F32),
            pltpu.VMEM((1, tokens), F32),
            pltpu.VMEM((width // 2, tokens), F32),
            pltpu.VMEM((shards // 2, width // 2, tokens), BF16),
        ]
        + [pltpu.SemaphoreType.DMA((shards,))] * 2
        + [pltpu.SemaphoreType.DMA] * 2
        + [pltpu.SemaphoreType.DMA((max(2, shards // 2),))] * 2
        + [pltpu.SemaphoreType.DMA] * 2,
        compiler_params=pltpu.CompilerParams(
            collective_id=3, has_side_effects=True, vmem_limit_bytes=62 << 20
        ),
        name="vocabulary_head",
    )(n3, targets, table)


def body(
    token_ids,
    target_ids,
    embedding,
    w_qkv,
    w_out,
    w_up,
    w_down,
    norm_gains,
    embed_mom,
    qkv_mom,
    out_mom,
    up_mom,
    down_mom,
    gain_mom,
    embed_err,
    qkv_err,
    out_err,
    up_err,
    down_err,
    embed_factor,
    qkv_factor,
    out_factor,
    up_factor,
    down_factor,
):
    seq_count, length = token_ids.shape
    tok_count = seq_count * length
    workers = lax.axis_size("rep")
    slices = (w_qkv, w_out, w_up, w_down)
    shards = lax.axis_size("voc")
    x0, qkv_all = opening(token_ids, embedding, w_qkv, shards, "voc")
    wqkv = qkv_all.reshape(-1, w_qkv.shape[1])
    half = HD // 2
    inverse = np.float32(10000.0) ** (-np.arange(half, dtype=np.float32) / np.float32(half))
    angles = inverse[:, None] * np.arange(length, dtype=np.float32)[None, :]
    cos_t, sin_t = jnp.asarray(np.cos(angles)), jnp.asarray(np.sin(angles))
    *kept, n3, wo, wu, wd, hid = layer_forward(
        x0, norm_gains, cos_t, sin_t, wqkv, slices[1:], shards, "voc"
    )
    kept = (*kept, n3, hid)
    projections = (wqkv, *(w.reshape(-1, w.shape[2]) for w in (wo, wu, wd)))
    grad_table_head, dn3_t, loss_tile = vocabulary_head(
        n3, target_ids.reshape(1, -1), embedding, lax.axis_size("voc"), "voc"
    )
    grad_in, *grad_mats, grad_gains = layer_backward(
        "voc", [w.shape for w in slices], dn3_t, norm_gains, cos_t, sin_t, projections, x0, kept
    )
    errors = [e[0] for e in (embed_err, qkv_err, out_err, up_err, down_err)]
    starts_t = [
        f[0].T for f in (embed_factor, qkv_factor, out_factor, up_factor, down_factor)
    ]
    full_grad, sketches = scatter_sketch(
        token_ids, grad_table_head, grad_in, grad_mats, errors, starts_t, "voc"
    )
    new_errors, new_moments, changed, rights, gain_change, next_gain_mom, loss, norm = settle(
        loss_tile,
        sketches,
        grad_gains,
        gain_mom,
        [full_grad, *grad_mats],
        errors,
        (embed_mom, qkv_mom, out_mom, up_mom, down_mom),
        slices,
        workers,
        shards,
    )
    return (
        loss,
        norm,
        *changed,
        gain_change,
        *new_moments,
        next_gain_mom,
        *(e[None] for e in new_errors),
        *(r.T[None] for r in rights),
    )


def solution(mesh):
    in_specs = (
        P("rep", None),
        P("rep", None),
        P("voc", None),
        P("voc", None),
        P("voc", None),
        P("voc", None),
        P("voc", None),
        P(),
        P("voc", None),
        P("voc", None),
        P("voc", None),
        P("voc", None),
        P("voc", None),
        P(),
        P("rep", "voc", None),
        P("rep", "voc", None),
        P("rep", "voc", None),
        P("rep", "voc", None),
        P("rep", "voc", None),
        P("voc", None, None),
        P("voc", None, None),
        P("voc", None, None),
        P("voc", None, None),
        P("voc", None, None),
    )
    out_specs = (
        P("rep"),
        P("rep"),
        P("voc", None),
        P("voc", None),
        P("voc", None),
        P("voc", None),
        P("voc", None),
        P(),
        P("voc", None),
        P("voc", None),
        P("voc", None),
        P("voc", None),
        P("voc", None),
        P(),
        P("rep", "voc", None),
        P("rep", "voc", None),
        P("rep", "voc", None),
        P("rep", "voc", None),
        P("rep", "voc", None),
        P("voc", None, None),
        P("voc", None, None),
        P("voc", None, None),
        P("voc", None, None),
        P("voc", None, None),
    )
    return jax.shard_map(body, mesh=mesh, in_specs=in_specs, out_specs=out_specs, check_vma=False)
```

```python
import functools

import jax
import jax.numpy as jnp
import numpy as np
from jax import lax
from jax.experimental import pallas as pl
from jax.experimental.pallas import tpu as pltpu
from jax.sharding import PartitionSpec as P

HD = 64


MOMENTUM = 0.9
LEARN_RATE = 10.0
CLIP_NORM = 1.0
ZLOSS_WEIGHT = 0.01


TB = 1024
RK = 8
F32 = jnp.float32
BF16 = jnp.bfloat16
MESH_ID = pl.DeviceIdType.MESH
VM = pl.BlockSpec(memory_space=pltpu.VMEM)
ANYWHERE = pl.BlockSpec(memory_space=pl.ANY)


def round_up(value, step):
    return (value + step - 1) // step * step


def halves(value):
    high = value.astype(BF16).astype(F32)
    return high, value - high


def dims_of(value, contract_left, contract_right):
    return (((contract_left,), (contract_right,)), ((), ()))


def left_of(matrix, start_t):
    s_high, s_low = halves(start_t)
    both = jnp.concatenate([s_high, s_low], axis=0).astype(BF16)
    high = matrix.astype(BF16)
    low = (matrix - high.astype(F32)).astype(BF16)
    nt = (((1,), (1,)), ((), ()))
    main = lax.dot_general(both, high, nt, preferred_element_type=F32)
    rest = lax.dot_general(s_high.astype(BF16), low, nt, preferred_element_type=F32)
    return main[:RK] + main[RK:] + rest


def left_of_bf16(matrix, start_t):
    s_high, s_low = halves(start_t)
    both = jnp.concatenate([s_high, s_low], axis=0).astype(BF16)
    main = lax.dot_general(both, matrix, (((1,), (1,)), ((), ())), preferred_element_type=F32)
    return main[:RK] + main[RK:]


def right_of(basis_t, matrix):
    b_high, b_low = halves(basis_t)
    both = jnp.concatenate([b_high, b_low], axis=0).astype(BF16)
    high = matrix.astype(BF16)
    low = (matrix - high.astype(F32)).astype(BF16)
    main = jnp.dot(both, high, preferred_element_type=F32)
    rest = jnp.dot(b_high.astype(BF16), low, preferred_element_type=F32)
    return main[:RK] + main[RK:] + rest


def product_of(basis_t, right_t):
    b_high, b_low = halves(basis_t)
    r_high, r_low = halves(right_t)
    zero_b, zero_r = jnp.zeros_like(b_high), jnp.zeros_like(r_high)
    left = jnp.concatenate([b_high, b_low, b_high, zero_b], axis=0).astype(BF16)
    right = jnp.concatenate([r_high, r_high, r_low, zero_r], axis=0).astype(BF16)
    return lax.dot_general(left, right, (((0,), (0,)), ((), ())), preferred_element_type=F32)


def keep_rows(value, first_row, rows):
    at = first_row + lax.broadcasted_iota(jnp.int32, value.shape, 0)
    return jnp.where(at < rows, value, jnp.zeros_like(value))


def fold_squares(value):
    squares = value * value
    rows, columns = value.shape
    by_sublane = jnp.sum(squares.reshape(rows // 8, 8, columns), axis=0)
    total = by_sublane[:, :512]
    for start in range(512, columns, 512):
        total = total + by_sublane[:, start : start + 512]
    return total


def small_places(rows_list):
    places, at = [], 0
    for rows in rows_list:
        places.append(at)
        at += round_up(rows, 128)
    return places, at


def whole(shape):
    return pl.BlockSpec(shape, lambda *_: (0,) * len(shape))


def clip_of(norm_tile):
    return jnp.minimum(1.0, CLIP_NORM / norm_tile[0:1, 0:1])


def orthonormal_t(parts):
    row_at = lax.broadcasted_iota(jnp.int32, (RK, 1), 0)
    for row in range(RK):
        total = None
        for part in parts:
            term = part * part[row : row + 1, :]
            for start in range(0, term.shape[1], 128):
                piece = term[:, start : start + 128]
                total = piece if total is None else total + piece
        dots = jnp.sum(total, axis=1, keepdims=True)
        inverse = lax.rsqrt(dots[row : row + 1, :] + 1e-20)
        scale = jnp.where(row_at == row, inverse, 1.0)
        taken = jnp.where(row_at > row, -dots * inverse * inverse, 0.0)
        parts = [part * scale + taken * part[row : row + 1, :] for part in parts]
    return parts


def greet(axes):
    barrier = pltpu.get_barrier_semaphore()
    greeted = 0
    for axis, count in axes:
        me = lax.axis_index(axis)
        for step in range(1, count):
            pl.semaphore_signal(
                barrier,
                inc=1,
                device_id={axis: lax.rem(me + step, count)},
                device_id_type=MESH_ID,
            )
        greeted += count - 1
    pl.semaphore_wait(barrier, greeted)


def ring_copies(axis, count, src, dst, send_sem, recv_sem, place):
    me = lax.axis_index(axis)
    copies = []
    for step in range(1, count):
        peer = lax.rem(me + step, count)
        from_at, to_at = place(me, peer, step)
        copies.append(
            pltpu.make_async_remote_copy(
                src_ref=src.at[from_at], dst_ref=dst.at[to_at],
                send_sem=send_sem.at[step], recv_sem=recv_sem.at[step],
                device_id={axis: peer}, device_id_type=MESH_ID,
            )
        )
    return copies


def ring_start(axis, count, x, landing, sems):
    for copy in ring_copies(axis, count, x, landing, sems[0], sems[1], lambda me, peer, step: (peer, step)):
        copy.start()


def ring_middle(axis, count, x, landing, y, sems):
    me = lax.axis_index(axis)
    firsts = ring_copies(axis, count, x, landing, sems[0], sems[1], lambda me, peer, step: (peer, step))
    total = x[me].astype(F32)
    for step in range(1, count):
        firsts[step - 1].wait_recv()
        total = total + landing[step].astype(F32)
    y[me] = total.astype(y.dtype)
    for copy in ring_copies(axis, count, y, y, sems[2], sems[3], lambda me, peer, step: (me, me)):
        copy.start()
    for copy in firsts:
        copy.wait_send()


def ring_end(axis, count, y, sems):
    me = lax.axis_index(axis)
    for step in range(1, count):
        source = lax.rem(me - step + count, count)
        pltpu.make_async_remote_copy(
            src_ref=y.at[source], dst_ref=y.at[source],
            send_sem=sems[2].at[step], recv_sem=sems[3].at[step],
            device_id={axis: source}, device_id_type=MESH_ID,
        ).wait_recv()
    for copy in ring_copies(axis, count, y, y, sems[2], sems[3], lambda me, peer, step: (me, me)):
        copy.wait_send()


def settle_kernel(workers, shards, rows, row_list, widths, *refs):
    gq_ref, eq_ref, gs_ref, es_ref, gains_ref, sq_ref = refs[0:6]
    anys = refs[6:16]
    ph, phs, own_ref, mean_ref, norm_ref, gain_ref = refs[16:22]
    (
        x, landing, y, small, sq_all, flat, x16, landing16, y16, table16, table_send, table_recv,
        sem_a, sem_b, sem_c, sem_d, sem_e, sem_f, sem_g, sem_h, sq_send, sq_recv, load_sem,
    ) = refs[22:-10]
    grads, errs = refs[-10:-5], refs[-5:]
    first_sems, second_sems = (sem_a, sem_b, sem_c, sem_d), (sem_e, sem_f, sem_g, sem_h)
    places, _ = small_places(row_list)
    starts = [sum(widths[:k]) for k in range(5)]
    gains_at = gs_ref.shape[1]
    blocks = pl.cdiv(rows, TB)
    tiles = [pl.ds(at * TB, min(TB, rows - at * TB)) for at in range(blocks)]
    pairs = [(anys[k].at[tile, :], kept.at[tile, :]) for k, kept in ((0, grads[0]), (5, errs[0])) for tile in tiles]
    pairs += [(anys[k], grads[k]) for k in range(1, 5)] + [(anys[5 + k], errs[k]) for k in range(1, 5)]
    loads = [pltpu.make_async_copy(src, dst, load_sem.at[at]) for at, (src, dst) in enumerate(pairs)]
    for copy in loads:
        copy.start()
    greet((("rep", workers), ("voc", shards)))
    shard = lax.axis_index("voc")
    own = jnp.sum(sq_ref[...].reshape(8, 4, 128), axis=1)
    own = jnp.sum(jnp.sum(own, axis=0, keepdims=True), axis=1, keepdims=True)
    sq_all[shard] = jnp.broadcast_to(own, (8, 128))
    copies = ring_copies("voc", shards, sq_all, sq_all, sq_send, sq_recv, lambda me, peer, step: (me, me))
    for copy in copies:
        copy.start()
    gains = gains_ref[...]
    total = jnp.sum(jnp.sum(gains * gains, axis=0, keepdims=True), axis=1, keepdims=True)
    small[...] = jnp.zeros_like(small)
    for gap in range(1, shards):
        source = lax.rem(shard - gap + shards, shards)
        pltpu.make_async_remote_copy(
            src_ref=sq_all.at[source], dst_ref=sq_all.at[source],
            send_sem=sq_send.at[gap], recv_sem=sq_recv.at[gap],
            device_id={"voc": source}, device_id_type=MESH_ID,
        ).wait_recv()
    for copy in copies:
        copy.wait_send()
    for peer in range(shards):
        total = total + sq_all[peer][0:1, 0:1]
    norm = jnp.sqrt(total)
    norm_ref[...] = jnp.broadcast_to(norm, (8, 128))
    clip = jnp.minimum(1.0, CLIP_NORM / norm)

    chunk = gq_ref.shape[1] // workers
    part = small.shape[1] // workers
    small[:, :gains_at] = clip * gs_ref[...] + es_ref[...]
    small[:, gains_at : gains_at + gains.shape[1]] = clip * gains
    for j in range(workers):
        lanes = slice(j * chunk, (j + 1) * chunk)
        x[j, :, :chunk] = clip * gq_ref[:, lanes] + eq_ref[:, lanes]
        x[j, :, chunk:] = small[:, j * part : (j + 1) * part]
    ring_start("rep", workers, x, landing, first_sems)
    ring_middle("rep", workers, x, landing, y, first_sems)
    for copy in loads:
        copy.wait()
    for k in range(1, 5):
        grads[k][...] = clip * grads[k][...] + errs[k][...].astype(F32)

    @pl.loop(0, blocks)
    def _(step):
        tile = pl.ds(pl.multiple_of(step * TB, TB), TB)
        matrix = clip * grads[0][tile, :] + errs[0][tile, :].astype(F32)
        grads[0][tile, :] = keep_rows(matrix, step * TB, rows)

    ring_end("rep", workers, y, first_sems)
    parts = orthonormal_t([y[j, :, :chunk] for j in range(workers)])
    for j in range(workers):
        ph[:, j * chunk : (j + 1) * chunk] = parts[j]
        small[:, j * part : (j + 1) * part] = y[j, :, chunk:]
    gain_ref[...] = small[:, gains_at : gains_at + gains.shape[1]] * (1.0 / workers)
    flat[...] = jnp.zeros_like(flat)
    for k in range(4):
        place, size = places[k], row_list[k]
        basis_t = orthonormal_t([small[:, place : place + round_up(size, 128)]])[0]
        phs[:, place : place + round_up(size, 128)] = basis_t
        basis_t = basis_t[:, :size]
        right_t = right_of(basis_t, grads[k + 1][...])
        flat[:, starts[k + 1] : starts[k + 1] + widths[k + 1]] = right_t
    half = x16.shape[2]
    for j in range(workers):
        low, high = starts[1] + j * 2 * half, starts[1] + (j * 2 + 1) * half
        pair = jnp.concatenate([flat[:, low : low + half], flat[:, high : high + half]], axis=0)
        x16[j] = pair.astype(BF16)
    ring_start("rep", workers, x16, landing16, second_sems)

    @pl.loop(0, blocks)
    def _(step):
        tile = pl.ds(pl.multiple_of(step * TB, TB), TB)
        flat[:, : widths[0]] += right_of(ph[:, tile], grads[0][tile, :])

    me = lax.axis_index("rep")
    split = widths[0] // 2
    table16[me] = jnp.concatenate([flat[:, :split], flat[:, split : 2 * split]], axis=0).astype(BF16)
    copies = ring_copies(
        "rep", workers, table16, table16, table_send, table_recv, lambda me, peer, step: (me, me)
    )
    for copy in copies:
        copy.start()
    own_ref[...] = flat[...]
    ring_middle("rep", workers, x16, landing16, y16, second_sems)
    ring_end("rep", workers, y16, second_sems)
    half = x16.shape[2]
    for j in range(workers):
        pair = y16[j].astype(F32) * (1.0 / workers)
        low, high = starts[1] + j * 2 * half, starts[1] + (j * 2 + 1) * half
        mean_ref[:, low : low + half] = pair[:8]
        mean_ref[:, high : high + half] = pair[8:]
    for gap in range(1, workers):
        source = lax.rem(me - gap + workers, workers)
        pltpu.make_async_remote_copy(
            src_ref=table16.at[source], dst_ref=table16.at[source],
            send_sem=table_send.at[gap], recv_sem=table_recv.at[gap],
            device_id={"rep": source}, device_id_type=MESH_ID,
        ).wait_recv()
    total = table16[0].astype(F32)
    for j in range(1, workers):
        total = total + table16[j].astype(F32)
    total = total * (1.0 / workers)
    mean_ref[:, :split] = total[:8]
    mean_ref[:, split : 2 * split] = total[8:]
    for copy in copies:
        copy.wait_send()


def finish_kernel(rows, row_list, widths, *refs):
    grads, errs, moms, weights = refs[0:5], refs[5:10], refs[10:15], refs[15:19]
    ph_ref, phs_ref, own_ref, mean_ref, norm_ref, gain_ref, gain_mom_ref, loss_ref = refs[19:27]
    new_errs, new_moms, changed, rights = refs[27:32], refs[32:37], refs[37:42], refs[42:47]
    gain_change_ref, next_gain_ref, loss_out, norm_out = refs[47:51]
    step = pl.program_id(0)
    places, _ = small_places(row_list)
    starts = [sum(widths[:k]) for k in range(5)]
    clip = clip_of(norm_ref[...])

    def settle_one(k, basis_t):
        lanes = slice(starts[k], starts[k] + widths[k])
        matrix = clip * grads[k][...] + errs[k][...].astype(F32)
        new_errs[k][...] = matrix - product_of(basis_t, own_ref[:, lanes])
        moved = MOMENTUM * moms[k][...].astype(F32) + product_of(basis_t, mean_ref[:, lanes])
        new_moms[k][...] = moved
        change = -LEARN_RATE * moved
        changed[k][...] = weights[k - 1][...] + change if k else change

    @pl.when(step == 0)
    def _():
        moved = MOMENTUM * gain_mom_ref[...].astype(F32) + gain_ref[: gain_mom_ref.shape[0], :]
        next_gain_ref[...] = moved
        gain_change_ref[...] = -LEARN_RATE * moved
        loss_out[0] = jnp.max(loss_ref[...])
        norm_out[0] = jnp.max(norm_ref[...])
        for k in range(5):
            rights[k][...] = mean_ref[:, starts[k] : starts[k] + widths[k]]
        for k in range(1, 5):
            settle_one(k, phs_ref[:, places[k - 1] : places[k - 1] + row_list[k - 1]])

    settle_one(0, ph_ref[...])


def held(shape):
    return pl.BlockSpec(shape, lambda *_: (0,) * len(shape), pipeline_mode=pl.Buffered(1))


def settle(loss_tile, sketches, gains, gain_mom, grads, errs, moms, weights, workers, shards):
    gq, eq, gs, es, sq = sketches
    rows, width = grads[0].shape
    blocks = pl.cdiv(rows, TB)
    row_list = [g.shape[0] for g in grads[1:]]
    widths = [g.shape[1] for g in grads]
    small = round_up(gs.shape[1] + gains.shape[1], workers * 128)
    lanes = (gq.shape[1] + small) // workers
    small_lanes = round_up(sum(widths[1:]), workers * 256)
    right_lanes = widths[0] + small_lanes
    half = small_lanes // workers // 2
    shape = jax.ShapeDtypeStruct
    block = pl.BlockSpec((TB, width), lambda i: (i, 0))
    small_specs = [held(g.shape) for g in grads[1:]]
    made = [
        shape((RK, blocks * TB), F32),
        shape(gs.shape, F32),
        shape((RK, right_lanes), F32),
        shape((RK, right_lanes), F32),
        shape((8, 128), F32),
        shape(gains.shape, F32),
    ]
    operands = (gq, eq, gs, es, gains, sq)
    sums = pl.pallas_call(
        functools.partial(settle_kernel, workers, shards, rows, row_list, widths),
        in_specs=[VM] * 6 + [ANYWHERE] * 10,
        out_specs=[VM] * 6,
        out_shape=made,
        scratch_shapes=[pltpu.VMEM((workers, RK, lanes), F32)] * 3
        + [
            pltpu.VMEM((RK, small), F32),
            pltpu.VMEM((shards, 8, 128), F32),
            pltpu.VMEM((RK, right_lanes), F32),
        ]
        + [pltpu.VMEM((workers, 16, half), BF16)] * 3
        + [pltpu.VMEM((workers, 16, width // 2), BF16)]
        + [pltpu.SemaphoreType.DMA((workers,))] * 2
        + [pltpu.SemaphoreType.DMA((workers,))] * 8
        + [pltpu.SemaphoreType.DMA((shards,))] * 2
        + [pltpu.SemaphoreType.DMA((2 * blocks + 8,))]
        + [pltpu.VMEM((blocks * TB, width), F32)]
        + [pltpu.VMEM(g.shape, F32) for g in grads[1:]]
        + [pltpu.VMEM((blocks * TB, width), BF16)]
        + [pltpu.VMEM(e.shape, BF16) for e in errs[1:]],
        compiler_params=pltpu.CompilerParams(
            collective_id=1, has_side_effects=True, vmem_limit_bytes=60 << 20
        ),
        name="settle_sums",
    )(*operands, *grads, *errs)
    ph, phs, own, mean, norm, gain = sums
    out = pl.pallas_call(
        functools.partial(finish_kernel, rows, row_list, widths),
        grid=(blocks,),
        in_specs=([block] + small_specs) * 3
        + small_specs
        + [pl.BlockSpec((RK, TB), lambda i: (0, i))]
        + [held(m.shape) for m in made[1:]]
        + [held(gain_mom.shape), held(loss_tile.shape)],
        out_specs=([block] + small_specs) * 3
        + [held((RK, w)) for w in widths]
        + [held(gain_mom.shape)] * 2
        + [pl.BlockSpec(memory_space=pltpu.SMEM)] * 2,
        out_shape=[shape(g.shape, F32) for g in grads] * 3
        + [shape((RK, w), F32) for w in widths]
        + [shape(gain_mom.shape, F32)] * 2
        + [shape((1,), F32)] * 2,
        compiler_params=pltpu.CompilerParams(vmem_limit_bytes=60 << 20),
        name="settle_finish",
    )(*grads, *errs, *moms, *weights, ph, phs, own, mean, norm, gain, gain_mom, loss_tile)
    return out[0:5], out[5:10], out[10:15], out[15:20], *out[20:24]


EPS = 1e-06
QB = 256
INV_SQRT2 = 0.7071067811865476
INV_SQRT_2PI = 0.3989422804014327


def nt_dot(a, b):
    return lax.dot_general(a, b, (((1,), (1,)), ((), ())), preferred_element_type=F32)


def nn_dot(a, b):
    return jnp.dot(a, b, preferred_element_type=F32)


def scaled_rms(value, gain):
    return value * lax.rsqrt(jnp.mean(value * value, axis=1, keepdims=True) + EPS) * gain


def rms_back(grad, value, gain):
    inverse = lax.rsqrt(jnp.mean(value * value, axis=1, keepdims=True) + EPS)
    scaled = grad * gain
    along = jnp.mean(scaled * value, axis=1, keepdims=True)
    back = inverse * (scaled - value * (inverse * inverse * along))
    return back, jnp.sum(grad * value * inverse, axis=0, keepdims=True)


def turned(value_t, cos_t, sin_t, half):
    first, second = value_t[:half], value_t[half:]
    return jnp.concatenate([first * cos_t - second * sin_t, first * sin_t + second * cos_t], axis=0)


def turned_back(value_t, cos_t, sin_t, half):
    first, second = value_t[:half], value_t[half:]
    return jnp.concatenate([first * cos_t + second * sin_t, second * cos_t - first * sin_t], axis=0)


def causal_tile(scores_t, fill):
    size = scores_t.shape[1]
    key_at = lax.broadcasted_iota(jnp.int32, (size, size), 0)
    query_at = lax.broadcasted_iota(jnp.int32, (size, size), 1)
    tail = jnp.where(key_at <= query_at, scores_t[-size:], fill)
    if scores_t.shape[0] == size:
        return tail
    return jnp.concatenate([scores_t[:-size], tail], axis=0)


def forward_kernel(
    shards, axis,
    x0_ref, gains_ref, cos_ref, sin_ref, wqkv_ref, wo_own, wu_own, wd_own,
    *refs,
):
    outs, hid_any = refs[:11], refs[11]
    made = refs[12:23]
    n1_ref, qkv_ref, lse_ref, mixed_ref, x1_ref, n2_ref, x2_ref, n3_ref, wo_all, wu_all, wd_all = made
    hid_ref, hid_sem, wo_sems, wu_sems, wd_sems, out_sem = refs[23:]
    leaving = [
        pltpu.make_async_copy(src, dst, out_sem.at[at]) for at, (src, dst) in enumerate(zip(made, outs))
    ]
    tokens, width = x0_ref.shape
    half = HD // 2
    row_blocks = tokens // QB
    greet_all(shards)
    shard = lax.axis_index(axis)
    spreads = []
    for own, full, sems in ((wo_own, wo_all, wo_sems), (wu_own, wu_all, wu_sems), (wd_own, wd_all, wd_sems)):
        full[shard] = own[...].astype(BF16)
        spreads.append(Spread(full, shards, sems))
    await_all(shards)
    for spread in spreads:
        spread.start()

    @pl.loop(0, row_blocks)
    def _(block):
        rows = pl.ds(pl.multiple_of(block * QB, QB), QB)
        n1_ref[rows, :] = scaled_rms(x0_ref[rows, :].astype(F32), gains_ref[0:1, :]).astype(BF16)

    group = 4 * HD

    @pl.loop(0, width // group)
    def _(at):
        n1 = n1_ref[...]
        for part in range(3):
            start = pl.multiple_of(part * width + at * group, group)
            packed_t = nn_dot(n1, wqkv_ref[:, pl.ds(start, group)]).T
            if part < 2:
                cos_t, sin_t = cos_ref[...], sin_ref[...]
                packed_t = jnp.concatenate(
                    [
                        turned(packed_t[head * HD : (head + 1) * HD], cos_t, sin_t, half)
                        for head in range(4)
                    ],
                    axis=0,
                )
            if part == 0:
                packed_t = packed_t * HD ** (-0.5)
            qkv_ref[part, pl.ds(pl.multiple_of(at * group, group), group), :] = packed_t.astype(BF16)

    spreads[0].relay()

    @pl.loop(0, width // (2 * HD))
    def _(pair):
        @pl.when(pair == 1)
        def _():
            spreads[1].relay()
            spreads[0].relay_across()

        @pl.when(pair == 2)
        def _():
            spreads[2].relay()

        @pl.when(pair == 3)
        def _():
            spreads[1].relay_across()

        places = [pl.ds(pl.multiple_of((pair * 2 + side) * HD, HD), HD) for side in range(2)]
        keys = [qkv_ref[1, places[side], :].T for side in range(2)]

        def scores_of(side, block):
            count = (block + 1) * QB
            query_t = qkv_ref[0, places[side], block * QB : count]
            return causal_tile(nn_dot(keys[side][:count], query_t), -1e30)

        work = [(side, block) for side in range(2) for block in range(row_blocks)]
        ahead = scores_of(*work[0])
        mixed_parts, lse_parts = ([], []), ([], [])
        for at, (side, block) in enumerate(work):
            scores = ahead
            if at + 1 < len(work):
                ahead = scores_of(*work[at + 1])
            top = jnp.max(scores, axis=0, keepdims=True)
            weight = jnp.exp(scores - top)
            total = jnp.sum(weight, axis=0, keepdims=True)
            probs = (weight * (1.0 / total)).astype(BF16)
            value_t = qkv_ref[2, places[side], : (block + 1) * QB]
            mixed_parts[side].append(nn_dot(value_t, probs))
            lse_parts[side].append(top + jnp.log(total))
        for side in range(2):
            mixed_ref[places[side], :] = jnp.concatenate(mixed_parts[side], axis=1).astype(BF16)
            lse_ref[pair * 2 + side] = jnp.concatenate(lse_parts[side], axis=1)

    spreads[0].finish()

    @pl.loop(0, row_blocks)
    def _(block):
        rows = pl.ds(pl.multiple_of(block * QB, QB), QB)
        mixed = mixed_ref[:, rows].T
        stream = x0_ref[rows, :].astype(F32) + nn_dot(mixed, wo_all[...].reshape(width, width))
        x1_ref[rows, :] = stream
        x2_ref[rows, :] = stream
        n2_ref[rows, :] = scaled_rms(stream, gains_ref[1:2, :]).astype(BF16)

    spreads[2].relay_across()
    for at in (1, 3, 0, 2, 4, 5, 8):
        leaving[at].start()
    spreads[1].finish()
    spreads[2].finish()
    leaving[9].start()
    leaving[10].start()
    chunk = hid_ref.shape[2]
    chunks = wu_all.shape[2] // chunk
    parts = chunk // wd_all.shape[1]

    def put(slot, at):
        return pltpu.make_async_copy(
            hid_ref.at[slot],
            hid_any.at[:, pl.ds(pl.multiple_of(at * chunk, chunk), chunk)],
            hid_sem.at[slot],
        )

    @pl.loop(0, chunks)
    def _(at):
        slot = lax.rem(at, 2)
        lanes = pl.ds(pl.multiple_of(at * chunk, chunk), chunk)

        @pl.when(at >= 2)
        def _():
            put(slot, at - 2).wait()

        for block in range(row_blocks):
            rows = slice(block * QB, (block + 1) * QB)
            hidden = nn_dot(n2_ref[rows, :], wu_all[:, :, lanes].reshape(width, chunk))
            hid_ref[slot, rows, :] = hidden
            active = (0.5 * hidden * (1.0 + lax.erf(hidden * INV_SQRT2))).astype(BF16)
            down = wd_all[pl.ds(at * parts, parts)].reshape(chunk, width)
            x2_ref[rows, :] += nn_dot(active, down)
        put(slot, at).start()

    @pl.loop(0, row_blocks)
    def _(block):
        rows = pl.ds(pl.multiple_of(block * QB, QB), QB)
        n3_ref[rows, :] = scaled_rms(x2_ref[rows, :], gains_ref[2:3, :]).astype(BF16)

    leaving[6].start()
    leaving[7].start()
    for at in range(max(0, chunks - 2), chunks):
        put(at % 2, at).wait()
    for copy in leaving:
        copy.wait()


def layer_forward(x0, gains, cos_t, sin_t, wqkv, slices, shards, axis):
    tokens, width = x0.shape
    hidden = slices[1].shape[1]
    shape = jax.ShapeDtypeStruct
    chunk = min(512, hidden)
    sems = pltpu.SemaphoreType.DMA((8, max(2, shards // 2)))
    made = [
        shape((tokens, width), BF16),
        shape((3, width, tokens), BF16),
        shape((width // HD, 1, tokens), F32),
        shape((width, tokens), BF16),
        shape((tokens, width), F32),
        shape((tokens, width), BF16),
        shape((tokens, width), F32),
        shape((tokens, width), BF16),
    ] + [shape((shards, *w.shape), BF16) for w in slices]
    return pl.pallas_call(
        functools.partial(forward_kernel, shards, axis),
        in_specs=[VM] * 8,
        out_specs=[ANYWHERE] * 12,
        out_shape=made + [shape((tokens, hidden), F32)],
        scratch_shapes=[pltpu.VMEM(m.shape, m.dtype) for m in made]
        + [
            pltpu.VMEM((2, tokens, chunk), F32),
            pltpu.SemaphoreType.DMA((2,)),
            sems,
            sems,
            sems,
            pltpu.SemaphoreType.DMA((len(made),)),
        ],
        compiler_params=pltpu.CompilerParams(
            collective_id=5, has_side_effects=True, vmem_limit_bytes=60 << 20
        ),
        name="layer_forward",
    )(x0, gains, cos_t, sin_t, wqkv, *slices)


def backward_kernel(shard_axis, *refs):
    anys, refs = refs[:13], refs[13:]
    gains_ref, cos_ref, sin_ref, lse_ref = refs[0:4]
    dx0_ref, gqkv_ref, gout_ref, gup_ref, gdown_ref, ggains_ref = refs[4:10]
    kept, refs = refs[10:23], refs[23:]
    dn3_ref, x2_ref, hid_ref, wd_ref, wu_ref, x1_ref, n2_ref, wo_ref, mixed_ref, qkv_ref, x0_ref, n1_ref, wqkv_ref = kept
    grad_ref, part_ref, low_ref, act_ref, dhid_ref, dmixed_ref, dpacked_ref, turn_ref, load_sem = refs
    shard = lax.axis_index(shard_axis) if shard_axis else 0
    tokens, width = x2_ref.shape
    half = HD // 2
    row_blocks = tokens // QB
    loads = [
        pltpu.make_async_copy(src, dst, load_sem.at[at])
        for at, (src, dst) in enumerate(zip(anys, kept))
    ]
    for load in loads[:5]:
        load.start()

    def block_rows(block):
        return pl.ds(pl.multiple_of(block * QB, QB), QB)

    loads[0].wait()
    loads[1].wait()
    for load in loads[5:]:
        load.start()
    ggains_ref[...] = jnp.zeros_like(ggains_ref)

    @pl.loop(0, row_blocks)
    def _(block):
        rows = block_rows(block)
        back, gain = rms_back(dn3_ref[:, rows].T, x2_ref[rows, :], gains_ref[2:3, :])
        grad_ref[rows, :] = back
        low_ref[rows, :] = back.astype(BF16)
        part_ref[rows, :] = jnp.zeros_like(back)
        ggains_ref[2:3, :] += gain

    for at in (2, 3, 4):
        loads[at].wait()
    chunk = min(512, wu_ref.shape[1])

    @pl.loop(0, wu_ref.shape[1] // chunk)
    def _(at):
        lanes = pl.ds(pl.multiple_of(at * chunk, chunk), chunk)
        for block in range(row_blocks):
            rows = slice(block * QB, (block + 1) * QB)
            grad_act = nt_dot(low_ref[rows, :], wd_ref[lanes, :])
            hidden = hid_ref[rows, lanes]
            share = 0.5 + 0.5 * lax.erf(hidden * INV_SQRT2)
            slope = share + hidden * (INV_SQRT_2PI * jnp.exp(-0.5 * hidden * hidden))
            act_ref[rows, lanes] = (hidden * share).astype(BF16)
            grad_hid = (slope * grad_act).astype(BF16)
            dhid_ref[rows, lanes] = grad_hid
            part_ref[rows, :] += nt_dot(grad_hid, wu_ref[:, lanes])

    own = gdown_ref.shape[0]
    gdown_ref[...] = nn_dot(act_ref[:, pl.ds(pl.multiple_of(shard * own, own), own)].T, low_ref[...])
    loads[5].wait()
    loads[6].wait()
    own = gup_ref.shape[0]
    turn_ref[...] = n2_ref[...].T
    own_rows = pl.ds(pl.multiple_of(shard * own, own), own)

    @pl.loop(0, wu_ref.shape[1] // chunk)
    def _(at):
        lanes = pl.ds(pl.multiple_of(at * chunk, chunk), chunk)
        gup_ref[:, lanes] = nn_dot(turn_ref[own_rows, :], dhid_ref[:, lanes])

    loads[7].wait()

    @pl.loop(0, row_blocks)
    def _(block):
        rows = block_rows(block)
        back, gain = rms_back(part_ref[rows, :], x1_ref[rows, :], gains_ref[1:2, :])
        back = grad_ref[rows, :] + back
        grad_ref[rows, :] = back
        low = back.astype(BF16)
        low_ref[rows, :] = low
        ggains_ref[1:2, :] += gain
        dmixed_ref[:, rows] = nt_dot(low, wo_ref[...]).astype(BF16).T

    loads[8].wait()
    loads[9].wait()
    own = gout_ref.shape[0]
    own_rows = pl.ds(pl.multiple_of(shard * own, own), own)
    gout_ref[...] = nn_dot(mixed_ref[own_rows, :], low_ref[...])

    @pl.loop(0, width // (2 * HD))
    def _(pair):
        made = ([], [], [])
        places = [pl.ds(pl.multiple_of((pair * 2 + side) * HD, HD), HD) for side in range(2)]
        natural = [
            [ref[rows, :].T for ref in (qkv_ref.at[0], qkv_ref.at[1], qkv_ref.at[2], dmixed_ref)]
            for rows in places
        ]

        def products_of(side, block):
            count = (block + 1) * QB
            at = slice(block * QB, count)
            _, key, value, _ = natural[side]
            scores = nn_dot(key[:count], qkv_ref[0, places[side], at])
            return scores, nn_dot(value[:count], dmixed_ref[places[side], at])

        work = [(side, block) for side in range(2) for block in range(row_blocks)]
        ahead = products_of(*work[0])
        dquery_parts = []
        for place, (side, block) in enumerate(work):
            if block == 0:
                dquery_parts = []
                dkey = [None] * row_blocks
                dvalue = [None] * row_blocks
            scores, dprobs = ahead
            if place + 1 < len(work):
                ahead = products_of(*work[place + 1])
            count = (block + 1) * QB
            at = slice(block * QB, count)
            query, _, _, dmix = natural[side]
            probs = causal_tile(jnp.exp(scores - lse_ref[pair * 2 + side][:, at]), 0.0)
            delta = jnp.sum(probs * dprobs, axis=0, keepdims=True)
            dscores = (probs * (dprobs - delta)).astype(BF16)
            dquery_parts.append(nn_dot(qkv_ref[1, places[side], :count], dscores))
            more_key = nn_dot(dscores, query[at])
            more_value = nn_dot(probs.astype(BF16), dmix[at])
            for piece in range(block + 1):
                cut = slice(piece * QB, (piece + 1) * QB)
                if dkey[piece] is None:
                    dkey[piece], dvalue[piece] = more_key[cut], more_value[cut]
                else:
                    dkey[piece] = dkey[piece] + more_key[cut]
                    dvalue[piece] = dvalue[piece] + more_value[cut]
            if block == row_blocks - 1:
                cos_t, sin_t = cos_ref[...], sin_ref[...]
                dquery_t = jnp.concatenate(dquery_parts, axis=1) * HD ** (-0.5)
                dkey_t = jnp.concatenate(dkey, axis=0).T
                made[0].append(turned_back(dquery_t, cos_t, sin_t, half).T)
                made[1].append(turned_back(dkey_t, cos_t, sin_t, half).T)
                made[2].append(jnp.concatenate(dvalue, axis=0))
        for part in range(3):
            lanes = pl.ds(pl.multiple_of(part * width + pair * 2 * HD, 2 * HD), 2 * HD)
            dpacked_ref[:, lanes] = jnp.concatenate(made[part], axis=1).astype(BF16)

    for at in (10, 11, 12):
        loads[at].wait()
    own = gqkv_ref.shape[0]
    turn_ref[...] = n1_ref[...].T
    own_rows = pl.ds(pl.multiple_of(shard * own, own), own)

    @pl.loop(0, 3)
    def _(at):
        lanes = pl.ds(pl.multiple_of(at * width, width), width)
        gqkv_ref[:, lanes] = nn_dot(turn_ref[own_rows, :], dpacked_ref[:, lanes])

    @pl.loop(0, row_blocks)
    def _(block):
        rows = block_rows(block)
        back, gain = rms_back(
            nt_dot(dpacked_ref[rows, :], wqkv_ref[...]), x0_ref[rows, :].astype(F32), gains_ref[0:1, :]
        )
        dx0_ref[rows, :] = grad_ref[rows, :] + back
        ggains_ref[0:1, :] += gain


def layer_backward(shard_axis, slice_shapes, dn3_t, gains, cos_t, sin_t, projections, x0, kept):
    n1, qkv, lse, mixed_t, x1, n2, x2, _, hid = kept
    wqkv, wo, wu, wd = projections
    tokens, width = x2.shape
    shape = jax.ShapeDtypeStruct
    moved = (dn3_t, x2, hid, wd, wu, x1, n2, wo, mixed_t, qkv, x0, n1, wqkv)
    return pl.pallas_call(
        functools.partial(backward_kernel, shard_axis),
        in_specs=[ANYWHERE] * 13 + [VM] * 3 + [VM],
        out_specs=[VM] * 6,
        out_shape=[shape((tokens, width), F32)]
        + [shape(s, F32) for s in slice_shapes]
        + [shape((8, width), F32)],
        scratch_shapes=[pltpu.VMEM(m.shape, m.dtype) for m in moved]
        + [
            pltpu.VMEM((tokens, width), F32),
            pltpu.VMEM((tokens, width), F32),
            pltpu.VMEM((tokens, width), BF16),
            pltpu.VMEM(hid.shape, BF16),
            pltpu.VMEM(hid.shape, BF16),
            pltpu.VMEM((width, tokens), BF16),
            pltpu.VMEM((tokens, 3 * width), BF16),
            pltpu.VMEM((width, tokens), BF16),
            pltpu.SemaphoreType.DMA((13,)),
        ],
        compiler_params=pltpu.CompilerParams(vmem_limit_bytes=62 << 20),
        name="layer_backward",
    )(*moved, gains, cos_t, sin_t, lse)


def scatter_sketch_kernel(axis, rows, row_list, ids_ref, *refs):
    anys, starts = refs[0:11], refs[11:16]
    full_any, gq_ref, eq_ref, gs_ref, es_ref, sq_ref = refs[16:22]
    dx0_ref, whole_ref, table_err_ref = refs[22:25]
    grads, errs = refs[25:29], refs[29:33]
    load_sem, small_sem, store_sem = refs[33:36]
    places, _ = small_places(row_list)
    blocks = pl.cdiv(rows, TB)
    padded = blocks * TB
    tiles = [pl.ds(at * TB, min(TB, rows - at * TB)) for at in range(blocks)]
    smalls = [
        pltpu.make_async_copy(src, dst, small_sem.at[at])
        for at, (src, dst) in enumerate(zip((*anys[2:6], *anys[7:11], anys[1]), (*grads, *errs, dx0_ref)))
    ]
    for copy in smalls[:8]:
        copy.start()
    loads = [
        pltpu.make_async_copy(anys[0].at[tile, :], whole_ref.at[tile, :], load_sem.at[0, at])
        for at, tile in enumerate(tiles)
    ]
    err_loads = [
        pltpu.make_async_copy(anys[6].at[tile, :], table_err_ref.at[tile, :], load_sem.at[1, at])
        for at, tile in enumerate(tiles)
    ]
    for copy in loads:
        copy.start()
    smalls[8].start()
    for copy in err_loads:
        copy.start()
    if padded > rows:
        rest = pl.ds(rows, padded - rows)
        whole_ref[rest, :] = jnp.zeros((padded - rows, whole_ref.shape[1]), F32)
        table_err_ref[rest, :] = jnp.zeros((padded - rows, whole_ref.shape[1]), BF16)
    gs_ref[...] = jnp.zeros_like(gs_ref)
    es_ref[...] = jnp.zeros_like(es_ref)
    for copy in smalls[:8]:
        copy.wait()
    total = jnp.zeros(sq_ref.shape, F32)
    for k in range(4):
        grad = grads[k][...]
        start_t = starts[k + 1][...]
        at = pl.ds(places[k], row_list[k])
        gs_ref[:, at] = left_of(grad, start_t)
        es_ref[:, at] = left_of_bf16(errs[k][...], start_t)
        total = total + fold_squares(grad)
    sq_ref[...] = total
    smalls[8].wait()
    for copy in loads:
        copy.wait()
    first = lax.axis_index(axis) * rows if axis else 0

    @pl.loop(0, dx0_ref.shape[0] // 8)
    def _(group):
        base = pl.multiple_of(group * 8, 8)
        for side in range(8):
            row = ids_ref[base + side] - first
            row = jnp.where((row >= 0) & (row < rows), row, padded)
            whole_ref[pl.ds(row, 1), :] += dx0_ref[pl.ds(base + side, 1), :]

    stores = [
        pltpu.make_async_copy(whole_ref.at[tile, :], full_any.at[tile, :], store_sem.at[at])
        for at, tile in enumerate(tiles)
    ]
    for copy in stores:
        copy.start()
    for copy in err_loads:
        copy.wait()

    @pl.loop(0, blocks)
    def _(step):
        at = pl.multiple_of(step * TB, TB)
        start_t = starts[0][...]
        grad = whole_ref[pl.ds(at, TB), :]
        gq_ref[:, pl.ds(at, TB)] = left_of(grad, start_t)
        eq_ref[:, pl.ds(at, TB)] = left_of_bf16(table_err_ref[pl.ds(at, TB), :], start_t)
        sq_ref[...] += fold_squares(grad)

    for copy in stores:
        copy.wait()


def scatter_sketch(token_ids, table_grad, dx0, grads, errs, starts_t, axis):
    rows, width = table_grad.shape
    blocks = pl.cdiv(rows, TB)
    row_list = [g.shape[0] for g in grads]
    _, small = small_places(row_list)

    def whole_at(shape):
        return pl.BlockSpec(shape, lambda *_: (0,) * len(shape), pipeline_mode=pl.Buffered(1))

    shape = jax.ShapeDtypeStruct
    made = [(RK, blocks * TB)] * 2 + [(RK, small)] * 2 + [(8, 512)]
    full, *sketches = pl.pallas_call(
        functools.partial(scatter_sketch_kernel, axis, rows, row_list),
        grid_spec=pltpu.PrefetchScalarGridSpec(
            num_scalar_prefetch=1,
            grid=(1,),
            in_specs=[ANYWHERE] * 11 + [whole_at(s.shape) for s in starts_t],
            out_specs=[ANYWHERE] + [whole_at(m) for m in made],
            scratch_shapes=[
                pltpu.VMEM(dx0.shape, F32),
                pltpu.VMEM((blocks * TB + 8, width), F32),
                pltpu.VMEM((blocks * TB, width), BF16),
            ]
            + [pltpu.VMEM(g.shape, F32) for g in grads]
            + [pltpu.VMEM(e.shape, BF16) for e in errs[1:]]
            + [
                pltpu.SemaphoreType.DMA((2, blocks)),
                pltpu.SemaphoreType.DMA((9,)),
                pltpu.SemaphoreType.DMA((blocks,)),
            ],
        ),
        out_shape=[shape((rows, width), F32)] + [shape(m, F32) for m in made],
        compiler_params=pltpu.CompilerParams(vmem_limit_bytes=60 << 20),
        name="scatter_sketch",
    )(token_ids.reshape(-1), table_grad, dx0, *grads, *errs, *starts_t)
    return full, sketches


class Spread:
    def __init__(self, full, shards, sems):
        self.full, self.sems = full, sems
        self.shard, self.worker = lax.axis_index("voc"), lax.axis_index("rep")
        self.core = lax.rem(self.shard, 2)
        self.chip = self.shard // 2
        self.chips = shards // 2
        self.side = lax.rem(self.worker, 2)
        self.rows = full.shape[1] // 2

    def region(self, slot, side):
        return self.full.at[slot, pl.ds(pl.multiple_of(side * self.rows, self.rows), self.rows), :]

    def copy(self, ref, at, pair, peer):
        return pltpu.make_async_remote_copy(
            src_ref=ref, dst_ref=ref, send_sem=self.sems.at[2 * pair, at], recv_sem=self.sems.at[2 * pair + 1, at],
            device_id=peer, device_id_type=MESH_ID,
        )

    def source(self, at):
        return lax.rem(self.chip - at + self.chips, self.chips)

    def own_to_chip(self, at):
        peer = lax.rem(self.chip + at, self.chips) * 2 + self.core
        return self.copy(self.region(self.shard, self.side), at, 0, {"voc": peer})

    def from_chip(self, at):
        slot = self.source(at) * 2 + self.core
        return self.copy(self.region(slot, self.side), at, 0, {"voc": slot})

    def across(self, at, side):
        slot = self.source(at) * 2 + self.core
        return self.copy(self.region(slot, side), at, 1, {"rep": self.worker + 1 - 2 * self.side})

    def to_core(self, at, side, pair, core):
        slot = self.source(at) * 2 + core
        return self.copy(self.region(slot, side), at, pair, {"voc": self.shard + 1 - 2 * self.core})

    def own_to_core(self, slot):
        return self.copy(self.full.at[slot], 0, 2, {"voc": self.shard + 1 - 2 * self.core})

    def start(self):
        for at in range(1, self.chips):
            self.own_to_chip(at).start()
        self.own_to_core(self.shard).start()

    def relay(self):
        for at in range(1, self.chips):
            self.from_chip(at).wait_recv()
            self.across(at, self.side).start()
            self.to_core(at, self.side, 2, self.core).start()

    def relay_across(self):
        for at in range(1, self.chips):
            self.across(at, 1 - self.side).wait_recv()
            self.to_core(at, 1 - self.side, 3, self.core).start()

    def finish(self):
        self.own_to_core(self.shard + 1 - 2 * self.core).wait_recv()
        for at in range(1, self.chips):
            self.to_core(at, self.side, 2, 1 - self.core).wait_recv()
            self.to_core(at, 1 - self.side, 3, 1 - self.core).wait_recv()
        self.own_to_core(self.shard).wait_send()
        for at in range(1, self.chips):
            self.own_to_chip(at).wait_send()
            self.across(at, self.side).wait_send()
            self.to_core(at, self.side, 2, self.core).wait_send()
            self.to_core(at, 1 - self.side, 3, self.core).wait_send()


def greet_all(shards):
    barrier = pltpu.get_barrier_semaphore()
    me = lax.axis_index("voc")
    for step in range(1, shards):
        pl.semaphore_signal(
            barrier, inc=1, device_id={"voc": lax.rem(me + step, shards)}, device_id_type=MESH_ID
        )
    worker = lax.axis_index("rep")
    pl.semaphore_signal(
        barrier, inc=1, device_id={"rep": worker + 1 - 2 * lax.rem(worker, 2)}, device_id_type=MESH_ID
    )


def await_all(shards):
    pl.semaphore_wait(pltpu.get_barrier_semaphore(), shards)


def open_kernel(
    shards, axis, count, ids_ref, lanes_ref, table_any, weight_ref, x0_ref, full_ref,
    own_ref, rows_ref, mask_ref, table_ref, table_sem,
    half_in, sums, core_send, core_recv, chip_send, chip_recv, back_send, back_recv, sems,
):
    tile_rows = count // table_sem.shape[0]
    loads = [
        pltpu.make_async_copy(
            table_any.at[pl.ds(at * tile_rows, tile_rows), :],
            table_ref.at[pl.ds(at * tile_rows, tile_rows), :],
            table_sem.at[at],
        )
        for at in range(table_sem.shape[0])
    ]
    for load in loads:
        load.start()
    greet_all(shards)
    shard = lax.axis_index(axis)
    core = lax.rem(shard, 2)
    chip = shard // 2
    partner = shard + 1 - 2 * core
    chips = shards // 2
    half = x0_ref.shape[0] // 2
    own_half = pl.ds(pl.multiple_of(core * half, half), half)
    other_half = pl.ds(pl.multiple_of((1 - core) * half, half), half)
    spread = Spread(full_ref, shards, sems)
    full_ref[shard] = weight_ref[...].astype(BF16)
    local = lanes_ref[...] - shard * count
    inside = jnp.where((local >= 0) & (local < count), 1.0, 0.0)
    mask_ref[...] = jnp.broadcast_to(inside, (128, local.shape[1])).T

    def take(side):
        @pl.loop(0, half // 8)
        def _(group):
            base = pl.multiple_of(side * half + group * 8, 8)
            for within in range(8):
                row = jnp.clip(ids_ref[base + within] - shard * count, 0, count - 1)
                rows_ref[pl.ds(base + within, 1), :] = table_ref[pl.ds(row, 1), :]

        rows = pl.ds(pl.multiple_of(side * half, half), half)
        own_ref[rows, :] = jnp.where(mask_ref[rows, 0:1] > 0.5, rows_ref[rows, :], 0.0).astype(BF16)

    def chip_copy(peer_chip, slot, at):
        return pltpu.make_async_remote_copy(
            src_ref=sums.at[slot], dst_ref=sums.at[slot],
            send_sem=chip_send.at[at], recv_sem=chip_recv.at[at],
            device_id={axis: peer_chip * 2 + core}, device_id_type=MESH_ID,
        )

    def back_copy(rows):
        return pltpu.make_async_remote_copy(
            src_ref=x0_ref.at[rows, :], dst_ref=x0_ref.at[rows, :],
            send_sem=back_send, recv_sem=back_recv,
            device_id={axis: partner}, device_id_type=MESH_ID,
        )

    await_all(shards)
    spread.start()
    for load in loads:
        load.wait()
    take(1 - core)
    first = pltpu.make_async_remote_copy(
        src_ref=own_ref.at[other_half, :], dst_ref=half_in,
        send_sem=core_send, recv_sem=core_recv,
        device_id={axis: partner}, device_id_type=MESH_ID,
    )
    first.start()
    take(core)
    first.wait_recv()
    sums[chip] = (own_ref[own_half, :].astype(F32) + half_in[...].astype(F32)).astype(BF16)
    for at in range(1, chips):
        chip_copy(lax.rem(chip + at, chips), chip, at).start()
    first.wait_send()
    spread.relay()
    total = sums[chip].astype(F32)
    for at in range(1, chips):
        source = lax.rem(chip - at + chips, chips)
        chip_copy(source, source, at).wait_recv()
        total = total + sums[source].astype(F32)
    x0_ref[own_half, :] = total.astype(BF16)
    back_copy(own_half).start()
    spread.relay_across()
    back_copy(other_half).wait_recv()
    for at in range(1, chips):
        chip_copy(lax.rem(chip + at, chips), chip, at).wait_send()
    back_copy(own_half).wait_send()
    spread.finish()


def opening(token_ids, table, weight, shards, axis):
    tokens, (count, width) = token_ids.shape[1], table.shape
    chips = shards // 2
    shape = jax.ShapeDtypeStruct
    return pl.pallas_call(
        functools.partial(open_kernel, shards, axis, count),
        in_specs=[pl.BlockSpec(memory_space=pltpu.SMEM), VM, ANYWHERE, VM],
        out_specs=[VM] * 2,
        out_shape=[shape((tokens, width), BF16), shape((shards, *weight.shape), BF16)],
        scratch_shapes=[
            pltpu.VMEM((tokens, width), BF16),
            pltpu.VMEM((tokens, width), F32),
            pltpu.VMEM((tokens, 128), F32),
            pltpu.VMEM((count, width), F32),
            pltpu.SemaphoreType.DMA((4,)),
            pltpu.VMEM((tokens // 2, width), BF16),
            pltpu.VMEM((chips, tokens // 2, width), BF16),
        ]
        + [pltpu.SemaphoreType.DMA] * 2
        + [pltpu.SemaphoreType.DMA((max(2, chips),))] * 2
        + [pltpu.SemaphoreType.DMA] * 2
        + [pltpu.SemaphoreType.DMA((8, max(2, chips)))],
        compiler_params=pltpu.CompilerParams(
            collective_id=4, has_side_effects=True, vmem_limit_bytes=60 << 20
        ),
        name="opening",
    )(token_ids.reshape(-1), token_ids, table, weight)


TOKEN_LANES = 256


def vocab_block(rows):
    best = 8
    for size in range(8, 1025, 8):
        if rows % size == 0:
            best = size
    return best


def head_kernel(
    shards, axis,
    n3_ref, target_ref, table_ref,
    gtable_ref, dn3_any, loss_ref,
    dn3_ref, back_in, out_sem, kept, n3_t, tops, running, stats, z_ref, half_in, half_out,
    stat_send, stat_recv, core_send, core_recv, chip_send, chip_recv, back_send, back_recv,
):
    phase, step = pl.program_id(0), pl.program_id(1)
    last = pl.num_programs(1) - 1
    shard = lax.axis_index(axis)
    core = lax.rem(shard, 2)
    chip = shard // 2
    partner = shard + 1 - 2 * core
    chips = shards // 2
    tokens, width = n3_ref.shape
    block_rows = table_ref.shape[0]
    half = width // 2
    own_half = pl.ds(pl.multiple_of(core * half, half), half)
    other_half = pl.ds(pl.multiple_of((1 - core) * half, half), half)

    def stat_copy(peer, slot, at):
        return pltpu.make_async_remote_copy(
            src_ref=stats.at[slot], dst_ref=stats.at[slot],
            send_sem=stat_send.at[at], recv_sem=stat_recv.at[at],
            device_id={axis: peer}, device_id_type=MESH_ID,
        )

    def core_copy():
        return pltpu.make_async_remote_copy(
            src_ref=dn3_ref.at[other_half, :], dst_ref=half_in,
            send_sem=core_send, recv_sem=core_recv,
            device_id={axis: partner}, device_id_type=MESH_ID,
        )

    def chip_copy(peer_chip, slot, at):
        return pltpu.make_async_remote_copy(
            src_ref=half_out.at[slot], dst_ref=half_out.at[slot],
            send_sem=chip_send.at[at], recv_sem=chip_recv.at[at],
            device_id={axis: peer_chip * 2 + core}, device_id_type=MESH_ID,
        )

    def back_copy():
        return pltpu.make_async_remote_copy(
            src_ref=dn3_ref.at[own_half, :], dst_ref=back_in,
            send_sem=back_send, recv_sem=back_recv,
            device_id={axis: partner}, device_id_type=MESH_ID,
        )

    @pl.when((phase == 0) & (step == 0))
    def _():
        barrier = pltpu.get_barrier_semaphore()
        for at in range(1, shards):
            pl.semaphore_signal(
                barrier, inc=1,
                device_id={axis: lax.rem(shard + at, shards)}, device_id_type=MESH_ID,
            )
        n3_t[...] = n3_ref[...].T
        row_at = lax.broadcasted_iota(jnp.int32, running.shape, 0)
        running[...] = jnp.where(row_at == 0, -1e30, 0.0)
        dn3_ref[...] = jnp.zeros_like(dn3_ref)

    def hits(lanes):
        row_at = lax.broadcasted_iota(jnp.int32, (block_rows, TOKEN_LANES), 0)
        return row_at == target_ref[:, lanes] - (shard * (last + 1) + step) * block_rows

    @pl.when(phase == 0)
    def _():
        table = table_ref[...].astype(BF16)
        ahead = nn_dot(table, n3_t[:, :TOKEN_LANES])
        for start in range(0, tokens, TOKEN_LANES):
            lanes = slice(start, start + TOKEN_LANES)
            logits = ahead
            if start + TOKEN_LANES < tokens:
                ahead = nn_dot(table, n3_t[:, start + TOKEN_LANES : start + 2 * TOKEN_LANES])
            top = jnp.max(logits, axis=0, keepdims=True)
            weight = jnp.exp(logits - top)
            kept[step, :, lanes] = weight
            tops[step, :, lanes] = top
            total = jnp.sum(weight, axis=0, keepdims=True)
            picked = jnp.sum(jnp.where(hits(lanes), logits, 0.0), axis=0, keepdims=True)
            old = running[0:1, lanes]
            new = jnp.maximum(old, top)
            running[0:1, lanes] = new
            running[1:2, lanes] = running[1:2, lanes] * jnp.exp(old - new) + total * jnp.exp(top - new)
            running[2:3, lanes] += picked

    @pl.when((phase == 1) & (step == 0))
    def _():
        stats[shard] = running[...]
        pl.semaphore_wait(pltpu.get_barrier_semaphore(), shards - 1)
        sends = [stat_copy(lax.rem(shard + at, shards), shard, at) for at in range(1, shards)]
        for send in sends:
            send.start()
        for at in range(1, shards):
            source = lax.rem(shard - at + shards, shards)
            stat_copy(source, source, at).wait_recv()
        for send in sends:
            send.wait_send()
        top = stats[0, 0:1, :]
        for at in range(1, shards):
            top = jnp.maximum(top, stats[at, 0:1, :])
        total, picked = jnp.zeros_like(top), jnp.zeros_like(top)
        for at in range(shards):
            total = total + stats[at, 1:2, :] * jnp.exp(stats[at, 0:1, :] - top)
            picked = picked + stats[at, 2:3, :]
        z = top + jnp.log(total)
        z_ref[...] = z
        terms = (z - picked) + ZLOSS_WEIGHT * (z * z)
        loss = jnp.sum(terms, axis=1, keepdims=True) * (1.0 / tokens)
        loss_ref[...] = jnp.broadcast_to(loss, loss_ref.shape)

    def grad_logits(lanes):
        z = z_ref[:, lanes]
        factor = jnp.exp(tops[step, :, lanes] - z) * (1.0 + 2.0 * ZLOSS_WEIGHT * z) * (1.0 / tokens)
        return (kept[step, :, lanes] * factor - jnp.where(hits(lanes), 1.0 / tokens, 0.0)).astype(BF16)

    @pl.when(phase == 1)
    def _():
        table_t = table_ref[...].astype(BF16).T
        for start in range(0, tokens, TOKEN_LANES):
            lanes = slice(start, start + TOKEN_LANES)
            dn3_ref[:, lanes] += nn_dot(table_t, grad_logits(lanes))

    @pl.when((phase == 2) & (step == 0))
    def _():
        core_copy().start()

    @pl.when((phase == 2) & (step == jnp.minimum(2, last)))
    def _():
        core_copy().wait()
        half_out[chip] = (dn3_ref[own_half, :] + half_in[...]).astype(BF16)
        for at in range(1, chips):
            chip_copy(lax.rem(chip + at, chips), chip, at).start()

    @pl.when(phase == 2)
    def _():
        total = None
        for start in range(0, tokens, TOKEN_LANES):
            lanes = slice(start, start + TOKEN_LANES)
            part = nn_dot(grad_logits(lanes), n3_ref[lanes, :])
            total = part if total is None else total + part
        gtable_ref[...] = total

    @pl.when((phase == 2) & (step == last))
    def _():
        for at in range(1, chips):
            source = lax.rem(chip - at + chips, chips)
            chip_copy(source, source, at).wait_recv()
        for at in range(1, chips):
            chip_copy(lax.rem(chip + at, chips), chip, at).wait_send()
        whole_sum = half_out[0].astype(F32)
        for at in range(1, chips):
            whole_sum = whole_sum + half_out[at].astype(F32)
        dn3_ref[own_half, :] = whole_sum
        back_copy().start()
        puts = [
            pltpu.make_async_copy(dn3_ref.at[own_half, :], dn3_any.at[own_half, :], out_sem.at[0]),
            pltpu.make_async_copy(back_in, dn3_any.at[other_half, :], out_sem.at[1]),
        ]
        puts[0].start()
        back_copy().wait()
        puts[1].start()
        for put in puts:
            put.wait()


def vocabulary_head(n3, targets, table, shards, axis):
    rows, width = table.shape
    tokens = n3.shape[0]
    size = vocab_block(rows)
    blocks = rows // size
    shape = jax.ShapeDtypeStruct
    return pl.pallas_call(
        functools.partial(head_kernel, shards, axis),
        grid=(3, blocks),
        in_specs=[
            whole((tokens, width)),
            whole((1, tokens)),
            pl.BlockSpec((size, width), lambda p, i: (jnp.where(p == 2, blocks - 1, i), 0)),
        ],
        out_specs=[
            pl.BlockSpec((size, width), lambda p, i: (jnp.where(p == 2, i, 0), 0)),
            pl.BlockSpec(memory_space=pl.ANY),
            whole((8, 128)),
        ],
        out_shape=[shape((rows, width), F32), shape((width, tokens), F32), shape((8, 128), F32)],
        scratch_shapes=[
            pltpu.VMEM((width, tokens), F32),
            pltpu.VMEM((width // 2, tokens), F32),
            pltpu.SemaphoreType.DMA((2,)),
            pltpu.VMEM((blocks, size, tokens), F32),
            pltpu.VMEM((width, tokens), BF16),
            pltpu.VMEM((blocks, 1, tokens), F32),
            pltpu.VMEM((8, tokens), F32),
            pltpu.VMEM((shards, 8, tokens), F32),
            pltpu.VMEM((1, tokens), F32),
            pltpu.VMEM((width // 2, tokens), F32),
            pltpu.VMEM((shards // 2, width // 2, tokens), BF16),
        ]
        + [pltpu.SemaphoreType.DMA((shards,))] * 2
        + [pltpu.SemaphoreType.DMA] * 2
        + [pltpu.SemaphoreType.DMA((max(2, shards // 2),))] * 2
        + [pltpu.SemaphoreType.DMA] * 2,
        compiler_params=pltpu.CompilerParams(
            collective_id=3, has_side_effects=True, vmem_limit_bytes=62 << 20
        ),
        name="vocabulary_head",
    )(n3, targets, table)


def body(
    token_ids,
    target_ids,
    embedding,
    w_qkv,
    w_out,
    w_up,
    w_down,
    norm_gains,
    embed_mom,
    qkv_mom,
    out_mom,
    up_mom,
    down_mom,
    gain_mom,
    embed_err,
    qkv_err,
    out_err,
    up_err,
    down_err,
    embed_factor,
    qkv_factor,
    out_factor,
    up_factor,
    down_factor,
):
    seq_count, length = token_ids.shape
    tok_count = seq_count * length
    workers = lax.axis_size("rep")
    slices = (w_qkv, w_out, w_up, w_down)
    shards = lax.axis_size("voc")
    x0, qkv_all = opening(token_ids, embedding, w_qkv, shards, "voc")
    wqkv = qkv_all.reshape(-1, w_qkv.shape[1])
    half = HD // 2
    inverse = np.float32(10000.0) ** (-np.arange(half, dtype=np.float32) / np.float32(half))
    angles = inverse[:, None] * np.arange(length, dtype=np.float32)[None, :]
    cos_t, sin_t = jnp.asarray(np.cos(angles)), jnp.asarray(np.sin(angles))
    *kept, n3, wo, wu, wd, hid = layer_forward(
        x0, norm_gains, cos_t, sin_t, wqkv, slices[1:], shards, "voc"
    )
    kept = (*kept, n3, hid)
    projections = (wqkv, *(w.reshape(-1, w.shape[2]) for w in (wo, wu, wd)))
    grad_table_head, dn3_t, loss_tile = vocabulary_head(
        n3, target_ids.reshape(1, -1), embedding, lax.axis_size("voc"), "voc"
    )
    grad_in, *grad_mats, grad_gains = layer_backward(
        "voc", [w.shape for w in slices], dn3_t, norm_gains, cos_t, sin_t, projections, x0, kept
    )
    errors = [e[0] for e in (embed_err, qkv_err, out_err, up_err, down_err)]
    starts_t = [
        f[0].T for f in (embed_factor, qkv_factor, out_factor, up_factor, down_factor)
    ]
    full_grad, sketches = scatter_sketch(
        token_ids, grad_table_head, grad_in, grad_mats, errors, starts_t, "voc"
    )
    new_errors, new_moments, changed, rights, gain_change, next_gain_mom, loss, norm = settle(
        loss_tile,
        sketches,
        grad_gains,
        gain_mom,
        [full_grad, *grad_mats],
        errors,
        (embed_mom, qkv_mom, out_mom, up_mom, down_mom),
        slices,
        workers,
        shards,
    )
    return (
        loss,
        norm,
        *changed,
        gain_change,
        *new_moments,
        next_gain_mom,
        *(e[None] for e in new_errors),
        *(r.T[None] for r in rights),
    )


def solution(mesh):
    in_specs = (
        P("rep", None),
        P("rep", None),
        P("voc", None),
        P("voc", None),
        P("voc", None),
        P("voc", None),
        P("voc", None),
        P(),
        P("voc", None),
        P("voc", None),
        P("voc", None),
        P("voc", None),
        P("voc", None),
        P(),
        P("rep", "voc", None),
        P("rep", "voc", None),
        P("rep", "voc", None),
        P("rep", "voc", None),
        P("rep", "voc", None),
        P("voc", None, None),
        P("voc", None, None),
        P("voc", None, None),
        P("voc", None, None),
        P("voc", None, None),
    )
    out_specs = (
        P("rep"),
        P("rep"),
        P("voc", None),
        P("voc", None),
        P("voc", None),
        P("voc", None),
        P("voc", None),
        P(),
        P("voc", None),
        P("voc", None),
        P("voc", None),
        P("voc", None),
        P("voc", None),
        P(),
        P("rep", "voc", None),
        P("rep", "voc", None),
        P("rep", "voc", None),
        P("rep", "voc", None),
        P("rep", "voc", None),
        P("voc", None, None),
        P("voc", None, None),
        P("voc", None, None),
        P("voc", None, None),
        P("voc", None, None),
    )
    return jax.shard_map(body, mesh=mesh, in_specs=in_specs, out_specs=out_specs, check_vma=False)
```
